32 devices in a mesh: dp: 8 (over y, x, core), tensor: 4 (over z).
Axes of the slice: x: 2, y: 2, z: 4, core: 2. Of those that a mesh axis runs over, the one named last changes fastest.
Arguments:
- content_stream: bfloat16 [16, 512, 768], P('dp', 'tensor'), may hold values from -6 to 6
- query_stream: bfloat16 [16, 512, 768], P('dp', 'tensor'), may hold values from -6 to 6
- memory: bfloat16 [16, 512, 768], P('dp', 'tensor'), may hold values from -6 to 6
- content_tangent: bfloat16 [16, 512, 768], P('dp', 'tensor'), may hold values from -6 to 6
- query_tangent: bfloat16 [16, 512, 768], P('dp', 'tensor'), may hold values from -6 to 6
- seq_lengths: int32 [16], P('dp'), may hold values from 128 to 512, as said below
- factor_order: int32 [16, 512], P('dp'), may hold values from 0 to 511, each once within a row
- memory_lengths: int32 [16], P('dp'), may hold values from 64 to 512, as said below
- slot_sequence: int32 [16], replicated, may hold values from 0 to 15, each once
- query_weight: bfloat16 [768, 768], P('dp', 'tensor'), may hold values from -0.21875 to 0.21875
- key_weight: bfloat16 [768, 768], P('dp', 'tensor'), may hold values from -0.21875 to 0.21875
- value_weight: bfloat16 [768, 768], P('dp', 'tensor'), may hold values from -0.21875 to 0.21875
- pos_weight: bfloat16 [768, 768], P('dp', 'tensor'), may hold values from -0.21875 to 0.21875
- out_weight: bfloat16 [768, 768], P('dp', 'tensor'), may hold values from -2 to 2
- up_weight: bfloat16 [768, 3072], P('dp', 'tensor'), may hold values from -0.21875 to 0.21875
- up_bias: float32 [3072], replicated, may hold values from -3 to 3
- down_weight: bfloat16 [768, 3072], P('dp', 'tensor'), may hold values from -0.109375 to 0.109375
- down_bias: float32 [768], replicated, may hold values from -2 to 2
- word_bias: float32 [12, 64], replicated, may hold values from -3 to 3
- pos_bias: float32 [12, 64], replicated, may hold values from -3 to 3
- first_gain: float32 [768], replicated, may hold values from 0.5 to 1.5
- first_shift: float32 [768], replicated, may hold values from -2 to 2
- second_gain: float32 [768], replicated, may hold values from 0.5 to 1.5
- second_shift: float32 [768], replicated, may hold values from -2 to 2
Outputs:
- content_out: bfloat16 [16, 512, 768], P('dp', 'tensor')
- query_out: bfloat16 [16, 512, 768], P('dp', 'tensor')
- content_grad: bfloat16 [16, 512, 768], P('dp', 'tensor')
- query_grad: bfloat16 [16, 512, 768], P('dp', 'tensor')
- grad_query: float32 [768, 768], P('dp', 'tensor')
- grad_key: float32 [768, 768], P('dp', 'tensor')
- grad_value: float32 [768, 768], P('dp', 'tensor')
- grad_pos: float32 [768, 768], P('dp', 'tensor')
- grad_out: float32 [768, 768], P('dp', 'tensor')
- grad_up: float32 [768, 3072], P('dp', 'tensor')
- grad_up_bias: float32 [3072], replicated
- grad_down: float32 [768, 3072], P('dp', 'tensor')
- grad_down_bias: float32 [768], replicated
- grad_word: float32 [12, 64], replicated
- grad_pos_bias: float32 [12, 64], replicated
- grad_first_gain: float32 [768], replicated
- grad_first_shift: float32 [768], replicated
- grad_second_gain: float32 [768], replicated
- grad_second_shift: float32 [768], replicated
The draws below stay inside these ranges and needn't reach their ends.
Inputs may be any that keep to these rules, and one draw needn't show every extreme that they name: Each row of factor_order holds every number from 0 to 511 once. slot_sequence holds every sequence number once. Positions at or past seq_lengths[s] are padding and never visible as keys. The valid memory rows of a slot are its last memory_lengths rows.
All inputs are finite; a program needn't handle non-finite values.
Results may differ from the reference program's by a relative error of at most 0.017.
Values may be sent and summed in bfloat16 or wider, within the bound.
A program may use at most 256 MiB of HBM per device.

```python
import jax
import jax.numpy as jnp
from jax import lax

D = 768
HEADS = 12
DH = 64
FF = 3072
LEN = 512
MEM = 512
SEQS = 16


def bounded_counts(key, lowest, highest):
    values = jax.random.randint(key, (SEQS,), lowest, highest + 1)
    first = jax.random.randint(jax.random.fold_in(key, 1), (), 0, SEQS)
    other = (first + 1 + jax.random.randint(jax.random.fold_in(key, 2), (), 0, SEQS - 1)) % SEQS
    return values.at[first].set(highest).at[other].set(lowest)


def draw_seq_lengths(key, part):
    return bounded_counts(jax.random.fold_in(key, 11), LEN // 4, LEN)


def draw_memory_lengths(key, part):
    return bounded_counts(jax.random.fold_in(key, 23), MEM // 8, MEM)


def steps_of(rng, shape, cuts, low, largest):
    factor_of = 1.0
    for axis_at, shards_of in cuts:
        steps = jax.random.uniform(jax.random.fold_in(jax.random.fold_in(rng, 6), axis_at), (shards_of,), jnp.float32, low / len(cuts), largest / len(cuts))
        factor_of = factor_of * jnp.repeat(jnp.exp(steps), shape[axis_at] // shards_of).reshape((-1,) + (1,) * (len(shape) - 1 - axis_at))
    return factor_of


def scatter_about(own_key, dims, deviation, reach, split=(), kind=jnp.bfloat16):
    array = jax.random.normal(own_key, dims, jnp.float32) * deviation
    if len(split) > 0:
        array = steps_of(own_key, dims, split, -0.22, 0.18) * array
    return jnp.clip(array, min=-reach, max=reach).astype(kind)


def setup_inputs(seed: int = 0) -> dict:
    key_list = jax.random.split(jax.random.key(seed), 25)
    content_stream = scatter_about(key_list[0], (SEQS, LEN, D), 1.0, 6.0, ((0, 8), (1, 4)))
    query_stream = scatter_about(key_list[1], (SEQS, LEN, D), 1.0, 6.0, ((0, 8), (1, 4)))
    memory = scatter_about(key_list[2], (SEQS, MEM, D), 1.0, 6.0, ((0, 8), (1, 4)))
    content_tangent = scatter_about(key_list[3], (SEQS, LEN, D), 1.0, 6.0, ((0, 8), (1, 4)))
    query_tangent = scatter_about(key_list[4], (SEQS, LEN, D), 1.0, 6.0, ((0, 8), (1, 4)))
    seq_lengths = draw_seq_lengths(jax.random.fold_in(key_list[24], 71), 0)
    factor_order = jax.vmap(lambda own: jax.random.permutation(own, LEN))(jax.random.split(key_list[6], SEQS)).reshape((SEQS, LEN)).astype(jnp.int32)
    memory_lengths = draw_memory_lengths(jax.random.fold_in(key_list[24], 71), 0)
    slot_sequence = jax.random.permutation(key_list[8], SEQS).astype(jnp.int32)
    query_weight = scatter_about(key_list[9], (D, HEADS * DH), D ** -0.5, 0.21875, ((0, 8), (1, 4)))
    key_weight = scatter_about(key_list[10], (D, HEADS * DH), D ** -0.5, 0.21875, ((0, 8), (1, 4)))
    value_weight = scatter_about(key_list[11], (D, HEADS * DH), D ** -0.5, 0.21875, ((0, 8), (1, 4)))
    pos_weight = scatter_about(key_list[12], (D, HEADS * DH), D ** -0.5, 0.21875, ((0, 8), (1, 4)))
    out_weight = scatter_about(key_list[13], (D, HEADS * DH), (DH // 8) ** -0.5, 2.0, ((0, 8), (1, 4)))
    up_weight = scatter_about(key_list[14], (D, FF), D ** -0.5, 0.21875, ((0, 8), (1, 4)))
    up_bias = scatter_about(key_list[15], (FF,), 0.5, 3.0, (), jnp.float32)
    down_weight = scatter_about(key_list[16], (D, FF), FF ** -0.5, 0.109375, ((0, 8), (1, 4)))
    down_bias = scatter_about(key_list[17], (D,), 0.3, 2.0, (), jnp.float32)
    word_bias = scatter_about(key_list[18], (HEADS, DH), 0.5, 3.0, (), jnp.float32)
    pos_bias = scatter_about(key_list[19], (HEADS, DH), 0.5, 3.0, (), jnp.float32)
    first_gain = jnp.clip(1.0 + 0.1 * jax.random.normal(key_list[20], (D,), jnp.float32), 0.5, 1.5)
    first_shift = scatter_about(key_list[21], (D,), 0.3, 2.0, (), jnp.float32)
    second_gain = jnp.clip(1.0 + 0.1 * jax.random.normal(key_list[22], (D,), jnp.float32), 0.5, 1.5)
    second_shift = scatter_about(key_list[23], (D,), 0.3, 2.0, (), jnp.float32)
    return {"content_stream": content_stream, "query_stream": query_stream, "memory": memory, "content_tangent": content_tangent, "query_tangent": query_tangent, "seq_lengths": seq_lengths, "factor_order": factor_order, "memory_lengths": memory_lengths, "slot_sequence": slot_sequence, "query_weight": query_weight, "key_weight": key_weight, "value_weight": value_weight, "pos_weight": pos_weight, "out_weight": out_weight, "up_weight": up_weight, "up_bias": up_bias, "down_weight": down_weight, "down_bias": down_bias, "word_bias": word_bias, "pos_bias": pos_bias, "first_gain": first_gain, "first_shift": first_shift, "second_gain": second_gain, "second_shift": second_shift}


EPS = 1e-06
HIGH = lax.Precision.HIGHEST

@jax.custom_vjp
def low(v):
    return lax.optimization_barrier(v.astype(jnp.bfloat16)).astype(jnp.float32)

@jax.custom_vjp
def low_back(v):
    return v

def low_keep(v):
    return (low(v), None)

def low_pass(kept, grad):
    return (grad,)

def back_keep(v):
    return (v, None)

def back_low(kept, grad):
    return (low(grad),)
low.defvjp(low_keep, low_pass)
low_back.defvjp(back_keep, back_low)

def matmul(left, right):
    return jnp.dot(left, right, precision=HIGH, preferred_element_type=jnp.float32)

def positions(count, first, width):
    dist = jnp.arange(count, dtype=jnp.float32) + first
    half = width // 2
    freq = 1.0 / 10000.0 ** (jnp.arange(half, dtype=jnp.float32) * (2.0 / width))
    angle = dist[:, None] * freq[None, :]
    return jnp.concatenate([jnp.sin(angle), jnp.cos(angle)], axis=1)

def norm_apply(value, gain, shift):
    center = value - lax.optimization_barrier(jnp.mean(value, axis=-1, keepdims=True))
    spread = lax.optimization_barrier(jnp.mean(center * center, axis=-1, keepdims=True))
    return center * lax.rsqrt(spread + EPS) * gain + shift

def attend(query, word, pos, keys, values, relative, rank, key_rank, mem_ok, content_ok, strict):
    block = min(512, LEN)
    klen = MEM + LEN
    q_word = low(query + word.reshape(-1))
    q_pos = low(query + pos.reshape(-1))
    keys3 = keys.reshape(klen, HEADS, DH)
    values3 = values.reshape(klen, HEADS, DH)
    key_pos = jnp.arange(klen, dtype=jnp.int32)

    def one(start):
        qw = lax.dynamic_slice_in_dim(q_word, start, block, 0).reshape(block, HEADS, DH)
        qr = lax.dynamic_slice_in_dim(q_pos, start, block, 0).reshape(block, HEADS, DH)
        rel = lax.dynamic_slice_in_dim(relative, start, klen + block - 1, 0).reshape(klen + block - 1, HEADS, DH)
        rank_blk = lax.dynamic_slice_in_dim(rank, start, block, 0)
        content = jnp.einsum('ihd,jhd->hij', qw, keys3, precision=HIGH)
        raw = jnp.einsum('ihd,rhd->hir', qr, rel, precision=HIGH)
        index = klen - 1 + jnp.arange(block, dtype=jnp.int32)[:, None] - key_pos[None, :]
        index = jnp.broadcast_to(index[None], (HEADS, block, klen))
        score = 0.125 * low_back(content + jnp.take_along_axis(raw, index, axis=2))
        if strict:
            earlier = key_rank[None, :] < rank_blk[:, None]
        else:
            earlier = key_rank[None, :] <= rank_blk[:, None]
        visible = mem_ok[None, :] | content_ok[None, :] & earlier
        masked = jnp.where(visible[None], score, -1e+30)
        top = lax.optimization_barrier(jnp.max(masked, axis=2, keepdims=True))
        expo = jnp.exp(masked - top)
        prob = expo / lax.optimization_barrier(jnp.sum(expo, axis=2, keepdims=True))
        result = jnp.einsum('hij,jhd->ihd', low(prob), values3, precision=HIGH)
        return result.reshape(block, HEADS * DH)
    starts = jnp.arange(LEN // block, dtype=jnp.int32) * block
    return lax.map(jax.checkpoint(one), starts).reshape(LEN, HEADS * DH)

def layer(params, content, query, memory, length, rank, mem_valid):
    query_w, key_w, value_w, pos_w, out_w, up_w, up_b, down_w, down_b, word, pos, gain_one, shift_one, gain_two, shift_two = params
    klen = MEM + LEN
    context = jnp.concatenate([memory, content], 0)
    keys = low(low_back(matmul(context, key_w)))
    values = low(low_back(matmul(context, value_w)))
    table = low(positions(MEM + 2 * LEN, 1 - LEN, D))
    relative = low(low_back(matmul(table, pos_w)))
    key_pos = jnp.arange(klen, dtype=jnp.int32)
    mem_ok = (key_pos < MEM) & (key_pos >= MEM - mem_valid)
    content_ok = (key_pos >= MEM) & (key_pos - MEM < length)
    key_rank = jnp.concatenate([jnp.zeros((MEM,), jnp.int32), rank.astype(jnp.int32)])
    results = []
    for stream, strict in ((content, False), (query, True)):
        proj = low_back(matmul(stream, query_w))
        vec = low(low_back(attend(proj, word, pos, keys, values, relative, rank, key_rank, mem_ok, content_ok, strict)))
        mixed = low_back(matmul(vec, out_w.T))
        first = norm_apply(mixed + stream, gain_one, shift_one)
        upper = low_back(matmul(low(first), up_w)) + up_b
        act = low(jax.nn.gelu(upper, approximate=True))
        down = low_back(matmul(act, down_w.T)) + down_b
        results.append(norm_apply(down + first, gain_two, shift_two))
    return (results[0], results[1])

def reference(content_stream, query_stream, memory, content_tangent, query_tangent, seq_lengths, factor_order, memory_lengths, slot_sequence, query_weight, key_weight, value_weight, pos_weight, out_weight, up_weight, up_bias, down_weight, down_bias, word_bias, pos_bias, first_gain, first_shift, second_gain, second_shift):
    params = tuple((item.astype(jnp.float32) for item in (query_weight, key_weight, value_weight, pos_weight, out_weight, up_weight, up_bias, down_weight, down_bias, word_bias, pos_bias, first_gain, first_shift, second_gain, second_shift)))
    slot_of = jnp.zeros((SEQS,), jnp.int32).at[slot_sequence].set(jnp.arange(SEQS, dtype=jnp.int32))

    def step(total, seq):
        slot = slot_of[seq]
        content = content_stream[seq].astype(jnp.float32)
        query = query_stream[seq].astype(jnp.float32)
        mem = memory[slot].astype(jnp.float32)
        length = seq_lengths[seq]
        rank = factor_order[seq]
        mem_valid = memory_lengths[slot]

        def forward(prm, left, right):
            return layer(prm, left, right, mem, length, rank, mem_valid)
        outs, pull = jax.vjp(forward, params, content, query)
        d_params, d_content, d_query = pull((content_tangent[seq].astype(jnp.float32), query_tangent[seq].astype(jnp.float32)))
        total = tuple((acc + add for acc, add in zip(total, d_params)))
        return (total, (outs[0].astype(jnp.bfloat16), outs[1].astype(jnp.bfloat16), d_content.astype(jnp.bfloat16), d_query.astype(jnp.bfloat16)))
    zeros = tuple((jnp.zeros_like(item) for item in params))
    total, (content_out, query_out, content_grad, query_grad) = lax.scan(step, zeros, jnp.arange(SEQS, dtype=jnp.int32))
    return (content_out, query_out, content_grad, query_grad, total[0], total[1], total[2], total[3], total[4], total[5], total[6], total[7], total[8], total[9], total[10], total[11], total[12], total[13], total[14])
```

```python
import functools

import jax
import jax.numpy as jnp
from jax import lax
from jax.experimental import pallas as pl
from jax.experimental.pallas import tpu as pltpu
from jax.sharding import PartitionSpec as P

HEADS = 12
DH = 64
PAIR = 2 * DH
EPS = 1e-06
BF = jnp.bfloat16
F32 = jnp.float32
LIMIT = 60 * 1024 * 1024


def nn(left, right):
    return jnp.dot(left, right, preferred_element_type=F32)


def nt(left, right):
    return lax.dot_general(left, right, (((1,), (1,)), ((), ())), preferred_element_type=F32)


def tn(left, right):
    return lax.dot_general(left, right, (((0,), (0,)), ((), ())), preferred_element_type=F32)


def tt(left, right):
    return lax.dot_general(left, right, (((0,), (1,)), ((), ())), preferred_element_type=F32)


def reversed_table(count, first, width):
    dist = first - jnp.arange(count, dtype=F32)
    half = width // 2
    freq = 1.0 / 10000.0 ** (jnp.arange(half, dtype=F32) * (2.0 / width))
    angle = dist[:, None] * freq[None, :]
    return jnp.concatenate([jnp.sin(angle), jnp.cos(angle)], axis=1).astype(BF)


def head_lanes(array, head):
    lane = lax.broadcasted_iota(jnp.int32, array.shape, 1)
    return jnp.where((lane >= DH) == (head == 1), array, jnp.zeros_like(array))


def attend_forward_kernel(
    block, qw_ref, qp_ref, k_ref, v_ref, rel_ref, thr_ref, kr_ref, vec_ref, prob_ref
):
    rows, klen = qw_ref.shape[0], k_ref.shape[0]
    width = klen + block
    keys, values = k_ref[...], v_ref[...]
    for part in range(rows // block):
        at = slice(part * block, (part + 1) * block)
        first = rows - (part + 1) * block
        qw, qp = qw_ref[at, :], qp_ref[at, :]
        rel = rel_ref[first : first + width, :]
        seen = kr_ref[...] < thr_ref[at, :]
        vecs = []
        for head in range(2):
            raw = nt(head_lanes(qp, head), rel)
            moved = pltpu.roll(raw, 0, 1, stride=1, stride_axis=0)[:, block:]
            score = nt(head_lanes(qw, head), keys) + moved
            score = jnp.where(seen, score, -1e30)
            expo = jnp.exp(score - jnp.max(score, axis=1, keepdims=True))
            prob = (expo * (1.0 / jnp.sum(expo, axis=1, keepdims=True))).astype(BF)
            prob_ref[head, at, :] = prob
            vecs.append(nn(prob, values))
        lane = lax.broadcasted_iota(jnp.int32, vecs[0].shape, 1)
        vec_ref[at, :] = jnp.where(lane < DH, vecs[0], vecs[1]).astype(BF)


def attend_forward(qw, qp, keys, values, rel, thr, key_rank, block):
    rows, width = qw.shape
    klen, span = keys.shape[0], rel.shape[0]
    col = lambda count: pl.BlockSpec((count, PAIR), lambda p: (0, p))
    return pl.pallas_call(
        functools.partial(attend_forward_kernel, block),
        grid=(width // PAIR,),
        in_specs=[
            col(rows),
            col(rows),
            col(klen),
            col(klen),
            col(span),
            pl.BlockSpec((rows, 1), lambda p: (0, 0)),
            pl.BlockSpec((1, klen), lambda p: (0, 0)),
        ],
        out_specs=[col(rows), pl.BlockSpec((2, rows, klen), lambda p: (p, 0, 0))],
        out_shape=[
            jax.ShapeDtypeStruct((rows, width), BF),
            jax.ShapeDtypeStruct((width // DH, rows, klen), BF),
        ],
        compiler_params=pltpu.CompilerParams(vmem_limit_bytes=LIMIT),
        cost_estimate=pl.CostEstimate(
            flops=8 * rows * klen * width, bytes_accessed=16 << 20, transcendentals=12 * rows * klen
        ),
        name="attend_forward",
    )(qw, qp, keys, values, rel, thr, key_rank)


def attend_backward_kernel(
    block,
    prob_ref,
    gvec_ref,
    qw_ref,
    qp_ref,
    k_ref,
    v_ref,
    rel_ref,
    dproj_ref,
    dk_ref,
    dv_ref,
    drel_ref,
    bias_ref,
    rel_acc,
):
    rows, klen = qw_ref.shape[0], k_ref.shape[0]
    width = klen + block
    keys, values = k_ref[...], v_ref[...]
    row = lax.broadcasted_iota(jnp.int32, (block, block), 0)
    col = lax.broadcasted_iota(jnp.int32, (block, block), 1)
    mirror = (row + col == block - 1).astype(BF)
    rel_acc[...] = jnp.zeros_like(rel_acc)
    d_keys, d_values = [None, None], [None, None]
    word_sum = jnp.zeros((1, PAIR), F32)
    pos_sum = jnp.zeros((1, PAIR), F32)
    for part in range(rows // block):
        at = slice(part * block, (part + 1) * block)
        first = rows - (part + 1) * block
        gvec, qw = gvec_ref[at, :], qw_ref[at, :]
        gvec_t = jnp.transpose(gvec.astype(F32)).astype(BF)
        qw_t = jnp.transpose(qw.astype(F32)).astype(BF)
        qp_t = jnp.transpose(nn(mirror, qp_ref[at, :])).astype(BF)
        rel = rel_ref[first : first + width, :]
        word_parts, pos_parts = [], []
        for head in range(2):
            own = slice(head * DH, (head + 1) * DH)
            prob = prob_ref[head, at, :]
            d_prob = nt(head_lanes(gvec, head), values)
            weight = prob.astype(F32)
            inner = jnp.sum(weight * d_prob, axis=1, keepdims=True)
            g_sum = (weight * (d_prob - inner) * 0.125).astype(BF)
            dv = nn(gvec_t[own, :], prob)
            dk = nn(qw_t[own, :], g_sum)
            d_values[head] = dv if part == 0 else d_values[head] + dv
            d_keys[head] = dk if part == 0 else d_keys[head] + dk
            turned = nn(mirror, g_sum)
            padded = jnp.concatenate([jnp.zeros((block, block), F32), turned], axis=1)
            moved = pltpu.roll(padded, width - block + 1, 1, stride=1, stride_axis=0).astype(BF)
            word_parts.append(nn(turned.astype(BF), keys))
            pos_parts.append(nn(moved, rel))
            rel_acc[own, first : first + width] += nn(qp_t[own, :], moved)
        lane = lax.broadcasted_iota(jnp.int32, word_parts[0].shape, 1)
        word = jnp.where(lane < DH, word_parts[0], word_parts[1])
        pos = jnp.where(lane < DH, pos_parts[0], pos_parts[1])
        word_sum = word_sum + jnp.sum(word, axis=0, keepdims=True)
        pos_sum = pos_sum + jnp.sum(pos, axis=0, keepdims=True)
        dproj_ref[at, :] = nn(mirror, (word + pos).astype(BF)).astype(BF)
    for head in range(2):
        own = slice(head * DH, (head + 1) * DH)
        dv_ref[own, :] = d_values[head].astype(BF)
        dk_ref[own, :] = (8.0 * d_keys[head]).astype(BF)
    drel_ref[...] = (8.0 * rel_acc[...]).astype(BF)
    bias_ref[0:1, :] = word_sum
    bias_ref[1:2, :] = pos_sum


def attend_backward(prob, gvec, qw, qp, keys, values, rel, block):
    rows, width = qw.shape
    klen, span = keys.shape[0], rel.shape[0]
    col = lambda count: pl.BlockSpec((count, PAIR), lambda p: (0, p))
    rowb = lambda count: pl.BlockSpec((PAIR, count), lambda p: (p, 0))
    return pl.pallas_call(
        functools.partial(attend_backward_kernel, block),
        grid=(width // PAIR,),
        in_specs=[
            pl.BlockSpec((2, rows, klen), lambda p: (p, 0, 0)),
            col(rows),
            col(rows),
            col(rows),
            col(klen),
            col(klen),
            col(span),
        ],
        out_specs=[col(rows), rowb(klen), rowb(klen), rowb(span), col(2)],
        out_shape=[
            jax.ShapeDtypeStruct((rows, width), BF),
            jax.ShapeDtypeStruct((width, klen), BF),
            jax.ShapeDtypeStruct((width, klen), BF),
            jax.ShapeDtypeStruct((width, span), BF),
            jax.ShapeDtypeStruct((2, width), F32),
        ],
        scratch_shapes=[pltpu.VMEM((PAIR, span), F32)],
        compiler_params=pltpu.CompilerParams(vmem_limit_bytes=LIMIT),
        cost_estimate=pl.CostEstimate(
            flops=16 * rows * klen * width, bytes_accessed=20 << 20, transcendentals=0
        ),
        name="attend_backward",
    )(prob, gvec, qw, qp, keys, values, rel)


def norm_parts(value):
    center = value - jnp.mean(value, axis=1, keepdims=True)
    scale = lax.rsqrt(jnp.mean(center * center, axis=1, keepdims=True) + EPS)
    return center * scale, scale


def norm_pull(normed, scale, err):
    inner = jnp.mean(err * normed, axis=1, keepdims=True)
    return (err - jnp.mean(err, axis=1, keepdims=True) - normed * inner) * scale


def sum_rows(value):
    return jnp.sum(value, axis=0, keepdims=True)


def feed_kernel(
    steps,
    vec_ref,
    x_ref,
    tan_ref,
    wo_ref,
    up_ref,
    dn_ref,
    upb_ref,
    dnb_ref,
    g1_ref,
    s1_ref,
    g2_ref,
    s2_ref,
    out_ref,
    dmix_ref,
    gvec_ref,
    go_ref,
    gup_ref,
    gdn_ref,
    gupb_ref,
    small_ref,
    n1_ref,
    r1_ref,
    fb_ref,
    fbt_ref,
    acc_ref,
    act_ref,
    slope_ref,
    gd_ref,
    gdt_ref,
):
    step = pl.program_id(0)

    @pl.when(step == 0)
    def _():
        normed, scale = norm_parts(nt(vec_ref[...], wo_ref[...]) + x_ref[...].astype(F32))
        n1_ref[...] = normed
        r1_ref[...] = scale
        first = normed * g1_ref[...] + s1_ref[...]
        fb_ref[...] = first.astype(BF)
        fbt_ref[...] = jnp.transpose(first).astype(BF)
        acc_ref[...] = first + dnb_ref[...]

    @pl.when(step < steps)
    def _():
        upper = nn(fb_ref[...], up_ref[...]) + upb_ref[...]
        square = upper * upper
        root = 0.7978845608028654
        bend = jnp.tanh(root * (upper + 0.044715 * (square * upper)))
        half = 0.5 * (1.0 + bend)
        act = (upper * half).astype(BF)
        act_ref[step] = act
        slope_ref[step] = half + 0.5 * upper * (1.0 - bend * bend) * (
            root + (3 * 0.044715 * root) * square
        )
        acc_ref[...] += nt(act, dn_ref[...])

    @pl.when(step == steps - 1)
    def _():
        normed, scale = norm_parts(acc_ref[...])
        out_ref[...] = (normed * g2_ref[...] + s2_ref[...]).astype(BF)
        tan = tan_ref[...].astype(F32)
        d_down = norm_pull(normed, scale, tan * g2_ref[...])
        small_ref[0:1, :] = sum_rows(d_down)
        small_ref[3:4, :] = sum_rows(tan * normed)
        small_ref[4:5, :] = sum_rows(tan)
        gd_ref[...] = d_down.astype(BF)
        gdt_ref[...] = jnp.transpose(d_down).astype(BF)
        acc_ref[...] = d_down

    @pl.when(step >= steps)
    def _():
        at = step - steps
        d_up = nn(gd_ref[...], dn_ref[...]) * slope_ref[at]
        gupb_ref[...] = sum_rows(d_up)
        g_up = d_up.astype(BF)
        gdn_ref[...] = nn(gdt_ref[...], act_ref[at]).astype(BF)
        gup_ref[...] = nn(fbt_ref[...], g_up).astype(BF)
        acc_ref[...] += nt(g_up, up_ref[...])

    @pl.when(step == 2 * steps - 1)
    def _():
        d_first, normed = acc_ref[...], n1_ref[...]
        small_ref[1:2, :] = sum_rows(d_first * normed)
        small_ref[2:3, :] = sum_rows(d_first)
        d_mixed = norm_pull(normed, r1_ref[...], d_first * g1_ref[...])
        dmix_ref[...] = d_mixed
        g_mixed = d_mixed.astype(BF)
        go_ref[...] = nn(jnp.transpose(d_mixed).astype(BF), vec_ref[...]).astype(BF)
        gvec_ref[...] = nn(g_mixed, wo_ref[...]).astype(BF)


def feed(vec, x, tan, wo, up, dn, upb, dnb, g1, s1, g2, s2):
    rows, width = vec.shape
    inner = up.shape[1]
    chunk = 512
    steps = inner // chunk
    whole = lambda a, b: pl.BlockSpec((a, b), lambda i: (0, 0))
    cols = lambda a: pl.BlockSpec((a, chunk), lambda i: (0, lax.rem(i, steps)))
    late = lambda a: pl.BlockSpec((a, chunk), lambda i: (0, jnp.maximum(i - steps, 0)))
    return pl.pallas_call(
        functools.partial(feed_kernel, steps),
        grid=(2 * steps,),
        in_specs=[
            whole(rows, width),
            whole(rows, width),
            whole(rows, width),
            whole(width, width),
            cols(width),
            cols(width),
            cols(1),
        ]
        + [whole(1, width)] * 5,
        out_specs=[
            whole(rows, width),
            whole(rows, width),
            whole(rows, width),
            whole(width, width),
            late(width),
            late(width),
            late(1),
            whole(8, width),
        ],
        out_shape=[
            jax.ShapeDtypeStruct((rows, width), BF),
            jax.ShapeDtypeStruct((rows, width), F32),
            jax.ShapeDtypeStruct((rows, width), BF),
            jax.ShapeDtypeStruct((width, width), BF),
            jax.ShapeDtypeStruct((width, inner), BF),
            jax.ShapeDtypeStruct((width, inner), BF),
            jax.ShapeDtypeStruct((1, inner), F32),
            jax.ShapeDtypeStruct((8, width), F32),
        ],
        scratch_shapes=[
            pltpu.VMEM((rows, width), F32),
            pltpu.VMEM((rows, 1), F32),
            pltpu.VMEM((rows, width), BF),
            pltpu.VMEM((width, rows), BF),
            pltpu.VMEM((rows, width), F32),
            pltpu.VMEM((steps, rows, chunk), BF),
            pltpu.VMEM((steps, rows, chunk), F32),
            pltpu.VMEM((rows, width), BF),
            pltpu.VMEM((width, rows), BF),
        ],
        compiler_params=pltpu.CompilerParams(vmem_limit_bytes=LIMIT),
        cost_estimate=pl.CostEstimate(
            flops=12 * rows * width * inner, bytes_accessed=36 << 20, transcendentals=rows * inner
        ),
        name="feed",
    )(vec, x, tan, wo, up, dn, upb, dnb, g1, s1, g2, s2)


def gather_weights(shards):
    rows, cols = shards[0].shape
    groups, tensors = lax.axis_size("dp"), lax.axis_size("tensor")
    stack = jnp.stack(shards)
    both = lax.all_gather(stack, ("dp", "tensor"), axis=0, tiled=False)
    both = both.reshape(groups, tensors, len(shards), rows, cols)
    both = both.transpose(2, 0, 3, 1, 4).reshape(len(shards), groups * rows, tensors * cols)
    return [both[i] for i in range(len(shards))]


def scatter_grads(grads):
    groups, tensors = lax.axis_size("dp"), lax.axis_size("tensor")
    rows, cols = grads[0].shape[0] // groups, grads[0].shape[1] // tensors
    stack = jnp.stack(grads).reshape(len(grads), groups, rows, tensors, cols)
    stack = stack.transpose(1, 3, 0, 2, 4).reshape(groups * tensors, len(grads), rows, cols)
    mine = lax.psum_scatter(stack, ("dp", "tensor"), scatter_dimension=0, tiled=True)
    mine = mine.reshape(len(grads), rows, cols).astype(F32)
    return [mine[i] for i in range(len(grads))]


def body(
    content_stream,
    query_stream,
    memory,
    content_tangent,
    query_tangent,
    seq_lengths,
    factor_order,
    memory_lengths,
    slot_sequence,
    query_weight,
    key_weight,
    value_weight,
    pos_weight,
    out_weight,
    up_weight,
    up_bias,
    down_weight,
    down_bias,
    word_bias,
    pos_bias,
    first_gain,
    first_shift,
    second_gain,
    second_shift,
):
    groups, tensors = lax.axis_size("dp"), lax.axis_size("tensor")
    micro, part_len, width = content_stream.shape
    mem_part = memory.shape[1]
    seq_len, mem_total = part_len * tensors, mem_part * tensors
    klen, span = mem_total + seq_len, mem_total + 2 * seq_len
    count = micro * groups
    here, lane = lax.axis_index("dp"), lax.axis_index("tensor")
    core = here % 2
    lead = core == 0
    block = 256
    assert 2 * micro == tensors
    pairs = [(i, i ^ 1) for i in range(groups)]

    def swap(arr):
        return lax.ppermute(arr, "dp", pairs)

    def to_unit(first, second):
        got = swap(jnp.where(lead, second, first))
        low = jnp.where(lead, first, got)
        high = jnp.where(lead, got, second)
        both = jnp.concatenate([low, high], 0)
        both = lax.all_to_all(both, "tensor", split_axis=0, concat_axis=0, tiled=True)
        return both.reshape(seq_len, width)

    def from_unit(arr):
        both = arr.reshape(tensors, part_len, width)
        both = lax.all_to_all(both, "tensor", split_axis=0, concat_axis=0, tiled=True)
        low, high = both[:micro], both[micro:]
        got = swap(jnp.where(lead, high, low))
        return jnp.where(lead, low, got), jnp.where(lead, got, high)

    seq_id = (here // 2) * tensors + lane
    ids = jnp.arange(count, dtype=jnp.int32)
    slot_of = jnp.sum(jnp.where(slot_sequence[None, :] == ids[:, None], ids[None, :], 0), axis=1)
    lengths = lax.all_gather(
        jnp.concatenate([seq_lengths, memory_lengths]), "dp", axis=0, tiled=False
    )
    length = lengths[:, :micro].reshape(count)[seq_id]
    mem_valid = lengths[:, micro:].reshape(count)[slot_of[seq_id]]
    other = swap(factor_order)
    orders = jnp.concatenate(
        [jnp.where(lead, factor_order, other), jnp.where(lead, other, factor_order)], 0
    )
    rank = lax.dynamic_index_in_dim(orders, lane, 0, keepdims=False)
    key_pos = jnp.arange(klen, dtype=jnp.int32)
    hidden = jnp.int32(1 << 20)
    mem_rank = jnp.where(key_pos[:mem_total] >= mem_total - mem_valid, -1, hidden)
    own_rank = jnp.where(key_pos[:seq_len] < length, rank, hidden)
    key_rank = jnp.concatenate([mem_rank, own_rank])[None, :]
    thr = (rank + jnp.where(lead, 1, 0))[:, None]

    stream = to_unit(content_stream, query_stream)
    content = jnp.where(lead, stream, swap(stream))

    piece = mem_part // groups
    spread = lax.all_to_all(
        memory.reshape(micro, groups, piece, width), "dp", split_axis=1, concat_axis=1, tiled=True
    )
    spread = spread.transpose(1, 0, 2, 3).reshape(count, piece, width)
    spread = jnp.take(spread, slot_of, axis=0)
    spread = spread.reshape(groups // 2, tensors, 2, piece // 2, width).transpose(0, 2, 1, 3, 4)
    spread = lax.all_to_all(
        spread.reshape(groups, tensors, piece // 2, width),
        "dp",
        split_axis=0,
        concat_axis=0,
        tiled=True,
    )
    spread = lax.all_to_all(spread, "tensor", split_axis=1, concat_axis=1, tiled=True)
    got = swap(spread)
    mem_rows = jnp.stack([jnp.where(lead, spread, got), jnp.where(lead, got, spread)])
    mem_rows = mem_rows.transpose(2, 1, 0, 3, 4).reshape(mem_total, width)

    tangent = to_unit(content_tangent, query_tangent)

    key_mat, value_mat, query_mat, pos_mat, out_mat = gather_weights(
        [key_weight, value_weight, query_weight, pos_weight, out_weight]
    )
    up_mat, down_mat = gather_weights([up_weight, down_weight])

    context = jnp.concatenate([mem_rows, content], 0)
    table = reversed_table(span, klen, width)
    keys = nn(context, key_mat).astype(BF)
    values = nn(context, value_mat).astype(BF)
    rel = nn(table, pos_mat).astype(BF)
    proj = nn(stream, query_mat)
    scale = jnp.asarray(0.125, BF)
    q_word = (proj + word_bias.reshape(1, width)).astype(BF) * scale
    q_pos = (proj + pos_bias.reshape(1, width)).astype(BF) * scale

    vec, prob = attend_forward(q_word, q_pos, keys, values, rel, thr, key_rank, block)
    row = lambda v: v.reshape(1, -1)
    out, d_mixed, g_vec, g_out, g_up, g_down, g_upb, small = feed(
        vec,
        stream,
        tangent,
        out_mat,
        up_mat,
        down_mat,
        row(up_bias),
        row(down_bias),
        row(first_gain),
        row(first_shift),
        row(second_gain),
        row(second_shift),
    )
    content_out, query_out = from_unit(out)
    grad_up, grad_down = scatter_grads([g_up, g_down])
    early = lax.psum(
        jnp.concatenate([g_upb.reshape(-1), small[:5].reshape(-1)]), ("dp", "tensor")
    )

    d_proj, dk_t, dv_t, drel_t, biases = attend_backward(
        prob, g_vec, q_word, q_pos, keys, values, rel, block
    )
    late = lax.psum(biases, ("dp", "tensor"))
    d_context = tt(dk_t[:, mem_total:], key_mat) + tt(dv_t[:, mem_total:], value_mat)
    partner = swap(d_context.astype(BF))
    d_stream = d_mixed + nt(d_proj, query_mat)
    d_stream = d_stream + jnp.where(lead, d_context + partner.astype(F32), 0.0)
    content_grad, query_grad = from_unit(d_stream.astype(BF))
    grad_query, grad_key, grad_value, grad_pos, grad_out = scatter_grads(
        [
            tn(stream, d_proj).astype(BF),
            tt(context, dk_t).astype(BF),
            tt(context, dv_t).astype(BF),
            tt(table, drel_t).astype(BF),
            g_out,
        ]
    )
    inner = up_bias.shape[0]
    rest = early[inner:].reshape(5, width)
    return (
        content_out,
        query_out,
        content_grad,
        query_grad,
        grad_query,
        grad_key,
        grad_value,
        grad_pos,
        grad_out,
        grad_up,
        early[:inner],
        grad_down,
        rest[0],
        late[0].reshape(HEADS, DH),
        late[1].reshape(HEADS, DH),
        rest[1],
        rest[2],
        rest[3],
        rest[4],
    )


def solution(mesh):
    rows = P("dp", "tensor", None)
    mat = P("dp", "tensor")
    return jax.shard_map(
        body,
        mesh=mesh,
        in_specs=(rows,) * 5
        + (P("dp"), P("dp", None), P("dp"), P())
        + (mat,) * 6
        + (P(), mat)
        + (P(),) * 7,
        out_specs=(rows,) * 4 + (mat,) * 6 + (P(), mat) + (P(),) * 7,
        check_vma=False,
    )
```

```python
import functools

import jax
import jax.numpy as jnp
from jax import lax
from jax.experimental import pallas as pl
from jax.experimental.pallas import tpu as pltpu
from jax.sharding import PartitionSpec as P

HEADS = 12
DH = 64
PAIR = 2 * DH
EPS = 1e-06
BF = jnp.bfloat16
F32 = jnp.float32
LIMIT = 60 * 1024 * 1024


def nn(left, right):
    return jnp.dot(left, right, preferred_element_type=F32)


def nt(left, right):
    return lax.dot_general(left, right, (((1,), (1,)), ((), ())), preferred_element_type=F32)


def tn(left, right):
    return lax.dot_general(left, right, (((0,), (0,)), ((), ())), preferred_element_type=F32)


def tt(left, right):
    return lax.dot_general(left, right, (((0,), (1,)), ((), ())), preferred_element_type=F32)


def reversed_table(count, first, width):
    dist = first - jnp.arange(count, dtype=F32)
    half = width // 2
    freq = 1.0 / 10000.0 ** (jnp.arange(half, dtype=F32) * (2.0 / width))
    angle = dist[:, None] * freq[None, :]
    return jnp.concatenate([jnp.sin(angle), jnp.cos(angle)], axis=1).astype(BF)


def head_lanes(array, head):
    lane = lax.broadcasted_iota(jnp.int32, array.shape, 1)
    return jnp.where((lane >= DH) == (head == 1), array, jnp.zeros_like(array))


def attend_forward_kernel(
    block, qw_ref, qp_ref, k_ref, v_ref, rel_ref, thr_ref, kr_ref, vec_ref, prob_ref
):
    rows, klen = qw_ref.shape[0], k_ref.shape[0]
    width = klen + block
    keys, values = k_ref[...], v_ref[...]
    for part in range(rows // block):
        at = slice(part * block, (part + 1) * block)
        first = rows - (part + 1) * block
        qw, qp = qw_ref[at, :], qp_ref[at, :]
        rel = rel_ref[first : first + width, :]
        seen = kr_ref[...] < thr_ref[at, :]
        vecs = []
        for head in range(2):
            raw = nt(head_lanes(qp, head), rel)
            moved = pltpu.roll(raw, 0, 1, stride=1, stride_axis=0)[:, block:]
            score = nt(head_lanes(qw, head), keys) + moved
            score = jnp.where(seen, score, -1e30)
            expo = jnp.exp(score - jnp.max(score, axis=1, keepdims=True))
            prob = (expo * (1.0 / jnp.sum(expo, axis=1, keepdims=True))).astype(BF)
            prob_ref[head, at, :] = prob
            vecs.append(nn(prob, values))
        lane = lax.broadcasted_iota(jnp.int32, vecs[0].shape, 1)
        vec_ref[at, :] = jnp.where(lane < DH, vecs[0], vecs[1]).astype(BF)


def attend_forward(qw, qp, keys, values, rel, thr, key_rank, block):
    rows, width = qw.shape
    klen, span = keys.shape[0], rel.shape[0]
    col = lambda count: pl.BlockSpec((count, PAIR), lambda p: (0, p))
    return pl.pallas_call(
        functools.partial(attend_forward_kernel, block),
        grid=(width // PAIR,),
        in_specs=[
            col(rows),
            col(rows),
            col(klen),
            col(klen),
            col(span),
            pl.BlockSpec((rows, 1), lambda p: (0, 0)),
            pl.BlockSpec((1, klen), lambda p: (0, 0)),
        ],
        out_specs=[col(rows), pl.BlockSpec((2, rows, klen), lambda p: (p, 0, 0))],
        out_shape=[
            jax.ShapeDtypeStruct((rows, width), BF),
            jax.ShapeDtypeStruct((width // DH, rows, klen), BF),
        ],
        compiler_params=pltpu.CompilerParams(vmem_limit_bytes=LIMIT),
        cost_estimate=pl.CostEstimate(
            flops=8 * rows * klen * width, bytes_accessed=16 << 20, transcendentals=12 * rows * klen
        ),
        name="attend_forward",
    )(qw, qp, keys, values, rel, thr, key_rank)


def attend_backward_kernel(
    block,
    prob_ref,
    gvec_ref,
    qw_ref,
    qp_ref,
    k_ref,
    v_ref,
    rel_ref,
    dproj_ref,
    dk_ref,
    dv_ref,
    drel_ref,
    bias_ref,
    rel_acc,
):
    rows, klen = qw_ref.shape[0], k_ref.shape[0]
    width = klen + block
    keys, values = k_ref[...], v_ref[...]
    row = lax.broadcasted_iota(jnp.int32, (block, block), 0)
    col = lax.broadcasted_iota(jnp.int32, (block, block), 1)
    mirror = (row + col == block - 1).astype(BF)
    rel_acc[...] = jnp.zeros_like(rel_acc)
    d_keys, d_values = [None, None], [None, None]
    word_sum = jnp.zeros((1, PAIR), F32)
    pos_sum = jnp.zeros((1, PAIR), F32)
    for part in range(rows // block):
        at = slice(part * block, (part + 1) * block)
        first = rows - (part + 1) * block
        gvec, qw = gvec_ref[at, :], qw_ref[at, :]
        gvec_t = jnp.transpose(gvec.astype(F32)).astype(BF)
        qw_t = jnp.transpose(qw.astype(F32)).astype(BF)
        qp_t = jnp.transpose(nn(mirror, qp_ref[at, :])).astype(BF)
        rel = rel_ref[first : first + width, :]
        word_parts, pos_parts = [], []
        for head in range(2):
            own = slice(head * DH, (head + 1) * DH)
            prob = prob_ref[head, at, :]
            d_prob = nt(head_lanes(gvec, head), values)
            weight = prob.astype(F32)
            inner = jnp.sum(weight * d_prob, axis=1, keepdims=True)
            g_sum = (weight * (d_prob - inner) * 0.125).astype(BF)
            dv = nn(gvec_t[own, :], prob)
            dk = nn(qw_t[own, :], g_sum)
            d_values[head] = dv if part == 0 else d_values[head] + dv
            d_keys[head] = dk if part == 0 else d_keys[head] + dk
            turned = nn(mirror, g_sum)
            padded = jnp.concatenate([jnp.zeros((block, block), F32), turned], axis=1)
            moved = pltpu.roll(padded, width - block + 1, 1, stride=1, stride_axis=0).astype(BF)
            word_parts.append(nn(turned.astype(BF), keys))
            pos_parts.append(nn(moved, rel))
            rel_acc[own, first : first + width] += nn(qp_t[own, :], moved)
        lane = lax.broadcasted_iota(jnp.int32, word_parts[0].shape, 1)
        word = jnp.where(lane < DH, word_parts[0], word_parts[1])
        pos = jnp.where(lane < DH, pos_parts[0], pos_parts[1])
        word_sum = word_sum + jnp.sum(word, axis=0, keepdims=True)
        pos_sum = pos_sum + jnp.sum(pos, axis=0, keepdims=True)
        dproj_ref[at, :] = nn(mirror, (word + pos).astype(BF)).astype(BF)
    for head in range(2):
        own = slice(head * DH, (head + 1) * DH)
        dv_ref[own, :] = d_values[head].astype(BF)
        dk_ref[own, :] = (8.0 * d_keys[head]).astype(BF)
    drel_ref[...] = (8.0 * rel_acc[...]).astype(BF)
    bias_ref[0:1, :] = word_sum
    bias_ref[1:2, :] = pos_sum


def attend_backward(prob, gvec, qw, qp, keys, values, rel, block):
    rows, width = qw.shape
    klen, span = keys.shape[0], rel.shape[0]
    col = lambda count: pl.BlockSpec((count, PAIR), lambda p: (0, p))
    rowb = lambda count: pl.BlockSpec((PAIR, count), lambda p: (p, 0))
    return pl.pallas_call(
        functools.partial(attend_backward_kernel, block),
        grid=(width // PAIR,),
        in_specs=[
            pl.BlockSpec((2, rows, klen), lambda p: (p, 0, 0)),
            col(rows),
            col(rows),
            col(rows),
            col(klen),
            col(klen),
            col(span),
        ],
        out_specs=[col(rows), rowb(klen), rowb(klen), rowb(span), col(2)],
        out_shape=[
            jax.ShapeDtypeStruct((rows, width), BF),
            jax.ShapeDtypeStruct((width, klen), BF),
            jax.ShapeDtypeStruct((width, klen), BF),
            jax.ShapeDtypeStruct((width, span), BF),
            jax.ShapeDtypeStruct((2, width), F32),
        ],
        scratch_shapes=[pltpu.VMEM((PAIR, span), F32)],
        compiler_params=pltpu.CompilerParams(vmem_limit_bytes=LIMIT),
        cost_estimate=pl.CostEstimate(
            flops=16 * rows * klen * width, bytes_accessed=20 << 20, transcendentals=0
        ),
        name="attend_backward",
    )(prob, gvec, qw, qp, keys, values, rel)


def norm_parts(value):
    center = value - jnp.mean(value, axis=1, keepdims=True)
    scale = lax.rsqrt(jnp.mean(center * center, axis=1, keepdims=True) + EPS)
    return center * scale, scale


def norm_pull(normed, scale, err):
    inner = jnp.mean(err * normed, axis=1, keepdims=True)
    return (err - jnp.mean(err, axis=1, keepdims=True) - normed * inner) * scale


def sum_rows(value):
    return jnp.sum(value, axis=0, keepdims=True)


def load_pieces(refs, offs_ref, dst_ref, sems):
    copies = []
    for i, ref in enumerate(refs):
        rows = ref.shape[1]
        at = pl.multiple_of(offs_ref[i], 16) if len(refs) > 1 else 0
        copies.append(pltpu.make_async_copy(ref, dst_ref.at[:, pl.ds(at, rows), :], sems.at[i]))
    for copy in copies:
        copy.start()
    return copies


def reorder_rows(value, order_ref, tmp_ref, dst_ref):
    blocks = order_ref.shape[0]
    if blocks == 1:
        dst_ref[...] = jnp.transpose(value).astype(BF)
        return
    tmp_ref[...] = jnp.transpose(value)
    rows = tmp_ref.shape[0] // blocks
    for i in range(blocks):
        at = pl.multiple_of(order_ref[i] * rows, 8)
        dst_ref[i * rows : (i + 1) * rows, :] = tmp_ref[pl.ds(at, rows), :].astype(BF)


def feed_kernel(steps, pieces, *refs):
    offs_ref, order_ref = refs[:2]
    ud_refs = refs[2 : 2 + pieces]
    wo_refs = refs[2 + pieces : 2 + 2 * pieces]
    (
        vec_ref,
        x_ref,
        tan_ref,
        upb_ref,
        dnb_ref,
        g1_ref,
        s1_ref,
        g2_ref,
        s2_ref,
        out_ref,
        dmix_ref,
        gvec_ref,
        goe_ref,
        goo_ref,
        ge_ref,
        gd2_ref,
        gupb_ref,
        small_ref,
        ud_ref,
        wo_ref,
        n1_ref,
        r1_ref,
        fb_ref,
        fbt_ref,
        acc_ref,
        act_ref,
        slope_ref,
        gd_ref,
        gdt_ref,
        tmp_ref,
        ud_sems,
        wo_sems,
    ) = refs[2 + 2 * pieces :]
    step = pl.program_id(0)
    chunk = act_ref.shape[2]
    half_rows = goe_ref.shape[0]
    cols = pl.ds(pl.multiple_of(lax.rem(step, steps) * chunk, chunk), chunk)

    @pl.when(step == 0)
    def _():
        out_copies = load_pieces(wo_refs, offs_ref, wo_ref, wo_sems)
        copies = load_pieces(ud_refs, offs_ref, ud_ref, ud_sems)
        for copy in out_copies:
            copy.wait()
        normed, scale = norm_parts(nt(vec_ref[...], wo_ref[0]) + x_ref[...].astype(F32))
        n1_ref[...] = normed
        r1_ref[...] = scale
        first = normed * g1_ref[...] + s1_ref[...]
        fb_ref[...] = first.astype(BF)
        reorder_rows(first, order_ref, tmp_ref, fbt_ref)
        acc_ref[...] = first + dnb_ref[...]
        for copy in copies:
            copy.wait()

    @pl.when(step < steps)
    def _():
        upper = nn(fb_ref[...], ud_ref[0, :, cols]) + upb_ref[...]
        square = upper * upper
        root = 0.7978845608028654
        bend = jnp.tanh(root * (upper + 0.044715 * (square * upper)))
        half = 0.5 * (1.0 + bend)
        act = (upper * half).astype(BF)
        act_ref[step] = act
        slope_ref[step] = half + 0.5 * upper * (1.0 - bend * bend) * (
            root + (3 * 0.044715 * root) * square
        )
        acc_ref[...] += nt(act, ud_ref[1, :, cols])

    @pl.when(step == steps - 1)
    def _():
        normed, scale = norm_parts(acc_ref[...])
        out_ref[...] = (normed * g2_ref[...] + s2_ref[...]).astype(BF)
        tan = tan_ref[...].astype(F32)
        d_down = norm_pull(normed, scale, tan * g2_ref[...])
        small_ref[0:1, :] = sum_rows(d_down)
        small_ref[3:4, :] = sum_rows(tan * normed)
        small_ref[4:5, :] = sum_rows(tan)
        gd_ref[...] = d_down.astype(BF)
        reorder_rows(d_down, order_ref, tmp_ref, gdt_ref)
        acc_ref[...] = d_down

    @pl.when(step >= steps)
    def _():
        at = step - steps
        d_up = nn(gd_ref[...], ud_ref[1, :, cols]) * slope_ref[at]
        gupb_ref[...] = sum_rows(d_up)
        g_up = d_up.astype(BF)
        acc_ref[...] += nt(g_up, ud_ref[0, :, cols])
        act = act_ref[at]
        for side, dst in ((0, ge_ref), (half_rows, gd2_ref)):
            rows = slice(side, side + half_rows)
            dst[0] = nn(fbt_ref[rows, :], g_up).astype(BF)
            dst[1] = nn(gdt_ref[rows, :], act).astype(BF)

    @pl.when(step == 2 * steps - 1)
    def _():
        d_first, normed = acc_ref[...], n1_ref[...]
        small_ref[1:2, :] = sum_rows(d_first * normed)
        small_ref[2:3, :] = sum_rows(d_first)
        d_mixed = norm_pull(normed, r1_ref[...], d_first * g1_ref[...])
        dmix_ref[...] = d_mixed
        gvec_ref[...] = nn(d_mixed.astype(BF), wo_ref[0]).astype(BF)
        reorder_rows(d_mixed, order_ref, tmp_ref, gdt_ref)
        goe_ref[...] = nn(gdt_ref[:half_rows, :], vec_ref[...]).astype(BF)
        goo_ref[...] = nn(gdt_ref[half_rows:, :], vec_ref[...]).astype(BF)


SMEM_SPEC = pl.BlockSpec(memory_space=pltpu.SMEM)
ANY_SPEC = pl.BlockSpec(memory_space=pl.ANY)


def feed(offs, order, ud_pieces, out_pieces, vec, x, tan, upb, dnb, g1, s1, g2, s2):
    rows, width = vec.shape
    inner = upb.shape[1]
    chunk = 512
    steps = inner // chunk
    half = width // 2
    count = len(ud_pieces)
    whole = lambda a, b: pl.BlockSpec((a, b), lambda i: (0, 0))
    late = lambda i: jnp.maximum(i - steps, 0)
    grads = pl.BlockSpec((2, half, chunk), lambda i: (0, 0, late(i)))
    return pl.pallas_call(
        functools.partial(feed_kernel, steps, count),
        grid=(2 * steps,),
        in_specs=[SMEM_SPEC, SMEM_SPEC]
        + [ANY_SPEC] * (2 * count)
        + [whole(rows, width)] * 3
        + [pl.BlockSpec((1, chunk), lambda i: (0, lax.rem(i, steps)))]
        + [whole(1, width)] * 5,
        out_specs=[
            whole(rows, width),
            whole(rows, width),
            whole(rows, width),
            whole(half, width),
            whole(half, width),
            grads,
            grads,
            pl.BlockSpec((1, chunk), lambda i: (0, late(i))),
            whole(8, width),
        ],
        out_shape=[
            jax.ShapeDtypeStruct((rows, width), BF),
            jax.ShapeDtypeStruct((rows, width), F32),
            jax.ShapeDtypeStruct((rows, width), BF),
            jax.ShapeDtypeStruct((half, width), BF),
            jax.ShapeDtypeStruct((half, width), BF),
            jax.ShapeDtypeStruct((2, half, inner), BF),
            jax.ShapeDtypeStruct((2, half, inner), BF),
            jax.ShapeDtypeStruct((1, inner), F32),
            jax.ShapeDtypeStruct((8, width), F32),
        ],
        scratch_shapes=[
            pltpu.VMEM((2, width, inner), BF),
            pltpu.VMEM((1, width, width), BF),
            pltpu.VMEM((rows, width), F32),
            pltpu.VMEM((rows, 1), F32),
            pltpu.VMEM((rows, width), BF),
            pltpu.VMEM((width, rows), BF),
            pltpu.VMEM((rows, width), F32),
            pltpu.VMEM((steps, rows, chunk), BF),
            pltpu.VMEM((steps, rows, chunk), F32),
            pltpu.VMEM((rows, width), BF),
            pltpu.VMEM((width, rows), BF),
            pltpu.VMEM((width, rows), F32),
            pltpu.SemaphoreType.DMA((count,)),
            pltpu.SemaphoreType.DMA((count,)),
        ],
        compiler_params=pltpu.CompilerParams(vmem_limit_bytes=LIMIT),
        cost_estimate=pl.CostEstimate(
            flops=12 * rows * width * inner, bytes_accessed=36 << 20, transcendentals=rows * inner
        ),
        name="feed",
    )(offs, order, *ud_pieces, *out_pieces, vec, x, tan, upb, dnb, g1, s1, g2, s2)


def project_kernel(pieces, *refs):
    offs_ref = refs[0]
    piece_refs = refs[1 : 1 + pieces]
    ctx_ref, x_ref, table_ref, wb_ref, pb_ref = refs[1 + pieces : 6 + pieces]
    k_ref, v_ref, rel_ref, qw_ref, qp_ref, w_ref, sems = refs[6 + pieces :]
    for copy in load_pieces(piece_refs, offs_ref, w_ref, sems):
        copy.wait()
    block = 256

    def loop(count, step):
        def run(i, carry):
            step(pl.ds(pl.multiple_of(i * block, block), block))
            return carry

        lax.fori_loop(0, count // block, run, 0)

    def context_step(at):
        k_ref[at, :] = nn(ctx_ref[at, :], w_ref[0]).astype(BF)
        v_ref[at, :] = nn(ctx_ref[at, :], w_ref[1]).astype(BF)

    def stream_step(at):
        proj = nn(x_ref[at, :], w_ref[2])
        qw_ref[at, :] = (0.125 * (proj + wb_ref[...]).astype(BF).astype(F32)).astype(BF)
        qp_ref[at, :] = (0.125 * (proj + pb_ref[...]).astype(BF).astype(F32)).astype(BF)

    def table_step(at):
        rel_ref[at, :] = nn(table_ref[at, :], w_ref[3]).astype(BF)

    loop(table_ref.shape[0], table_step)
    loop(x_ref.shape[0], stream_step)
    loop(ctx_ref.shape[0], context_step)


def project(offs, pieces, context, stream, table, wb, pb):
    rows, width = stream.shape
    klen, span = context.shape[0], table.shape[0]
    vmem = pl.BlockSpec(memory_space=pltpu.VMEM)
    return pl.pallas_call(
        functools.partial(project_kernel, len(pieces)),
        in_specs=[SMEM_SPEC] + [ANY_SPEC] * len(pieces) + [vmem] * 5,
        out_specs=[vmem] * 6,
        out_shape=[
            jax.ShapeDtypeStruct((klen, width), BF),
            jax.ShapeDtypeStruct((klen, width), BF),
            jax.ShapeDtypeStruct((span, width), BF),
            jax.ShapeDtypeStruct((rows, width), BF),
            jax.ShapeDtypeStruct((rows, width), BF),
            jax.ShapeDtypeStruct((4, width, width), BF),
        ],
        scratch_shapes=[pltpu.SemaphoreType.DMA((len(pieces),))],
        compiler_params=pltpu.CompilerParams(vmem_limit_bytes=LIMIT),
        cost_estimate=pl.CostEstimate(
            flops=2 * (2 * klen + rows + span) * width * width,
            bytes_accessed=20 << 20,
            transcendentals=0,
        ),
        name="project",
    )(offs, *pieces, context, stream, table, wb, pb)


def weight_grads_kernel(xt_ref, ct_ref, tt_ref, dp_ref, dk_ref, dv_ref, dr_ref, ge_ref, go_ref):
    half = ge_ref.shape[1]
    for side, dst in ((0, ge_ref), (half, go_ref)):
        rows = slice(side, side + half)
        dst[0] = nt(ct_ref[rows, :], dk_ref[...]).astype(BF)
        dst[1] = nt(ct_ref[rows, :], dv_ref[...]).astype(BF)
        dst[2] = nn(xt_ref[rows, :], dp_ref[...]).astype(BF)
        dst[3] = nt(tt_ref[rows, :], dr_ref[...]).astype(BF)


def weight_grads(x_t, ctx_t, table_t, d_proj, dk_t, dv_t, drel_t):
    width, rows = x_t.shape
    klen, span = ctx_t.shape[1], table_t.shape[1]
    half, chunk = width // 2, 256
    whole = lambda a, b: pl.BlockSpec((a, b), lambda i: (0, 0))
    out = pl.BlockSpec((4, half, chunk), lambda i: (0, 0, i))
    rowb = lambda b: pl.BlockSpec((chunk, b), lambda i: (i, 0))
    return pl.pallas_call(
        weight_grads_kernel,
        grid=(width // chunk,),
        in_specs=[
            whole(width, rows),
            whole(width, klen),
            whole(width, span),
            pl.BlockSpec((rows, chunk), lambda i: (0, i)),
            rowb(klen),
            rowb(klen),
            rowb(span),
        ],
        out_specs=[out, out],
        out_shape=[jax.ShapeDtypeStruct((4, half, width), BF)] * 2,
        compiler_params=pltpu.CompilerParams(vmem_limit_bytes=LIMIT),
        cost_estimate=pl.CostEstimate(
            flops=2 * (rows + 2 * klen + span) * width * width,
            bytes_accessed=20 << 20,
            transcendentals=0,
        ),
        name="weight_grads",
    )(x_t, ctx_t, table_t, d_proj, dk_t, dv_t, drel_t)


CORE, XBIT, YBIT = 1, 2, 4
ORDER = (0, 2, 4, 6, 1, 3, 5, 7)


def flip(arr, bit):
    return lax.ppermute(arr, "dp", [(i, i ^ bit) for i in range(lax.axis_size("dp"))])


def flip_z(arr, bit):
    return lax.ppermute(arr, "tensor", [(i, i ^ bit) for i in range(lax.axis_size("tensor"))])


def by_bits(parts, bits):
    step = 1
    for bit in bits:
        parts = [
            jnp.where(bit == 1, parts[i ^ step], parts[i]) for i in range(len(parts))
        ]
        step *= 2
    return parts


def gather_columns(shard):
    tensors, lane = lax.axis_size("tensor"), lax.axis_index("tensor")
    assert tensors == 4
    parts = [shard] + [flip_z(shard, bit) for bit in (1, 2, 3)]
    return jnp.concatenate(by_bits(parts, (lane & 1, lane >> 1)), axis=2)


def gather_pieces(shard):
    rows = shard.shape[1]
    if lax.axis_size("dp") != 8:
        return [lax.all_gather(shard, "dp", axis=1, tiled=True)]
    one, two = shard[:, : rows // 2], shard[:, rows // 2 :]
    pieces = []
    for part, first, second in ((one, XBIT, YBIT), (two, YBIT, XBIT)):
        near = flip(part, first)
        mine = [part, near, flip(part, second), flip(near, second)]
        pieces += mine + [flip(p, CORE) for p in mine]
    return pieces


def piece_offsets(rows):
    if lax.axis_size("dp") != 8:
        return jnp.zeros((1,), jnp.int32)
    here = lax.axis_index("dp")
    offs = []
    for start, first, second in ((0, XBIT, YBIT), (rows // 2, YBIT, XBIT)):
        for core in (0, CORE):
            for bits in (0, first, second, first | second):
                offs.append((here ^ (bits | core)) * rows + start)
    return jnp.stack(offs)


def row_order():
    if lax.axis_size("dp") != 8:
        return jnp.zeros((1,), jnp.int32)
    return lax.axis_index("dp") ^ jnp.asarray(ORDER, jnp.int32)


def reorder_blocks(array, order):
    turned = jnp.transpose(array)
    if order.shape[0] == 1:
        return turned
    blocks = turned.reshape(order.shape[0], -1, turned.shape[1])
    return jnp.take(blocks, order, axis=0).reshape(turned.shape)


def scatter_sum(even, odd):
    count, half, cols = even.shape
    groups, tensors = lax.axis_size("dp"), lax.axis_size("tensor")
    rows = 2 * half // groups
    if groups != 8:
        full = jnp.concatenate([even, odd], axis=1)
        mine = lax.psum_scatter(full, "dp", scatter_dimension=1, tiled=True)
    else:
        add = lambda a, b: (a.astype(F32) + b.astype(F32)).astype(BF)
        got = flip(odd, CORE).reshape(count, 4, rows, cols)
        own = even.reshape(count, 4, rows, cols)
        parts = []
        for at, first, second in ((slice(0, rows // 2), 1, 2), (slice(rows // 2, rows), 2, 1)):
            block = lambda i: add(own[:, i, at], got[:, i, at])
            send = jnp.stack([block(first), block(3)])
            near = flip(send, 2 * first)
            keep, last = add(block(0), near[0]), add(block(second), near[1])
            parts.append(add(keep, flip(last, 2 * second)))
        mine = jnp.concatenate(parts, axis=1)
    mine = mine.reshape(count, rows, tensors, cols // tensors).transpose(2, 0, 1, 3)
    mine = lax.all_to_all(mine, "tensor", split_axis=0, concat_axis=0, tiled=True)
    return jnp.sum(mine.astype(F32), axis=0)


def sum_all(value):
    if lax.axis_size("dp") != 8:
        return lax.psum(value, ("dp", "tensor"))
    for bit in (1, 2, 4):
        value = value + flip(value, bit)
    for bit in (1, 2):
        value = value + flip_z(value, bit)
    return value


def body(
    content_stream,
    query_stream,
    memory,
    content_tangent,
    query_tangent,
    seq_lengths,
    factor_order,
    memory_lengths,
    slot_sequence,
    query_weight,
    key_weight,
    value_weight,
    pos_weight,
    out_weight,
    up_weight,
    up_bias,
    down_weight,
    down_bias,
    word_bias,
    pos_bias,
    first_gain,
    first_shift,
    second_gain,
    second_shift,
):
    groups, tensors = lax.axis_size("dp"), lax.axis_size("tensor")
    micro, part_len, width = content_stream.shape
    mem_part = memory.shape[1]
    seq_len, mem_total = part_len * tensors, mem_part * tensors
    klen, span = mem_total + seq_len, mem_total + 2 * seq_len
    count = micro * groups
    here, lane = lax.axis_index("dp"), lax.axis_index("tensor")
    core = here % 2
    lead = core == 0
    block = 256
    assert 2 * micro == tensors

    def swap(arr):
        return flip(arr, CORE)

    def to_unit(first, second):
        got = swap(jnp.where(lead, second, first))
        low = jnp.where(lead, first, got)
        high = jnp.where(lead, got, second)
        both = jnp.concatenate([low, high], 0)
        both = lax.all_to_all(both, "tensor", split_axis=0, concat_axis=0, tiled=True)
        return both.reshape(seq_len, width)

    def from_unit(arr):
        both = arr.reshape(tensors, part_len, width)
        both = lax.all_to_all(both, "tensor", split_axis=0, concat_axis=0, tiled=True)
        low, high = both[:micro], both[micro:]
        got = swap(jnp.where(lead, high, low))
        return jnp.where(lead, low, got), jnp.where(lead, got, high)

    seq_id = (here // 2) * tensors + lane
    ids = jnp.arange(count, dtype=jnp.int32)
    slot_of = jnp.sum(jnp.where(slot_sequence[None, :] == ids[:, None], ids[None, :], 0), axis=1)
    counts = jnp.concatenate([seq_lengths, memory_lengths])
    if groups == 8:
        lengths = jnp.stack([counts] + [flip(counts, bit) for bit in range(1, groups)])
        turn = here
    else:
        lengths = lax.all_gather(counts, "dp", axis=0, tiled=False)
        turn = 0
    slot = slot_of[seq_id]
    length = lengths[turn ^ (seq_id // micro), seq_id % micro]
    mem_valid = lengths[turn ^ (slot // micro), micro + slot % micro]
    other = swap(factor_order)
    orders = jnp.concatenate(
        [jnp.where(lead, factor_order, other), jnp.where(lead, other, factor_order)], 0
    )
    rank = lax.dynamic_index_in_dim(orders, lane, 0, keepdims=False)
    key_pos = jnp.arange(klen, dtype=jnp.int32)
    hidden = jnp.int32(1 << 20)
    mem_rank = jnp.where(key_pos[:mem_total] >= mem_total - mem_valid, -1, hidden)
    own_rank = jnp.where(key_pos[:seq_len] < length, rank, hidden)
    key_rank = jnp.concatenate([mem_rank, own_rank])[None, :]
    thr = (rank + jnp.where(lead, 1, 0))[:, None]

    stream = to_unit(content_stream, query_stream)
    content = jnp.where(lead, stream, swap(stream))

    piece = mem_part // groups
    spread = lax.all_to_all(
        memory.reshape(micro, groups, piece, width), "dp", split_axis=1, concat_axis=1, tiled=True
    )
    spread = spread.transpose(1, 0, 2, 3).reshape(count, piece, width)
    spread = jnp.take(spread, slot_of, axis=0)
    spread = spread.reshape(groups // 2, tensors, 2, piece // 2, width).transpose(0, 2, 1, 3, 4)
    spread = lax.all_to_all(
        spread.reshape(groups, tensors, piece // 2, width),
        "dp",
        split_axis=0,
        concat_axis=0,
        tiled=True,
    )
    spread = lax.all_to_all(spread, "tensor", split_axis=1, concat_axis=1, tiled=True)
    got = swap(spread)
    mem_rows = jnp.stack([jnp.where(lead, spread, got), jnp.where(lead, got, spread)])
    mem_rows = mem_rows.transpose(2, 1, 0, 3, 4).reshape(mem_total, width)

    tangent = to_unit(content_tangent, query_tangent)

    rows = key_weight.shape[0]
    offs, order = piece_offsets(rows), row_order()
    pieces = gather_pieces(
        gather_columns(jnp.stack([key_weight, value_weight, query_weight, pos_weight]))
    )
    out_pieces = gather_pieces(gather_columns(out_weight[None]))
    ud_pieces = gather_pieces(gather_columns(jnp.stack([up_weight, down_weight])))

    context = jnp.concatenate([mem_rows, content], 0)
    table = reversed_table(span, klen, width)
    row = lambda v: v.reshape(1, -1)
    keys, values, rel, q_word, q_pos, mats = project(
        offs, pieces, context, stream, table, row(word_bias), row(pos_bias)
    )
    stream_t = reorder_blocks(stream, order)
    context_t = reorder_blocks(context, order)
    table_t = reorder_blocks(table, order)

    vec, prob = attend_forward(q_word, q_pos, keys, values, rel, thr, key_rank, block)
    out, d_mixed, g_vec, g_out_e, g_out_o, g_ud_e, g_ud_o, g_upb, small = feed(
        offs,
        order,
        ud_pieces,
        out_pieces,
        vec,
        stream,
        tangent,
        row(up_bias),
        row(down_bias),
        row(first_gain),
        row(first_shift),
        row(second_gain),
        row(second_shift),
    )
    content_out, query_out = from_unit(out)
    grad_up, grad_down = scatter_sum(g_ud_e, g_ud_o)
    (grad_out,) = scatter_sum(g_out_e[None], g_out_o[None])
    early = sum_all(jnp.concatenate([g_upb.reshape(-1), small[:5].reshape(-1)]))

    d_proj, dk_t, dv_t, drel_t, biases = attend_backward(
        prob, g_vec, q_word, q_pos, keys, values, rel, block
    )
    late = sum_all(biases)
    d_context = tt(dk_t[:, mem_total:], mats[0]) + tt(dv_t[:, mem_total:], mats[1])
    partner = swap(d_context.astype(BF))
    d_stream = d_mixed + nt(d_proj, mats[2])
    d_stream = d_stream + jnp.where(lead, d_context + partner.astype(F32), 0.0)
    content_grad, query_grad = from_unit(d_stream.astype(BF))
    grad_key, grad_value, grad_query, grad_pos = scatter_sum(
        *weight_grads(stream_t, context_t, table_t, d_proj, dk_t, dv_t, drel_t)
    )
    inner = up_bias.shape[0]
    rest = early[inner:].reshape(5, width)
    return (
        content_out,
        query_out,
        content_grad,
        query_grad,
        grad_query,
        grad_key,
        grad_value,
        grad_pos,
        grad_out,
        grad_up,
        early[:inner],
        grad_down,
        rest[0],
        late[0].reshape(HEADS, DH),
        late[1].reshape(HEADS, DH),
        rest[1],
        rest[2],
        rest[3],
        rest[4],
    )


def solution(mesh):
    rows = P("dp", "tensor", None)
    mat = P("dp", "tensor")
    return jax.shard_map(
        body,
        mesh=mesh,
        in_specs=(rows,) * 5
        + (P("dp"), P("dp", None), P("dp"), P())
        + (mat,) * 6
        + (P(), mat)
        + (P(),) * 7,
        out_specs=(rows,) * 4 + (mat,) * 6 + (P(), mat) + (P(),) * 7,
        check_vma=False,
    )
```

```python
import functools

import jax
import jax.numpy as jnp
import numpy as np
from jax import lax
from jax.experimental import pallas as pl
from jax.experimental.pallas import tpu as pltpu
from jax.sharding import PartitionSpec as P

HEADS = 12
DH = 64
PAIR = 2 * DH
EPS = 1e-06
BF = jnp.bfloat16
F32 = jnp.float32
LIMIT = 60 * 1024 * 1024
SMEM_SPEC = pl.BlockSpec(memory_space=pltpu.SMEM)
ANY_SPEC = pl.BlockSpec(memory_space=pl.ANY)


def nn(left, right):
    return jnp.dot(left, right, preferred_element_type=F32)


def nt(left, right):
    return lax.dot_general(left, right, (((1,), (1,)), ((), ())), preferred_element_type=F32)


def tn(left, right):
    return lax.dot_general(left, right, (((0,), (0,)), ((), ())), preferred_element_type=F32)


def tt(left, right):
    return lax.dot_general(left, right, (((0,), (1,)), ((), ())), preferred_element_type=F32)


def reversed_table(count, first, width):
    dist = (first - np.arange(count)).astype(np.float32)
    half = width // 2
    power = np.arange(half).astype(np.float32) * np.float32(2.0 / width)
    freq = np.float32(1.0) / np.float32(10000.0) ** power
    angle = (dist[:, None] * freq[None, :]).astype(np.float64)
    return np.concatenate([np.sin(angle), np.cos(angle)], axis=1).astype(np.float32).astype(BF)


MESH = pl.DeviceIdType.MESH
CORE, XBIT, YBIT = 1, 2, 4


class Place:
    def __init__(self):
        self.d, self.z = lax.axis_index("dp"), lax.axis_index("tensor")
        self.core = lax.rem(self.d, 2)
        self.x = lax.rem(lax.div(self.d, 2), 2)
        self.y = lax.div(self.d, 4)

    def dp(self, bits):
        at = self.d
        if bits & CORE:
            at = at + (1 - 2 * self.core)
        if bits & XBIT:
            at = at + (2 - 4 * self.x)
        if bits & YBIT:
            at = at + (4 - 8 * self.y)
        return at

    def up(self, step):
        return lax.rem(self.z + step, 4) if step else self.z


def push(src, dst, send, recv, dp, z):
    return pltpu.make_async_remote_copy(
        src_ref=src,
        dst_ref=dst,
        send_sem=send,
        recv_sem=recv,
        device_id=(dp, z),
        device_id_type=MESH,
    )


def settle(ref, sem):
    pltpu.make_async_copy(ref, ref, sem).wait()


def greet(partners):
    barrier = pltpu.get_barrier_semaphore()
    for partner in partners:
        pl.semaphore_signal(barrier, inc=1, device_id=partner, device_id_type=MESH)
    pl.semaphore_wait(barrier, len(partners))


GATHER = (
    (0, 0, XBIT),
    (0, 1, YBIT),
    (0, 0, YBIT),
    (0, 1, XBIT),
    (XBIT, 0, YBIT),
    (YBIT, 1, XBIT),
    (0, 0, CORE),
    (0, 1, CORE),
    (XBIT, 0, CORE),
    (YBIT, 1, CORE),
    (YBIT, 0, CORE),
    (XBIT, 1, CORE),
    (XBIT | YBIT, 0, CORE),
    (XBIT | YBIT, 1, CORE),
)


class Gather:
    def __init__(self, place, dst, own, send, recv):
        self.place, self.dst, self.own = place, dst, own
        self.send, self.recv = send, recv
        self.half = dst.shape[1] // 16

    def region(self, owner, half):
        at = self.place.dp(owner) * (2 * self.half) + half * self.half
        return self.dst.at[:, pl.ds(pl.multiple_of(at, 16), self.half), :]

    def copy(self, i):
        owner, half, to = GATHER[i]
        src = self.region(owner, half)
        if owner == 0:
            src = self.own.at[:, half * self.half : (half + 1) * self.half, :]
        place = self.place
        return push(
            src, self.region(owner, half), self.send.at[i], self.recv.at[i], place.dp(to), place.z
        )

    def begin(self):
        for i in (0, 1, 2, 3, 6, 7):
            self.copy(i).start()

    def after(self, arrived, started):
        for i, more in zip(arrived, started):
            self.copy(i).wait_recv()
            for j in more:
                self.copy(j).start()

    def middle(self):
        self.after((0, 1), ((4, 8), (5, 9)))

    def late(self):
        self.after((2, 3), ((10,), (11,)))

    def last(self):
        self.after((4, 5), ((12,), (13,)))

    def end(self):
        for i in range(6, 14):
            self.copy(i).wait_recv()
        for i in range(14):
            self.copy(i).wait_send()


def exchange_kernel(
    slot_ref,
    content,
    query,
    memory,
    ints,
    *refs,
):
    mats, (upw, dnw) = refs[:5], refs[5:7]
    context, stream, all_ints, whole, out_slab, ud_slab = refs[7:13]
    (
        spread,
        picked,
        shards,
        slab,
        mat_send,
        ud_send,
        int_send,
        spread_send,
        pick_send,
        stream_send,
        gather_send,
        gather_recv,
        recv,
    ) = refs[13:]
    place = Place()
    d, z, core = place.d, place.z, place.core
    part = content.shape[1]
    mem_total = part * 4
    piece = part // 8
    greet([(place.dp(r), place.up(k)) for r in range(8) for k in range(4) if r or k])

    spread_copies = []
    for r in range(8):
        to = place.dp(r)
        src = memory.at[:, pl.ds(pl.multiple_of(to * piece, 16), piece), :]
        dst = spread.at[pl.ds(2 * d, 2)]
        if r == 0:
            pltpu.make_async_copy(src, dst, recv.at[0]).start()
        else:
            spread_copies.append(push(src, dst, spread_send.at[r - 1], recv.at[0], to, z))
    mat_copies = []
    for m, mat in enumerate(mats):
        pltpu.make_async_copy(mat, shards.at[m, z], recv.at[1]).start()
        for k in range(1, 4):
            at = mat_send.at[3 * m + k - 1]
            mat_copies.append(push(mat, shards.at[m, z], at, recv.at[1], d, place.up(k)))
    int_copies = []
    for r in range(8):
        if r == 0:
            pltpu.make_async_copy(ints, all_ints.at[d], recv.at[2]).start()
        else:
            int_copies.append(
                push(ints, all_ints.at[d], int_send.at[r - 1], recv.at[2], place.dp(r), z)
            )
    for copy in mat_copies + spread_copies + int_copies:
        copy.start()

    def stream_copy(i, act):
        j, kind = i // 3, i % 3
        to, row = 2 * core + j, pl.multiple_of(z * part, 16)
        if kind < 2:
            dp = d - core + kind
            src, dst, sem = content.at[j], context.at[pl.ds(mem_total + row, part), :], recv.at[3]
        else:
            dp = d - core + 1
            src, dst, sem = query.at[j], stream.at[pl.ds(row, part), :], recv.at[4]
        here = jnp.logical_and(dp == d, to == z)
        local = pltpu.make_async_copy(src, dst, sem)
        remote = push(src, dst, stream_send.at[i], sem, dp, to)
        if act == "start":
            pl.when(here)(local.start)
            pl.when(jnp.logical_not(here))(remote.start)
        else:
            pl.when(jnp.logical_not(here))(remote.wait_send)

    for i in range(6):
        stream_copy(i, "start")

    settle(shards, recv.at[1])
    for m in range(5):
        slab[m] = jnp.concatenate([shards[m, k] for k in range(4)], axis=1)
    rows = slab.shape[1]
    own_rows = pl.ds(pl.multiple_of(d * rows, 16), rows)
    gather = Gather(place, whole, slab.at[0:4], gather_send, gather_recv)
    gather.begin()
    pltpu.make_async_copy(slab.at[0:4], whole.at[:, own_rows, :], recv.at[6]).start()
    pltpu.make_async_copy(slab.at[4:5], out_slab, recv.at[7]).start()

    settle(spread, recv.at[0])
    for q in range(16):
        picked[q] = spread[slot_ref[q]]
    pick_copies = []
    row = pl.multiple_of(z * part + d * piece, 16)
    for r in range(8):
        for k in range(4):
            to, lane = place.dp(r), place.up(k)
            src = picked.at[4 * lax.div(to, 2) + lane]
            dst = context.at[pl.ds(row, piece), :]
            if r or k:
                copy = push(src, dst, pick_send.at[4 * r + k - 1], recv.at[5], to, lane)
                pick_copies.append(copy)
            else:
                copy = pltpu.make_async_copy(src, dst, recv.at[5])
            copy.start()

    width = upw.shape[1]
    cols = pl.ds(pl.multiple_of(z * width, 128), width)
    ud_copies = []
    for m, mat in enumerate((upw, dnw)):
        pltpu.make_async_copy(mat, ud_slab.at[m, :, cols], recv.at[8]).start()
        for k in range(1, 4):
            at = ud_send.at[3 * m + k - 1]
            ud_copies.append(push(mat, ud_slab.at[m, :, cols], at, recv.at[8], d, place.up(k)))
            ud_copies[-1].start()

    gather.middle()
    gather.late()
    gather.last()
    gather.end()
    settle(whole.at[:, own_rows, :], recv.at[6])
    settle(out_slab, recv.at[7])
    settle(ud_slab, recv.at[8])
    settle(all_ints, recv.at[2])
    settle(context.at[mem_total:, :], recv.at[3])
    settle(context.at[:mem_total, :], recv.at[5])

    @pl.when(core == 1)
    def _():
        settle(stream, recv.at[4])

    for i in range(6):
        stream_copy(i, "wait")
    for copy in mat_copies + spread_copies + int_copies + pick_copies + ud_copies:
        copy.wait_send()


def exchange(slot_of, content, query, memory, ints, mats, upw, dnw):
    micro, part, width = content.shape
    rows = mats[0].shape[0]
    inner = upw.shape[1] * 4
    vmem = pl.BlockSpec(memory_space=pltpu.VMEM)
    dma = lambda n: pltpu.SemaphoreType.DMA((n,))
    return pl.pallas_call(
        exchange_kernel,
        in_specs=[SMEM_SPEC] + [ANY_SPEC] * 3 + [vmem] * 8,
        out_specs=[ANY_SPEC] * 6,
        out_shape=[
            jax.ShapeDtypeStruct((8 * part, width), BF),
            jax.ShapeDtypeStruct((4 * part, width), BF),
            jax.ShapeDtypeStruct((8,) + ints.shape, jnp.int32),
            jax.ShapeDtypeStruct((4, 8 * rows, width), BF),
            jax.ShapeDtypeStruct((1, rows, width), BF),
            jax.ShapeDtypeStruct((2, rows, inner), BF),
        ],
        scratch_shapes=[
            pltpu.VMEM((16, part // 8, width), BF),
            pltpu.VMEM((16, part // 8, width), BF),
            pltpu.VMEM((5, 4, rows, width // 4), BF),
            pltpu.VMEM((5, rows, width), BF),
            dma(15),
            dma(6),
            dma(7),
            dma(7),
            dma(31),
            dma(6),
            dma(14),
            dma(14),
            dma(9),
        ],
        compiler_params=pltpu.CompilerParams(
            collective_id=1, has_side_effects=True, vmem_limit_bytes=LIMIT
        ),
        cost_estimate=pl.CostEstimate(flops=0, bytes_accessed=64 << 20, transcendentals=0),
        name="exchange",
    )(slot_of, content, query, memory, ints, *mats, upw, dnw)


def head_lanes(array, head):
    lane = lax.broadcasted_iota(jnp.int32, array.shape, 1)
    return jnp.where((lane >= DH) == (head == 1), array, jnp.zeros_like(array))


def attend_forward_step(
    block, qw_ref, qp_ref, k_ref, v_ref, rel_ref, thr_ref, kr_ref, vec_ref, prob_ref
):
    rows, klen = qw_ref.shape[0], k_ref.shape[0]
    width = klen + block
    keys, values = k_ref[...], v_ref[...]
    for part in range(rows // block):
        at = slice(part * block, (part + 1) * block)
        first = rows - (part + 1) * block
        qw, qp = qw_ref[at, :], qp_ref[at, :]
        rel = rel_ref[first : first + width, :]
        seen = kr_ref[...] < thr_ref[at, :]
        vecs = []
        for head in range(2):
            raw = nt(head_lanes(qp, head), rel)
            moved = pltpu.roll(raw, 0, 1, stride=1, stride_axis=0)[:, block:]
            score = nt(head_lanes(qw, head), keys) + moved
            score = jnp.where(seen, score, -1e30)
            expo = jnp.exp(score - jnp.max(score, axis=1, keepdims=True))
            prob = (expo * (1.0 / jnp.sum(expo, axis=1, keepdims=True))).astype(BF)
            prob_ref[head, at, :] = prob
            vecs.append(nn(prob, values))
        lane = lax.broadcasted_iota(jnp.int32, vecs[0].shape, 1)
        vec_ref[at, :] = jnp.where(lane < DH, vecs[0], vecs[1]).astype(BF)


def attend_forward_kernel(block, wired, *refs):
    if not wired:
        attend_forward_step(block, *refs)
        return
    ins, (out_slab, ud_slab, ctan, qtan) = refs[:7], refs[7:11]
    outs, (wo, ud, tangent) = refs[11:13], refs[13:16]
    out_send, out_recv, ud_send, ud_recv, tan_send, recv = refs[16:]
    step, steps = pl.program_id(0), pl.num_programs(0)
    place = Place()
    d, z, core = place.d, place.z, place.core
    gathers = (
        Gather(place, ud, ud_slab, ud_send, ud_recv),
        Gather(place, wo, out_slab, out_send, out_recv),
    )
    rows, part = out_slab.shape[1], ctan.shape[1]
    own_rows = pl.ds(pl.multiple_of(d * rows, 16), rows)

    def tan_copy(i, act):
        j, kind = i // 2, i % 2
        to, dp = 2 * core + j, d - core + kind
        src = (ctan, qtan)[kind].at[j]
        dst = tangent.at[pl.ds(pl.multiple_of(z * part, 16), part), :]
        here = jnp.logical_and(dp == d, to == z)
        local = pltpu.make_async_copy(src, dst, recv.at[0])
        remote = push(src, dst, tan_send.at[i], recv.at[0], dp, to)
        if act == "start":
            pl.when(here)(local.start)
            pl.when(jnp.logical_not(here))(remote.start)
        else:
            pl.when(jnp.logical_not(here))(remote.wait_send)

    @pl.when(step == 0)
    def _():
        partners = [(place.dp(r), z) for r in (CORE, XBIT, YBIT)]
        partners += [(place.dp(r), place.up(k)) for k in (1, 2, 3) for r in (0, CORE)]
        greet(partners)
        for gather in gathers:
            gather.begin()
        pltpu.make_async_copy(ud_slab, ud.at[:, own_rows, :], recv.at[1]).start()
        pltpu.make_async_copy(out_slab, wo.at[:, own_rows, :], recv.at[2]).start()
        for i in range(4):
            tan_copy(i, "start")

    @pl.when(step == 3)
    def _():
        for gather in gathers:
            gather.middle()

    attend_forward_step(block, *ins, *outs)

    @pl.when(step == steps - 1)
    def _():
        for gather in gathers:
            gather.late()
        for gather in gathers:
            gather.last()
        for gather in gathers:
            gather.end()
        settle(ud.at[:, own_rows, :], recv.at[1])
        settle(wo.at[:, own_rows, :], recv.at[2])
        settle(tangent, recv.at[0])
        for i in range(4):
            tan_copy(i, "wait")


def attend_forward(qw, qp, keys, values, rel, thr, key_rank, block, wires=()):
    rows, width = qw.shape
    klen, span = keys.shape[0], rel.shape[0]
    col = lambda count: pl.BlockSpec((count, PAIR), lambda p: (0, p))
    in_specs = [
        col(rows),
        col(rows),
        col(klen),
        col(klen),
        col(span),
        pl.BlockSpec((rows, 1), lambda p: (0, 0)),
        pl.BlockSpec((1, klen), lambda p: (0, 0)),
    ]
    out_specs = [col(rows), pl.BlockSpec((2, rows, klen), lambda p: (p, 0, 0))]
    out_shape = [
        jax.ShapeDtypeStruct((rows, width), BF),
        jax.ShapeDtypeStruct((width // DH, rows, klen), BF),
    ]
    params = dict(vmem_limit_bytes=LIMIT)
    scratch = []
    if wires:
        vmem = pl.BlockSpec(memory_space=pltpu.VMEM)
        in_specs += [vmem, vmem, ANY_SPEC, ANY_SPEC]
        out_specs += [ANY_SPEC] * 3
        inner = wires[1].shape[2]
        out_shape += [
            jax.ShapeDtypeStruct((1, width, width), BF),
            jax.ShapeDtypeStruct((2, width, inner), BF),
            jax.ShapeDtypeStruct((rows, width), BF),
        ]
        scratch = [pltpu.SemaphoreType.DMA((n,)) for n in (14, 14, 14, 14, 4, 3)]
        params.update(collective_id=2, has_side_effects=True)
    return pl.pallas_call(
        functools.partial(attend_forward_kernel, block, bool(wires)),
        grid=(width // PAIR,),
        in_specs=in_specs,
        out_specs=out_specs,
        out_shape=out_shape,
        scratch_shapes=scratch,
        compiler_params=pltpu.CompilerParams(**params),
        cost_estimate=pl.CostEstimate(
            flops=8 * rows * klen * width, bytes_accessed=16 << 20, transcendentals=12 * rows * klen
        ),
        name="attend_forward",
    )(qw, qp, keys, values, rel, thr, key_rank, *wires)


def attend_backward_kernel(
    block,
    prob_ref,
    gvec_ref,
    qw_ref,
    qp_ref,
    k_ref,
    v_ref,
    rel_ref,
    dproj_ref,
    dk_ref,
    dv_ref,
    drel_ref,
    bias_ref,
    rel_acc,
):
    rows, klen = qw_ref.shape[0], k_ref.shape[0]
    width = klen + block
    keys, values = k_ref[...], v_ref[...]
    row = lax.broadcasted_iota(jnp.int32, (block, block), 0)
    col = lax.broadcasted_iota(jnp.int32, (block, block), 1)
    mirror = (row + col == block - 1).astype(BF)
    rel_acc[...] = jnp.zeros_like(rel_acc)
    d_keys, d_values = [None, None], [None, None]
    word_sum = jnp.zeros((1, PAIR), F32)
    pos_sum = jnp.zeros((1, PAIR), F32)
    for part in range(rows // block):
        at = slice(part * block, (part + 1) * block)
        first = rows - (part + 1) * block
        gvec, qw = gvec_ref[at, :], qw_ref[at, :]
        gvec_t = jnp.transpose(gvec.astype(F32)).astype(BF)
        qw_t = jnp.transpose(qw.astype(F32)).astype(BF)
        qp_t = jnp.transpose(nn(mirror, qp_ref[at, :])).astype(BF)
        rel = rel_ref[first : first + width, :]
        word_parts, pos_parts = [], []
        for head in range(2):
            own = slice(head * DH, (head + 1) * DH)
            prob = prob_ref[head, at, :]
            d_prob = nt(head_lanes(gvec, head), values)
            weight = prob.astype(F32)
            inner = jnp.sum(weight * d_prob, axis=1, keepdims=True)
            g_sum = (weight * (d_prob - inner) * 0.125).astype(BF)
            dv = nn(gvec_t[own, :], prob)
            dk = nn(qw_t[own, :], g_sum)
            d_values[head] = dv if part == 0 else d_values[head] + dv
            d_keys[head] = dk if part == 0 else d_keys[head] + dk
            turned = nn(mirror, g_sum)
            padded = jnp.concatenate([jnp.zeros((block, block), F32), turned], axis=1)
            moved = pltpu.roll(padded, width - block + 1, 1, stride=1, stride_axis=0).astype(BF)
            word_parts.append(nn(turned.astype(BF), keys))
            pos_parts.append(nn(moved, rel))
            rel_acc[own, first : first + width] += nn(qp_t[own, :], moved)
        lane = lax.broadcasted_iota(jnp.int32, word_parts[0].shape, 1)
        word = jnp.where(lane < DH, word_parts[0], word_parts[1])
        pos = jnp.where(lane < DH, pos_parts[0], pos_parts[1])
        word_sum = word_sum + jnp.sum(word, axis=0, keepdims=True)
        pos_sum = pos_sum + jnp.sum(pos, axis=0, keepdims=True)
        dproj_ref[at, :] = nn(mirror, (word + pos).astype(BF)).astype(BF)
    for head in range(2):
        own = slice(head * DH, (head + 1) * DH)
        dv_ref[own, :] = d_values[head].astype(BF)
        dk_ref[own, :] = (8.0 * d_keys[head]).astype(BF)
    drel_ref[...] = (8.0 * rel_acc[...]).astype(BF)
    bias_ref[0:1, :] = word_sum
    bias_ref[1:2, :] = pos_sum


def attend_backward(prob, gvec, qw, qp, keys, values, rel, block):
    rows, width = qw.shape
    klen, span = keys.shape[0], rel.shape[0]
    col = lambda count: pl.BlockSpec((count, PAIR), lambda p: (0, p))
    rowb = lambda count: pl.BlockSpec((PAIR, count), lambda p: (p, 0))
    return pl.pallas_call(
        functools.partial(attend_backward_kernel, block),
        grid=(width // PAIR,),
        in_specs=[
            pl.BlockSpec((2, rows, klen), lambda p: (p, 0, 0)),
            col(rows),
            col(rows),
            col(rows),
            col(klen),
            col(klen),
            col(span),
        ],
        out_specs=[col(rows), rowb(klen), rowb(klen), rowb(span), col(2)],
        out_shape=[
            jax.ShapeDtypeStruct((rows, width), BF),
            jax.ShapeDtypeStruct((width, klen), BF),
            jax.ShapeDtypeStruct((width, klen), BF),
            jax.ShapeDtypeStruct((width, span), BF),
            jax.ShapeDtypeStruct((2, width), F32),
        ],
        scratch_shapes=[pltpu.VMEM((PAIR, span), F32)],
        compiler_params=pltpu.CompilerParams(vmem_limit_bytes=LIMIT),
        cost_estimate=pl.CostEstimate(
            flops=16 * rows * klen * width, bytes_accessed=20 << 20, transcendentals=0
        ),
        name="attend_backward",
    )(prob, gvec, qw, qp, keys, values, rel)


def norm_parts(value):
    center = value - jnp.mean(value, axis=1, keepdims=True)
    scale = lax.rsqrt(jnp.mean(center * center, axis=1, keepdims=True) + EPS)
    return center * scale, scale


def norm_pull(normed, scale, err):
    inner = jnp.mean(err * normed, axis=1, keepdims=True)
    return (err - jnp.mean(err, axis=1, keepdims=True) - normed * inner) * scale


def sum_rows(value):
    return jnp.sum(value, axis=0, keepdims=True)


def feed_kernel(steps, *refs):
    (
        ud_hbm,
        wo_hbm,
        vec_ref,
        x_ref,
        tan_ref,
        upb_ref,
        dnb_ref,
        g1_ref,
        s1_ref,
        g2_ref,
        s2_ref,
        out_ref,
        dmix_ref,
        gvec_ref,
        go_ref,
        gud_ref,
        gupb_ref,
        small_ref,
        ud_ref,
        wo_ref,
        n1_ref,
        r1_ref,
        fb_ref,
        fbt_ref,
        acc_ref,
        act_ref,
        slope_ref,
        gd_ref,
        gdt_ref,
        sems,
    ) = refs
    step = pl.program_id(0)
    chunk = act_ref.shape[2]
    cols = pl.ds(pl.multiple_of(lax.rem(step, steps) * chunk, chunk), chunk)

    @pl.when(step == 0)
    def _():
        wo_copy = pltpu.make_async_copy(wo_hbm, wo_ref, sems.at[0])
        ud_copy = pltpu.make_async_copy(ud_hbm, ud_ref, sems.at[1])
        wo_copy.start()
        ud_copy.start()
        wo_copy.wait()
        normed, scale = norm_parts(nt(vec_ref[...], wo_ref[0]) + x_ref[...].astype(F32))
        n1_ref[...] = normed
        r1_ref[...] = scale
        first = normed * g1_ref[...] + s1_ref[...]
        fb_ref[...] = first.astype(BF)
        fbt_ref[...] = jnp.transpose(first).astype(BF)
        acc_ref[...] = first + dnb_ref[...]
        ud_copy.wait()

    @pl.when(step < steps)
    def _():
        upper = nn(fb_ref[...], ud_ref[0, :, cols]) + upb_ref[...]
        square = upper * upper
        root = 0.7978845608028654
        bend = jnp.tanh(root * (upper + 0.044715 * (square * upper)))
        half = 0.5 * (1.0 + bend)
        act = (upper * half).astype(BF)
        act_ref[step] = act
        slope_ref[step] = half + 0.5 * upper * (1.0 - bend * bend) * (
            root + (3 * 0.044715 * root) * square
        )
        acc_ref[...] += nt(act, ud_ref[1, :, cols])

    @pl.when(step == steps - 1)
    def _():
        normed, scale = norm_parts(acc_ref[...])
        out_ref[...] = (normed * g2_ref[...] + s2_ref[...]).astype(BF)
        tan = tan_ref[...].astype(F32)
        d_down = norm_pull(normed, scale, tan * g2_ref[...])
        small_ref[0:1, :] = sum_rows(d_down)
        small_ref[3:4, :] = sum_rows(tan * normed)
        small_ref[4:5, :] = sum_rows(tan)
        gd_ref[...] = d_down.astype(BF)
        gdt_ref[...] = jnp.transpose(d_down).astype(BF)
        acc_ref[...] = d_down

    @pl.when(step >= steps)
    def _():
        at = step - steps
        d_up = nn(gd_ref[...], ud_ref[1, :, cols]) * slope_ref[at]
        gupb_ref[...] = sum_rows(d_up)
        g_up = d_up.astype(BF)
        acc_ref[...] += nt(g_up, ud_ref[0, :, cols])
        gud_ref[0] = nn(fbt_ref[...], g_up).astype(BF)
        gud_ref[1] = nn(gdt_ref[...], act_ref[at]).astype(BF)

    @pl.when(step == 2 * steps - 1)
    def _():
        d_first, normed = acc_ref[...], n1_ref[...]
        small_ref[1:2, :] = sum_rows(d_first * normed)
        small_ref[2:3, :] = sum_rows(d_first)
        d_mixed = norm_pull(normed, r1_ref[...], d_first * g1_ref[...])
        dmix_ref[...] = d_mixed
        gvec_ref[...] = nn(d_mixed.astype(BF), wo_ref[0]).astype(BF)
        gdt_ref[...] = jnp.transpose(d_mixed).astype(BF)
        go_ref[...] = nn(gdt_ref[...], vec_ref[...]).astype(BF)


def feed(ud, wo, vec, x, tan, upb, dnb, g1, s1, g2, s2):
    rows, width = vec.shape
    inner = upb.shape[1]
    chunk = 512
    steps = inner // chunk
    whole = lambda a, b: pl.BlockSpec((a, b), lambda i: (0, 0))
    late = lambda i: jnp.maximum(i - steps, 0)
    grads = pl.BlockSpec((2, width, chunk), lambda i: (0, 0, late(i)))
    return pl.pallas_call(
        functools.partial(feed_kernel, steps),
        grid=(2 * steps,),
        in_specs=[ANY_SPEC] * 2
        + [whole(rows, width)] * 3
        + [pl.BlockSpec((1, chunk), lambda i: (0, lax.rem(i, steps)))]
        + [whole(1, width)] * 5,
        out_specs=[
            whole(rows, width),
            whole(rows, width),
            whole(rows, width),
            whole(width, width),
            grads,
            pl.BlockSpec((1, chunk), lambda i: (0, late(i))),
            whole(8, width),
        ],
        out_shape=[
            jax.ShapeDtypeStruct((rows, width), BF),
            jax.ShapeDtypeStruct((rows, width), F32),
            jax.ShapeDtypeStruct((rows, width), BF),
            jax.ShapeDtypeStruct((width, width), BF),
            jax.ShapeDtypeStruct((2, width, inner), BF),
            jax.ShapeDtypeStruct((1, inner), F32),
            jax.ShapeDtypeStruct((8, width), F32),
        ],
        scratch_shapes=[
            pltpu.VMEM((2, width, inner), BF),
            pltpu.VMEM((1, width, width), BF),
            pltpu.VMEM((rows, width), F32),
            pltpu.VMEM((rows, 1), F32),
            pltpu.VMEM((rows, width), BF),
            pltpu.VMEM((width, rows), BF),
            pltpu.VMEM((rows, width), F32),
            pltpu.VMEM((steps, rows, chunk), BF),
            pltpu.VMEM((steps, rows, chunk), F32),
            pltpu.VMEM((rows, width), BF),
            pltpu.VMEM((width, rows), BF),
            pltpu.SemaphoreType.DMA((2,)),
        ],
        compiler_params=pltpu.CompilerParams(vmem_limit_bytes=LIMIT),
        cost_estimate=pl.CostEstimate(
            flops=12 * rows * width * inner, bytes_accessed=36 << 20, transcendentals=rows * inner
        ),
        name="feed",
    )(ud, wo, vec, x, tan, upb, dnb, g1, s1, g2, s2)


def project_kernel(
    w_ref, ctx_ref, q_ref, table_ref, wb_ref, pb_ref, k_ref, v_ref, rel_ref, qw_ref, qp_ref, x_ref
):
    lead = lax.rem(lax.axis_index("dp"), 2) == 0
    back = ctx_ref.shape[0] - q_ref.shape[0]
    block = 256

    def loop(count, step):
        def run(i, carry):
            step(pl.ds(pl.multiple_of(i * block, block), block))
            return carry

        lax.fori_loop(0, count // block, run, 0)

    def context_step(at):
        k_ref[at, :] = nn(ctx_ref[at, :], w_ref[0]).astype(BF)
        v_ref[at, :] = nn(ctx_ref[at, :], w_ref[1]).astype(BF)

    def stream_step(at):
        own = ctx_ref[pl.ds(pl.multiple_of(at.start + back, block), block), :]
        x_ref[at, :] = jnp.where(lead, own, q_ref[at, :])
        proj = nn(x_ref[at, :], w_ref[2])
        qw_ref[at, :] = (0.125 * (proj + wb_ref[...]).astype(BF).astype(F32)).astype(BF)
        qp_ref[at, :] = (0.125 * (proj + pb_ref[...]).astype(BF).astype(F32)).astype(BF)

    def table_step(at):
        rel_ref[at, :] = nn(table_ref[at, :], w_ref[3]).astype(BF)

    loop(table_ref.shape[0], table_step)
    loop(q_ref.shape[0], stream_step)
    loop(ctx_ref.shape[0], context_step)


def project(mats, context, query, table, wb, pb):
    rows, width = query.shape
    klen, span = context.shape[0], table.shape[0]
    vmem = pl.BlockSpec(memory_space=pltpu.VMEM)
    return pl.pallas_call(
        project_kernel,
        in_specs=[vmem] * 6,
        out_specs=[vmem] * 6,
        out_shape=[
            jax.ShapeDtypeStruct((klen, width), BF),
            jax.ShapeDtypeStruct((klen, width), BF),
            jax.ShapeDtypeStruct((span, width), BF),
            jax.ShapeDtypeStruct((rows, width), BF),
            jax.ShapeDtypeStruct((rows, width), BF),
            jax.ShapeDtypeStruct((rows, width), BF),
        ],
        compiler_params=pltpu.CompilerParams(vmem_limit_bytes=LIMIT),
        cost_estimate=pl.CostEstimate(
            flops=2 * (2 * klen + rows + span) * width * width,
            bytes_accessed=20 << 20,
            transcendentals=0,
        ),
        name="project",
    )(mats, context, query, table, wb, pb)


def weight_grads_kernel(xt_ref, ct_ref, tt_ref, dp_ref, dk_ref, dv_ref, dr_ref, g_ref):
    g_ref[0] = nt(ct_ref[...], dk_ref[...]).astype(BF)
    g_ref[1] = nt(ct_ref[...], dv_ref[...]).astype(BF)
    g_ref[2] = nn(xt_ref[...], dp_ref[...]).astype(BF)
    g_ref[3] = nt(tt_ref[...], dr_ref[...]).astype(BF)


def weight_grads(x_t, ctx_t, table_t, d_proj, dk_t, dv_t, drel_t):
    width, rows = x_t.shape
    klen, span = ctx_t.shape[1], table_t.shape[1]
    chunk = 256
    whole = lambda a, b: pl.BlockSpec((a, b), lambda i: (0, 0))
    rowb = lambda b: pl.BlockSpec((chunk, b), lambda i: (i, 0))
    return pl.pallas_call(
        weight_grads_kernel,
        grid=(width // chunk,),
        in_specs=[
            whole(width, rows),
            whole(width, klen),
            whole(width, span),
            pl.BlockSpec((rows, chunk), lambda i: (0, i)),
            rowb(klen),
            rowb(klen),
            rowb(span),
        ],
        out_specs=pl.BlockSpec((4, width, chunk), lambda i: (0, 0, i)),
        out_shape=jax.ShapeDtypeStruct((4, width, width), BF),
        compiler_params=pltpu.CompilerParams(vmem_limit_bytes=LIMIT),
        cost_estimate=pl.CostEstimate(
            flops=2 * (rows + 2 * klen + span) * width * width,
            bytes_accessed=20 << 20,
            transcendentals=0,
        ),
        name="weight_grads",
    )(x_t, ctx_t, table_t, d_proj, dk_t, dv_t, drel_t)


def flip(arr, bit):
    return lax.ppermute(arr, "dp", [(i, i ^ bit) for i in range(lax.axis_size("dp"))])


def flip_z(arr, bit):
    return lax.ppermute(arr, "tensor", [(i, i ^ bit) for i in range(lax.axis_size("tensor"))])


def by_bits(parts, bits):
    step = 1
    for bit in bits:
        parts = [
            jnp.where(bit == 1, parts[i ^ step], parts[i]) for i in range(len(parts))
        ]
        step *= 2
    return parts


def scatter_sum(grads):
    mine = lax.psum_scatter(grads, "dp", scatter_dimension=1, tiled=True)
    return lax.psum_scatter(mine, "tensor", scatter_dimension=2, tiled=True).astype(F32)


def sum_all(value):
    if lax.axis_size("dp") != 8:
        return lax.psum(value, ("dp", "tensor"))
    for bit in (1, 2, 4):
        value = value + flip(value, bit)
    for bit in (1, 2):
        value = value + flip_z(value, bit)
    return value


def body(
    content_stream,
    query_stream,
    memory,
    content_tangent,
    query_tangent,
    seq_lengths,
    factor_order,
    memory_lengths,
    slot_sequence,
    query_weight,
    key_weight,
    value_weight,
    pos_weight,
    out_weight,
    up_weight,
    up_bias,
    down_weight,
    down_bias,
    word_bias,
    pos_bias,
    first_gain,
    first_shift,
    second_gain,
    second_shift,
):
    groups, tensors = lax.axis_size("dp"), lax.axis_size("tensor")
    micro, part_len, width = content_stream.shape
    mem_part = memory.shape[1]
    seq_len, mem_total = part_len * tensors, mem_part * tensors
    klen, span = mem_total + seq_len, mem_total + 2 * seq_len
    count = micro * groups
    here, lane = lax.axis_index("dp"), lax.axis_index("tensor")
    core = here % 2
    lead = core == 0
    block = 256
    assert 2 * micro == tensors

    def swap(arr):
        return flip(arr, CORE)

    def to_unit(first, second):
        got = swap(jnp.where(lead, second, first))
        low = jnp.where(lead, first, got)
        high = jnp.where(lead, got, second)
        both = jnp.concatenate([low, high], 0)
        both = lax.all_to_all(both, "tensor", split_axis=0, concat_axis=0, tiled=True)
        return both.reshape(seq_len, width)

    def from_unit(arr):
        both = arr.reshape(tensors, part_len, width)
        both = lax.all_to_all(both, "tensor", split_axis=0, concat_axis=0, tiled=True)
        low, high = both[:micro], both[micro:]
        got = swap(jnp.where(lead, high, low))
        return jnp.where(lead, low, got), jnp.where(lead, got, high)

    seq_id = (here // 2) * tensors + lane
    ids = jnp.arange(count, dtype=jnp.int32)
    slot_of = jnp.sum(jnp.where(slot_sequence[None, :] == ids[:, None], ids[None, :], 0), axis=1)
    counts = jnp.concatenate([seq_lengths, memory_lengths])
    slot = slot_of[seq_id]
    mats = [key_weight, value_weight, query_weight, pos_weight, out_weight]
    table = jnp.asarray(reversed_table(span, klen, width))
    wires = ()
    if groups == 8:
        ints = jnp.pad(factor_order, ((0, 6), (0, 0)))
        ints = lax.dynamic_update_slice(ints, counts[None, :], (micro, 0))
        context, query, all_ints, weights, out_slab, ud_slab = exchange(
            slot_of, content_stream, query_stream, memory, ints, mats, up_weight, down_weight
        )
        wires = (out_slab, ud_slab, content_tangent, query_tangent)
        lengths = all_ints[:, micro, : 2 * micro]
        orders = all_ints[seq_id // micro, :micro]
    else:
        lengths = lax.all_gather(counts, "dp", axis=0, tiled=False)
        orders = lax.all_gather(factor_order, "dp", axis=0, tiled=False)[seq_id // micro]
        stream = to_unit(content_stream, query_stream)
        content, query = jnp.where(lead, stream, swap(stream)), stream
        tangent = to_unit(content_tangent, query_tangent)
        piece = mem_part // groups
        spread = lax.all_to_all(
            memory.reshape(micro, groups, piece, width), "dp", split_axis=1, concat_axis=1, tiled=True
        )
        spread = spread.transpose(1, 0, 2, 3).reshape(count, piece, width)
        spread = jnp.take(spread, slot_of, axis=0)
        spread = spread.reshape(groups // 2, tensors, 2, piece // 2, width).transpose(0, 2, 1, 3, 4)
        spread = lax.all_to_all(
            spread.reshape(groups, tensors, piece // 2, width),
            "dp",
            split_axis=0,
            concat_axis=0,
            tiled=True,
        )
        spread = lax.all_to_all(spread, "tensor", split_axis=1, concat_axis=1, tiled=True)
        got = swap(spread)
        mem_rows = jnp.stack([jnp.where(lead, spread, got), jnp.where(lead, got, spread)])
        mem_rows = mem_rows.transpose(2, 1, 0, 3, 4).reshape(mem_total, width)
        context = jnp.concatenate([mem_rows, content], 0)

        def whole(mat):
            mat = lax.all_gather(mat, "tensor", axis=1, tiled=True)
            return lax.all_gather(mat, "dp", axis=0, tiled=True)

        weights = jnp.stack([whole(mat) for mat in mats[:4]])
        wo = whole(out_weight)[None]
        ud = jnp.stack([whole(up_weight), whole(down_weight)])

    length = lengths[seq_id // micro, seq_id % micro]
    mem_valid = lengths[slot // micro, micro + slot % micro]
    rank = orders[seq_id % micro]
    key_pos = jnp.arange(klen, dtype=jnp.int32)
    hidden = jnp.int32(1 << 20)
    mem_rank = jnp.where(key_pos[:mem_total] >= mem_total - mem_valid, -1, hidden)
    own_rank = jnp.where(key_pos[:seq_len] < length, rank, hidden)
    key_rank = jnp.concatenate([mem_rank, own_rank])[None, :]
    thr = (rank + jnp.where(lead, 1, 0))[:, None]

    row = lambda v: v.reshape(1, -1)
    keys, values, rel, q_word, q_pos, stream = project(
        weights, context, query, table, row(word_bias), row(pos_bias)
    )
    vec, prob, *arrived = attend_forward(
        q_word, q_pos, keys, values, rel, thr, key_rank, block, wires
    )
    if wires:
        wo, ud, tangent = arrived
    out, d_mixed, g_vec, g_out, g_ud, g_upb, small = feed(
        ud,
        wo,
        vec,
        stream,
        tangent,
        row(up_bias),
        row(down_bias),
        row(first_gain),
        row(first_shift),
        row(second_gain),
        row(second_shift),
    )
    content_out, query_out = from_unit(out)
    grad_up, grad_down = scatter_sum(g_ud)
    (grad_out,) = scatter_sum(g_out[None])
    early = sum_all(jnp.concatenate([g_upb.reshape(-1), small[:5].reshape(-1)]))

    d_proj, dk_t, dv_t, drel_t, biases = attend_backward(
        prob, g_vec, q_word, q_pos, keys, values, rel, block
    )
    late = sum_all(biases)
    d_context = tt(dk_t[:, mem_total:], weights[0]) + tt(dv_t[:, mem_total:], weights[1])
    partner = swap(d_context.astype(BF))
    d_stream = d_mixed + nt(d_proj, weights[2])
    d_stream = d_stream + jnp.where(lead, d_context + partner.astype(F32), 0.0)
    content_grad, query_grad = from_unit(d_stream.astype(BF))
    grad_key, grad_value, grad_query, grad_pos = scatter_sum(
        weight_grads(
            jnp.transpose(stream), jnp.transpose(context), jnp.transpose(table), d_proj, dk_t, dv_t, drel_t
        )
    )
    inner = up_bias.shape[0]
    rest = early[inner:].reshape(5, width)
    return (
        content_out,
        query_out,
        content_grad,
        query_grad,
        grad_query,
        grad_key,
        grad_value,
        grad_pos,
        grad_out,
        grad_up,
        early[:inner],
        grad_down,
        rest[0],
        late[0].reshape(HEADS, DH),
        late[1].reshape(HEADS, DH),
        rest[1],
        rest[2],
        rest[3],
        rest[4],
    )


def solution(mesh):
    rows = P("dp", "tensor", None)
    mat = P("dp", "tensor")
    return jax.shard_map(
        body,
        mesh=mesh,
        in_specs=(rows,) * 5
        + (P("dp"), P("dp", None), P("dp"), P())
        + (mat,) * 6
        + (P(), mat)
        + (P(),) * 7,
        out_specs=(rows,) * 4 + (mat,) * 6 + (P(), mat) + (P(),) * 7,
        check_vma=False,
    )
```

```python
import functools

import jax
import jax.numpy as jnp
import numpy as np
from jax import lax
from jax.experimental import pallas as pl
from jax.experimental.pallas import tpu as pltpu
from jax.sharding import PartitionSpec as P

HEADS = 12
DH = 64
PAIR = 2 * DH
EPS = 1e-06
BF = jnp.bfloat16
F32 = jnp.float32
LIMIT = 60 * 1024 * 1024
SMEM_SPEC = pl.BlockSpec(memory_space=pltpu.SMEM)
ANY_SPEC = pl.BlockSpec(memory_space=pl.ANY)


def nn(left, right):
    return jnp.dot(left, right, preferred_element_type=F32)


def nt(left, right):
    return lax.dot_general(left, right, (((1,), (1,)), ((), ())), preferred_element_type=F32)


def tn(left, right):
    return lax.dot_general(left, right, (((0,), (0,)), ((), ())), preferred_element_type=F32)


def tt(left, right):
    return lax.dot_general(left, right, (((0,), (1,)), ((), ())), preferred_element_type=F32)


def reversed_table(count, first, width):
    dist = (first - np.arange(count)).astype(np.float32)
    half = width // 2
    power = np.arange(half).astype(np.float32) * np.float32(2.0 / width)
    freq = np.float32(1.0) / np.float32(10000.0) ** power
    angle = (dist[:, None] * freq[None, :]).astype(np.float64)
    return np.concatenate([np.sin(angle), np.cos(angle)], axis=1).astype(np.float32).astype(BF)


MESH = pl.DeviceIdType.MESH
CORE, XBIT, YBIT = 1, 2, 4


class Place:
    def __init__(self):
        self.d, self.z = lax.axis_index("dp"), lax.axis_index("tensor")
        self.core = lax.rem(self.d, 2)
        self.x = lax.rem(lax.div(self.d, 2), 2)
        self.y = lax.div(self.d, 4)

    def dp(self, bits):
        at = self.d
        if bits & CORE:
            at = at + (1 - 2 * self.core)
        if bits & XBIT:
            at = at + (2 - 4 * self.x)
        if bits & YBIT:
            at = at + (4 - 8 * self.y)
        return at

    def up(self, step):
        return lax.rem(self.z + step, 4) if step else self.z


def push(src, dst, send, recv, dp, z):
    return pltpu.make_async_remote_copy(
        src_ref=src,
        dst_ref=dst,
        send_sem=send,
        recv_sem=recv,
        device_id=(dp, z),
        device_id_type=MESH,
    )


def settle(ref, sem):
    pltpu.make_async_copy(ref, ref, sem).wait()


def greet(partners):
    barrier = pltpu.get_barrier_semaphore()
    for partner in partners:
        pl.semaphore_signal(barrier, inc=1, device_id=partner, device_id_type=MESH)
    pl.semaphore_wait(barrier, len(partners))


GATHER = (
    (0, 0, XBIT),
    (0, 1, YBIT),
    (0, 0, YBIT),
    (0, 1, XBIT),
    (XBIT, 0, YBIT),
    (YBIT, 1, XBIT),
    (0, 0, CORE),
    (0, 1, CORE),
    (XBIT, 0, CORE),
    (YBIT, 1, CORE),
    (YBIT, 0, CORE),
    (XBIT, 1, CORE),
    (XBIT | YBIT, 0, CORE),
    (XBIT | YBIT, 1, CORE),
)


class Gather:
    def __init__(self, place, dst, own, send, recv):
        self.place, self.dst, self.own = place, dst, own
        self.send, self.recv = send, recv
        self.half = dst.shape[1] // 16

    def region(self, owner, half):
        at = self.place.dp(owner) * (2 * self.half) + half * self.half
        return self.dst.at[:, pl.ds(pl.multiple_of(at, 16), self.half), :]

    def copy(self, i):
        owner, half, to = GATHER[i]
        src = self.region(owner, half)
        if owner == 0:
            src = self.own.at[:, half * self.half : (half + 1) * self.half, :]
        place = self.place
        return push(
            src, self.region(owner, half), self.send.at[i], self.recv.at[i], place.dp(to), place.z
        )

    def begin(self):
        for i in (0, 1, 2, 3, 6, 7):
            self.copy(i).start()

    def after(self, arrived, started):
        for i, more in zip(arrived, started):
            self.copy(i).wait_recv()
            for j in more:
                self.copy(j).start()

    def middle(self):
        self.after((0, 1), ((4, 8), (5, 9)))

    def late(self):
        self.after((2, 3), ((10,), (11,)))

    def last(self):
        self.after((4, 5), ((12,), (13,)))

    def end(self):
        for i in range(6, 14):
            self.copy(i).wait_recv()
        for i in range(14):
            self.copy(i).wait_send()


def chip_bits(j):
    return (XBIT if j & 1 else 0) | (YBIT if j & 2 else 0)


def add_into(dst, src):
    def run(i, carry):
        at = pl.ds(pl.multiple_of(i * 16, 16), 16)
        dst[:, at, :] = (dst[:, at, :].astype(F32) + src[:, at, :].astype(F32)).astype(BF)
        return carry

    lax.fori_loop(0, dst.shape[1] // 16, run, 0)


class Reduce:
    def __init__(self, place, sources, scratch, out):
        self.place, self.sources, self.out = place, sources, out
        self.total, self.pair, self.near, self.far, self.quarter, self.stage = scratch[:6]
        self.pair_send, self.pair_recv, self.load, self.send, self.recv, self.z_send, self.z_recv = scratch[6:]
        self.rows = self.total.shape[2]

    @staticmethod
    def scratch(count, n, rows, cols):
        part = cols // 4
        dma = lambda k: pltpu.SemaphoreType.DMA((k,))
        return [
            pltpu.VMEM((n, 4, rows, cols), BF),
            pltpu.VMEM((n, 4, rows, cols), BF),
            pltpu.VMEM((n, 2, 2, rows // 2, cols), BF),
            pltpu.VMEM((n, 2, rows // 2, cols), BF),
            pltpu.VMEM((4, n, rows, part), BF),
            pltpu.VMEM((4, n, rows, part) if part % 128 else (8, 128), BF),
            dma(4 * count),
            dma(4 * count),
            dma(4 * count),
            dma(6),
            dma(6),
            dma(3),
            dma(1),
        ]

    def pair_copies(self, j):
        place, rows = self.place, self.rows
        copies, at = [], 0
        for i, src in enumerate(self.sources):
            slot, n = len(self.sources) * j + i, src.shape[0]
            block = lambda bits: src.at[:, pl.ds(pl.multiple_of(place.dp(bits) * rows, 16), rows), :]
            remote = push(
                block(chip_bits(j) | CORE),
                self.pair.at[at : at + n, j],
                self.pair_send.at[slot],
                self.pair_recv.at[slot],
                place.dp(CORE),
                place.z,
            )
            local = pltpu.make_async_copy(
                block(chip_bits(j)), self.total.at[at : at + n, j], self.load.at[slot]
            )
            copies.append((remote, local))
            at += n
        return copies

    def half(self, j, h):
        size = self.rows // 2
        return self.total.at[:, j, h * size : (h + 1) * size, :]

    MOVES = ((3, 0, XBIT, 1), (3, 1, YBIT, 1), (1, 0, XBIT, 0), (2, 1, YBIT, 0), (2, 0, YBIT, 0), (1, 1, XBIT, 1))

    def move(self, i):
        j, h, to, where = self.MOVES[i]
        dst = self.near.at[:, h, where] if i < 4 else self.far.at[:, where]
        place = self.place
        return push(self.half(j, h), dst, self.send.at[i], self.recv.at[i], place.dp(to), place.z)

    def z_copy(self, k):
        place, part = self.place, self.quarter.shape[3]
        to = place.up(k)
        if part % 128:
            src = self.stage.at[to]
        else:
            src = self.total.at[:, 0, :, pl.ds(pl.multiple_of(to * part, 128), part)]
        dst = self.quarter.at[place.z]
        if k == 0:
            return pltpu.make_async_copy(src, dst, self.z_recv.at[0])
        return push(src, dst, self.z_send.at[k - 1], self.z_recv.at[0], place.d, to)

    def begin(self):
        for j in (3, 1, 2, 0):
            for remote, local in self.pair_copies(j):
                remote.start()
                local.start()

    def pairs(self):
        for j, moves in ((3, (0, 1)), (1, (2,)), (2, (3,)), (0, ())):
            for remote, local in self.pair_copies(j):
                local.wait()
                remote.wait_recv()
            add_into(self.total.at[:, j], self.pair.at[:, j])
            for i in moves:
                self.move(i).start()

    def middle(self):
        for i, j, h, where, more in ((0, 2, 0, 1, 4), (1, 1, 1, 1, 5), (2, 0, 0, 0, None), (3, 0, 1, 0, None)):
            self.move(i).wait_recv()
            add_into(self.half(j, h), self.near.at[:, h, where])
            if more is not None:
                self.move(more).start()

    def late(self):
        for i, h in ((4, 0), (5, 1)):
            self.move(i).wait_recv()
            add_into(self.half(0, h), self.far.at[:, h])
        part = self.quarter.shape[3]
        if part % 128:
            for k in range(4):
                for m in range(self.total.shape[0]):
                    self.stage[k, m] = self.total[m, 0, :, k * part : (k + 1) * part]
        for k in (2, 1, 3, 0):
            self.z_copy(k).start()

    def end(self):
        settle(self.quarter, self.z_recv.at[0])
        parts = [self.quarter[k].astype(F32) for k in range(4)]
        self.out[...] = (parts[0] + parts[1]) + (parts[2] + parts[3])
        for j in range(4):
            for remote, _ in self.pair_copies(j):
                remote.wait_send()
        for i in range(6):
            self.move(i).wait_send()
        for k in range(1, 4):
            self.z_copy(k).wait_send()


class Homeward:
    def __init__(self, place, src, home, send, recv):
        self.place, self.src, self.home, self.send, self.recv = place, src, home, send, recv
        self.part = home.shape[2]

    def act(self, what):
        place, part = self.place, self.part
        for k in (2, 1, 3, 0):
            to, dp = place.up(k), place.d - place.core + lax.div(place.z, 2)
            src = self.src.at[pl.ds(pl.multiple_of(to * part, 16), part), :]
            dst = self.home.at[place.core, lax.rem(place.z, 2)]
            here = jnp.logical_and(dp == place.d, to == place.z)
            remote = push(src, dst, self.send.at[k], self.recv, dp, to)
            if what == "start":
                pl.when(here)(pltpu.make_async_copy(src, dst, self.recv).start)
                pl.when(jnp.logical_not(here))(remote.start)
            else:
                pl.when(jnp.logical_not(here))(remote.wait_send)

    def start(self):
        self.act("start")

    def end(self):
        settle(self.home, self.recv)
        self.act("wait")


def pair_and_z(place):
    return [(place.dp(r), place.up(k)) for k in range(4) for r in (0, CORE) if r or k]


def near_partners(place):
    return pair_and_z(place) + [(place.dp(r), place.z) for r in (XBIT, YBIT)]


def finish_kernel(g_ref, go_ref, base_ref, ctx_ref, small_ref, *refs):
    grads_ref, home_ref, sums_ref = refs[:3]
    stream, partner, slots, part_sum, chips = refs[3:8]
    home_send, slot_send, chip_send, one_send, recv = refs[8:13]
    place = Place()
    d, z, core = place.d, place.z, place.core
    greet(near_partners(place) + [(place.dp(XBIT | YBIT), z)])
    reduce = Reduce(place, (g_ref, go_ref), refs[13:], grads_ref)
    swap = push(ctx_ref, partner, one_send.at[0], recv.at[0], place.dp(CORE), z)
    swap.start()
    reduce.begin()
    slot_copies = []
    others = [(r, k) for k in range(4) for r in (0, CORE) if r or k]
    for i, (r, k) in enumerate(others):
        copy = push(small_ref, slots.at[4 * core + z], slot_send.at[i], recv.at[1], place.dp(r), place.up(k))
        copy.start()
        slot_copies.append(copy)
    pltpu.make_async_copy(small_ref, slots.at[4 * core + z], recv.at[1]).start()

    home = Homeward(place, stream, home_ref, home_send, recv.at[2])
    swap.wait()
    block = 64

    def add_partner(i, carry):
        at = pl.ds(pl.multiple_of(i * block, block), block)
        more = jnp.where(core == 0, partner[at, :].astype(F32), 0.0)
        stream[at, :] = (base_ref[at, :] + more).astype(BF)
        return carry

    lax.fori_loop(0, stream.shape[0] // block, add_partner, 0)
    home.start()
    reduce.pairs()

    settle(slots, recv.at[1])
    total = slots[0]
    for i in range(1, 8):
        total = total + slots[i]
    part_sum[...] = total
    chip = lax.div(d, 2)
    chip_copies = []
    for i, r in enumerate((XBIT, YBIT, XBIT | YBIT)):
        copy = push(part_sum, chips.at[chip], chip_send.at[i], recv.at[3], place.dp(r), z)
        copy.start()
        chip_copies.append(copy)
    pltpu.make_async_copy(part_sum, chips.at[chip], recv.at[3]).start()

    reduce.middle()
    settle(chips, recv.at[3])
    sums_ref[...] = (chips[0] + chips[1]) + (chips[2] + chips[3])
    reduce.late()
    reduce.end()
    home.end()
    for copy in slot_copies + chip_copies:
        copy.wait_send()


def finish(grads, g_out, base, ctx, small):
    n, width, cols = grads.shape
    rows, total = width // 8, base.shape[0]
    vmem = pl.BlockSpec(memory_space=pltpu.VMEM)
    dma = lambda k: pltpu.SemaphoreType.DMA((k,))
    return pl.pallas_call(
        finish_kernel,
        in_specs=[ANY_SPEC] * 2 + [vmem] * 3,
        out_specs=[vmem, ANY_SPEC, vmem],
        out_shape=[
            jax.ShapeDtypeStruct((n + 1, rows, cols // 4), F32),
            jax.ShapeDtypeStruct((2, 2, total // 4, width), BF),
            jax.ShapeDtypeStruct(small.shape, F32),
        ],
        scratch_shapes=[
            pltpu.VMEM((total, width), BF),
            pltpu.VMEM((total, width), BF),
            pltpu.VMEM((8,) + small.shape, F32),
            pltpu.VMEM(small.shape, F32),
            pltpu.VMEM((4,) + small.shape, F32),
            dma(4),
            dma(7),
            dma(3),
            dma(1),
            dma(4),
        ]
        + Reduce.scratch(2, n + 1, rows, cols),
        compiler_params=pltpu.CompilerParams(
            collective_id=4, has_side_effects=True, vmem_limit_bytes=LIMIT
        ),
        cost_estimate=pl.CostEstimate(flops=0, bytes_accessed=64 << 20, transcendentals=0),
        name="finish",
    )(grads, g_out, base, ctx, small)


def exchange_kernel(
    slot_ref,
    content,
    query,
    memory,
    ints,
    *refs,
):
    mats, (upw, dnw) = refs[:5], refs[5:7]
    context, stream, all_ints, whole, out_slab, ud_slab = refs[7:13]
    (
        spread,
        picked,
        shards,
        slab,
        mat_send,
        ud_send,
        int_send,
        spread_send,
        pick_send,
        stream_send,
        gather_send,
        gather_recv,
        recv,
    ) = refs[13:]
    place = Place()
    d, z, core = place.d, place.z, place.core
    part = content.shape[1]
    mem_total = part * 4
    piece = part // 8
    greet([(place.dp(r), place.up(k)) for r in range(8) for k in range(4) if r or k])

    spread_copies = []
    for r in range(8):
        to = place.dp(r)
        src = memory.at[:, pl.ds(pl.multiple_of(to * piece, 16), piece), :]
        dst = spread.at[pl.ds(2 * d, 2)]
        if r == 0:
            pltpu.make_async_copy(src, dst, recv.at[0]).start()
        else:
            spread_copies.append(push(src, dst, spread_send.at[r - 1], recv.at[0], to, z))
    mat_copies = []
    for m, mat in enumerate(mats):
        pltpu.make_async_copy(mat, shards.at[m, z], recv.at[1]).start()
        for k in range(1, 4):
            at = mat_send.at[3 * m + k - 1]
            mat_copies.append(push(mat, shards.at[m, z], at, recv.at[1], d, place.up(k)))
    int_copies = []
    for r in range(8):
        if r == 0:
            pltpu.make_async_copy(ints, all_ints.at[d], recv.at[2]).start()
        else:
            int_copies.append(
                push(ints, all_ints.at[d], int_send.at[r - 1], recv.at[2], place.dp(r), z)
            )
    for copy in mat_copies + spread_copies + int_copies:
        copy.start()

    def stream_copy(i, act):
        j, kind = i // 3, i % 3
        to, row = 2 * core + j, pl.multiple_of(z * part, 16)
        if kind < 2:
            dp = d - core + kind
            src, dst, sem = content.at[j], context.at[pl.ds(mem_total + row, part), :], recv.at[3]
        else:
            dp = d - core + 1
            src, dst, sem = query.at[j], stream.at[pl.ds(row, part), :], recv.at[4]
        here = jnp.logical_and(dp == d, to == z)
        local = pltpu.make_async_copy(src, dst, sem)
        remote = push(src, dst, stream_send.at[i], sem, dp, to)
        if act == "start":
            pl.when(here)(local.start)
            pl.when(jnp.logical_not(here))(remote.start)
        else:
            pl.when(jnp.logical_not(here))(remote.wait_send)

    for i in range(6):
        stream_copy(i, "start")

    settle(shards, recv.at[1])
    for m in range(5):
        slab[m] = jnp.concatenate([shards[m, k] for k in range(4)], axis=1)
    rows = slab.shape[1]
    own_rows = pl.ds(pl.multiple_of(d * rows, 16), rows)
    gather = Gather(place, whole, slab.at[0:4], gather_send, gather_recv)
    gather.begin()
    pltpu.make_async_copy(slab.at[0:4], whole.at[:, own_rows, :], recv.at[6]).start()
    pltpu.make_async_copy(slab.at[4:5], out_slab, recv.at[7]).start()

    settle(spread, recv.at[0])
    for q in range(16):
        picked[q] = spread[slot_ref[q]]
    pick_copies = []
    row = pl.multiple_of(z * part + d * piece, 16)
    for r in range(8):
        for k in range(4):
            to, lane = place.dp(r), place.up(k)
            src = picked.at[4 * lax.div(to, 2) + lane]
            dst = context.at[pl.ds(row, piece), :]
            if r or k:
                copy = push(src, dst, pick_send.at[4 * r + k - 1], recv.at[5], to, lane)
                pick_copies.append(copy)
            else:
                copy = pltpu.make_async_copy(src, dst, recv.at[5])
            copy.start()

    width = upw.shape[1]
    cols = pl.ds(pl.multiple_of(z * width, 128), width)
    ud_copies = []
    for m, mat in enumerate((upw, dnw)):
        pltpu.make_async_copy(mat, ud_slab.at[m, :, cols], recv.at[8]).start()
        for k in range(1, 4):
            at = ud_send.at[3 * m + k - 1]
            ud_copies.append(push(mat, ud_slab.at[m, :, cols], at, recv.at[8], d, place.up(k)))
            ud_copies[-1].start()

    gather.middle()
    gather.late()
    gather.last()
    gather.end()
    settle(whole.at[:, own_rows, :], recv.at[6])
    settle(out_slab, recv.at[7])
    settle(ud_slab, recv.at[8])
    settle(all_ints, recv.at[2])
    settle(context.at[mem_total:, :], recv.at[3])
    settle(context.at[:mem_total, :], recv.at[5])

    @pl.when(core == 1)
    def _():
        settle(stream, recv.at[4])

    for i in range(6):
        stream_copy(i, "wait")
    for copy in mat_copies + spread_copies + int_copies + pick_copies + ud_copies:
        copy.wait_send()


def exchange(slot_of, content, query, memory, ints, mats, upw, dnw):
    micro, part, width = content.shape
    rows = mats[0].shape[0]
    inner = upw.shape[1] * 4
    vmem = pl.BlockSpec(memory_space=pltpu.VMEM)
    dma = lambda n: pltpu.SemaphoreType.DMA((n,))
    return pl.pallas_call(
        exchange_kernel,
        in_specs=[SMEM_SPEC] + [ANY_SPEC] * 3 + [vmem] * 8,
        out_specs=[ANY_SPEC] * 6,
        out_shape=[
            jax.ShapeDtypeStruct((8 * part, width), BF),
            jax.ShapeDtypeStruct((4 * part, width), BF),
            jax.ShapeDtypeStruct((8,) + ints.shape, jnp.int32),
            jax.ShapeDtypeStruct((4, 8 * rows, width), BF),
            jax.ShapeDtypeStruct((1, rows, width), BF),
            jax.ShapeDtypeStruct((2, rows, inner), BF),
        ],
        scratch_shapes=[
            pltpu.VMEM((16, part // 8, width), BF),
            pltpu.VMEM((16, part // 8, width), BF),
            pltpu.VMEM((5, 4, rows, width // 4), BF),
            pltpu.VMEM((5, rows, width), BF),
            dma(15),
            dma(6),
            dma(7),
            dma(7),
            dma(31),
            dma(6),
            dma(14),
            dma(14),
            dma(9),
        ],
        compiler_params=pltpu.CompilerParams(
            collective_id=1, has_side_effects=True, vmem_limit_bytes=LIMIT
        ),
        cost_estimate=pl.CostEstimate(flops=0, bytes_accessed=64 << 20, transcendentals=0),
        name="exchange",
    )(slot_of, content, query, memory, ints, *mats, upw, dnw)


def head_lanes(array, head):
    lane = lax.broadcasted_iota(jnp.int32, array.shape, 1)
    return jnp.where((lane >= DH) == (head == 1), array, jnp.zeros_like(array))


def attend_forward_step(
    block, qw_ref, qp_ref, k_ref, v_ref, rel_ref, thr_ref, kr_ref, vec_ref, prob_ref
):
    rows, klen = qw_ref.shape[0], k_ref.shape[0]
    width = klen + block
    keys, values = k_ref[...], v_ref[...]
    for part in range(rows // block):
        at = slice(part * block, (part + 1) * block)
        first = rows - (part + 1) * block
        qw, qp = qw_ref[at, :], qp_ref[at, :]
        rel = rel_ref[first : first + width, :]
        seen = kr_ref[...] < thr_ref[at, :]
        vecs = []
        for head in range(2):
            raw = nt(head_lanes(qp, head), rel)
            moved = pltpu.roll(raw, 0, 1, stride=1, stride_axis=0)[:, block:]
            score = nt(head_lanes(qw, head), keys) + moved
            score = jnp.where(seen, score, -1e30)
            expo = jnp.exp(score - jnp.max(score, axis=1, keepdims=True))
            prob = (expo * (1.0 / jnp.sum(expo, axis=1, keepdims=True))).astype(BF)
            prob_ref[head, at, :] = prob
            vecs.append(nn(prob, values))
        lane = lax.broadcasted_iota(jnp.int32, vecs[0].shape, 1)
        vec_ref[at, :] = jnp.where(lane < DH, vecs[0], vecs[1]).astype(BF)


def attend_forward_kernel(block, wired, *refs):
    if not wired:
        attend_forward_step(block, *refs)
        return
    ins, (out_slab, ud_slab, ctan, qtan) = refs[:7], refs[7:11]
    outs, (wo, ud, tangent) = refs[11:13], refs[13:16]
    out_send, out_recv, ud_send, ud_recv, tan_send, recv = refs[16:]
    step, steps = pl.program_id(0), pl.num_programs(0)
    place = Place()
    d, z, core = place.d, place.z, place.core
    gathers = (
        Gather(place, ud, ud_slab, ud_send, ud_recv),
        Gather(place, wo, out_slab, out_send, out_recv),
    )
    rows, part = out_slab.shape[1], ctan.shape[1]
    own_rows = pl.ds(pl.multiple_of(d * rows, 16), rows)

    def tan_copy(i, act):
        j, kind = i // 2, i % 2
        to, dp = 2 * core + j, d - core + kind
        src = (ctan, qtan)[kind].at[j]
        dst = tangent.at[pl.ds(pl.multiple_of(z * part, 16), part), :]
        here = jnp.logical_and(dp == d, to == z)
        local = pltpu.make_async_copy(src, dst, recv.at[0])
        remote = push(src, dst, tan_send.at[i], recv.at[0], dp, to)
        if act == "start":
            pl.when(here)(local.start)
            pl.when(jnp.logical_not(here))(remote.start)
        else:
            pl.when(jnp.logical_not(here))(remote.wait_send)

    @pl.when(step == 0)
    def _():
        partners = [(place.dp(r), z) for r in (CORE, XBIT, YBIT)]
        partners += [(place.dp(r), place.up(k)) for k in (1, 2, 3) for r in (0, CORE)]
        greet(partners)
        for gather in gathers:
            gather.begin()
        pltpu.make_async_copy(ud_slab, ud.at[:, own_rows, :], recv.at[1]).start()
        pltpu.make_async_copy(out_slab, wo.at[:, own_rows, :], recv.at[2]).start()
        for i in range(4):
            tan_copy(i, "start")

    @pl.when(step == 3)
    def _():
        for gather in gathers:
            gather.middle()

    attend_forward_step(block, *ins, *outs)

    @pl.when(step == steps - 1)
    def _():
        for gather in gathers:
            gather.late()
        for gather in gathers:
            gather.last()
        for gather in gathers:
            gather.end()
        settle(ud.at[:, own_rows, :], recv.at[1])
        settle(wo.at[:, own_rows, :], recv.at[2])
        settle(tangent, recv.at[0])
        for i in range(4):
            tan_copy(i, "wait")


def attend_forward(qw, qp, keys, values, rel, thr, key_rank, block, wires=()):
    rows, width = qw.shape
    klen, span = keys.shape[0], rel.shape[0]
    col = lambda count: pl.BlockSpec((count, PAIR), lambda p: (0, p))
    in_specs = [
        col(rows),
        col(rows),
        col(klen),
        col(klen),
        col(span),
        pl.BlockSpec((rows, 1), lambda p: (0, 0)),
        pl.BlockSpec((1, klen), lambda p: (0, 0)),
    ]
    out_specs = [col(rows), pl.BlockSpec((2, rows, klen), lambda p: (p, 0, 0))]
    out_shape = [
        jax.ShapeDtypeStruct((rows, width), BF),
        jax.ShapeDtypeStruct((width // DH, rows, klen), BF),
    ]
    params = dict(vmem_limit_bytes=LIMIT)
    scratch = []
    if wires:
        vmem = pl.BlockSpec(memory_space=pltpu.VMEM)
        in_specs += [vmem, vmem, ANY_SPEC, ANY_SPEC]
        out_specs += [ANY_SPEC] * 3
        inner = wires[1].shape[2]
        out_shape += [
            jax.ShapeDtypeStruct((1, width, width), BF),
            jax.ShapeDtypeStruct((2, width, inner), BF),
            jax.ShapeDtypeStruct((rows, width), BF),
        ]
        scratch = [pltpu.SemaphoreType.DMA((n,)) for n in (14, 14, 14, 14, 4, 3)]
        params.update(collective_id=2, has_side_effects=True)
    return pl.pallas_call(
        functools.partial(attend_forward_kernel, block, bool(wires)),
        grid=(width // PAIR,),
        in_specs=in_specs,
        out_specs=out_specs,
        out_shape=out_shape,
        scratch_shapes=scratch,
        compiler_params=pltpu.CompilerParams(**params),
        cost_estimate=pl.CostEstimate(
            flops=8 * rows * klen * width, bytes_accessed=16 << 20, transcendentals=12 * rows * klen
        ),
        name="attend_forward",
    )(qw, qp, keys, values, rel, thr, key_rank, *wires)


def attend_backward_kernel(block, wired, *refs):
    if not wired:
        attend_backward_step(block, *refs)
        return
    ins, (g_ud, src) = refs[:7], refs[7:9]
    outs, (grads_ref, home_ref) = refs[9:14], refs[14:16]
    rel_acc, home_send, home_recv = refs[16:19]
    step, steps = pl.program_id(0), pl.num_programs(0)
    place = Place()
    count = len(refs[19:]) // 2
    reduces = [
        Reduce(place, (g_ud.at[m : m + 1],), refs[19 + m * count : 19 + (m + 1) * count], grads_ref.at[m : m + 1])
        for m in range(2)
    ]
    home = Homeward(place, src, home_ref, home_send, home_recv.at[0])

    @pl.when(step == 0)
    def _():
        greet(near_partners(place))
        for reduce in reduces:
            reduce.begin()
        home.start()

    @pl.when(step == 2)
    def _():
        reduces[0].pairs()

    @pl.when(step == 3)
    def _():
        reduces[1].pairs()

    @pl.when(step == 5)
    def _():
        reduces[0].middle()

    attend_backward_step(block, *ins, *outs, rel_acc)

    @pl.when(step == steps - 1)
    def _():
        reduces[0].late()
        reduces[1].middle()
        reduces[1].late()
        reduces[0].end()
        reduces[1].end()
        home.end()


def attend_backward_step(
    block,
    prob_ref,
    gvec_ref,
    qw_ref,
    qp_ref,
    k_ref,
    v_ref,
    rel_ref,
    dproj_ref,
    dk_ref,
    dv_ref,
    drel_ref,
    bias_ref,
    rel_acc,
):
    rows, klen = qw_ref.shape[0], k_ref.shape[0]
    width = klen + block
    keys, values = k_ref[...], v_ref[...]
    row = lax.broadcasted_iota(jnp.int32, (block, block), 0)
    col = lax.broadcasted_iota(jnp.int32, (block, block), 1)
    mirror = (row + col == block - 1).astype(BF)
    rel_acc[...] = jnp.zeros_like(rel_acc)
    d_keys, d_values = [None, None], [None, None]
    word_sum = jnp.zeros((1, PAIR), F32)
    pos_sum = jnp.zeros((1, PAIR), F32)
    for part in range(rows // block):
        at = slice(part * block, (part + 1) * block)
        first = rows - (part + 1) * block
        gvec, qw = gvec_ref[at, :], qw_ref[at, :]
        gvec_t = jnp.transpose(gvec.astype(F32)).astype(BF)
        qw_t = jnp.transpose(qw.astype(F32)).astype(BF)
        qp_t = jnp.transpose(nn(mirror, qp_ref[at, :])).astype(BF)
        rel = rel_ref[first : first + width, :]
        word_parts, pos_parts = [], []
        for head in range(2):
            own = slice(head * DH, (head + 1) * DH)
            prob = prob_ref[head, at, :]
            d_prob = nt(head_lanes(gvec, head), values)
            weight = prob.astype(F32)
            inner = jnp.sum(weight * d_prob, axis=1, keepdims=True)
            g_sum = (weight * (d_prob - inner) * 0.125).astype(BF)
            dv = nn(gvec_t[own, :], prob)
            dk = nn(qw_t[own, :], g_sum)
            d_values[head] = dv if part == 0 else d_values[head] + dv
            d_keys[head] = dk if part == 0 else d_keys[head] + dk
            turned = nn(mirror, g_sum)
            padded = jnp.concatenate([jnp.zeros((block, block), F32), turned], axis=1)
            moved = pltpu.roll(padded, width - block + 1, 1, stride=1, stride_axis=0).astype(BF)
            word_parts.append(nn(turned.astype(BF), keys))
            pos_parts.append(nn(moved, rel))
            rel_acc[own, first : first + width] += nn(qp_t[own, :], moved)
        lane = lax.broadcasted_iota(jnp.int32, word_parts[0].shape, 1)
        word = jnp.where(lane < DH, word_parts[0], word_parts[1])
        pos = jnp.where(lane < DH, pos_parts[0], pos_parts[1])
        word_sum = word_sum + jnp.sum(word, axis=0, keepdims=True)
        pos_sum = pos_sum + jnp.sum(pos, axis=0, keepdims=True)
        dproj_ref[at, :] = nn(mirror, (word + pos).astype(BF)).astype(BF)
    for head in range(2):
        own = slice(head * DH, (head + 1) * DH)
        dv_ref[own, :] = d_values[head].astype(BF)
        dk_ref[own, :] = (8.0 * d_keys[head]).astype(BF)
    drel_ref[...] = (8.0 * rel_acc[...]).astype(BF)
    bias_ref[0:1, :] = word_sum
    bias_ref[1:2, :] = pos_sum


def attend_backward(prob, gvec, qw, qp, keys, values, rel, block, wires=()):
    rows, width = qw.shape
    klen, span = keys.shape[0], rel.shape[0]
    col = lambda count: pl.BlockSpec((count, PAIR), lambda p: (0, p))
    rowb = lambda count: pl.BlockSpec((PAIR, count), lambda p: (p, 0))
    in_specs = [
        pl.BlockSpec((2, rows, klen), lambda p: (p, 0, 0)),
        col(rows),
        col(rows),
        col(rows),
        col(klen),
        col(klen),
        col(span),
    ]
    out_specs = [col(rows), rowb(klen), rowb(klen), rowb(span), col(2)]
    out_shape = [
        jax.ShapeDtypeStruct((rows, width), BF),
        jax.ShapeDtypeStruct((width, klen), BF),
        jax.ShapeDtypeStruct((width, klen), BF),
        jax.ShapeDtypeStruct((width, span), BF),
        jax.ShapeDtypeStruct((2, width), F32),
    ]
    scratch = [pltpu.VMEM((PAIR, span), F32)]
    params = dict(vmem_limit_bytes=LIMIT)
    if wires:
        inner, mine = wires[0].shape[2], width // 8
        in_specs += [ANY_SPEC, ANY_SPEC]
        out_specs += [pl.BlockSpec(memory_space=pltpu.VMEM), ANY_SPEC]
        out_shape += [
            jax.ShapeDtypeStruct((2, mine, inner // 4), F32),
            jax.ShapeDtypeStruct((2, 2, rows // 4, width), BF),
        ]
        scratch += [pltpu.SemaphoreType.DMA((4,)), pltpu.SemaphoreType.DMA((1,))]
        scratch += 2 * Reduce.scratch(1, 1, mine, inner)
        params.update(collective_id=3, has_side_effects=True)
    return pl.pallas_call(
        functools.partial(attend_backward_kernel, block, bool(wires)),
        grid=(width // PAIR,),
        in_specs=in_specs,
        out_specs=out_specs,
        out_shape=out_shape,
        scratch_shapes=scratch,
        compiler_params=pltpu.CompilerParams(**params),
        cost_estimate=pl.CostEstimate(
            flops=16 * rows * klen * width, bytes_accessed=20 << 20, transcendentals=0
        ),
        name="attend_backward",
    )(prob, gvec, qw, qp, keys, values, rel, *wires)


def norm_parts(value):
    center = value - jnp.mean(value, axis=1, keepdims=True)
    scale = lax.rsqrt(jnp.mean(center * center, axis=1, keepdims=True) + EPS)
    return center * scale, scale


def norm_pull(normed, scale, err):
    inner = jnp.mean(err * normed, axis=1, keepdims=True)
    return (err - jnp.mean(err, axis=1, keepdims=True) - normed * inner) * scale


def sum_rows(value):
    return jnp.sum(value, axis=0, keepdims=True)


def feed_kernel(steps, *refs):
    (
        ud_hbm,
        wo_hbm,
        vec_ref,
        x_ref,
        tan_ref,
        upb_ref,
        dnb_ref,
        g1_ref,
        s1_ref,
        g2_ref,
        s2_ref,
        out_ref,
        dmix_ref,
        gvec_ref,
        go_ref,
        gud_ref,
        gupb_ref,
        small_ref,
        ud_ref,
        wo_ref,
        n1_ref,
        r1_ref,
        fb_ref,
        fbt_ref,
        acc_ref,
        act_ref,
        slope_ref,
        gd_ref,
        gdt_ref,
        sems,
    ) = refs
    step = pl.program_id(0)
    chunk = act_ref.shape[2]
    cols = pl.ds(pl.multiple_of(lax.rem(step, steps) * chunk, chunk), chunk)

    @pl.when(step == 0)
    def _():
        wo_copy = pltpu.make_async_copy(wo_hbm, wo_ref, sems.at[0])
        ud_copy = pltpu.make_async_copy(ud_hbm, ud_ref, sems.at[1])
        wo_copy.start()
        ud_copy.start()
        wo_copy.wait()
        normed, scale = norm_parts(nt(vec_ref[...], wo_ref[0]) + x_ref[...].astype(F32))
        n1_ref[...] = normed
        r1_ref[...] = scale
        first = normed * g1_ref[...] + s1_ref[...]
        fb_ref[...] = first.astype(BF)
        fbt_ref[...] = jnp.transpose(first).astype(BF)
        acc_ref[...] = first + dnb_ref[...]
        ud_copy.wait()

    @pl.when(step < steps)
    def _():
        upper = nn(fb_ref[...], ud_ref[0, :, cols]) + upb_ref[...]
        square = upper * upper
        root = 0.7978845608028654
        bend = jnp.tanh(root * (upper + 0.044715 * (square * upper)))
        half = 0.5 * (1.0 + bend)
        act = (upper * half).astype(BF)
        act_ref[step] = act
        slope_ref[step] = half + 0.5 * upper * (1.0 - bend * bend) * (
            root + (3 * 0.044715 * root) * square
        )
        acc_ref[...] += nt(act, ud_ref[1, :, cols])

    @pl.when(step == steps - 1)
    def _():
        normed, scale = norm_parts(acc_ref[...])
        out_ref[...] = (normed * g2_ref[...] + s2_ref[...]).astype(BF)
        tan = tan_ref[...].astype(F32)
        d_down = norm_pull(normed, scale, tan * g2_ref[...])
        small_ref[0:1, :] = sum_rows(d_down)
        small_ref[3:4, :] = sum_rows(tan * normed)
        small_ref[4:5, :] = sum_rows(tan)
        gd_ref[...] = d_down.astype(BF)
        gdt_ref[...] = jnp.transpose(d_down).astype(BF)
        acc_ref[...] = d_down

    @pl.when(step >= steps)
    def _():
        at = step - steps
        d_up = nn(gd_ref[...], ud_ref[1, :, cols]) * slope_ref[at]
        gupb_ref[...] = sum_rows(d_up)
        g_up = d_up.astype(BF)
        acc_ref[...] += nt(g_up, ud_ref[0, :, cols])
        gud_ref[0] = nn(fbt_ref[...], g_up).astype(BF)
        gud_ref[1] = nn(gdt_ref[...], act_ref[at]).astype(BF)

    @pl.when(step == 2 * steps - 1)
    def _():
        d_first, normed = acc_ref[...], n1_ref[...]
        small_ref[1:2, :] = sum_rows(d_first * normed)
        small_ref[2:3, :] = sum_rows(d_first)
        d_mixed = norm_pull(normed, r1_ref[...], d_first * g1_ref[...])
        dmix_ref[...] = d_mixed
        gvec_ref[...] = nn(d_mixed.astype(BF), wo_ref[0]).astype(BF)
        gdt_ref[...] = jnp.transpose(d_mixed).astype(BF)
        go_ref[...] = nn(gdt_ref[...], vec_ref[...]).astype(BF)


def feed(ud, wo, vec, x, tan, upb, dnb, g1, s1, g2, s2):
    rows, width = vec.shape
    inner = upb.shape[1]
    chunk = 512
    steps = inner // chunk
    whole = lambda a, b: pl.BlockSpec((a, b), lambda i: (0, 0))
    late = lambda i: jnp.maximum(i - steps, 0)
    grads = pl.BlockSpec((2, width, chunk), lambda i: (0, 0, late(i)))
    return pl.pallas_call(
        functools.partial(feed_kernel, steps),
        grid=(2 * steps,),
        in_specs=[ANY_SPEC] * 2
        + [whole(rows, width)] * 3
        + [pl.BlockSpec((1, chunk), lambda i: (0, lax.rem(i, steps)))]
        + [whole(1, width)] * 5,
        out_specs=[
            whole(rows, width),
            whole(rows, width),
            whole(rows, width),
            whole(width, width),
            grads,
            pl.BlockSpec((1, chunk), lambda i: (0, late(i))),
            whole(8, width),
        ],
        out_shape=[
            jax.ShapeDtypeStruct((rows, width), BF),
            jax.ShapeDtypeStruct((rows, width), F32),
            jax.ShapeDtypeStruct((rows, width), BF),
            jax.ShapeDtypeStruct((width, width), BF),
            jax.ShapeDtypeStruct((2, width, inner), BF),
            jax.ShapeDtypeStruct((1, inner), F32),
            jax.ShapeDtypeStruct((8, width), F32),
        ],
        scratch_shapes=[
            pltpu.VMEM((2, width, inner), BF),
            pltpu.VMEM((1, width, width), BF),
            pltpu.VMEM((rows, width), F32),
            pltpu.VMEM((rows, 1), F32),
            pltpu.VMEM((rows, width), BF),
            pltpu.VMEM((width, rows), BF),
            pltpu.VMEM((rows, width), F32),
            pltpu.VMEM((steps, rows, chunk), BF),
            pltpu.VMEM((steps, rows, chunk), F32),
            pltpu.VMEM((rows, width), BF),
            pltpu.VMEM((width, rows), BF),
            pltpu.SemaphoreType.DMA((2,)),
        ],
        compiler_params=pltpu.CompilerParams(vmem_limit_bytes=LIMIT),
        cost_estimate=pl.CostEstimate(
            flops=12 * rows * width * inner, bytes_accessed=36 << 20, transcendentals=rows * inner
        ),
        name="feed",
    )(ud, wo, vec, x, tan, upb, dnb, g1, s1, g2, s2)


def project_kernel(
    w_ref, ctx_ref, q_ref, table_ref, wb_ref, pb_ref, k_ref, v_ref, rel_ref, qw_ref, qp_ref, x_ref
):
    lead = lax.rem(lax.axis_index("dp"), 2) == 0
    back = ctx_ref.shape[0] - q_ref.shape[0]
    block = 256

    def loop(count, step):
        def run(i, carry):
            step(pl.ds(pl.multiple_of(i * block, block), block))
            return carry

        lax.fori_loop(0, count // block, run, 0)

    def context_step(at):
        k_ref[at, :] = nn(ctx_ref[at, :], w_ref[0]).astype(BF)
        v_ref[at, :] = nn(ctx_ref[at, :], w_ref[1]).astype(BF)

    def stream_step(at):
        own = ctx_ref[pl.ds(pl.multiple_of(at.start + back, block), block), :]
        x_ref[at, :] = jnp.where(lead, own, q_ref[at, :])
        proj = nn(x_ref[at, :], w_ref[2])
        qw_ref[at, :] = (0.125 * (proj + wb_ref[...]).astype(BF).astype(F32)).astype(BF)
        qp_ref[at, :] = (0.125 * (proj + pb_ref[...]).astype(BF).astype(F32)).astype(BF)

    def table_step(at):
        rel_ref[at, :] = nn(table_ref[at, :], w_ref[3]).astype(BF)

    loop(table_ref.shape[0], table_step)
    loop(q_ref.shape[0], stream_step)
    loop(ctx_ref.shape[0], context_step)


def project(mats, context, query, table, wb, pb):
    rows, width = query.shape
    klen, span = context.shape[0], table.shape[0]
    vmem = pl.BlockSpec(memory_space=pltpu.VMEM)
    return pl.pallas_call(
        project_kernel,
        in_specs=[vmem] * 6,
        out_specs=[vmem] * 6,
        out_shape=[
            jax.ShapeDtypeStruct((klen, width), BF),
            jax.ShapeDtypeStruct((klen, width), BF),
            jax.ShapeDtypeStruct((span, width), BF),
            jax.ShapeDtypeStruct((rows, width), BF),
            jax.ShapeDtypeStruct((rows, width), BF),
            jax.ShapeDtypeStruct((rows, width), BF),
        ],
        compiler_params=pltpu.CompilerParams(vmem_limit_bytes=LIMIT),
        cost_estimate=pl.CostEstimate(
            flops=2 * (2 * klen + rows + span) * width * width,
            bytes_accessed=20 << 20,
            transcendentals=0,
        ),
        name="project",
    )(mats, context, query, table, wb, pb)


def weight_grads_kernel(xt_ref, ct_ref, tt_ref, dp_ref, dk_ref, dv_ref, dr_ref, g_ref):
    g_ref[0] = nt(ct_ref[...], dk_ref[...]).astype(BF)
    g_ref[1] = nt(ct_ref[...], dv_ref[...]).astype(BF)
    g_ref[2] = nn(xt_ref[...], dp_ref[...]).astype(BF)
    g_ref[3] = nt(tt_ref[...], dr_ref[...]).astype(BF)


def weight_grads(x_t, ctx_t, table_t, d_proj, dk_t, dv_t, drel_t):
    width, rows = x_t.shape
    klen, span = ctx_t.shape[1], table_t.shape[1]
    chunk = 256
    whole = lambda a, b: pl.BlockSpec((a, b), lambda i: (0, 0))
    rowb = lambda b: pl.BlockSpec((chunk, b), lambda i: (i, 0))
    return pl.pallas_call(
        weight_grads_kernel,
        grid=(width // chunk,),
        in_specs=[
            whole(width, rows),
            whole(width, klen),
            whole(width, span),
            pl.BlockSpec((rows, chunk), lambda i: (0, i)),
            rowb(klen),
            rowb(klen),
            rowb(span),
        ],
        out_specs=pl.BlockSpec((4, width, chunk), lambda i: (0, 0, i)),
        out_shape=jax.ShapeDtypeStruct((4, width, width), BF),
        compiler_params=pltpu.CompilerParams(vmem_limit_bytes=LIMIT),
        cost_estimate=pl.CostEstimate(
            flops=2 * (rows + 2 * klen + span) * width * width,
            bytes_accessed=20 << 20,
            transcendentals=0,
        ),
        name="weight_grads",
    )(x_t, ctx_t, table_t, d_proj, dk_t, dv_t, drel_t)


def flip(arr, bit):
    return lax.ppermute(arr, "dp", [(i, i ^ bit) for i in range(lax.axis_size("dp"))])


def scatter_sum(grads):
    mine = lax.psum_scatter(grads, "dp", scatter_dimension=1, tiled=True)
    return lax.psum_scatter(mine, "tensor", scatter_dimension=2, tiled=True).astype(F32)


def body(
    content_stream,
    query_stream,
    memory,
    content_tangent,
    query_tangent,
    seq_lengths,
    factor_order,
    memory_lengths,
    slot_sequence,
    query_weight,
    key_weight,
    value_weight,
    pos_weight,
    out_weight,
    up_weight,
    up_bias,
    down_weight,
    down_bias,
    word_bias,
    pos_bias,
    first_gain,
    first_shift,
    second_gain,
    second_shift,
):
    groups, tensors = lax.axis_size("dp"), lax.axis_size("tensor")
    micro, part_len, width = content_stream.shape
    mem_part = memory.shape[1]
    seq_len, mem_total = part_len * tensors, mem_part * tensors
    klen, span = mem_total + seq_len, mem_total + 2 * seq_len
    count = micro * groups
    here, lane = lax.axis_index("dp"), lax.axis_index("tensor")
    core = here % 2
    lead = core == 0
    block = 256
    assert 2 * micro == tensors

    def swap(arr):
        return flip(arr, CORE)

    def to_unit(first, second):
        got = swap(jnp.where(lead, second, first))
        low = jnp.where(lead, first, got)
        high = jnp.where(lead, got, second)
        both = jnp.concatenate([low, high], 0)
        both = lax.all_to_all(both, "tensor", split_axis=0, concat_axis=0, tiled=True)
        return both.reshape(seq_len, width)

    def from_unit(arr):
        both = arr.reshape(tensors, part_len, width)
        both = lax.all_to_all(both, "tensor", split_axis=0, concat_axis=0, tiled=True)
        low, high = both[:micro], both[micro:]
        got = swap(jnp.where(lead, high, low))
        return jnp.where(lead, low, got), jnp.where(lead, got, high)

    seq_id = (here // 2) * tensors + lane
    ids = jnp.arange(count, dtype=jnp.int32)
    slot_of = jnp.sum(jnp.where(slot_sequence[None, :] == ids[:, None], ids[None, :], 0), axis=1)
    counts = jnp.concatenate([seq_lengths, memory_lengths])
    slot = slot_of[seq_id]
    mats = [key_weight, value_weight, query_weight, pos_weight, out_weight]
    table = jnp.asarray(reversed_table(span, klen, width))
    wires = ()
    if groups == 8:
        ints = jnp.pad(factor_order, ((0, 6), (0, 0)))
        ints = lax.dynamic_update_slice(ints, counts[None, :], (micro, 0))
        context, query, all_ints, weights, out_slab, ud_slab = exchange(
            slot_of, content_stream, query_stream, memory, ints, mats, up_weight, down_weight
        )
        wires = (out_slab, ud_slab, content_tangent, query_tangent)
        lengths = all_ints[:, micro, : 2 * micro]
        orders = all_ints[seq_id // micro, :micro]
    else:
        lengths = lax.all_gather(counts, "dp", axis=0, tiled=False)
        orders = lax.all_gather(factor_order, "dp", axis=0, tiled=False)[seq_id // micro]
        stream = to_unit(content_stream, query_stream)
        content, query = jnp.where(lead, stream, swap(stream)), stream
        tangent = to_unit(content_tangent, query_tangent)
        piece = mem_part // groups
        spread = lax.all_to_all(
            memory.reshape(micro, groups, piece, width), "dp", split_axis=1, concat_axis=1, tiled=True
        )
        spread = spread.transpose(1, 0, 2, 3).reshape(count, piece, width)
        spread = jnp.take(spread, slot_of, axis=0)
        spread = spread.reshape(groups // 2, tensors, 2, piece // 2, width).transpose(0, 2, 1, 3, 4)
        spread = lax.all_to_all(
            spread.reshape(groups, tensors, piece // 2, width),
            "dp",
            split_axis=0,
            concat_axis=0,
            tiled=True,
        )
        spread = lax.all_to_all(spread, "tensor", split_axis=1, concat_axis=1, tiled=True)
        got = swap(spread)
        mem_rows = jnp.stack([jnp.where(lead, spread, got), jnp.where(lead, got, spread)])
        mem_rows = mem_rows.transpose(2, 1, 0, 3, 4).reshape(mem_total, width)
        context = jnp.concatenate([mem_rows, content], 0)

        def whole(mat):
            mat = lax.all_gather(mat, "tensor", axis=1, tiled=True)
            return lax.all_gather(mat, "dp", axis=0, tiled=True)

        weights = jnp.stack([whole(mat) for mat in mats[:4]])
        wo = whole(out_weight)[None]
        ud = jnp.stack([whole(up_weight), whole(down_weight)])

    length = lengths[seq_id // micro, seq_id % micro]
    mem_valid = lengths[slot // micro, micro + slot % micro]
    rank = orders[seq_id % micro]
    key_pos = jnp.arange(klen, dtype=jnp.int32)
    hidden = jnp.int32(1 << 20)
    mem_rank = jnp.where(key_pos[:mem_total] >= mem_total - mem_valid, -1, hidden)
    own_rank = jnp.where(key_pos[:seq_len] < length, rank, hidden)
    key_rank = jnp.concatenate([mem_rank, own_rank])[None, :]
    thr = (rank + jnp.where(lead, 1, 0))[:, None]

    row = lambda v: v.reshape(1, -1)
    keys, values, rel, q_word, q_pos, stream = project(
        weights, context, query, table, row(word_bias), row(pos_bias)
    )
    vec, prob, *arrived = attend_forward(
        q_word, q_pos, keys, values, rel, thr, key_rank, block, wires
    )
    if wires:
        wo, ud, tangent = arrived
    out, d_mixed, g_vec, g_out, g_ud, g_upb, small = feed(
        ud,
        wo,
        vec,
        stream,
        tangent,
        row(up_bias),
        row(down_bias),
        row(first_gain),
        row(first_shift),
        row(second_gain),
        row(second_shift),
    )
    backward = (prob, g_vec, q_word, q_pos, keys, values, rel, block)
    if groups == 8:
        d_proj, dk_t, dv_t, drel_t, biases, (grad_up, grad_down), outs = attend_backward(
            *backward, (g_ud, out)
        )
        content_out, query_out = outs[0], outs[1]
    else:
        d_proj, dk_t, dv_t, drel_t, biases = attend_backward(*backward)
        content_out, query_out = from_unit(out)
        grad_up, grad_down = scatter_sum(g_ud)
    small = jnp.concatenate([g_upb.reshape(-1), small[:5].reshape(-1), biases.reshape(-1)])
    d_context = tt(dk_t[:, mem_total:], weights[0]) + tt(dv_t[:, mem_total:], weights[1])
    d_stream = d_mixed + nt(d_proj, weights[2])
    d_stream = d_stream + jnp.where(lead, d_context, 0.0)
    grads = weight_grads(
        jnp.transpose(stream),
        jnp.transpose(context),
        jnp.transpose(table),
        d_proj,
        dk_t,
        dv_t,
        drel_t,
    )
    inner = up_bias.shape[0]
    if groups == 8:
        size = small.shape[0]
        small = jnp.pad(small, (0, -size % 1024)).reshape(-1, 128)
        grads, homes, small = finish(grads, g_out[None], d_stream, d_context.astype(BF), small)
        grad_key, grad_value, grad_query, grad_pos, grad_out = grads
        content_grad, query_grad = homes[0], homes[1]
        small = small.reshape(-1)[:size]
    else:
        partner = swap(d_context.astype(BF)).astype(F32)
        d_stream = d_stream + jnp.where(lead, partner, 0.0)
        content_grad, query_grad = from_unit(d_stream.astype(BF))
        grad_key, grad_value, grad_query, grad_pos = scatter_sum(grads)
        (grad_out,) = scatter_sum(g_out[None])
        small = lax.psum(small, ("dp", "tensor"))
    rest = small[inner:].reshape(7, width)
    return (
        content_out,
        query_out,
        content_grad,
        query_grad,
        grad_query,
        grad_key,
        grad_value,
        grad_pos,
        grad_out,
        grad_up,
        small[:inner],
        grad_down,
        rest[0],
        rest[5].reshape(HEADS, DH),
        rest[6].reshape(HEADS, DH),
        rest[1],
        rest[2],
        rest[3],
        rest[4],
    )


def solution(mesh):
    rows = P("dp", "tensor", None)
    mat = P("dp", "tensor")
    return jax.shard_map(
        body,
        mesh=mesh,
        in_specs=(rows,) * 5
        + (P("dp"), P("dp", None), P("dp"), P())
        + (mat,) * 6
        + (P(), mat)
        + (P(),) * 7,
        out_specs=(rows,) * 4 + (mat,) * 6 + (P(), mat) + (P(),) * 7,
        check_vma=False,
    )
```

```python
import functools

import jax
import jax.numpy as jnp
import numpy as np
from jax import lax
from jax.experimental import pallas as pl
from jax.experimental.pallas import tpu as pltpu
from jax.sharding import PartitionSpec as P

HEADS = 12
DH = 64
PAIR = 2 * DH
EPS = 1e-06
BF = jnp.bfloat16
F32 = jnp.float32
LIMIT = 60 * 1024 * 1024
SMEM_SPEC = pl.BlockSpec(memory_space=pltpu.SMEM)
ANY_SPEC = pl.BlockSpec(memory_space=pl.ANY)


def nn(left, right):
    return jnp.dot(left, right, preferred_element_type=F32)


def nt(left, right):
    return lax.dot_general(left, right, (((1,), (1,)), ((), ())), preferred_element_type=F32)


def tn(left, right):
    return lax.dot_general(left, right, (((0,), (0,)), ((), ())), preferred_element_type=F32)


def tt(left, right):
    return lax.dot_general(left, right, (((0,), (1,)), ((), ())), preferred_element_type=F32)


def reversed_table(count, first, width):
    dist = (first - np.arange(count)).astype(np.float32)
    half = width // 2
    power = np.arange(half).astype(np.float32) * np.float32(2.0 / width)
    freq = np.float32(1.0) / np.float32(10000.0) ** power
    angle = (dist[:, None] * freq[None, :]).astype(np.float64)
    return np.concatenate([np.sin(angle), np.cos(angle)], axis=1).astype(np.float32).astype(BF)


MESH = pl.DeviceIdType.MESH
CORE, XBIT, YBIT = 1, 2, 4


class Place:
    def __init__(self):
        self.d, self.z = lax.axis_index("dp"), lax.axis_index("tensor")
        self.core = lax.rem(self.d, 2)
        self.x = lax.rem(lax.div(self.d, 2), 2)
        self.y = lax.div(self.d, 4)

    def dp(self, bits):
        at = self.d
        if bits & CORE:
            at = at + (1 - 2 * self.core)
        if bits & XBIT:
            at = at + (2 - 4 * self.x)
        if bits & YBIT:
            at = at + (4 - 8 * self.y)
        return at

    def up(self, step):
        return lax.rem(self.z + step, 4) if step else self.z


def push(src, dst, send, recv, dp, z):
    return pltpu.make_async_remote_copy(
        src_ref=src,
        dst_ref=dst,
        send_sem=send,
        recv_sem=recv,
        device_id=(dp, z),
        device_id_type=MESH,
    )


def settle(ref, sem):
    pltpu.make_async_copy(ref, ref, sem).wait()


def greet(partners):
    barrier = pltpu.get_barrier_semaphore()
    for partner in partners:
        pl.semaphore_signal(barrier, inc=1, device_id=partner, device_id_type=MESH)
    pl.semaphore_wait(barrier, len(partners))


GATHER = (
    (0, 0, XBIT),
    (0, 1, YBIT),
    (0, 0, YBIT),
    (0, 1, XBIT),
    (XBIT, 0, YBIT),
    (YBIT, 1, XBIT),
    (0, 0, CORE),
    (0, 1, CORE),
    (XBIT, 0, CORE),
    (YBIT, 1, CORE),
    (YBIT, 0, CORE),
    (XBIT, 1, CORE),
    (XBIT | YBIT, 0, CORE),
    (XBIT | YBIT, 1, CORE),
)


class Gather:
    def __init__(self, place, dst, own, send, recv):
        self.place, self.dst, self.own = place, dst, own
        self.send, self.recv = send, recv
        self.half = dst.shape[1] // 16

    def region(self, owner, half):
        at = self.place.dp(owner) * (2 * self.half) + half * self.half
        return self.dst.at[:, pl.ds(pl.multiple_of(at, 16), self.half), :]

    def copy(self, i):
        owner, half, to = GATHER[i]
        src = self.region(owner, half)
        if owner == 0 and self.own is not None:
            src = self.own.at[:, half * self.half : (half + 1) * self.half, :]
        place = self.place
        return push(
            src, self.region(owner, half), self.send.at[i], self.recv.at[i], place.dp(to), place.z
        )

    def start(self, *which):
        for i in which:
            self.copy(i).start()

    def wait(self, received, sent):
        for i in received:
            self.copy(i).wait_recv()
        for i in sent:
            self.copy(i).wait_send()

    def after(self, arrived, started):
        for i, more in zip(arrived, started):
            self.copy(i).wait_recv()
            for j in more:
                self.copy(j).start()

    def middle(self):
        self.after((0, 1), ((4, 8), (5, 9)))

    def last(self):
        self.after((2, 3, 4, 5), ((10,), (11,), (12,), (13,)))


def chip_bits(j):
    return (XBIT if j & 1 else 0) | (YBIT if j & 2 else 0)


def add_into(dst, src):
    def run(i, carry):
        at = pl.ds(pl.multiple_of(i * 16, 16), 16)
        dst[:, at, :] = (dst[:, at, :].astype(F32) + src[:, at, :].astype(F32)).astype(BF)
        return carry

    lax.fori_loop(0, dst.shape[1] // 16, run, 0)


class Reduce:
    def __init__(self, place, sources, scratch, out):
        self.place, self.sources, self.out = place, sources, out
        self.total, self.pair, self.near, self.far, self.quarter, self.stage = scratch[:6]
        self.pair_send, self.pair_recv, self.load, self.send, self.recv, self.z_send, self.z_recv = scratch[6:]
        self.rows = self.total.shape[2]

    @staticmethod
    def scratch(count, n, rows, cols):
        part = cols // 4
        dma = lambda k: pltpu.SemaphoreType.DMA((k,))
        return [
            pltpu.VMEM((n, 4, rows, cols), BF),
            pltpu.VMEM((n, 4, rows, cols), BF),
            pltpu.VMEM((n, 2, 2, rows // 2, cols), BF),
            pltpu.VMEM((n, 2, rows // 2, cols), BF),
            pltpu.VMEM((4, n, rows, part), BF),
            pltpu.VMEM((4, n, rows, part) if part % 128 else (8, 128), BF),
            dma(4 * count),
            dma(4 * count),
            dma(4 * count),
            dma(6),
            dma(6),
            dma(3),
            dma(1),
        ]

    def pair_copies(self, j):
        place, rows = self.place, self.rows
        copies, at = [], 0
        for i, src in enumerate(self.sources):
            slot, n = len(self.sources) * j + i, src.shape[0]
            block = lambda bits: src.at[:, pl.ds(pl.multiple_of(place.dp(bits) * rows, 16), rows), :]
            remote = push(
                block(chip_bits(j) | CORE),
                self.pair.at[at : at + n, j],
                self.pair_send.at[slot],
                self.pair_recv.at[slot],
                place.dp(CORE),
                place.z,
            )
            local = pltpu.make_async_copy(
                block(chip_bits(j)), self.total.at[at : at + n, j], self.load.at[slot]
            )
            copies.append((remote, local))
            at += n
        return copies

    def half(self, j, h):
        size = self.rows // 2
        return self.total.at[:, j, h * size : (h + 1) * size, :]

    MOVES = ((3, 0, XBIT, 1), (3, 1, YBIT, 1), (1, 0, XBIT, 0), (2, 1, YBIT, 0), (2, 0, YBIT, 0), (1, 1, XBIT, 1))

    def move(self, i):
        j, h, to, where = self.MOVES[i]
        dst = self.near.at[:, h, where] if i < 4 else self.far.at[:, where]
        place = self.place
        return push(self.half(j, h), dst, self.send.at[i], self.recv.at[i], place.dp(to), place.z)

    def z_copy(self, k):
        place, part = self.place, self.quarter.shape[3]
        to = place.up(k)
        if part % 128:
            src = self.stage.at[to]
        else:
            src = self.total.at[:, 0, :, pl.ds(pl.multiple_of(to * part, 128), part)]
        dst = self.quarter.at[place.z]
        if k == 0:
            return pltpu.make_async_copy(src, dst, self.z_recv.at[0])
        return push(src, dst, self.z_send.at[k - 1], self.z_recv.at[0], place.d, to)

    def begin(self):
        for j in (3, 1, 2, 0):
            for remote, local in self.pair_copies(j):
                remote.start()
                local.start()

    def pairs(self):
        for j, moves in ((3, (0, 1)), (1, (2,)), (2, (3,)), (0, ())):
            for remote, local in self.pair_copies(j):
                local.wait()
                remote.wait_recv()
            add_into(self.total.at[:, j], self.pair.at[:, j])
            for i in moves:
                self.move(i).start()

    def middle(self):
        for i, j, h, where, more in ((0, 2, 0, 1, 4), (1, 1, 1, 1, 5), (2, 0, 0, 0, None), (3, 0, 1, 0, None)):
            self.move(i).wait_recv()
            add_into(self.half(j, h), self.near.at[:, h, where])
            if more is not None:
                self.move(more).start()

    def late(self):
        for i, h in ((4, 0), (5, 1)):
            self.move(i).wait_recv()
            add_into(self.half(0, h), self.far.at[:, h])
        part = self.quarter.shape[3]
        if part % 128:
            for k in range(4):
                for m in range(self.total.shape[0]):
                    self.stage[k, m] = self.total[m, 0, :, k * part : (k + 1) * part]
        for k in (2, 1, 3, 0):
            self.z_copy(k).start()

    def end(self):
        settle(self.quarter, self.z_recv.at[0])
        parts = [self.quarter[k].astype(F32) for k in range(4)]
        self.out[...] = (parts[0] + parts[1]) + (parts[2] + parts[3])
        for j in range(4):
            for remote, _ in self.pair_copies(j):
                remote.wait_send()
        for i in range(6):
            self.move(i).wait_send()
        for k in range(1, 4):
            self.z_copy(k).wait_send()


class Homeward:
    def __init__(self, place, src, home, send, recv):
        self.place, self.src, self.home, self.send, self.recv = place, src, home, send, recv
        self.part = home.shape[2]

    def act(self, what):
        place, part = self.place, self.part
        for k in (2, 1, 3, 0):
            to, dp = place.up(k), place.d - place.core + lax.div(place.z, 2)
            src = self.src.at[pl.ds(pl.multiple_of(to * part, 16), part), :]
            dst = self.home.at[place.core, lax.rem(place.z, 2)]
            here = jnp.logical_and(dp == place.d, to == place.z)
            remote = push(src, dst, self.send.at[k], self.recv, dp, to)
            if what == "start":
                pl.when(here)(pltpu.make_async_copy(src, dst, self.recv).start)
                pl.when(jnp.logical_not(here))(remote.start)
            else:
                pl.when(jnp.logical_not(here))(remote.wait_send)

    def start(self):
        self.act("start")

    def end(self):
        settle(self.home, self.recv)
        self.act("wait")


def pair_and_z(place):
    return [(place.dp(r), place.up(k)) for k in range(4) for r in (0, CORE) if r or k]


def near_partners(place):
    return pair_and_z(place) + [(place.dp(r), place.z) for r in (XBIT, YBIT)]


def finish_kernel(g_ref, go_ref, base_ref, ctx_ref, small_ref, *refs):
    grads_ref, home_ref, sums_ref = refs[:3]
    stream, partner, slots, part_sum, chips = refs[3:8]
    home_send, slot_send, chip_send, one_send, recv = refs[8:13]
    place = Place()
    d, z, core = place.d, place.z, place.core
    greet(near_partners(place) + [(place.dp(XBIT | YBIT), z)])
    reduce = Reduce(place, (g_ref, go_ref), refs[13:], grads_ref)
    swap = push(ctx_ref, partner, one_send.at[0], recv.at[0], place.dp(CORE), z)
    swap.start()
    reduce.begin()
    slot_copies = []
    others = [(r, k) for k in range(4) for r in (0, CORE) if r or k]
    for i, (r, k) in enumerate(others):
        copy = push(small_ref, slots.at[4 * core + z], slot_send.at[i], recv.at[1], place.dp(r), place.up(k))
        copy.start()
        slot_copies.append(copy)
    pltpu.make_async_copy(small_ref, slots.at[4 * core + z], recv.at[1]).start()

    home = Homeward(place, stream, home_ref, home_send, recv.at[2])
    swap.wait()
    block = 64

    def add_partner(i, carry):
        at = pl.ds(pl.multiple_of(i * block, block), block)
        more = jnp.where(core == 0, partner[at, :].astype(F32), 0.0)
        stream[at, :] = (base_ref[at, :] + more).astype(BF)
        return carry

    lax.fori_loop(0, stream.shape[0] // block, add_partner, 0)
    home.start()
    reduce.pairs()

    settle(slots, recv.at[1])
    total = slots[0]
    for i in range(1, 8):
        total = total + slots[i]
    part_sum[...] = total
    chip = lax.div(d, 2)
    chip_copies = []
    for i, r in enumerate((XBIT, YBIT, XBIT | YBIT)):
        copy = push(part_sum, chips.at[chip], chip_send.at[i], recv.at[3], place.dp(r), z)
        copy.start()
        chip_copies.append(copy)
    pltpu.make_async_copy(part_sum, chips.at[chip], recv.at[3]).start()

    reduce.middle()
    settle(chips, recv.at[3])
    sums_ref[...] = (chips[0] + chips[1]) + (chips[2] + chips[3])
    reduce.late()
    reduce.end()
    home.end()
    for copy in slot_copies + chip_copies:
        copy.wait_send()


def finish(grads, g_out, base, ctx, small):
    n, width, cols = grads.shape
    rows, total = width // 8, base.shape[0]
    vmem = pl.BlockSpec(memory_space=pltpu.VMEM)
    dma = lambda k: pltpu.SemaphoreType.DMA((k,))
    return pl.pallas_call(
        finish_kernel,
        in_specs=[ANY_SPEC] * 2 + [vmem] * 3,
        out_specs=[vmem, ANY_SPEC, vmem],
        out_shape=[
            jax.ShapeDtypeStruct((n + 1, rows, cols // 4), F32),
            jax.ShapeDtypeStruct((2, 2, total // 4, width), BF),
            jax.ShapeDtypeStruct(small.shape, F32),
        ],
        scratch_shapes=[
            pltpu.VMEM((total, width), BF),
            pltpu.VMEM((total, width), BF),
            pltpu.VMEM((8,) + small.shape, F32),
            pltpu.VMEM(small.shape, F32),
            pltpu.VMEM((4,) + small.shape, F32),
            dma(4),
            dma(7),
            dma(3),
            dma(1),
            dma(4),
        ]
        + Reduce.scratch(2, n + 1, rows, cols),
        compiler_params=pltpu.CompilerParams(
            collective_id=4, has_side_effects=True, vmem_limit_bytes=LIMIT
        ),
        cost_estimate=pl.CostEstimate(flops=0, bytes_accessed=64 << 20, transcendentals=0),
        name="finish",
    )(grads, g_out, base, ctx, small)


def pack(mat):
    half = mat.shape[0] // 2
    return jnp.concatenate([mat[:, :128], jnp.concatenate([mat[:half, 128:], mat[half:, 128:]], axis=1)], axis=0)


def unpack(packed):
    rows = packed.shape[0] * 2 // 3
    rest = packed[rows:, :]
    return jnp.concatenate([packed[:rows, :], jnp.concatenate([rest[:, :64], rest[:, 64:]], axis=0)], axis=1)


def exchange_kernel(slot_ref, content, query, memory, ints, *refs):
    mats, (upw, dnw) = refs[:5], refs[5:7]
    context, stream, all_ints, whole, out_slab, ud_slab = refs[7:13]
    (
        spread,
        picked,
        shards,
        slab,
        mat_send,
        mat_recv,
        ud_send,
        ud_recv,
        int_send,
        spread_send,
        pick_send,
        stream_send,
        pair_send,
        gather_send,
        gather_recv,
        recv,
    ) = refs[13:]
    place = Place()
    d, z, core = place.d, place.z, place.core
    up, down, far = place.up(1), place.up(3), place.up(2)
    part = query.shape[1]
    piece = spread.shape[1]
    blocks = part // piece // 2
    first = 4 * blocks
    greet([(place.dp(r), place.up(k)) for r in range(8) for k in range(4) if r or k])

    spread_copies = []
    for r in range(8):
        to = place.dp(r)
        src = memory.at[:, pl.ds(pl.multiple_of(to * piece, 16), piece), :]
        dst = spread.at[pl.ds(2 * d, 2)]
        if r == 0:
            pltpu.make_async_copy(src, dst, recv.at[0]).start()
        else:
            spread_copies.append(push(src, dst, spread_send.at[r - 1], recv.at[0], to, z))
            spread_copies[-1].start()

    for m, mat in enumerate(mats):
        shards[z, m] = pack(mat[...])
    cutoff = shards.shape[2] * 5 // 9

    def mat_copy(i):
        own = shards.at[z]
        low, high = shards.at[down, :, :cutoff], shards.at[up, :, cutoff:]
        src = (own, own, low, high)[i]
        return push(src, src, mat_send.at[i], mat_recv.at[i], d, (up, down, up, down)[i])

    mat_copy(0).start()
    mat_copy(1).start()
    int_copies = []
    for r in range(8):
        if r == 0:
            pltpu.make_async_copy(ints, all_ints.at[d], recv.at[2]).start()
        else:
            copy = push(ints, all_ints.at[d], int_send.at[r - 1], recv.at[2], place.dp(r), z)
            int_copies.append(copy)
            copy.start()

    def stream_copy(i, act):
        j, kind = i // 2, i % 2
        to, dp = 2 * core + j, d - core + kind
        if kind == 0:
            src, sem = content.at[j], recv.at[3]
            dst = context.at[pl.ds(first + blocks * z, blocks)]
        else:
            src, sem = query.at[j], recv.at[4]
            dst = stream.at[pl.ds(pl.multiple_of(z * part, 16), part), :]
        here = jnp.logical_and(dp == d, to == z)
        remote = push(src, dst, stream_send.at[i], sem, dp, to)
        if act == "start":
            pl.when(here)(pltpu.make_async_copy(src, dst, sem).start)
            pl.when(jnp.logical_not(here))(remote.start)
        else:
            pl.when(jnp.logical_not(here))(remote.wait_send)

    mat_copy(0).wait_recv()
    mat_copy(2).start()
    mat_copy(1).wait_recv()
    mat_copy(3).start()
    for i in range(4):
        stream_copy(i, "start")

    settle(spread, recv.at[0])
    for q in range(16):
        picked[q] = spread[slot_ref[q]]
    pick_copies = []
    for r in (YBIT | XBIT, XBIT, YBIT, 0):
        for k in range(4):
            to, lane = place.dp(r), place.up(k)
            src = picked.at[4 * lax.div(to, 2) + lane]
            dst = context.at[blocks * z + lax.div(d, 2), core]
            if r or k:
                copy = push(src, dst, pick_send.at[2 * r + k - 1], recv.at[5], to, lane)
                pick_copies.append(copy)
            else:
                copy = pltpu.make_async_copy(src, dst, recv.at[5])
            copy.start()

    mat_copy(2).wait_recv()
    mat_copy(3).wait_recv()
    for m in range(5):
        slab[m] = jnp.concatenate([unpack(shards[k, m]) for k in range(4)], axis=1)
    rows = slab.shape[1]
    own_rows = pl.ds(pl.multiple_of(d * rows, 16), rows)
    gather = Gather(place, whole, slab.at[0:4], gather_send, gather_recv)
    gather.start(0, 1, 2, 3, 6, 7)
    pltpu.make_async_copy(slab.at[0:4], whole.at[:, own_rows, :], recv.at[6]).start()
    pltpu.make_async_copy(slab.at[4:5], out_slab, recv.at[7]).start()

    width = upw.shape[1]

    def columns(at, rows=slice(None)):
        return ud_slab.at[:, rows, pl.ds(pl.multiple_of(at * width, 128), width)]

    def ud_copy(i):
        if i < 4:
            src, dst = (upw, dnw)[i % 2], columns(z).at[i % 2]
            return push(src, dst, ud_send.at[i], ud_recv.at[i // 2], d, (up, down)[i // 2])
        half = rows // 2
        src = columns(down, slice(0, half)) if i == 4 else columns(up, slice(half, rows))
        return push(src, src, ud_send.at[i], ud_recv.at[i - 2], d, (up, down)[i - 4])

    for i in range(4):
        ud_copy(i).start()
    for m, mat in enumerate((upw, dnw)):
        pltpu.make_async_copy(mat, columns(z).at[m], recv.at[8]).start()

    pick_pair = push(
        context.at[0:first, core], context.at[0:first, core], pair_send.at[0], recv.at[1], place.dp(CORE), z
    )
    settle(context.at[0:first, core], recv.at[5])
    pick_pair.start()
    gather.middle()
    settle(columns(down), ud_recv.at[0])
    ud_copy(4).start()
    settle(columns(up), ud_recv.at[1])
    ud_copy(5).start()

    lead_copy = push(
        context.at[first:], context.at[first:], pair_send.at[1], recv.at[3], place.dp(CORE), z
    )

    @pl.when(core == 0)
    def _():
        settle(context.at[first:], recv.at[3])
        lead_copy.start()

    gather.last()
    gather.wait(range(6, 14), range(14))
    settle(whole.at[:, own_rows, :], recv.at[6])
    settle(out_slab, recv.at[7])
    settle(columns(z), recv.at[8])
    ud_copy(4).wait_recv()
    ud_copy(5).wait_recv()
    settle(all_ints, recv.at[2])
    pick_pair.wait()

    @pl.when(core == 0)
    def _():
        lead_copy.wait_send()

    @pl.when(core == 1)
    def _():
        settle(context.at[first:], recv.at[3])
        settle(stream, recv.at[4])

    for i in range(4):
        stream_copy(i, "wait")
        mat_copy(i).wait_send()
    for i in range(6):
        ud_copy(i).wait_send()
    for copy in spread_copies + int_copies + pick_copies:
        copy.wait_send()


def exchange(slot_of, content, query, memory, ints, mats, upw, dnw):
    micro, part, width = content.shape
    rows = mats[0].shape[0]
    inner = upw.shape[1] * 4
    piece = part // 8
    vmem = pl.BlockSpec(memory_space=pltpu.VMEM)
    dma = lambda n: pltpu.SemaphoreType.DMA((n,))
    context, *rest = pl.pallas_call(
        exchange_kernel,
        in_specs=[SMEM_SPEC] + [ANY_SPEC] * 3 + [vmem] * 8,
        out_specs=[ANY_SPEC] * 6,
        out_shape=[
            jax.ShapeDtypeStruct((32, 2, piece, width), BF),
            jax.ShapeDtypeStruct((4 * part, width), BF),
            jax.ShapeDtypeStruct((8,) + ints.shape, jnp.int32),
            jax.ShapeDtypeStruct((4, 8 * rows, width), BF),
            jax.ShapeDtypeStruct((1, rows, width), BF),
            jax.ShapeDtypeStruct((2, rows, inner), BF),
        ],
        scratch_shapes=[
            pltpu.VMEM((16, piece, width), BF),
            pltpu.VMEM((16, piece, width), BF),
            pltpu.VMEM((4, 5, rows * 3 // 2, 128), BF),
            pltpu.VMEM((5, rows, width), BF),
            dma(4),
            dma(4),
            dma(6),
            dma(4),
            dma(7),
            dma(7),
            dma(15),
            dma(4),
            dma(2),
            dma(14),
            dma(14),
            dma(9),
        ],
        compiler_params=pltpu.CompilerParams(
            collective_id=1, has_side_effects=True, vmem_limit_bytes=LIMIT
        ),
        cost_estimate=pl.CostEstimate(flops=0, bytes_accessed=64 << 20, transcendentals=0),
        name="exchange",
    )(slot_of, content.reshape(micro, 4, 2, piece, width), query, memory, ints, *mats, upw, dnw)
    return [context.reshape(8 * part, width)] + rest


def head_lanes(array, head):
    lane = lax.broadcasted_iota(jnp.int32, array.shape, 1)
    return jnp.where((lane >= DH) == (head == 1), array, jnp.zeros_like(array))


def attend_forward_step(
    block, qw_ref, qp_ref, k_ref, v_ref, rel_ref, thr_ref, kr_ref, vec_ref, prob_ref
):
    rows, klen = qw_ref.shape[0], k_ref.shape[0]
    width = klen + block
    keys, values = k_ref[...], v_ref[...]
    for part in range(rows // block):
        at = slice(part * block, (part + 1) * block)
        first = rows - (part + 1) * block
        qw, qp = qw_ref[at, :], qp_ref[at, :]
        rel = rel_ref[first : first + width, :]
        seen = kr_ref[...] < thr_ref[at, :]
        vecs = []
        for head in range(2):
            raw = nt(head_lanes(qp, head), rel)
            moved = pltpu.roll(raw, 0, 1, stride=1, stride_axis=0)[:, block:]
            score = nt(head_lanes(qw, head), keys) + moved
            score = jnp.where(seen, score, -1e30)
            expo = jnp.exp(score - jnp.max(score, axis=1, keepdims=True))
            prob = (expo * (1.0 / jnp.sum(expo, axis=1, keepdims=True))).astype(BF)
            prob_ref[head, at, :] = prob
            vecs.append(nn(prob, values))
        lane = lax.broadcasted_iota(jnp.int32, vecs[0].shape, 1)
        vec_ref[at, :] = jnp.where(lane < DH, vecs[0], vecs[1]).astype(BF)


def attend_forward_kernel(block, wired, *refs):
    if not wired:
        attend_forward_step(block, *refs)
        return
    ins, (ctan, qtan) = refs[:7], refs[9:11]
    outs, (wo, ud, tangent) = refs[11:13], refs[13:16]
    out_send, out_recv, ud_send, ud_recv, tan_send, recv = refs[16:]
    step, steps = pl.program_id(0), pl.num_programs(0)
    place = Place()
    d, z, core = place.d, place.z, place.core
    gathers = (
        Gather(place, ud, None, ud_send, ud_recv),
        Gather(place, wo, None, out_send, out_recv),
    )
    part = ctan.shape[1]

    def tan_copy(i, act):
        j, kind = i // 2, i % 2
        to, dp = 2 * core + j, d - core + kind
        src = (ctan, qtan)[kind].at[j]
        dst = tangent.at[pl.ds(pl.multiple_of(z * part, 16), part), :]
        here = jnp.logical_and(dp == d, to == z)
        local = pltpu.make_async_copy(src, dst, recv.at[0])
        remote = push(src, dst, tan_send.at[i], recv.at[0], dp, to)
        if act == "start":
            pl.when(here)(local.start)
            pl.when(jnp.logical_not(here))(remote.start)
        else:
            pl.when(jnp.logical_not(here))(remote.wait_send)

    @pl.when(step == 0)
    def _():
        greet(near_partners(place))
        for gather in gathers:
            gather.start(2, 3, 4, 5, 8, 9)
        for i in range(4):
            tan_copy(i, "start")

    attend_forward_step(block, *ins, *outs)

    @pl.when(step == steps - 1)
    def _():
        for gather in gathers:
            gather.last()
        for gather in gathers:
            gather.wait(range(8, 14), (2, 3, 4, 5) + tuple(range(8, 14)))
        settle(tangent, recv.at[0])
        for i in range(4):
            tan_copy(i, "wait")


def attend_forward(qw, qp, keys, values, rel, thr, key_rank, block, wires=()):
    rows, width = qw.shape
    klen, span = keys.shape[0], rel.shape[0]
    col = lambda count: pl.BlockSpec((count, PAIR), lambda p: (0, p))
    in_specs = [
        col(rows),
        col(rows),
        col(klen),
        col(klen),
        col(span),
        pl.BlockSpec((rows, 1), lambda p: (0, 0)),
        pl.BlockSpec((1, klen), lambda p: (0, 0)),
    ]
    out_specs = [col(rows), pl.BlockSpec((2, rows, klen), lambda p: (p, 0, 0))]
    out_shape = [
        jax.ShapeDtypeStruct((rows, width), BF),
        jax.ShapeDtypeStruct((width // DH, rows, klen), BF),
    ]
    params = dict(vmem_limit_bytes=LIMIT)
    scratch = []
    if wires:
        in_specs += [ANY_SPEC] * 4
        out_specs += [ANY_SPEC] * 3
        out_shape += [
            jax.ShapeDtypeStruct(wires[0].shape, BF),
            jax.ShapeDtypeStruct(wires[1].shape, BF),
            jax.ShapeDtypeStruct((rows, width), BF),
        ]
        scratch = [pltpu.SemaphoreType.DMA((n,)) for n in (14, 14, 14, 14, 4, 1)]
        params.update(collective_id=2, has_side_effects=True)
    return pl.pallas_call(
        functools.partial(attend_forward_kernel, block, bool(wires)),
        grid=(width // PAIR,),
        in_specs=in_specs,
        out_specs=out_specs,
        out_shape=out_shape,
        scratch_shapes=scratch,
        input_output_aliases={7: 2, 8: 3} if wires else {},
        compiler_params=pltpu.CompilerParams(**params),
        cost_estimate=pl.CostEstimate(
            flops=8 * rows * klen * width, bytes_accessed=16 << 20, transcendentals=12 * rows * klen
        ),
        name="attend_forward",
    )(qw, qp, keys, values, rel, thr, key_rank, *wires)


def attend_backward_kernel(block, wired, *refs):
    if not wired:
        attend_backward_step(block, *refs)
        return
    ins, (g_ud, src) = refs[:7], refs[7:9]
    outs, (grads_ref, home_ref) = refs[9:14], refs[14:16]
    rel_acc, home_send, home_recv = refs[16:19]
    step, steps = pl.program_id(0), pl.num_programs(0)
    place = Place()
    count = len(refs[19:]) // 2
    reduces = [
        Reduce(place, (g_ud.at[m : m + 1],), refs[19 + m * count : 19 + (m + 1) * count], grads_ref.at[m : m + 1])
        for m in range(2)
    ]
    home = Homeward(place, src, home_ref, home_send, home_recv.at[0])

    @pl.when(step == 0)
    def _():
        greet(near_partners(place))
        for reduce in reduces:
            reduce.begin()
        home.start()

    @pl.when(step == 2)
    def _():
        reduces[0].pairs()

    @pl.when(step == 3)
    def _():
        reduces[1].pairs()

    @pl.when(step == 5)
    def _():
        reduces[0].middle()

    attend_backward_step(block, *ins, *outs, rel_acc)

    @pl.when(step == steps - 1)
    def _():
        reduces[0].late()
        reduces[1].middle()
        reduces[1].late()
        reduces[0].end()
        reduces[1].end()
        home.end()


def attend_backward_step(
    block,
    prob_ref,
    gvec_ref,
    qw_ref,
    qp_ref,
    k_ref,
    v_ref,
    rel_ref,
    dproj_ref,
    dk_ref,
    dv_ref,
    drel_ref,
    bias_ref,
    rel_acc,
):
    rows, klen = qw_ref.shape[0], k_ref.shape[0]
    width = klen + block
    keys, values = k_ref[...], v_ref[...]
    row = lax.broadcasted_iota(jnp.int32, (block, block), 0)
    col = lax.broadcasted_iota(jnp.int32, (block, block), 1)
    mirror = (row + col == block - 1).astype(BF)
    rel_acc[...] = jnp.zeros_like(rel_acc)
    d_keys, d_values = [None, None], [None, None]
    word_sum = jnp.zeros((1, PAIR), F32)
    pos_sum = jnp.zeros((1, PAIR), F32)
    for part in range(rows // block):
        at = slice(part * block, (part + 1) * block)
        first = rows - (part + 1) * block
        gvec, qw = gvec_ref[at, :], qw_ref[at, :]
        gvec_t = jnp.transpose(gvec.astype(F32)).astype(BF)
        qw_t = jnp.transpose(qw.astype(F32)).astype(BF)
        qp_t = jnp.transpose(nn(mirror, qp_ref[at, :])).astype(BF)
        rel = rel_ref[first : first + width, :]
        word_parts, pos_parts = [], []
        for head in range(2):
            own = slice(head * DH, (head + 1) * DH)
            prob = prob_ref[head, at, :]
            d_prob = nt(head_lanes(gvec, head), values)
            weight = prob.astype(F32)
            inner = jnp.sum(weight * d_prob, axis=1, keepdims=True)
            g_sum = (weight * (d_prob - inner) * 0.125).astype(BF)
            dv = nn(gvec_t[own, :], prob)
            dk = nn(qw_t[own, :], g_sum)
            d_values[head] = dv if part == 0 else d_values[head] + dv
            d_keys[head] = dk if part == 0 else d_keys[head] + dk
            turned = nn(mirror, g_sum)
            padded = jnp.concatenate([jnp.zeros((block, block), F32), turned], axis=1)
            moved = pltpu.roll(padded, width - block + 1, 1, stride=1, stride_axis=0).astype(BF)
            word_parts.append(nn(turned.astype(BF), keys))
            pos_parts.append(nn(moved, rel))
            rel_acc[own, first : first + width] += nn(qp_t[own, :], moved)
        lane = lax.broadcasted_iota(jnp.int32, word_parts[0].shape, 1)
        word = jnp.where(lane < DH, word_parts[0], word_parts[1])
        pos = jnp.where(lane < DH, pos_parts[0], pos_parts[1])
        word_sum = word_sum + jnp.sum(word, axis=0, keepdims=True)
        pos_sum = pos_sum + jnp.sum(pos, axis=0, keepdims=True)
        dproj_ref[at, :] = nn(mirror, (word + pos).astype(BF)).astype(BF)
    for head in range(2):
        own = slice(head * DH, (head + 1) * DH)
        dv_ref[own, :] = d_values[head].astype(BF)
        dk_ref[own, :] = (8.0 * d_keys[head]).astype(BF)
    drel_ref[...] = (8.0 * rel_acc[...]).astype(BF)
    bias_ref[0:1, :] = word_sum
    bias_ref[1:2, :] = pos_sum


def attend_backward(prob, gvec, qw, qp, keys, values, rel, block, wires=()):
    rows, width = qw.shape
    klen, span = keys.shape[0], rel.shape[0]
    col = lambda count: pl.BlockSpec((count, PAIR), lambda p: (0, p))
    rowb = lambda count: pl.BlockSpec((PAIR, count), lambda p: (p, 0))
    in_specs = [
        pl.BlockSpec((2, rows, klen), lambda p: (p, 0, 0)),
        col(rows),
        col(rows),
        col(rows),
        col(klen),
        col(klen),
        col(span),
    ]
    out_specs = [col(rows), rowb(klen), rowb(klen), rowb(span), col(2)]
    out_shape = [
        jax.ShapeDtypeStruct((rows, width), BF),
        jax.ShapeDtypeStruct((width, klen), BF),
        jax.ShapeDtypeStruct((width, klen), BF),
        jax.ShapeDtypeStruct((width, span), BF),
        jax.ShapeDtypeStruct((2, width), F32),
    ]
    scratch = [pltpu.VMEM((PAIR, span), F32)]
    params = dict(vmem_limit_bytes=LIMIT)
    if wires:
        inner, mine = wires[0].shape[2], width // 8
        in_specs += [ANY_SPEC, ANY_SPEC]
        out_specs += [pl.BlockSpec(memory_space=pltpu.VMEM), ANY_SPEC]
        out_shape += [
            jax.ShapeDtypeStruct((2, mine, inner // 4), F32),
            jax.ShapeDtypeStruct((2, 2, rows // 4, width), BF),
        ]
        scratch += [pltpu.SemaphoreType.DMA((4,)), pltpu.SemaphoreType.DMA((1,))]
        scratch += 2 * Reduce.scratch(1, 1, mine, inner)
        params.update(collective_id=3, has_side_effects=True)
    return pl.pallas_call(
        functools.partial(attend_backward_kernel, block, bool(wires)),
        grid=(width // PAIR,),
        in_specs=in_specs,
        out_specs=out_specs,
        out_shape=out_shape,
        scratch_shapes=scratch,
        compiler_params=pltpu.CompilerParams(**params),
        cost_estimate=pl.CostEstimate(
            flops=16 * rows * klen * width, bytes_accessed=20 << 20, transcendentals=0
        ),
        name="attend_backward",
    )(prob, gvec, qw, qp, keys, values, rel, *wires)


def norm_parts(value):
    center = value - jnp.mean(value, axis=1, keepdims=True)
    scale = lax.rsqrt(jnp.mean(center * center, axis=1, keepdims=True) + EPS)
    return center * scale, scale


def norm_pull(normed, scale, err):
    inner = jnp.mean(err * normed, axis=1, keepdims=True)
    return (err - jnp.mean(err, axis=1, keepdims=True) - normed * inner) * scale


def sum_rows(value):
    return jnp.sum(value, axis=0, keepdims=True)


def feed_kernel(steps, *refs):
    (
        ud_hbm,
        wo_hbm,
        vec_ref,
        x_ref,
        tan_ref,
        upb_ref,
        dnb_ref,
        g1_ref,
        s1_ref,
        g2_ref,
        s2_ref,
        out_ref,
        dmix_ref,
        gvec_ref,
        go_ref,
        gud_ref,
        gupb_ref,
        small_ref,
        ud_ref,
        wo_ref,
        n1_ref,
        r1_ref,
        fb_ref,
        fbt_ref,
        acc_ref,
        act_ref,
        slope_ref,
        gd_ref,
        gdt_ref,
        sems,
    ) = refs
    step = pl.program_id(0)
    chunk = act_ref.shape[2]
    cols = pl.ds(pl.multiple_of(lax.rem(step, steps) * chunk, chunk), chunk)

    @pl.when(step == 0)
    def _():
        wo_copy = pltpu.make_async_copy(wo_hbm, wo_ref, sems.at[0])
        ud_copy = pltpu.make_async_copy(ud_hbm, ud_ref, sems.at[1])
        wo_copy.start()
        ud_copy.start()
        wo_copy.wait()
        normed, scale = norm_parts(nt(vec_ref[...], wo_ref[0]) + x_ref[...].astype(F32))
        n1_ref[...] = normed
        r1_ref[...] = scale
        first = normed * g1_ref[...] + s1_ref[...]
        fb_ref[...] = first.astype(BF)
        fbt_ref[...] = jnp.transpose(first).astype(BF)
        acc_ref[...] = first + dnb_ref[...]
        ud_copy.wait()

    @pl.when(step < steps)
    def _():
        upper = nn(fb_ref[...], ud_ref[0, :, cols]) + upb_ref[...]
        square = upper * upper
        root = 0.7978845608028654
        bend = jnp.tanh(root * (upper + 0.044715 * (square * upper)))
        half = 0.5 * (1.0 + bend)
        act = (upper * half).astype(BF)
        act_ref[step] = act
        slope_ref[step] = half + 0.5 * upper * (1.0 - bend * bend) * (
            root + (3 * 0.044715 * root) * square
        )
        acc_ref[...] += nt(act, ud_ref[1, :, cols])

    @pl.when(step == steps - 1)
    def _():
        normed, scale = norm_parts(acc_ref[...])
        out_ref[...] = (normed * g2_ref[...] + s2_ref[...]).astype(BF)
        tan = tan_ref[...].astype(F32)
        d_down = norm_pull(normed, scale, tan * g2_ref[...])
        small_ref[0:1, :] = sum_rows(d_down)
        small_ref[3:4, :] = sum_rows(tan * normed)
        small_ref[4:5, :] = sum_rows(tan)
        gd_ref[...] = d_down.astype(BF)
        gdt_ref[...] = jnp.transpose(d_down).astype(BF)
        acc_ref[...] = d_down

    @pl.when(step >= steps)
    def _():
        at = step - steps
        d_up = nn(gd_ref[...], ud_ref[1, :, cols]) * slope_ref[at]
        gupb_ref[...] = sum_rows(d_up)
        g_up = d_up.astype(BF)
        acc_ref[...] += nt(g_up, ud_ref[0, :, cols])
        gud_ref[0] = nn(fbt_ref[...], g_up).astype(BF)
        gud_ref[1] = nn(gdt_ref[...], act_ref[at]).astype(BF)

    @pl.when(step == 2 * steps - 1)
    def _():
        d_first, normed = acc_ref[...], n1_ref[...]
        small_ref[1:2, :] = sum_rows(d_first * normed)
        small_ref[2:3, :] = sum_rows(d_first)
        d_mixed = norm_pull(normed, r1_ref[...], d_first * g1_ref[...])
        dmix_ref[...] = d_mixed
        gvec_ref[...] = nn(d_mixed.astype(BF), wo_ref[0]).astype(BF)
        gdt_ref[...] = jnp.transpose(d_mixed).astype(BF)
        go_ref[...] = nn(gdt_ref[...], vec_ref[...]).astype(BF)


def feed(ud, wo, vec, x, tan, upb, dnb, g1, s1, g2, s2):
    rows, width = vec.shape
    inner = upb.shape[1]
    chunk = 512
    steps = inner // chunk
    whole = lambda a, b: pl.BlockSpec((a, b), lambda i: (0, 0))
    late = lambda i: jnp.maximum(i - steps, 0)
    grads = pl.BlockSpec((2, width, chunk), lambda i: (0, 0, late(i)))
    return pl.pallas_call(
        functools.partial(feed_kernel, steps),
        grid=(2 * steps,),
        in_specs=[ANY_SPEC] * 2
        + [whole(rows, width)] * 3
        + [pl.BlockSpec((1, chunk), lambda i: (0, lax.rem(i, steps)))]
        + [whole(1, width)] * 5,
        out_specs=[
            whole(rows, width),
            whole(rows, width),
            whole(rows, width),
            whole(width, width),
            grads,
            pl.BlockSpec((1, chunk), lambda i: (0, late(i))),
            whole(8, width),
        ],
        out_shape=[
            jax.ShapeDtypeStruct((rows, width), BF),
            jax.ShapeDtypeStruct((rows, width), F32),
            jax.ShapeDtypeStruct((rows, width), BF),
            jax.ShapeDtypeStruct((width, width), BF),
            jax.ShapeDtypeStruct((2, width, inner), BF),
            jax.ShapeDtypeStruct((1, inner), F32),
            jax.ShapeDtypeStruct((8, width), F32),
        ],
        scratch_shapes=[
            pltpu.VMEM((2, width, inner), BF),
            pltpu.VMEM((1, width, width), BF),
            pltpu.VMEM((rows, width), F32),
            pltpu.VMEM((rows, 1), F32),
            pltpu.VMEM((rows, width), BF),
            pltpu.VMEM((width, rows), BF),
            pltpu.VMEM((rows, width), F32),
            pltpu.VMEM((steps, rows, chunk), BF),
            pltpu.VMEM((steps, rows, chunk), F32),
            pltpu.VMEM((rows, width), BF),
            pltpu.VMEM((width, rows), BF),
            pltpu.SemaphoreType.DMA((2,)),
        ],
        compiler_params=pltpu.CompilerParams(vmem_limit_bytes=LIMIT),
        cost_estimate=pl.CostEstimate(
            flops=12 * rows * width * inner, bytes_accessed=36 << 20, transcendentals=rows * inner
        ),
        name="feed",
    )(ud, wo, vec, x, tan, upb, dnb, g1, s1, g2, s2)


def project_kernel(wired, *refs):
    if not wired:
        project_step(*refs)
        return
    ins, (out_slab, ud_slab) = refs[:6], refs[6:8]
    outs, (wo, ud) = refs[8:14], refs[14:16]
    out_send, out_recv, ud_send, ud_recv, own = refs[16:]
    place = Place()
    gathers = (
        Gather(place, ud, ud_slab, ud_send, ud_recv),
        Gather(place, wo, out_slab, out_send, out_recv),
    )
    rows = out_slab.shape[1]
    own_rows = pl.ds(pl.multiple_of(place.d * rows, 16), rows)
    locals_ = (
        pltpu.make_async_copy(ud_slab, ud.at[:, own_rows, :], own.at[0]),
        pltpu.make_async_copy(out_slab, wo.at[:, own_rows, :], own.at[1]),
    )
    greet([(place.dp(r), place.z) for r in (CORE, XBIT, YBIT)])
    for gather in gathers:
        gather.start(0, 1, 6, 7)
    for copy in locals_:
        copy.start()
    project_step(*ins, *outs)
    for gather in gathers:
        gather.wait((0, 1, 6, 7), (0, 1, 6, 7))
    for copy in locals_:
        copy.wait()


def project_step(
    w_ref, ctx_ref, q_ref, table_ref, wb_ref, pb_ref, k_ref, v_ref, rel_ref, qw_ref, qp_ref, x_ref
):
    lead = lax.rem(lax.axis_index("dp"), 2) == 0
    back = ctx_ref.shape[0] - q_ref.shape[0]
    block = 256

    def loop(count, step):
        def run(i, carry):
            step(pl.ds(pl.multiple_of(i * block, block), block))
            return carry

        lax.fori_loop(0, count // block, run, 0)

    def context_step(at):
        k_ref[at, :] = nn(ctx_ref[at, :], w_ref[0]).astype(BF)
        v_ref[at, :] = nn(ctx_ref[at, :], w_ref[1]).astype(BF)

    def stream_step(at):
        own = ctx_ref[pl.ds(pl.multiple_of(at.start + back, block), block), :]
        x_ref[at, :] = jnp.where(lead, own, q_ref[at, :])
        proj = nn(x_ref[at, :], w_ref[2])
        qw_ref[at, :] = (0.125 * (proj + wb_ref[...]).astype(BF).astype(F32)).astype(BF)
        qp_ref[at, :] = (0.125 * (proj + pb_ref[...]).astype(BF).astype(F32)).astype(BF)

    def table_step(at):
        rel_ref[at, :] = nn(table_ref[at, :], w_ref[3]).astype(BF)

    loop(table_ref.shape[0], table_step)
    loop(q_ref.shape[0], stream_step)
    loop(ctx_ref.shape[0], context_step)


def project(mats, context, query, table, wb, pb, wires=()):
    rows, width = query.shape
    klen, span = context.shape[0], table.shape[0]
    vmem = pl.BlockSpec(memory_space=pltpu.VMEM)
    out_shape = [
        jax.ShapeDtypeStruct((klen, width), BF),
        jax.ShapeDtypeStruct((klen, width), BF),
        jax.ShapeDtypeStruct((span, width), BF),
        jax.ShapeDtypeStruct((rows, width), BF),
        jax.ShapeDtypeStruct((rows, width), BF),
        jax.ShapeDtypeStruct((rows, width), BF),
    ]
    params = dict(vmem_limit_bytes=LIMIT)
    scratch = []
    if wires:
        params.update(collective_id=5, has_side_effects=True)
        scratch = [pltpu.SemaphoreType.DMA((n,)) for n in (14, 14, 14, 14, 2)]
        out_shape += [
            jax.ShapeDtypeStruct((slab.shape[0], width, slab.shape[2]), BF) for slab in wires
        ]
    return pl.pallas_call(
        functools.partial(project_kernel, bool(wires)),
        in_specs=[vmem] * (6 + len(wires)),
        out_specs=[vmem] * 6 + [ANY_SPEC] * len(wires),
        out_shape=out_shape,
        scratch_shapes=scratch,
        compiler_params=pltpu.CompilerParams(**params),
        cost_estimate=pl.CostEstimate(
            flops=2 * (2 * klen + rows + span) * width * width,
            bytes_accessed=20 << 20,
            transcendentals=0,
        ),
        name="project",
    )(mats, context, query, table, wb, pb, *wires)


def weight_grads_kernel(xt_ref, ct_ref, tt_ref, dp_ref, dk_ref, dv_ref, dr_ref, g_ref):
    g_ref[0] = nt(ct_ref[...], dk_ref[...]).astype(BF)
    g_ref[1] = nt(ct_ref[...], dv_ref[...]).astype(BF)
    g_ref[2] = nn(xt_ref[...], dp_ref[...]).astype(BF)
    g_ref[3] = nt(tt_ref[...], dr_ref[...]).astype(BF)


def weight_grads(x_t, ctx_t, table_t, d_proj, dk_t, dv_t, drel_t):
    width, rows = x_t.shape
    klen, span = ctx_t.shape[1], table_t.shape[1]
    chunk = 256
    whole = lambda a, b: pl.BlockSpec((a, b), lambda i: (0, 0))
    rowb = lambda b: pl.BlockSpec((chunk, b), lambda i: (i, 0))
    return pl.pallas_call(
        weight_grads_kernel,
        grid=(width // chunk,),
        in_specs=[
            whole(width, rows),
            whole(width, klen),
            whole(width, span),
            pl.BlockSpec((rows, chunk), lambda i: (0, i)),
            rowb(klen),
            rowb(klen),
            rowb(span),
        ],
        out_specs=pl.BlockSpec((4, width, chunk), lambda i: (0, 0, i)),
        out_shape=jax.ShapeDtypeStruct((4, width, width), BF),
        compiler_params=pltpu.CompilerParams(vmem_limit_bytes=LIMIT),
        cost_estimate=pl.CostEstimate(
            flops=2 * (rows + 2 * klen + span) * width * width,
            bytes_accessed=20 << 20,
            transcendentals=0,
        ),
        name="weight_grads",
    )(x_t, ctx_t, table_t, d_proj, dk_t, dv_t, drel_t)


def flip(arr, bit):
    return lax.ppermute(arr, "dp", [(i, i ^ bit) for i in range(lax.axis_size("dp"))])


def scatter_sum(grads):
    mine = lax.psum_scatter(grads, "dp", scatter_dimension=1, tiled=True)
    return lax.psum_scatter(mine, "tensor", scatter_dimension=2, tiled=True).astype(F32)


def body(
    content_stream,
    query_stream,
    memory,
    content_tangent,
    query_tangent,
    seq_lengths,
    factor_order,
    memory_lengths,
    slot_sequence,
    query_weight,
    key_weight,
    value_weight,
    pos_weight,
    out_weight,
    up_weight,
    up_bias,
    down_weight,
    down_bias,
    word_bias,
    pos_bias,
    first_gain,
    first_shift,
    second_gain,
    second_shift,
):
    groups, tensors = lax.axis_size("dp"), lax.axis_size("tensor")
    micro, part_len, width = content_stream.shape
    mem_part = memory.shape[1]
    seq_len, mem_total = part_len * tensors, mem_part * tensors
    klen, span = mem_total + seq_len, mem_total + 2 * seq_len
    count = micro * groups
    here, lane = lax.axis_index("dp"), lax.axis_index("tensor")
    core = here % 2
    lead = core == 0
    block = 256
    assert 2 * micro == tensors

    def swap(arr):
        return flip(arr, CORE)

    def to_unit(first, second):
        got = swap(jnp.where(lead, second, first))
        low = jnp.where(lead, first, got)
        high = jnp.where(lead, got, second)
        both = jnp.concatenate([low, high], 0)
        both = lax.all_to_all(both, "tensor", split_axis=0, concat_axis=0, tiled=True)
        return both.reshape(seq_len, width)

    def from_unit(arr):
        both = arr.reshape(tensors, part_len, width)
        both = lax.all_to_all(both, "tensor", split_axis=0, concat_axis=0, tiled=True)
        low, high = both[:micro], both[micro:]
        got = swap(jnp.where(lead, high, low))
        return jnp.where(lead, low, got), jnp.where(lead, got, high)

    seq_id = (here // 2) * tensors + lane
    ids = jnp.arange(count, dtype=jnp.int32)
    slot_of = jnp.sum(jnp.where(slot_sequence[None, :] == ids[:, None], ids[None, :], 0), axis=1)
    counts = jnp.concatenate([seq_lengths, memory_lengths])
    slot = slot_of[seq_id]
    mats = [key_weight, value_weight, query_weight, pos_weight, out_weight]
    table = jnp.asarray(reversed_table(span, klen, width))
    wires = ()
    if groups == 8:
        ints = jnp.pad(factor_order, ((0, 6), (0, 0)))
        ints = lax.dynamic_update_slice(ints, counts[None, :], (micro, 0))
        context, query, all_ints, weights, out_slab, ud_slab = exchange(
            slot_of, content_stream, query_stream, memory, ints, mats, up_weight, down_weight
        )
        wires = (out_slab, ud_slab)
        lengths = all_ints[:, micro, : 2 * micro]
        orders = all_ints[seq_id // micro, :micro]
    else:
        lengths = lax.all_gather(counts, "dp", axis=0, tiled=False)
        orders = lax.all_gather(factor_order, "dp", axis=0, tiled=False)[seq_id // micro]
        stream = to_unit(content_stream, query_stream)
        content, query = jnp.where(lead, stream, swap(stream)), stream
        tangent = to_unit(content_tangent, query_tangent)
        piece = mem_part // groups
        spread = lax.all_to_all(
            memory.reshape(micro, groups, piece, width), "dp", split_axis=1, concat_axis=1, tiled=True
        )
        spread = spread.transpose(1, 0, 2, 3).reshape(count, piece, width)
        spread = jnp.take(spread, slot_of, axis=0)
        spread = spread.reshape(groups // 2, tensors, 2, piece // 2, width).transpose(0, 2, 1, 3, 4)
        spread = lax.all_to_all(
            spread.reshape(groups, tensors, piece // 2, width),
            "dp",
            split_axis=0,
            concat_axis=0,
            tiled=True,
        )
        spread = lax.all_to_all(spread, "tensor", split_axis=1, concat_axis=1, tiled=True)
        got = swap(spread)
        mem_rows = jnp.stack([jnp.where(lead, spread, got), jnp.where(lead, got, spread)])
        mem_rows = mem_rows.transpose(2, 1, 0, 3, 4).reshape(mem_total, width)
        context = jnp.concatenate([mem_rows, content], 0)

        def whole(mat):
            mat = lax.all_gather(mat, "tensor", axis=1, tiled=True)
            return lax.all_gather(mat, "dp", axis=0, tiled=True)

        weights = jnp.stack([whole(mat) for mat in mats[:4]])
        wo = whole(out_weight)[None]
        ud = jnp.stack([whole(up_weight), whole(down_weight)])

    length = lengths[seq_id // micro, seq_id % micro]
    mem_valid = lengths[slot // micro, micro + slot % micro]
    rank = orders[seq_id % micro]
    key_pos = jnp.arange(klen, dtype=jnp.int32)
    hidden = jnp.int32(1 << 20)
    mem_rank = jnp.where(key_pos[:mem_total] >= mem_total - mem_valid, -1, hidden)
    own_rank = jnp.where(key_pos[:seq_len] < length, rank, hidden)
    key_rank = jnp.concatenate([mem_rank, own_rank])[None, :]
    thr = (rank + jnp.where(lead, 1, 0))[:, None]

    row = lambda v: v.reshape(1, -1)
    keys, values, rel, q_word, q_pos, stream, *wires = project(
        weights, context, query, table, row(word_bias), row(pos_bias), wires
    )
    if wires:
        wires += [content_tangent, query_tangent]
    vec, prob, *arrived = attend_forward(
        q_word, q_pos, keys, values, rel, thr, key_rank, block, wires
    )
    if wires:
        wo, ud, tangent = arrived
    out, d_mixed, g_vec, g_out, g_ud, g_upb, small = feed(
        ud,
        wo,
        vec,
        stream,
        tangent,
        row(up_bias),
        row(down_bias),
        row(first_gain),
        row(first_shift),
        row(second_gain),
        row(second_shift),
    )
    backward = (prob, g_vec, q_word, q_pos, keys, values, rel, block)
    if groups == 8:
        d_proj, dk_t, dv_t, drel_t, biases, (grad_up, grad_down), outs = attend_backward(
            *backward, (g_ud, out)
        )
        content_out, query_out = outs[0], outs[1]
    else:
        d_proj, dk_t, dv_t, drel_t, biases = attend_backward(*backward)
        content_out, query_out = from_unit(out)
        grad_up, grad_down = scatter_sum(g_ud)
    small = jnp.concatenate([g_upb.reshape(-1), small[:5].reshape(-1), biases.reshape(-1)])
    d_context = tt(dk_t[:, mem_total:], weights[0]) + tt(dv_t[:, mem_total:], weights[1])
    d_stream = d_mixed + nt(d_proj, weights[2])
    d_stream = d_stream + jnp.where(lead, d_context, 0.0)
    grads = weight_grads(
        jnp.transpose(stream),
        jnp.transpose(context),
        jnp.transpose(table),
        d_proj,
        dk_t,
        dv_t,
        drel_t,
    )
    inner = up_bias.shape[0]
    if groups == 8:
        size = small.shape[0]
        small = jnp.pad(small, (0, -size % 1024)).reshape(-1, 128)
        grads, homes, small = finish(grads, g_out[None], d_stream, d_context.astype(BF), small)
        grad_key, grad_value, grad_query, grad_pos, grad_out = grads
        content_grad, query_grad = homes[0], homes[1]
        small = small.reshape(-1)[:size]
    else:
        partner = swap(d_context.astype(BF)).astype(F32)
        d_stream = d_stream + jnp.where(lead, partner, 0.0)
        content_grad, query_grad = from_unit(d_stream.astype(BF))
        grad_key, grad_value, grad_query, grad_pos = scatter_sum(grads)
        (grad_out,) = scatter_sum(g_out[None])
        small = lax.psum(small, ("dp", "tensor"))
    rest = small[inner:].reshape(7, width)
    return (
        content_out,
        query_out,
        content_grad,
        query_grad,
        grad_query,
        grad_key,
        grad_value,
        grad_pos,
        grad_out,
        grad_up,
        small[:inner],
        grad_down,
        rest[0],
        rest[5].reshape(HEADS, DH),
        rest[6].reshape(HEADS, DH),
        rest[1],
        rest[2],
        rest[3],
        rest[4],
    )


def solution(mesh):
    rows = P("dp", "tensor", None)
    mat = P("dp", "tensor")
    return jax.shard_map(
        body,
        mesh=mesh,
        in_specs=(rows,) * 5
        + (P("dp"), P("dp", None), P("dp"), P())
        + (mat,) * 6
        + (P(), mat)
        + (P(),) * 7,
        out_specs=(rows,) * 4 + (mat,) * 6 + (P(), mat) + (P(),) * 7,
        check_vma=False,
    )
```

```python
import functools

import jax
import jax.numpy as jnp
import numpy as np
from jax import lax
from jax.experimental import pallas as pl
from jax.experimental.pallas import tpu as pltpu
from jax.sharding import PartitionSpec as P

HEADS = 12
DH = 64
PAIR = 2 * DH
EPS = 1e-06
BF = jnp.bfloat16
F32 = jnp.float32
LIMIT = 60 * 1024 * 1024
SMEM_SPEC = pl.BlockSpec(memory_space=pltpu.SMEM)
ANY_SPEC = pl.BlockSpec(memory_space=pl.ANY)


def nn(left, right):
    return jnp.dot(left, right, preferred_element_type=F32)


def nt(left, right):
    return lax.dot_general(left, right, (((1,), (1,)), ((), ())), preferred_element_type=F32)


def tn(left, right):
    return lax.dot_general(left, right, (((0,), (0,)), ((), ())), preferred_element_type=F32)


def tt(left, right):
    return lax.dot_general(left, right, (((0,), (1,)), ((), ())), preferred_element_type=F32)


def reversed_table(count, first, width):
    dist = (first - np.arange(count)).astype(np.float32)
    half = width // 2
    power = np.arange(half).astype(np.float32) * np.float32(2.0 / width)
    freq = np.float32(1.0) / np.float32(10000.0) ** power
    angle = (dist[:, None] * freq[None, :]).astype(np.float64)
    return np.concatenate([np.sin(angle), np.cos(angle)], axis=1).astype(np.float32).astype(BF)


MESH = pl.DeviceIdType.MESH
CORE, XBIT, YBIT = 1, 2, 4


class Place:
    def __init__(self):
        self.d, self.z = lax.axis_index("dp"), lax.axis_index("tensor")
        self.core = lax.rem(self.d, 2)
        self.x = lax.rem(lax.div(self.d, 2), 2)
        self.y = lax.div(self.d, 4)

    def dp(self, bits):
        at = self.d
        if bits & CORE:
            at = at + (1 - 2 * self.core)
        if bits & XBIT:
            at = at + (2 - 4 * self.x)
        if bits & YBIT:
            at = at + (4 - 8 * self.y)
        return at

    def up(self, step):
        return lax.rem(self.z + step, 4) if step else self.z


def push(src, dst, send, recv, dp, z):
    return pltpu.make_async_remote_copy(
        src_ref=src,
        dst_ref=dst,
        send_sem=send,
        recv_sem=recv,
        device_id=(dp, z),
        device_id_type=MESH,
    )


def settle(ref, sem):
    pltpu.make_async_copy(ref, ref, sem).wait()


def greet(partners):
    barrier = pltpu.get_barrier_semaphore()
    for partner in partners:
        pl.semaphore_signal(barrier, inc=1, device_id=partner, device_id_type=MESH)
    pl.semaphore_wait(barrier, len(partners))


GATHER = (
    (0, 0, XBIT),
    (0, 1, YBIT),
    (0, 0, YBIT),
    (0, 1, XBIT),
    (XBIT, 0, YBIT),
    (YBIT, 1, XBIT),
    (0, 0, CORE),
    (0, 1, CORE),
    (XBIT, 0, CORE),
    (YBIT, 1, CORE),
    (YBIT, 0, CORE),
    (XBIT, 1, CORE),
    (XBIT | YBIT, 0, CORE),
    (XBIT | YBIT, 1, CORE),
)


class Gather:
    def __init__(self, place, dst, own, send, recv):
        self.place, self.dst, self.own = place, dst, own
        self.send, self.recv = send, recv
        self.half = dst.shape[1] // 16

    def region(self, owner, half):
        at = self.place.dp(owner) * (2 * self.half) + half * self.half
        return self.dst.at[:, pl.ds(pl.multiple_of(at, 16), self.half), :]

    def copy(self, i):
        owner, half, to = GATHER[i]
        src = self.region(owner, half)
        if owner == 0 and self.own is not None:
            src = self.own.at[:, half * self.half : (half + 1) * self.half, :]
        place = self.place
        return push(
            src, self.region(owner, half), self.send.at[i], self.recv.at[i], place.dp(to), place.z
        )

    def start(self, *which):
        for i in which:
            self.copy(i).start()

    def wait(self, received, sent):
        for i in received:
            self.copy(i).wait_recv()
        for i in sent:
            self.copy(i).wait_send()

    def after(self, arrived, started):
        for i, more in zip(arrived, started):
            self.copy(i).wait_recv()
            for j in more:
                self.copy(j).start()

    def middle(self):
        self.after((0, 1), ((4, 8), (5, 9)))

    def last(self):
        self.after((2, 3, 4, 5), ((10,), (11,), (12,), (13,)))


def chip_bits(j):
    return (XBIT if j & 1 else 0) | (YBIT if j & 2 else 0)


def add_into(dst, src):
    def run(i, carry):
        at = pl.ds(pl.multiple_of(i * 16, 16), 16)
        dst[:, at, :] = (dst[:, at, :].astype(F32) + src[:, at, :].astype(F32)).astype(BF)
        return carry

    lax.fori_loop(0, dst.shape[1] // 16, run, 0)


class Reduce:
    def __init__(self, place, sources, scratch, out):
        self.place, self.sources, self.out = place, sources, out
        self.total, self.pair, self.near, self.far, self.quarter, self.stage = scratch[:6]
        self.pair_send, self.pair_recv, self.load, self.send, self.recv, self.z_send, self.z_recv = scratch[6:]
        self.rows = self.total.shape[2]

    @staticmethod
    def scratch(count, n, rows, cols):
        part = cols // 4
        dma = lambda k: pltpu.SemaphoreType.DMA((k,))
        return [
            pltpu.VMEM((n, 4, rows, cols), BF),
            pltpu.VMEM((n, 4, rows, cols), BF),
            pltpu.VMEM((n, 2, 2, rows // 2, cols), BF),
            pltpu.VMEM((n, 2, rows // 2, cols), BF),
            pltpu.VMEM((4, n, rows, part), BF),
            pltpu.VMEM((4, n, rows, part) if part % 128 else (8, 128), BF),
            dma(4 * count),
            dma(4 * count),
            dma(4 * count),
            dma(6),
            dma(6),
            dma(3),
            dma(1),
        ]

    def pair_copies(self, j):
        place, rows = self.place, self.rows
        copies, at = [], 0
        for i, src in enumerate(self.sources):
            slot, n = len(self.sources) * j + i, src.shape[0]
            block = lambda bits: src.at[:, pl.ds(pl.multiple_of(place.dp(bits) * rows, 16), rows), :]
            remote = push(
                block(chip_bits(j) | CORE),
                self.pair.at[at : at + n, j],
                self.pair_send.at[slot],
                self.pair_recv.at[slot],
                place.dp(CORE),
                place.z,
            )
            local = pltpu.make_async_copy(
                block(chip_bits(j)), self.total.at[at : at + n, j], self.load.at[slot]
            )
            copies.append((remote, local))
            at += n
        return copies

    def half(self, j, h):
        size = self.rows // 2
        return self.total.at[:, j, h * size : (h + 1) * size, :]

    MOVES = ((3, 0, XBIT, 1), (3, 1, YBIT, 1), (1, 0, XBIT, 0), (2, 1, YBIT, 0), (2, 0, YBIT, 0), (1, 1, XBIT, 1))

    def move(self, i):
        j, h, to, where = self.MOVES[i]
        dst = self.near.at[:, h, where] if i < 4 else self.far.at[:, where]
        place = self.place
        return push(self.half(j, h), dst, self.send.at[i], self.recv.at[i], place.dp(to), place.z)

    def z_copy(self, k):
        place, part = self.place, self.quarter.shape[3]
        to = place.up(k)
        if part % 128:
            src = self.stage.at[to]
        else:
            src = self.total.at[:, 0, :, pl.ds(pl.multiple_of(to * part, 128), part)]
        dst = self.quarter.at[place.z]
        if k == 0:
            return pltpu.make_async_copy(src, dst, self.z_recv.at[0])
        return push(src, dst, self.z_send.at[k - 1], self.z_recv.at[0], place.d, to)

    def begin(self):
        for j in (3, 1, 2, 0):
            for remote, local in self.pair_copies(j):
                remote.start()
                local.start()

    def pairs(self):
        for j, moves in ((3, (0, 1)), (1, (2,)), (2, (3,)), (0, ())):
            for remote, local in self.pair_copies(j):
                local.wait()
                remote.wait_recv()
            add_into(self.total.at[:, j], self.pair.at[:, j])
            for i in moves:
                self.move(i).start()

    def middle(self):
        for i, j, h, where, more in ((0, 2, 0, 1, 4), (1, 1, 1, 1, 5), (2, 0, 0, 0, None), (3, 0, 1, 0, None)):
            self.move(i).wait_recv()
            add_into(self.half(j, h), self.near.at[:, h, where])
            if more is not None:
                self.move(more).start()

    def late(self):
        for i, h in ((4, 0), (5, 1)):
            self.move(i).wait_recv()
            add_into(self.half(0, h), self.far.at[:, h])
        part = self.quarter.shape[3]
        if part % 128:
            for k in range(4):
                for m in range(self.total.shape[0]):
                    self.stage[k, m] = self.total[m, 0, :, k * part : (k + 1) * part]
        for k in (2, 1, 3, 0):
            self.z_copy(k).start()

    def end(self):
        settle(self.quarter, self.z_recv.at[0])
        parts = [self.quarter[k].astype(F32) for k in range(4)]
        self.out[...] = (parts[0] + parts[1]) + (parts[2] + parts[3])
        for j in range(4):
            for remote, _ in self.pair_copies(j):
                remote.wait_send()
        for i in range(6):
            self.move(i).wait_send()
        for k in range(1, 4):
            self.z_copy(k).wait_send()


class Homeward:
    def __init__(self, place, src, home, send, recv):
        self.place, self.src, self.home, self.send, self.recv = place, src, home, send, recv
        self.part = home.shape[2]

    def act(self, what):
        place, part = self.place, self.part
        for k in (2, 1, 3, 0):
            to, dp = place.up(k), place.d - place.core + lax.div(place.z, 2)
            src = self.src.at[pl.ds(pl.multiple_of(to * part, 16), part), :]
            dst = self.home.at[place.core, lax.rem(place.z, 2)]
            here = jnp.logical_and(dp == place.d, to == place.z)
            remote = push(src, dst, self.send.at[k], self.recv, dp, to)
            if what == "start":
                pl.when(here)(pltpu.make_async_copy(src, dst, self.recv).start)
                pl.when(jnp.logical_not(here))(remote.start)
            else:
                pl.when(jnp.logical_not(here))(remote.wait_send)

    def start(self):
        self.act("start")

    def end(self):
        settle(self.home, self.recv)
        self.act("wait")


def pair_and_z(place):
    return [(place.dp(r), place.up(k)) for k in range(4) for r in (0, CORE) if r or k]


def near_partners(place):
    return pair_and_z(place) + [(place.dp(r), place.z) for r in (XBIT, YBIT)]


INPUTS = 11


def finish_kernel(*refs):
    hbm, (go_ref, small_ref) = refs[:INPUTS], refs[INPUTS : INPUTS + 2]
    grads_ref, home_ref, sums_ref = refs[INPUTS + 2 : INPUTS + 5]
    refs = refs[INPUTS + 5 :]
    held, refs = refs[:INPUTS], refs[INPUTS:]
    loads, g_ref, base, ctx, partner, stream, slots, part_sum, chips = refs[:9]
    home_send, slot_send, chip_send, one_send, recv = refs[9:14]
    refs = refs[14:]
    count = len(refs) // 5
    place = Place()
    d, z, core = place.d, place.z, place.core
    copies = [pltpu.make_async_copy(a, b, loads.at[i]) for i, (a, b) in enumerate(zip(hbm, held))]
    for copy in copies:
        copy.start()

    def need(*which):
        for i in which:
            copies[i].wait()
        return [held[i] for i in which]

    greet(near_partners(place) + [(place.dp(XBIT | YBIT), z)])
    sources = [g_ref.at[m : m + 1] for m in range(4)] + [go_ref]
    key, value, query, pos, out = [
        Reduce(place, (src,), refs[m * count : (m + 1) * count], grads_ref.at[m : m + 1])
        for m, src in enumerate(sources)
    ]
    out.begin()
    slot_copies = []
    others = [(r, k) for k in range(4) for r in (0, CORE) if r or k]
    for i, (r, k) in enumerate(others):
        copy = push(small_ref, slots.at[4 * core + z], slot_send.at[i], recv.at[1], place.dp(r), place.up(k))
        copy.start()
        slot_copies.append(copy)
    pltpu.make_async_copy(small_ref, slots.at[4 * core + z], recv.at[1]).start()

    width, block = g_ref.shape[1], 256

    def product(m, left, right, dot):
        def run(i, carry):
            at = pl.ds(pl.multiple_of(i * block, block), block)
            g_ref[m, at, :] = dot(left[at, :], right[...]).astype(BF)
            return carry

        lax.fori_loop(0, width // block, run, 0)

    x_t, d_proj = need(0, 1)
    product(2, x_t, d_proj, nn)
    query.begin()
    ctx_t, dk_t = need(2, 3)
    product(0, ctx_t, dk_t, nt)
    key.begin()
    out.pairs()

    dv_t, w_key, w_value, w_query, d_mixed = need(4, 5, 6, 7, 8)
    back = dk_t.shape[1] - base.shape[0]

    def from_context(i, carry):
        at = pl.ds(pl.multiple_of(i * block, block), block)
        cols = pl.ds(pl.multiple_of(i * block + back, block), block)
        turned = nn(w_key[...], dk_t[:, cols]) + nn(w_value[...], dv_t[:, cols])
        turned = jnp.transpose(turned)
        base[at, :] = turned
        ctx[at, :] = turned.astype(BF)
        return carry

    lax.fori_loop(0, base.shape[0] // block, from_context, 0)
    swap = push(ctx, partner, one_send.at[0], recv.at[0], place.dp(CORE), z)
    swap.start()

    def from_proj(i, carry):
        at = pl.ds(pl.multiple_of(i * block, block), block)
        own = d_mixed[at, :] + nt(d_proj[at, :], w_query[...])
        base[at, :] = own + jnp.where(core == 0, base[at, :], 0.0)
        return carry

    lax.fori_loop(0, base.shape[0] // block, from_proj, 0)
    query.pairs()
    product(1, ctx_t, dv_t, nt)
    value.begin()
    key.pairs()

    swap.wait()
    small_block = 64

    def add_partner(i, carry):
        at = pl.ds(pl.multiple_of(i * small_block, small_block), small_block)
        more = jnp.where(core == 0, partner[at, :].astype(F32), 0.0)
        stream[at, :] = (base[at, :] + more).astype(BF)
        return carry

    lax.fori_loop(0, stream.shape[0] // small_block, add_partner, 0)
    home = Homeward(place, stream, home_ref, home_send, recv.at[2])
    home.start()
    out.middle()

    table_t, dr_t = need(9, 10)
    product(3, table_t, dr_t, nt)
    pos.begin()
    value.pairs()
    query.middle()
    out.late()

    settle(slots, recv.at[1])
    total = slots[0]
    for i in range(1, 8):
        total = total + slots[i]
    part_sum[...] = total
    chip = lax.div(d, 2)
    chip_copies = []
    for i, r in enumerate((XBIT, YBIT, XBIT | YBIT)):
        copy = push(part_sum, chips.at[chip], chip_send.at[i], recv.at[3], place.dp(r), z)
        copy.start()
        chip_copies.append(copy)
    pltpu.make_async_copy(part_sum, chips.at[chip], recv.at[3]).start()

    pos.pairs()
    key.middle()
    query.late()
    value.middle()
    key.late()
    pos.middle()
    value.late()
    settle(chips, recv.at[3])
    sums_ref[...] = (chips[0] + chips[1]) + (chips[2] + chips[3])
    pos.late()
    for reduce in (out, query, key, value, pos):
        reduce.end()
    home.end()
    for copy in slot_copies + chip_copies:
        copy.wait_send()


def finish(arrays, g_out, small):
    x_t, d_proj = arrays[:2]
    width, total = x_t.shape
    rows = width // 8
    vmem = pl.BlockSpec(memory_space=pltpu.VMEM)
    dma = lambda k: pltpu.SemaphoreType.DMA((k,))
    scratch = [pltpu.VMEM(a.shape, a.dtype) for a in arrays] + [
        dma(INPUTS),
        pltpu.VMEM((4, width, width), BF),
        pltpu.VMEM((total, width), F32),
        pltpu.VMEM((total, width), BF),
        pltpu.VMEM((total, width), BF),
        pltpu.VMEM((total, width), BF),
        pltpu.VMEM((8,) + small.shape, F32),
        pltpu.VMEM(small.shape, F32),
        pltpu.VMEM((4,) + small.shape, F32),
        dma(4),
        dma(7),
        dma(3),
        dma(1),
        dma(4),
    ]
    for _ in range(5):
        scratch += Reduce.scratch(1, 1, rows, width)
    return pl.pallas_call(
        finish_kernel,
        in_specs=[ANY_SPEC] * (INPUTS + 1) + [vmem],
        out_specs=[vmem, ANY_SPEC, vmem],
        out_shape=[
            jax.ShapeDtypeStruct((5, rows, width // 4), F32),
            jax.ShapeDtypeStruct((2, 2, total // 4, width), BF),
            jax.ShapeDtypeStruct(small.shape, F32),
        ],
        scratch_shapes=scratch,
        compiler_params=pltpu.CompilerParams(
            collective_id=4, has_side_effects=True, vmem_limit_bytes=LIMIT
        ),
        cost_estimate=pl.CostEstimate(flops=20 << 30, bytes_accessed=64 << 20, transcendentals=0),
        name="finish",
    )(*arrays, g_out, small)


def pack(mat):
    half = mat.shape[0] // 2
    return jnp.concatenate([mat[:, :128], jnp.concatenate([mat[:half, 128:], mat[half:, 128:]], axis=1)], axis=0)


def unpack(packed):
    rows = packed.shape[0] * 2 // 3
    rest = packed[rows:, :]
    return jnp.concatenate([packed[:rows, :], jnp.concatenate([rest[:, :64], rest[:, 64:]], axis=0)], axis=1)


def exchange_kernel(slot_ref, content, query, memory, ints, *refs):
    mats, (upw, dnw) = refs[:5], refs[5:7]
    context, stream, all_ints, whole, out_slab, ud_slab = refs[7:13]
    (
        spread,
        picked,
        shards,
        slab,
        mat_send,
        mat_recv,
        ud_send,
        ud_recv,
        int_send,
        spread_send,
        pick_send,
        stream_send,
        pair_send,
        gather_send,
        gather_recv,
        recv,
    ) = refs[13:]
    place = Place()
    d, z, core = place.d, place.z, place.core
    up, down, far = place.up(1), place.up(3), place.up(2)
    part = query.shape[1]
    piece = spread.shape[1]
    blocks = part // piece // 2
    first = 4 * blocks
    greet([(place.dp(r), place.up(k)) for r in range(8) for k in range(4) if r or k])

    spread_copies = []
    for r in range(8):
        to = place.dp(r)
        src = memory.at[:, pl.ds(pl.multiple_of(to * piece, 16), piece), :]
        dst = spread.at[pl.ds(2 * d, 2)]
        if r == 0:
            pltpu.make_async_copy(src, dst, recv.at[0]).start()
        else:
            spread_copies.append(push(src, dst, spread_send.at[r - 1], recv.at[0], to, z))
            spread_copies[-1].start()

    for m, mat in enumerate(mats):
        shards[z, m] = pack(mat[...])
    cutoff = shards.shape[2] * 5 // 9

    def mat_copy(i):
        own = shards.at[z]
        low, high = shards.at[down, :, :cutoff], shards.at[up, :, cutoff:]
        src = (own, own, low, high)[i]
        return push(src, src, mat_send.at[i], mat_recv.at[i], d, (up, down, up, down)[i])

    mat_copy(0).start()
    mat_copy(1).start()
    int_copies = []
    for r in range(8):
        if r == 0:
            pltpu.make_async_copy(ints, all_ints.at[d], recv.at[2]).start()
        else:
            copy = push(ints, all_ints.at[d], int_send.at[r - 1], recv.at[2], place.dp(r), z)
            int_copies.append(copy)
            copy.start()

    def stream_copy(i, act):
        j, kind = i // 2, i % 2
        to, dp = 2 * core + j, d - core + kind
        if kind == 0:
            src, sem = content.at[j], recv.at[3]
            dst = context.at[pl.ds(first + blocks * z, blocks)]
        else:
            src, sem = query.at[j], recv.at[4]
            dst = stream.at[pl.ds(pl.multiple_of(z * part, 16), part), :]
        here = jnp.logical_and(dp == d, to == z)
        remote = push(src, dst, stream_send.at[i], sem, dp, to)
        if act == "start":
            pl.when(here)(pltpu.make_async_copy(src, dst, sem).start)
            pl.when(jnp.logical_not(here))(remote.start)
        else:
            pl.when(jnp.logical_not(here))(remote.wait_send)

    mat_copy(0).wait_recv()
    mat_copy(2).start()
    mat_copy(1).wait_recv()
    mat_copy(3).start()
    for i in range(4):
        stream_copy(i, "start")

    settle(spread, recv.at[0])
    for q in range(16):
        picked[q] = spread[slot_ref[q]]
    pick_copies = []
    for r in (YBIT | XBIT, XBIT, YBIT, 0):
        for k in range(4):
            to, lane = place.dp(r), place.up(k)
            src = picked.at[4 * lax.div(to, 2) + lane]
            dst = context.at[blocks * z + lax.div(d, 2), core]
            if r or k:
                copy = push(src, dst, pick_send.at[2 * r + k - 1], recv.at[5], to, lane)
                pick_copies.append(copy)
            else:
                copy = pltpu.make_async_copy(src, dst, recv.at[5])
            copy.start()

    mat_copy(2).wait_recv()
    mat_copy(3).wait_recv()
    for m in range(5):
        slab[m] = jnp.concatenate([unpack(shards[k, m]) for k in range(4)], axis=1)
    rows = slab.shape[1]
    own_rows = pl.ds(pl.multiple_of(d * rows, 16), rows)
    gather = Gather(place, whole, slab.at[0:4], gather_send, gather_recv)
    gather.start(0, 1, 2, 3, 6, 7)
    pltpu.make_async_copy(slab.at[0:4], whole.at[:, own_rows, :], recv.at[6]).start()
    pltpu.make_async_copy(slab.at[4:5], out_slab, recv.at[7]).start()

    width = upw.shape[1]

    def columns(at, rows=slice(None)):
        return ud_slab.at[:, rows, pl.ds(pl.multiple_of(at * width, 128), width)]

    def ud_copy(i):
        if i < 4:
            src, dst = (upw, dnw)[i % 2], columns(z).at[i % 2]
            return push(src, dst, ud_send.at[i], ud_recv.at[i // 2], d, (up, down)[i // 2])
        half = rows // 2
        src = columns(down, slice(0, half)) if i == 4 else columns(up, slice(half, rows))
        return push(src, src, ud_send.at[i], ud_recv.at[i - 2], d, (up, down)[i - 4])

    for i in range(4):
        ud_copy(i).start()
    for m, mat in enumerate((upw, dnw)):
        pltpu.make_async_copy(mat, columns(z).at[m], recv.at[8]).start()

    pick_pair = push(
        context.at[0:first, core], context.at[0:first, core], pair_send.at[0], recv.at[1], place.dp(CORE), z
    )
    settle(context.at[0:first, core], recv.at[5])
    pick_pair.start()
    gather.middle()
    settle(columns(down), ud_recv.at[0])
    ud_copy(4).start()
    settle(columns(up), ud_recv.at[1])
    ud_copy(5).start()

    lead_copy = push(
        context.at[first:], context.at[first:], pair_send.at[1], recv.at[3], place.dp(CORE), z
    )

    @pl.when(core == 0)
    def _():
        settle(context.at[first:], recv.at[3])
        lead_copy.start()

    gather.last()
    gather.wait(range(6, 14), range(14))
    settle(whole.at[:, own_rows, :], recv.at[6])
    settle(out_slab, recv.at[7])
    settle(columns(z), recv.at[8])
    ud_copy(4).wait_recv()
    ud_copy(5).wait_recv()
    settle(all_ints, recv.at[2])
    pick_pair.wait()

    @pl.when(core == 0)
    def _():
        lead_copy.wait_send()

    @pl.when(core == 1)
    def _():
        settle(context.at[first:], recv.at[3])
        settle(stream, recv.at[4])

    for i in range(4):
        stream_copy(i, "wait")
        mat_copy(i).wait_send()
    for i in range(6):
        ud_copy(i).wait_send()
    for copy in spread_copies + int_copies + pick_copies:
        copy.wait_send()


def exchange(slot_of, content, query, memory, ints, mats, upw, dnw):
    micro, part, width = content.shape
    rows = mats[0].shape[0]
    inner = upw.shape[1] * 4
    piece = part // 8
    vmem = pl.BlockSpec(memory_space=pltpu.VMEM)
    dma = lambda n: pltpu.SemaphoreType.DMA((n,))
    context, *rest = pl.pallas_call(
        exchange_kernel,
        in_specs=[SMEM_SPEC] + [ANY_SPEC] * 3 + [vmem] * 8,
        out_specs=[ANY_SPEC] * 6,
        out_shape=[
            jax.ShapeDtypeStruct((32, 2, piece, width), BF),
            jax.ShapeDtypeStruct((4 * part, width), BF),
            jax.ShapeDtypeStruct((8,) + ints.shape, jnp.int32),
            jax.ShapeDtypeStruct((4, 8 * rows, width), BF),
            jax.ShapeDtypeStruct((1, rows, width), BF),
            jax.ShapeDtypeStruct((2, rows, inner), BF),
        ],
        scratch_shapes=[
            pltpu.VMEM((16, piece, width), BF),
            pltpu.VMEM((16, piece, width), BF),
            pltpu.VMEM((4, 5, rows * 3 // 2, 128), BF),
            pltpu.VMEM((5, rows, width), BF),
            dma(4),
            dma(4),
            dma(6),
            dma(4),
            dma(7),
            dma(7),
            dma(15),
            dma(4),
            dma(2),
            dma(14),
            dma(14),
            dma(9),
        ],
        compiler_params=pltpu.CompilerParams(
            collective_id=1, has_side_effects=True, vmem_limit_bytes=LIMIT
        ),
        cost_estimate=pl.CostEstimate(flops=0, bytes_accessed=64 << 20, transcendentals=0),
        name="exchange",
    )(slot_of, content.reshape(micro, 4, 2, piece, width), query, memory, ints, *mats, upw, dnw)
    return [context.reshape(8 * part, width)] + rest


def head_lanes(array, head):
    lane = lax.broadcasted_iota(jnp.int32, array.shape, 1)
    return jnp.where((lane >= DH) == (head == 1), array, jnp.zeros_like(array))


def attend_forward_step(
    block, qw_ref, qp_ref, k_ref, v_ref, rel_ref, thr_ref, kr_ref, vec_ref, prob_ref
):
    rows, klen = qw_ref.shape[0], k_ref.shape[0]
    width = klen + block
    keys, values = k_ref[...], v_ref[...]
    for part in range(rows // block):
        at = slice(part * block, (part + 1) * block)
        first = rows - (part + 1) * block
        qw, qp = qw_ref[at, :], qp_ref[at, :]
        rel = rel_ref[first : first + width, :]
        seen = kr_ref[...] < thr_ref[at, :]
        vecs = []
        for head in range(2):
            raw = nt(head_lanes(qp, head), rel)
            moved = pltpu.roll(raw, 0, 1, stride=1, stride_axis=0)[:, block:]
            score = nt(head_lanes(qw, head), keys) + moved
            score = jnp.where(seen, score, -1e30)
            expo = jnp.exp(score - jnp.max(score, axis=1, keepdims=True))
            prob = (expo * (1.0 / jnp.sum(expo, axis=1, keepdims=True))).astype(BF)
            prob_ref[head, at, :] = prob
            vecs.append(nn(prob, values))
        lane = lax.broadcasted_iota(jnp.int32, vecs[0].shape, 1)
        vec_ref[at, :] = jnp.where(lane < DH, vecs[0], vecs[1]).astype(BF)


def attend_forward_kernel(block, wired, *refs):
    if not wired:
        attend_forward_step(block, *refs)
        return
    ins, (ctan, qtan) = refs[:7], refs[9:11]
    outs, (wo, ud, tangent) = refs[11:13], refs[13:16]
    out_send, out_recv, ud_send, ud_recv, tan_send, recv = refs[16:]
    step, steps = pl.program_id(0), pl.num_programs(0)
    place = Place()
    d, z, core = place.d, place.z, place.core
    gathers = (
        Gather(place, ud, None, ud_send, ud_recv),
        Gather(place, wo, None, out_send, out_recv),
    )
    part = ctan.shape[1]

    def tan_copy(i, act):
        j, kind = i // 2, i % 2
        to, dp = 2 * core + j, d - core + kind
        src = (ctan, qtan)[kind].at[j]
        dst = tangent.at[pl.ds(pl.multiple_of(z * part, 16), part), :]
        here = jnp.logical_and(dp == d, to == z)
        local = pltpu.make_async_copy(src, dst, recv.at[0])
        remote = push(src, dst, tan_send.at[i], recv.at[0], dp, to)
        if act == "start":
            pl.when(here)(local.start)
            pl.when(jnp.logical_not(here))(remote.start)
        else:
            pl.when(jnp.logical_not(here))(remote.wait_send)

    @pl.when(step == 0)
    def _():
        greet(near_partners(place))
        for gather in gathers:
            gather.start(2, 3, 4, 5, 8, 9)
        for i in range(4):
            tan_copy(i, "start")

    attend_forward_step(block, *ins, *outs)

    @pl.when(step == steps - 1)
    def _():
        for gather in gathers:
            gather.last()
        for gather in gathers:
            gather.wait(range(8, 14), (2, 3, 4, 5) + tuple(range(8, 14)))
        settle(tangent, recv.at[0])
        for i in range(4):
            tan_copy(i, "wait")


def attend_forward(qw, qp, keys, values, rel, thr, key_rank, block, wires=()):
    rows, width = qw.shape
    klen, span = keys.shape[0], rel.shape[0]
    col = lambda count: pl.BlockSpec((count, PAIR), lambda p: (0, p))
    in_specs = [
        col(rows),
        col(rows),
        col(klen),
        col(klen),
        col(span),
        pl.BlockSpec((rows, 1), lambda p: (0, 0)),
        pl.BlockSpec((1, klen), lambda p: (0, 0)),
    ]
    out_specs = [col(rows), pl.BlockSpec((2, rows, klen), lambda p: (p, 0, 0))]
    out_shape = [
        jax.ShapeDtypeStruct((rows, width), BF),
        jax.ShapeDtypeStruct((width // DH, rows, klen), BF),
    ]
    params = dict(vmem_limit_bytes=LIMIT)
    scratch = []
    if wires:
        in_specs += [ANY_SPEC] * 4
        out_specs += [ANY_SPEC] * 3
        out_shape += [
            jax.ShapeDtypeStruct(wires[0].shape, BF),
            jax.ShapeDtypeStruct(wires[1].shape, BF),
            jax.ShapeDtypeStruct((rows, width), BF),
        ]
        scratch = [pltpu.SemaphoreType.DMA((n,)) for n in (14, 14, 14, 14, 4, 1)]
        params.update(collective_id=2, has_side_effects=True)
    return pl.pallas_call(
        functools.partial(attend_forward_kernel, block, bool(wires)),
        grid=(width // PAIR,),
        in_specs=in_specs,
        out_specs=out_specs,
        out_shape=out_shape,
        scratch_shapes=scratch,
        input_output_aliases={7: 2, 8: 3} if wires else {},
        compiler_params=pltpu.CompilerParams(**params),
        cost_estimate=pl.CostEstimate(
            flops=8 * rows * klen * width, bytes_accessed=16 << 20, transcendentals=12 * rows * klen
        ),
        name="attend_forward",
    )(qw, qp, keys, values, rel, thr, key_rank, *wires)


def attend_backward_kernel(block, wired, *refs):
    if not wired:
        attend_backward_step(block, *refs)
        return
    ins, (g_ud, src) = refs[:7], refs[7:9]
    outs, (grads_ref, home_ref) = refs[9:14], refs[14:16]
    rel_acc, home_send, home_recv = refs[16:19]
    step, steps = pl.program_id(0), pl.num_programs(0)
    place = Place()
    count = len(refs[19:]) // 2
    reduces = [
        Reduce(place, (g_ud.at[m : m + 1],), refs[19 + m * count : 19 + (m + 1) * count], grads_ref.at[m : m + 1])
        for m in range(2)
    ]
    home = Homeward(place, src, home_ref, home_send, home_recv.at[0])

    @pl.when(step == 0)
    def _():
        greet(near_partners(place))
        for reduce in reduces:
            reduce.begin()
        home.start()

    @pl.when(step == 2)
    def _():
        reduces[0].pairs()

    @pl.when(step == 3)
    def _():
        reduces[1].pairs()

    @pl.when(step == 5)
    def _():
        reduces[0].middle()

    attend_backward_step(block, *ins, *outs, rel_acc)

    @pl.when(step == steps - 1)
    def _():
        reduces[0].late()
        reduces[1].middle()
        reduces[1].late()
        reduces[0].end()
        reduces[1].end()
        home.end()


def attend_backward_step(
    block,
    prob_ref,
    gvec_ref,
    qw_ref,
    qp_ref,
    k_ref,
    v_ref,
    rel_ref,
    dproj_ref,
    dk_ref,
    dv_ref,
    drel_ref,
    bias_ref,
    rel_acc,
):
    rows, klen = qw_ref.shape[0], k_ref.shape[0]
    width = klen + block
    keys, values = k_ref[...], v_ref[...]
    row = lax.broadcasted_iota(jnp.int32, (block, block), 0)
    col = lax.broadcasted_iota(jnp.int32, (block, block), 1)
    mirror = (row + col == block - 1).astype(BF)
    rel_acc[...] = jnp.zeros_like(rel_acc)
    d_keys, d_values = [None, None], [None, None]
    word_sum = jnp.zeros((1, PAIR), F32)
    pos_sum = jnp.zeros((1, PAIR), F32)
    for part in range(rows // block):
        at = slice(part * block, (part + 1) * block)
        first = rows - (part + 1) * block
        gvec, qw = gvec_ref[at, :], qw_ref[at, :]
        gvec_t = jnp.transpose(gvec.astype(F32)).astype(BF)
        qw_t = jnp.transpose(qw.astype(F32)).astype(BF)
        qp_t = jnp.transpose(nn(mirror, qp_ref[at, :])).astype(BF)
        rel = rel_ref[first : first + width, :]
        word_parts, pos_parts = [], []
        for head in range(2):
            own = slice(head * DH, (head + 1) * DH)
            prob = prob_ref[head, at, :]
            d_prob = nt(head_lanes(gvec, head), values)
            weight = prob.astype(F32)
            inner = jnp.sum(weight * d_prob, axis=1, keepdims=True)
            g_sum = (weight * (d_prob - inner) * 0.125).astype(BF)
            dv = nn(gvec_t[own, :], prob)
            dk = nn(qw_t[own, :], g_sum)
            d_values[head] = dv if part == 0 else d_values[head] + dv
            d_keys[head] = dk if part == 0 else d_keys[head] + dk
            turned = nn(mirror, g_sum)
            padded = jnp.concatenate([jnp.zeros((block, block), F32), turned], axis=1)
            moved = pltpu.roll(padded, width - block + 1, 1, stride=1, stride_axis=0).astype(BF)
            word_parts.append(nn(turned.astype(BF), keys))
            pos_parts.append(nn(moved, rel))
            rel_acc[own, first : first + width] += nn(qp_t[own, :], moved)
        lane = lax.broadcasted_iota(jnp.int32, word_parts[0].shape, 1)
        word = jnp.where(lane < DH, word_parts[0], word_parts[1])
        pos = jnp.where(lane < DH, pos_parts[0], pos_parts[1])
        word_sum = word_sum + jnp.sum(word, axis=0, keepdims=True)
        pos_sum = pos_sum + jnp.sum(pos, axis=0, keepdims=True)
        dproj_ref[at, :] = nn(mirror, (word + pos).astype(BF)).astype(BF)
    for head in range(2):
        own = slice(head * DH, (head + 1) * DH)
        dv_ref[own, :] = d_values[head].astype(BF)
        dk_ref[own, :] = (8.0 * d_keys[head]).astype(BF)
    drel_ref[...] = (8.0 * rel_acc[...]).astype(BF)
    bias_ref[0:1, :] = word_sum
    bias_ref[1:2, :] = pos_sum


def attend_backward(prob, gvec, qw, qp, keys, values, rel, block, wires=()):
    rows, width = qw.shape
    klen, span = keys.shape[0], rel.shape[0]
    col = lambda count: pl.BlockSpec((count, PAIR), lambda p: (0, p))
    rowb = lambda count: pl.BlockSpec((PAIR, count), lambda p: (p, 0))
    in_specs = [
        pl.BlockSpec((2, rows, klen), lambda p: (p, 0, 0)),
        col(rows),
        col(rows),
        col(rows),
        col(klen),
        col(klen),
        col(span),
    ]
    out_specs = [col(rows), rowb(klen), rowb(klen), rowb(span), col(2)]
    out_shape = [
        jax.ShapeDtypeStruct((rows, width), BF),
        jax.ShapeDtypeStruct((width, klen), BF),
        jax.ShapeDtypeStruct((width, klen), BF),
        jax.ShapeDtypeStruct((width, span), BF),
        jax.ShapeDtypeStruct((2, width), F32),
    ]
    scratch = [pltpu.VMEM((PAIR, span), F32)]
    params = dict(vmem_limit_bytes=LIMIT)
    if wires:
        inner, mine = wires[0].shape[2], width // 8
        in_specs += [ANY_SPEC, ANY_SPEC]
        out_specs += [pl.BlockSpec(memory_space=pltpu.VMEM), ANY_SPEC]
        out_shape += [
            jax.ShapeDtypeStruct((2, mine, inner // 4), F32),
            jax.ShapeDtypeStruct((2, 2, rows // 4, width), BF),
        ]
        scratch += [pltpu.SemaphoreType.DMA((4,)), pltpu.SemaphoreType.DMA((1,))]
        scratch += 2 * Reduce.scratch(1, 1, mine, inner)
        params.update(collective_id=3, has_side_effects=True)
    return pl.pallas_call(
        functools.partial(attend_backward_kernel, block, bool(wires)),
        grid=(width // PAIR,),
        in_specs=in_specs,
        out_specs=out_specs,
        out_shape=out_shape,
        scratch_shapes=scratch,
        compiler_params=pltpu.CompilerParams(**params),
        cost_estimate=pl.CostEstimate(
            flops=16 * rows * klen * width, bytes_accessed=20 << 20, transcendentals=0
        ),
        name="attend_backward",
    )(prob, gvec, qw, qp, keys, values, rel, *wires)


def norm_parts(value):
    center = value - jnp.mean(value, axis=1, keepdims=True)
    scale = lax.rsqrt(jnp.mean(center * center, axis=1, keepdims=True) + EPS)
    return center * scale, scale


def norm_pull(normed, scale, err):
    inner = jnp.mean(err * normed, axis=1, keepdims=True)
    return (err - jnp.mean(err, axis=1, keepdims=True) - normed * inner) * scale


def sum_rows(value):
    return jnp.sum(value, axis=0, keepdims=True)


def feed_kernel(steps, *refs):
    (
        ud_hbm,
        wo_hbm,
        vec_ref,
        x_ref,
        tan_ref,
        upb_ref,
        dnb_ref,
        g1_ref,
        s1_ref,
        g2_ref,
        s2_ref,
        out_ref,
        dmix_ref,
        gvec_ref,
        go_ref,
        gud_ref,
        gupb_ref,
        small_ref,
        ud_ref,
        wo_ref,
        n1_ref,
        r1_ref,
        fb_ref,
        fbt_ref,
        acc_ref,
        act_ref,
        slope_ref,
        gd_ref,
        gdt_ref,
        sems,
    ) = refs
    step = pl.program_id(0)
    chunk = act_ref.shape[2]
    cols = pl.ds(pl.multiple_of(lax.rem(step, steps) * chunk, chunk), chunk)

    @pl.when(step == 0)
    def _():
        wo_copy = pltpu.make_async_copy(wo_hbm, wo_ref, sems.at[0])
        ud_copy = pltpu.make_async_copy(ud_hbm, ud_ref, sems.at[1])
        wo_copy.start()
        ud_copy.start()
        wo_copy.wait()
        normed, scale = norm_parts(nt(vec_ref[...], wo_ref[0]) + x_ref[...].astype(F32))
        n1_ref[...] = normed
        r1_ref[...] = scale
        first = normed * g1_ref[...] + s1_ref[...]
        fb_ref[...] = first.astype(BF)
        fbt_ref[...] = jnp.transpose(first).astype(BF)
        acc_ref[...] = first + dnb_ref[...]
        ud_copy.wait()

    @pl.when(step < steps)
    def _():
        upper = nn(fb_ref[...], ud_ref[0, :, cols]) + upb_ref[...]
        square = upper * upper
        root = 0.7978845608028654
        bend = jnp.tanh(root * (upper + 0.044715 * (square * upper)))
        half = 0.5 * (1.0 + bend)
        act = (upper * half).astype(BF)
        act_ref[step] = act
        slope_ref[step] = half + 0.5 * upper * (1.0 - bend * bend) * (
            root + (3 * 0.044715 * root) * square
        )
        acc_ref[...] += nt(act, ud_ref[1, :, cols])

    @pl.when(step == steps - 1)
    def _():
        normed, scale = norm_parts(acc_ref[...])
        out_ref[...] = (normed * g2_ref[...] + s2_ref[...]).astype(BF)
        tan = tan_ref[...].astype(F32)
        d_down = norm_pull(normed, scale, tan * g2_ref[...])
        small_ref[0:1, :] = sum_rows(d_down)
        small_ref[3:4, :] = sum_rows(tan * normed)
        small_ref[4:5, :] = sum_rows(tan)
        gd_ref[...] = d_down.astype(BF)
        gdt_ref[...] = jnp.transpose(d_down).astype(BF)
        acc_ref[...] = d_down

    @pl.when(step >= steps)
    def _():
        at = step - steps
        d_up = nn(gd_ref[...], ud_ref[1, :, cols]) * slope_ref[at]
        gupb_ref[...] = sum_rows(d_up)
        g_up = d_up.astype(BF)
        acc_ref[...] += nt(g_up, ud_ref[0, :, cols])
        gud_ref[0] = nn(fbt_ref[...], g_up).astype(BF)
        gud_ref[1] = nn(gdt_ref[...], act_ref[at]).astype(BF)

    @pl.when(step == 2 * steps - 1)
    def _():
        d_first, normed = acc_ref[...], n1_ref[...]
        small_ref[1:2, :] = sum_rows(d_first * normed)
        small_ref[2:3, :] = sum_rows(d_first)
        d_mixed = norm_pull(normed, r1_ref[...], d_first * g1_ref[...])
        dmix_ref[...] = d_mixed
        gvec_ref[...] = nn(d_mixed.astype(BF), wo_ref[0]).astype(BF)
        gdt_ref[...] = jnp.transpose(d_mixed).astype(BF)
        go_ref[...] = nn(gdt_ref[...], vec_ref[...]).astype(BF)


def feed(ud, wo, vec, x, tan, upb, dnb, g1, s1, g2, s2):
    rows, width = vec.shape
    inner = upb.shape[1]
    chunk = 512
    steps = inner // chunk
    whole = lambda a, b: pl.BlockSpec((a, b), lambda i: (0, 0))
    late = lambda i: jnp.maximum(i - steps, 0)
    grads = pl.BlockSpec((2, width, chunk), lambda i: (0, 0, late(i)))
    return pl.pallas_call(
        functools.partial(feed_kernel, steps),
        grid=(2 * steps,),
        in_specs=[ANY_SPEC] * 2
        + [whole(rows, width)] * 3
        + [pl.BlockSpec((1, chunk), lambda i: (0, lax.rem(i, steps)))]
        + [whole(1, width)] * 5,
        out_specs=[
            whole(rows, width),
            whole(rows, width),
            whole(rows, width),
            whole(width, width),
            grads,
            pl.BlockSpec((1, chunk), lambda i: (0, late(i))),
            whole(8, width),
        ],
        out_shape=[
            jax.ShapeDtypeStruct((rows, width), BF),
            jax.ShapeDtypeStruct((rows, width), F32),
            jax.ShapeDtypeStruct((rows, width), BF),
            jax.ShapeDtypeStruct((width, width), BF),
            jax.ShapeDtypeStruct((2, width, inner), BF),
            jax.ShapeDtypeStruct((1, inner), F32),
            jax.ShapeDtypeStruct((8, width), F32),
        ],
        scratch_shapes=[
            pltpu.VMEM((2, width, inner), BF),
            pltpu.VMEM((1, width, width), BF),
            pltpu.VMEM((rows, width), F32),
            pltpu.VMEM((rows, 1), F32),
            pltpu.VMEM((rows, width), BF),
            pltpu.VMEM((width, rows), BF),
            pltpu.VMEM((rows, width), F32),
            pltpu.VMEM((steps, rows, chunk), BF),
            pltpu.VMEM((steps, rows, chunk), F32),
            pltpu.VMEM((rows, width), BF),
            pltpu.VMEM((width, rows), BF),
            pltpu.SemaphoreType.DMA((2,)),
        ],
        compiler_params=pltpu.CompilerParams(vmem_limit_bytes=LIMIT),
        cost_estimate=pl.CostEstimate(
            flops=12 * rows * width * inner, bytes_accessed=36 << 20, transcendentals=rows * inner
        ),
        name="feed",
    )(ud, wo, vec, x, tan, upb, dnb, g1, s1, g2, s2)


def project_kernel(wired, *refs):
    if not wired:
        project_step(*refs)
        return
    ins, (out_slab, ud_slab) = refs[:6], refs[6:8]
    outs, (wo, ud) = refs[8:14], refs[14:16]
    out_send, out_recv, ud_send, ud_recv, own = refs[16:]
    place = Place()
    gathers = (
        Gather(place, ud, ud_slab, ud_send, ud_recv),
        Gather(place, wo, out_slab, out_send, out_recv),
    )
    rows = out_slab.shape[1]
    own_rows = pl.ds(pl.multiple_of(place.d * rows, 16), rows)
    locals_ = (
        pltpu.make_async_copy(ud_slab, ud.at[:, own_rows, :], own.at[0]),
        pltpu.make_async_copy(out_slab, wo.at[:, own_rows, :], own.at[1]),
    )
    greet([(place.dp(r), place.z) for r in (CORE, XBIT, YBIT)])
    for gather in gathers:
        gather.start(0, 1, 6, 7)
    for copy in locals_:
        copy.start()
    project_step(*ins, *outs)
    for gather in gathers:
        gather.wait((0, 1, 6, 7), (0, 1, 6, 7))
    for copy in locals_:
        copy.wait()


def project_step(
    w_ref, ctx_ref, q_ref, table_ref, wb_ref, pb_ref, k_ref, v_ref, rel_ref, qw_ref, qp_ref, x_ref
):
    lead = lax.rem(lax.axis_index("dp"), 2) == 0
    back = ctx_ref.shape[0] - q_ref.shape[0]
    block = 256

    def loop(count, step):
        def run(i, carry):
            step(pl.ds(pl.multiple_of(i * block, block), block))
            return carry

        lax.fori_loop(0, count // block, run, 0)

    def context_step(at):
        k_ref[at, :] = nn(ctx_ref[at, :], w_ref[0]).astype(BF)
        v_ref[at, :] = nn(ctx_ref[at, :], w_ref[1]).astype(BF)

    def stream_step(at):
        own = ctx_ref[pl.ds(pl.multiple_of(at.start + back, block), block), :]
        x_ref[at, :] = jnp.where(lead, own, q_ref[at, :])
        proj = nn(x_ref[at, :], w_ref[2])
        qw_ref[at, :] = (0.125 * (proj + wb_ref[...]).astype(BF).astype(F32)).astype(BF)
        qp_ref[at, :] = (0.125 * (proj + pb_ref[...]).astype(BF).astype(F32)).astype(BF)

    def table_step(at):
        rel_ref[at, :] = nn(table_ref[at, :], w_ref[3]).astype(BF)

    loop(table_ref.shape[0], table_step)
    loop(q_ref.shape[0], stream_step)
    loop(ctx_ref.shape[0], context_step)


def project(mats, context, query, table, wb, pb, wires=()):
    rows, width = query.shape
    klen, span = context.shape[0], table.shape[0]
    vmem = pl.BlockSpec(memory_space=pltpu.VMEM)
    out_shape = [
        jax.ShapeDtypeStruct((klen, width), BF),
        jax.ShapeDtypeStruct((klen, width), BF),
        jax.ShapeDtypeStruct((span, width), BF),
        jax.ShapeDtypeStruct((rows, width), BF),
        jax.ShapeDtypeStruct((rows, width), BF),
        jax.ShapeDtypeStruct((rows, width), BF),
    ]
    params = dict(vmem_limit_bytes=LIMIT)
    scratch = []
    if wires:
        params.update(collective_id=5, has_side_effects=True)
        scratch = [pltpu.SemaphoreType.DMA((n,)) for n in (14, 14, 14, 14, 2)]
        out_shape += [
            jax.ShapeDtypeStruct((slab.shape[0], width, slab.shape[2]), BF) for slab in wires
        ]
    return pl.pallas_call(
        functools.partial(project_kernel, bool(wires)),
        in_specs=[vmem] * (6 + len(wires)),
        out_specs=[vmem] * 6 + [ANY_SPEC] * len(wires),
        out_shape=out_shape,
        scratch_shapes=scratch,
        compiler_params=pltpu.CompilerParams(**params),
        cost_estimate=pl.CostEstimate(
            flops=2 * (2 * klen + rows + span) * width * width,
            bytes_accessed=20 << 20,
            transcendentals=0,
        ),
        name="project",
    )(mats, context, query, table, wb, pb, *wires)


def weight_grads_kernel(xt_ref, ct_ref, tt_ref, dp_ref, dk_ref, dv_ref, dr_ref, g_ref):
    g_ref[0] = nt(ct_ref[...], dk_ref[...]).astype(BF)
    g_ref[1] = nt(ct_ref[...], dv_ref[...]).astype(BF)
    g_ref[2] = nn(xt_ref[...], dp_ref[...]).astype(BF)
    g_ref[3] = nt(tt_ref[...], dr_ref[...]).astype(BF)


def weight_grads(x_t, ctx_t, table_t, d_proj, dk_t, dv_t, drel_t):
    width, rows = x_t.shape
    klen, span = ctx_t.shape[1], table_t.shape[1]
    chunk = 256
    whole = lambda a, b: pl.BlockSpec((a, b), lambda i: (0, 0))
    rowb = lambda b: pl.BlockSpec((chunk, b), lambda i: (i, 0))
    return pl.pallas_call(
        weight_grads_kernel,
        grid=(width // chunk,),
        in_specs=[
            whole(width, rows),
            whole(width, klen),
            whole(width, span),
            pl.BlockSpec((rows, chunk), lambda i: (0, i)),
            rowb(klen),
            rowb(klen),
            rowb(span),
        ],
        out_specs=pl.BlockSpec((4, width, chunk), lambda i: (0, 0, i)),
        out_shape=jax.ShapeDtypeStruct((4, width, width), BF),
        compiler_params=pltpu.CompilerParams(vmem_limit_bytes=LIMIT),
        cost_estimate=pl.CostEstimate(
            flops=2 * (rows + 2 * klen + span) * width * width,
            bytes_accessed=20 << 20,
            transcendentals=0,
        ),
        name="weight_grads",
    )(x_t, ctx_t, table_t, d_proj, dk_t, dv_t, drel_t)


def flip(arr, bit):
    return lax.ppermute(arr, "dp", [(i, i ^ bit) for i in range(lax.axis_size("dp"))])


def scatter_sum(grads):
    mine = lax.psum_scatter(grads, "dp", scatter_dimension=1, tiled=True)
    return lax.psum_scatter(mine, "tensor", scatter_dimension=2, tiled=True).astype(F32)


def body(
    content_stream,
    query_stream,
    memory,
    content_tangent,
    query_tangent,
    seq_lengths,
    factor_order,
    memory_lengths,
    slot_sequence,
    query_weight,
    key_weight,
    value_weight,
    pos_weight,
    out_weight,
    up_weight,
    up_bias,
    down_weight,
    down_bias,
    word_bias,
    pos_bias,
    first_gain,
    first_shift,
    second_gain,
    second_shift,
):
    groups, tensors = lax.axis_size("dp"), lax.axis_size("tensor")
    micro, part_len, width = content_stream.shape
    mem_part = memory.shape[1]
    seq_len, mem_total = part_len * tensors, mem_part * tensors
    klen, span = mem_total + seq_len, mem_total + 2 * seq_len
    count = micro * groups
    here, lane = lax.axis_index("dp"), lax.axis_index("tensor")
    core = here % 2
    lead = core == 0
    block = 256
    assert 2 * micro == tensors

    def swap(arr):
        return flip(arr, CORE)

    def to_unit(first, second):
        got = swap(jnp.where(lead, second, first))
        low = jnp.where(lead, first, got)
        high = jnp.where(lead, got, second)
        both = jnp.concatenate([low, high], 0)
        both = lax.all_to_all(both, "tensor", split_axis=0, concat_axis=0, tiled=True)
        return both.reshape(seq_len, width)

    def from_unit(arr):
        both = arr.reshape(tensors, part_len, width)
        both = lax.all_to_all(both, "tensor", split_axis=0, concat_axis=0, tiled=True)
        low, high = both[:micro], both[micro:]
        got = swap(jnp.where(lead, high, low))
        return jnp.where(lead, low, got), jnp.where(lead, got, high)

    seq_id = (here // 2) * tensors + lane
    ids = jnp.arange(count, dtype=jnp.int32)
    slot_of = jnp.sum(jnp.where(slot_sequence[None, :] == ids[:, None], ids[None, :], 0), axis=1)
    counts = jnp.concatenate([seq_lengths, memory_lengths])
    slot = slot_of[seq_id]
    mats = [key_weight, value_weight, query_weight, pos_weight, out_weight]
    table = jnp.asarray(reversed_table(span, klen, width))
    wires = ()
    if groups == 8:
        ints = jnp.pad(factor_order, ((0, 6), (0, 0)))
        ints = lax.dynamic_update_slice(ints, counts[None, :], (micro, 0))
        context, query, all_ints, weights, out_slab, ud_slab = exchange(
            slot_of, content_stream, query_stream, memory, ints, mats, up_weight, down_weight
        )
        wires = (out_slab, ud_slab)
        lengths = all_ints[:, micro, : 2 * micro]
        orders = all_ints[seq_id // micro, :micro]
    else:
        lengths = lax.all_gather(counts, "dp", axis=0, tiled=False)
        orders = lax.all_gather(factor_order, "dp", axis=0, tiled=False)[seq_id // micro]
        stream = to_unit(content_stream, query_stream)
        content, query = jnp.where(lead, stream, swap(stream)), stream
        tangent = to_unit(content_tangent, query_tangent)
        piece = mem_part // groups
        spread = lax.all_to_all(
            memory.reshape(micro, groups, piece, width), "dp", split_axis=1, concat_axis=1, tiled=True
        )
        spread = spread.transpose(1, 0, 2, 3).reshape(count, piece, width)
        spread = jnp.take(spread, slot_of, axis=0)
        spread = spread.reshape(groups // 2, tensors, 2, piece // 2, width).transpose(0, 2, 1, 3, 4)
        spread = lax.all_to_all(
            spread.reshape(groups, tensors, piece // 2, width),
            "dp",
            split_axis=0,
            concat_axis=0,
            tiled=True,
        )
        spread = lax.all_to_all(spread, "tensor", split_axis=1, concat_axis=1, tiled=True)
        got = swap(spread)
        mem_rows = jnp.stack([jnp.where(lead, spread, got), jnp.where(lead, got, spread)])
        mem_rows = mem_rows.transpose(2, 1, 0, 3, 4).reshape(mem_total, width)
        context = jnp.concatenate([mem_rows, content], 0)

        def whole(mat):
            mat = lax.all_gather(mat, "tensor", axis=1, tiled=True)
            return lax.all_gather(mat, "dp", axis=0, tiled=True)

        weights = jnp.stack([whole(mat) for mat in mats[:4]])
        wo = whole(out_weight)[None]
        ud = jnp.stack([whole(up_weight), whole(down_weight)])

    length = lengths[seq_id // micro, seq_id % micro]
    mem_valid = lengths[slot // micro, micro + slot % micro]
    rank = orders[seq_id % micro]
    key_pos = jnp.arange(klen, dtype=jnp.int32)
    hidden = jnp.int32(1 << 20)
    mem_rank = jnp.where(key_pos[:mem_total] >= mem_total - mem_valid, -1, hidden)
    own_rank = jnp.where(key_pos[:seq_len] < length, rank, hidden)
    key_rank = jnp.concatenate([mem_rank, own_rank])[None, :]
    thr = (rank + jnp.where(lead, 1, 0))[:, None]

    row = lambda v: v.reshape(1, -1)
    keys, values, rel, q_word, q_pos, stream, *wires = project(
        weights, context, query, table, row(word_bias), row(pos_bias), wires
    )
    if wires:
        wires += [content_tangent, query_tangent]
    vec, prob, *arrived = attend_forward(
        q_word, q_pos, keys, values, rel, thr, key_rank, block, wires
    )
    if wires:
        wo, ud, tangent = arrived
    out, d_mixed, g_vec, g_out, g_ud, g_upb, small = feed(
        ud,
        wo,
        vec,
        stream,
        tangent,
        row(up_bias),
        row(down_bias),
        row(first_gain),
        row(first_shift),
        row(second_gain),
        row(second_shift),
    )
    backward = (prob, g_vec, q_word, q_pos, keys, values, rel, block)
    if groups == 8:
        d_proj, dk_t, dv_t, drel_t, biases, (grad_up, grad_down), outs = attend_backward(
            *backward, (g_ud, out)
        )
        content_out, query_out = outs[0], outs[1]
    else:
        d_proj, dk_t, dv_t, drel_t, biases = attend_backward(*backward)
        content_out, query_out = from_unit(out)
        grad_up, grad_down = scatter_sum(g_ud)
    small = jnp.concatenate([g_upb.reshape(-1), small[:5].reshape(-1), biases.reshape(-1)])
    inner = up_bias.shape[0]
    stream_t, context_t, table_t = (jnp.transpose(a) for a in (stream, context, table))
    if groups == 8:
        size = small.shape[0]
        small = jnp.pad(small, (0, -size % 1024)).reshape(-1, 128)
        arrays = [stream_t, d_proj, context_t, dk_t, dv_t, weights[0], weights[1], weights[2]]
        arrays += [d_mixed, table_t, drel_t]
        grads, homes, small = finish(arrays, g_out[None], small)
        grad_key, grad_value, grad_query, grad_pos, grad_out = grads
        content_grad, query_grad = homes[0], homes[1]
        small = small.reshape(-1)[:size]
    else:
        d_context = tt(dk_t[:, mem_total:], weights[0]) + tt(dv_t[:, mem_total:], weights[1])
        partner = swap(d_context.astype(BF)).astype(F32)
        d_stream = d_mixed + nt(d_proj, weights[2]) + jnp.where(lead, d_context + partner, 0.0)
        content_grad, query_grad = from_unit(d_stream.astype(BF))
        grad_key, grad_value, grad_query, grad_pos = scatter_sum(
            weight_grads(stream_t, context_t, table_t, d_proj, dk_t, dv_t, drel_t)
        )
        (grad_out,) = scatter_sum(g_out[None])
        small = lax.psum(small, ("dp", "tensor"))
    rest = small[inner:].reshape(7, width)
    return (
        content_out,
        query_out,
        content_grad,
        query_grad,
        grad_query,
        grad_key,
        grad_value,
        grad_pos,
        grad_out,
        grad_up,
        small[:inner],
        grad_down,
        rest[0],
        rest[5].reshape(HEADS, DH),
        rest[6].reshape(HEADS, DH),
        rest[1],
        rest[2],
        rest[3],
        rest[4],
    )


def solution(mesh):
    rows = P("dp", "tensor", None)
    mat = P("dp", "tensor")
    return jax.shard_map(
        body,
        mesh=mesh,
        in_specs=(rows,) * 5
        + (P("dp"), P("dp", None), P("dp"), P())
        + (mat,) * 6
        + (P(), mat)
        + (P(),) * 7,
        out_specs=(rows,) * 4 + (mat,) * 6 + (P(), mat) + (P(),) * 7,
        check_vma=False,
    )
```

```python
import functools

import jax
import jax.numpy as jnp
import numpy as np
from jax import lax
from jax.experimental import pallas as pl
from jax.experimental.pallas import tpu as pltpu
from jax.sharding import PartitionSpec as P

HEADS = 12
DH = 64
PAIR = 2 * DH
EPS = 1e-06
BF = jnp.bfloat16
F32 = jnp.float32
LIMIT = 60 * 1024 * 1024
SMEM_SPEC = pl.BlockSpec(memory_space=pltpu.SMEM)
ANY_SPEC = pl.BlockSpec(memory_space=pl.ANY)


def nn(left, right):
    return jnp.dot(left, right, preferred_element_type=F32)


def nt(left, right):
    return lax.dot_general(left, right, (((1,), (1,)), ((), ())), preferred_element_type=F32)


def tn(left, right):
    return lax.dot_general(left, right, (((0,), (0,)), ((), ())), preferred_element_type=F32)


def tt(left, right):
    return lax.dot_general(left, right, (((0,), (1,)), ((), ())), preferred_element_type=F32)


def reversed_table(count, first, width):
    dist = (first - np.arange(count)).astype(np.float32)
    half = width // 2
    power = np.arange(half).astype(np.float32) * np.float32(2.0 / width)
    freq = np.float32(1.0) / np.float32(10000.0) ** power
    angle = (dist[:, None] * freq[None, :]).astype(np.float64)
    return np.concatenate([np.sin(angle), np.cos(angle)], axis=1).astype(np.float32).astype(BF)


MESH = pl.DeviceIdType.MESH
CORE, XBIT, YBIT = 1, 2, 4


class Place:
    def __init__(self):
        self.d, self.z = lax.axis_index("dp"), lax.axis_index("tensor")
        self.core = lax.rem(self.d, 2)
        self.x = lax.rem(lax.div(self.d, 2), 2)
        self.y = lax.div(self.d, 4)

    def dp(self, bits):
        at = self.d
        if bits & CORE:
            at = at + (1 - 2 * self.core)
        if bits & XBIT:
            at = at + (2 - 4 * self.x)
        if bits & YBIT:
            at = at + (4 - 8 * self.y)
        return at

    def up(self, step):
        return lax.rem(self.z + step, 4) if step else self.z


def push(src, dst, send, recv, dp, z):
    return pltpu.make_async_remote_copy(
        src_ref=src,
        dst_ref=dst,
        send_sem=send,
        recv_sem=recv,
        device_id=(dp, z),
        device_id_type=MESH,
    )


def settle(ref, sem):
    pltpu.make_async_copy(ref, ref, sem).wait()


def greet(partners):
    barrier = pltpu.get_barrier_semaphore()
    for partner in partners:
        pl.semaphore_signal(barrier, inc=1, device_id=partner, device_id_type=MESH)
    pl.semaphore_wait(barrier, len(partners))


GATHER = (
    (0, 0, XBIT),
    (0, 1, YBIT),
    (0, 0, YBIT),
    (0, 1, XBIT),
    (XBIT, 0, YBIT),
    (YBIT, 1, XBIT),
    (0, 0, CORE),
    (0, 1, CORE),
    (XBIT, 0, CORE),
    (YBIT, 1, CORE),
    (YBIT, 0, CORE),
    (XBIT, 1, CORE),
    (XBIT | YBIT, 0, CORE),
    (XBIT | YBIT, 1, CORE),
)


class Gather:
    def __init__(self, place, dst, own, send, recv):
        self.place, self.dst, self.own = place, dst, own
        self.send, self.recv = send, recv
        self.half = dst.shape[1] // 16

    def region(self, owner, half):
        at = self.place.dp(owner) * (2 * self.half) + half * self.half
        return self.dst.at[:, pl.ds(pl.multiple_of(at, 16), self.half), :]

    def copy(self, i):
        owner, half, to = GATHER[i]
        src = self.region(owner, half)
        if owner == 0 and self.own is not None:
            src = self.own.at[:, half * self.half : (half + 1) * self.half, :]
        place = self.place
        return push(
            src, self.region(owner, half), self.send.at[i], self.recv.at[i], place.dp(to), place.z
        )

    def start(self, *which):
        for i in which:
            self.copy(i).start()

    def wait(self, received, sent):
        for i in received:
            self.copy(i).wait_recv()
        for i in sent:
            self.copy(i).wait_send()

    def after(self, arrived, started):
        for i, more in zip(arrived, started):
            self.copy(i).wait_recv()
            for j in more:
                self.copy(j).start()

    def middle(self):
        self.after((0, 1), ((4, 8), (5, 9)))

    def last(self):
        self.after((2, 3, 4, 5), ((10,), (11,), (12,), (13,)))


def chip_bits(j):
    return (XBIT if j & 1 else 0) | (YBIT if j & 2 else 0)


def add_into(dst, src):
    def run(i, carry):
        at = pl.ds(pl.multiple_of(i * 16, 16), 16)
        dst[:, at, :] = (dst[:, at, :].astype(F32) + src[:, at, :].astype(F32)).astype(BF)
        return carry

    lax.fori_loop(0, dst.shape[1] // 16, run, 0)


class Reduce:
    def __init__(self, place, sources, scratch, out):
        self.place, self.sources, self.out = place, sources, out
        self.total, self.pair, self.near, self.far, self.quarter, self.stage = scratch[:6]
        self.pair_send, self.pair_recv, self.load, self.send, self.recv, self.z_send, self.z_recv = scratch[6:]
        self.rows = self.total.shape[2]

    @staticmethod
    def scratch(count, n, rows, cols):
        part = cols // 4
        dma = lambda k: pltpu.SemaphoreType.DMA((k,))
        return [
            pltpu.VMEM((n, 4, rows, cols), BF),
            pltpu.VMEM((n, 4, rows, cols), BF),
            pltpu.VMEM((n, 2, 2, rows // 2, cols), BF),
            pltpu.VMEM((n, 2, rows // 2, cols), BF),
            pltpu.VMEM((4, n, rows, part), BF),
            pltpu.VMEM((4, n, rows, part) if part % 128 else (8, 128), BF),
            dma(4 * count),
            dma(4 * count),
            dma(4 * count),
            dma(6),
            dma(6),
            dma(3),
            dma(1),
        ]

    def pair_copies(self, j):
        place, rows = self.place, self.rows
        copies, at = [], 0
        for i, src in enumerate(self.sources):
            slot, n = len(self.sources) * j + i, src.shape[0]
            block = lambda bits: src.at[:, pl.ds(pl.multiple_of(place.dp(bits) * rows, 16), rows), :]
            remote = push(
                block(chip_bits(j) | CORE),
                self.pair.at[at : at + n, j],
                self.pair_send.at[slot],
                self.pair_recv.at[slot],
                place.dp(CORE),
                place.z,
            )
            local = pltpu.make_async_copy(
                block(chip_bits(j)), self.total.at[at : at + n, j], self.load.at[slot]
            )
            copies.append((remote, local))
            at += n
        return copies

    def half(self, j, h):
        size = self.rows // 2
        return self.total.at[:, j, h * size : (h + 1) * size, :]

    MOVES = ((3, 0, XBIT, 1), (3, 1, YBIT, 1), (1, 0, XBIT, 0), (2, 1, YBIT, 0), (2, 0, YBIT, 0), (1, 1, XBIT, 1))

    def move(self, i):
        j, h, to, where = self.MOVES[i]
        dst = self.near.at[:, h, where] if i < 4 else self.far.at[:, where]
        place = self.place
        return push(self.half(j, h), dst, self.send.at[i], self.recv.at[i], place.dp(to), place.z)

    def z_copy(self, k):
        place, part = self.place, self.quarter.shape[3]
        to = place.up(k)
        if part % 128:
            src = self.stage.at[to]
        else:
            src = self.total.at[:, 0, :, pl.ds(pl.multiple_of(to * part, 128), part)]
        dst = self.quarter.at[place.z]
        if k == 0:
            return pltpu.make_async_copy(src, dst, self.z_recv.at[0])
        return push(src, dst, self.z_send.at[k - 1], self.z_recv.at[0], place.d, to)

    def begin(self):
        for j in (3, 1, 2, 0):
            for remote, local in self.pair_copies(j):
                remote.start()
                local.start()

    def pairs(self):
        for j, moves in ((3, (0, 1)), (1, (2,)), (2, (3,)), (0, ())):
            for remote, local in self.pair_copies(j):
                local.wait()
                remote.wait_recv()
            add_into(self.total.at[:, j], self.pair.at[:, j])
            for i in moves:
                self.move(i).start()

    def middle(self):
        for i, j, h, where, more in ((0, 2, 0, 1, 4), (1, 1, 1, 1, 5), (2, 0, 0, 0, None), (3, 0, 1, 0, None)):
            self.move(i).wait_recv()
            add_into(self.half(j, h), self.near.at[:, h, where])
            if more is not None:
                self.move(more).start()

    def late(self):
        for i, h in ((4, 0), (5, 1)):
            self.move(i).wait_recv()
            add_into(self.half(0, h), self.far.at[:, h])
        part = self.quarter.shape[3]
        if part % 128:
            for k in range(4):
                for m in range(self.total.shape[0]):
                    self.stage[k, m] = self.total[m, 0, :, k * part : (k + 1) * part]
        for k in (2, 1, 3, 0):
            self.z_copy(k).start()

    def end(self):
        settle(self.quarter, self.z_recv.at[0])
        parts = [self.quarter[k].astype(F32) for k in range(4)]
        total = (parts[0] + parts[1]) + (parts[2] + parts[3])
        self.out[...] = total.reshape(self.out.shape)
        for j in range(4):
            for remote, _ in self.pair_copies(j):
                remote.wait_send()
        for i in range(6):
            self.move(i).wait_send()
        for k in range(1, 4):
            self.z_copy(k).wait_send()


class Homeward:
    def __init__(self, place, src, homes, send, recv):
        self.place, self.src, self.homes, self.send, self.recv = place, src, homes, send, recv
        self.part = homes[0].shape[1]

    def act(self, what):
        place, part = self.place, self.part
        for u in range(2):

            @pl.when(place.core == u)
            def _():
                for k in (2, 1, 3, 0):
                    to, dp = place.up(k), place.d - place.core + lax.div(place.z, 2)
                    src = self.src.at[pl.ds(pl.multiple_of(to * part, 16), part), :]
                    dst = self.homes[u].at[lax.rem(place.z, 2)]
                    recv = self.recv.at[u]
                    here = jnp.logical_and(dp == place.d, to == place.z)
                    remote = push(src, dst, self.send.at[k], recv, dp, to)
                    if what == "start":
                        pl.when(here)(pltpu.make_async_copy(src, dst, recv).start)
                        pl.when(jnp.logical_not(here))(remote.start)
                    else:
                        pl.when(jnp.logical_not(here))(remote.wait_send)

    def start(self):
        self.act("start")

    def end(self):
        for u in range(2):
            settle(self.homes[u], self.recv.at[u])
        self.act("wait")


def pair_and_z(place):
    return [(place.dp(r), place.up(k)) for k in range(4) for r in (0, CORE) if r or k]


def near_partners(place):
    return pair_and_z(place) + [(place.dp(r), place.z) for r in (XBIT, YBIT)]


INPUTS = 8


def finish_kernel(*refs):
    hbm, (go_ref, mixed_ref, small_ref) = refs[:INPUTS], refs[INPUTS : INPUTS + 3]
    grad_refs, home_refs, sums_ref = refs[INPUTS + 3 : INPUTS + 8], refs[INPUTS + 8 : INPUTS + 10], refs[INPUTS + 10]
    refs = refs[INPUTS + 11 :]
    held, refs = refs[:INPUTS], refs[INPUTS:]
    loads, x_t, ctx_t, g_ref, base, ctx, partner, stream, slots, part_sum, chips = refs[:11]
    home_send, slot_send, chip_send, one_send, recv = refs[11:16]
    refs = refs[16:]
    count = len(refs) // 5
    place = Place()
    d, z, core = place.d, place.z, place.core
    copies = [
        pltpu.make_async_copy(a.at[0:3] if i == 5 else a, b, loads.at[i])
        for i, (a, b) in enumerate(zip(hbm, held))
    ]
    for copy in copies:
        copy.start()

    def need(*which):
        for i in which:
            copies[i].wait()
        return [held[i] for i in which]

    greet(near_partners(place) + [(place.dp(XBIT | YBIT), z)])
    sources = [g_ref.at[m : m + 1] for m in range(4)] + [go_ref]
    key, value, query, pos, out = [
        Reduce(place, (src,), refs[m * count : (m + 1) * count], grad_refs[m])
        for m, src in enumerate(sources)
    ]
    out.begin()
    slot_copies = []
    others = [(r, k) for k in range(4) for r in (0, CORE) if r or k]
    for i, (r, k) in enumerate(others):
        copy = push(small_ref, slots.at[4 * core + z], slot_send.at[i], recv.at[1], place.dp(r), place.up(k))
        copy.start()
        slot_copies.append(copy)
    pltpu.make_async_copy(small_ref, slots.at[4 * core + z], recv.at[1]).start()

    width, block = g_ref.shape[1], 256

    def product(m, left, right, dot):
        def run(i, carry):
            at = pl.ds(pl.multiple_of(i * block, block), block)
            g_ref[m, at, :] = dot(left[at, :], right[...]).astype(BF)
            return carry

        lax.fori_loop(0, width // block, run, 0)

    def turn(src, dst):
        def run(i, carry):
            at = pl.ds(pl.multiple_of(i * block, block), block)
            dst[:, at] = jnp.transpose(src[at, :].astype(F32)).astype(BF)
            return carry

        lax.fori_loop(0, src.shape[0] // block, run, 0)

    x_ref, d_proj = need(0, 1)
    turn(x_ref, x_t)
    product(2, x_t, d_proj, nn)
    query.begin()
    ctx_ref, dk_t = need(2, 3)
    turn(ctx_ref, ctx_t)
    product(0, ctx_t, dk_t, nt)
    key.begin()
    out.pairs()

    dv_t, mats = need(4, 5)
    back = dk_t.shape[1] - base.shape[0]

    def from_context(i, carry):
        at = pl.ds(pl.multiple_of(i * block, block), block)
        cols = pl.ds(pl.multiple_of(i * block + back, block), block)
        turned = nn(mats[0], dk_t[:, cols]) + nn(mats[1], dv_t[:, cols])
        turned = jnp.transpose(turned)
        base[at, :] = turned
        ctx[at, :] = turned.astype(BF)
        return carry

    lax.fori_loop(0, base.shape[0] // block, from_context, 0)
    swap = push(ctx, partner, one_send.at[0], recv.at[0], place.dp(CORE), z)
    swap.start()

    def from_proj(i, carry):
        at = pl.ds(pl.multiple_of(i * block, block), block)
        own = mixed_ref[at, :] + nt(d_proj[at, :], mats[2])
        base[at, :] = own + jnp.where(core == 0, base[at, :], 0.0)
        return carry

    lax.fori_loop(0, base.shape[0] // block, from_proj, 0)
    query.pairs()
    product(1, ctx_t, dv_t, nt)
    value.begin()
    key.pairs()

    swap.wait()
    small_block = 64

    def add_partner(i, carry):
        at = pl.ds(pl.multiple_of(i * small_block, small_block), small_block)
        more = jnp.where(core == 0, partner[at, :].astype(F32), 0.0)
        stream[at, :] = (base[at, :] + more).astype(BF)
        return carry

    lax.fori_loop(0, stream.shape[0] // small_block, add_partner, 0)
    home = Homeward(place, stream, home_refs, home_send, recv.at[2:4])
    home.start()
    out.middle()

    table_t, dr_t = need(6, 7)
    product(3, table_t, dr_t, nt)
    pos.begin()
    value.pairs()
    query.middle()
    out.late()

    settle(slots, recv.at[1])
    total = slots[0]
    for i in range(1, 8):
        total = total + slots[i]
    part_sum[...] = total
    chip = lax.div(d, 2)
    chip_copies = []
    for i, r in enumerate((XBIT, YBIT, XBIT | YBIT)):
        copy = push(part_sum, chips.at[chip], chip_send.at[i], recv.at[4], place.dp(r), z)
        copy.start()
        chip_copies.append(copy)
    pltpu.make_async_copy(part_sum, chips.at[chip], recv.at[4]).start()

    pos.pairs()
    key.middle()
    query.late()
    value.middle()
    key.late()
    pos.middle()
    value.late()
    settle(chips, recv.at[4])
    sums_ref[...] = (chips[0] + chips[1]) + (chips[2] + chips[3])
    pos.late()
    for reduce in (out, query, key, value, pos):
        reduce.end()
    home.end()
    for copy in slot_copies + chip_copies:
        copy.wait_send()


def finish(arrays, g_out, mixed, small):
    total, width = arrays[0].shape
    klen = arrays[2].shape[0]
    rows = width // 8
    vmem = pl.BlockSpec(memory_space=pltpu.VMEM)
    dma = lambda k: pltpu.SemaphoreType.DMA((k,))
    scratch = [pltpu.VMEM((3,) + a.shape[1:] if a.ndim == 3 else a.shape, BF) for a in arrays]
    scratch += [
        dma(INPUTS),
        pltpu.VMEM((width, total), BF),
        pltpu.VMEM((width, klen), BF),
        pltpu.VMEM((4, width, width), BF),
        pltpu.VMEM((total, width), F32),
        pltpu.VMEM((total, width), BF),
        pltpu.VMEM((total, width), BF),
        pltpu.VMEM((total, width), BF),
        pltpu.VMEM((8,) + small.shape, F32),
        pltpu.VMEM(small.shape, F32),
        pltpu.VMEM((4,) + small.shape, F32),
        dma(4),
        dma(7),
        dma(3),
        dma(1),
        dma(5),
    ]
    for _ in range(5):
        scratch += Reduce.scratch(1, 1, rows, width)
    return pl.pallas_call(
        finish_kernel,
        in_specs=[ANY_SPEC] * (INPUTS + 1) + [vmem] * 2,
        out_specs=[vmem] * 5 + [ANY_SPEC] * 2 + [vmem],
        out_shape=[jax.ShapeDtypeStruct((rows, width // 4), F32)] * 5
        + [jax.ShapeDtypeStruct((2, total // 4, width), BF)] * 2
        + [
            jax.ShapeDtypeStruct(small.shape, F32),
        ],
        scratch_shapes=scratch,
        compiler_params=pltpu.CompilerParams(
            collective_id=4, has_side_effects=True, vmem_limit_bytes=LIMIT
        ),
        cost_estimate=pl.CostEstimate(flops=20 << 30, bytes_accessed=64 << 20, transcendentals=0),
        name="finish",
    )(*arrays, g_out, mixed, small)


def pack(mat):
    half = mat.shape[0] // 2
    return jnp.concatenate([mat[:, :128], jnp.concatenate([mat[:half, 128:], mat[half:, 128:]], axis=1)], axis=0)


def unpack(packed):
    rows = packed.shape[0] * 2 // 3
    rest = packed[rows:, :]
    return jnp.concatenate([packed[:rows, :], jnp.concatenate([rest[:, :64], rest[:, 64:]], axis=0)], axis=1)


def enter_kernel(slot_ref, content, query, memory, table_hbm, ints, *refs):
    mats, (upw, dnw), (wb_ref, pb_ref) = refs[:5], refs[5:7], refs[7:9]
    outs, (all_ints, whole_out, context_out, wo, ud) = refs[9:15], refs[15:20]
    (
        whole,
        context,
        stream,
        table,
        spread,
        picked,
        shards,
        slab,
        mat_send,
        mat_recv,
        ud_send,
        ud_recv,
        int_send,
        spread_send,
        pick_send,
        stream_send,
        pair_send,
        gather_send,
        gather_recv,
        wo_send,
        wo_recv,
        far_send,
        far_recv,
        recv,
        local,
    ) = refs[20:]
    place = Place()
    d, z, core = place.d, place.z, place.core
    up, down, far = place.up(1), place.up(3), place.up(2)
    part = query.shape[1]
    pltpu.make_async_copy(table_hbm, table, local.at[0]).start()
    piece = spread.shape[1]
    blocks = part // piece // 2
    first = 4 * blocks
    greet([(place.dp(r), place.up(k)) for r in range(8) for k in range(4) if r or k])

    spread_copies = []
    for r in range(8):
        to = place.dp(r)
        src = memory.at[:, pl.ds(pl.multiple_of(to * piece, 16), piece), :]
        dst = spread.at[pl.ds(2 * d, 2)]
        if r == 0:
            pltpu.make_async_copy(src, dst, recv.at[0]).start()
        else:
            spread_copies.append(push(src, dst, spread_send.at[r - 1], recv.at[0], to, z))
            spread_copies[-1].start()

    for m, mat in enumerate(mats):
        shards[z, m] = pack(mat[...])
    cutoff = shards.shape[2] * 5 // 9

    def mat_copy(i):
        own = shards.at[z]
        low, high = shards.at[down, :, :cutoff], shards.at[up, :, cutoff:]
        src = (own, own, low, high)[i]
        return push(src, src, mat_send.at[i], mat_recv.at[i], d, (up, down, up, down)[i])

    mat_copy(0).start()
    mat_copy(1).start()
    int_copies = []
    for r in range(8):
        if r == 0:
            pltpu.make_async_copy(ints, all_ints.at[d], recv.at[2]).start()
        else:
            copy = push(ints, all_ints.at[d], int_send.at[r - 1], recv.at[2], place.dp(r), z)
            int_copies.append(copy)
            copy.start()

    def stream_copy(i, act):
        j, kind = i // 2, i % 2
        to, dp = 2 * core + j, d - core + kind
        if kind == 0:
            src, sem = content.at[j], recv.at[3]
            dst = context.at[pl.ds(first + blocks * z, blocks)]
        else:
            src, sem = query.at[j], recv.at[4]
            dst = stream.at[pl.ds(pl.multiple_of(z * part, 16), part), :]
        here = jnp.logical_and(dp == d, to == z)
        remote = push(src, dst, stream_send.at[i], sem, dp, to)
        if act == "start":
            pl.when(here)(pltpu.make_async_copy(src, dst, sem).start)
            pl.when(jnp.logical_not(here))(remote.start)
        else:
            pl.when(jnp.logical_not(here))(remote.wait_send)

    mat_copy(0).wait_recv()
    mat_copy(2).start()
    mat_copy(1).wait_recv()
    mat_copy(3).start()
    for i in range(4):
        stream_copy(i, "start")

    settle(spread, recv.at[0])
    for q in range(16):
        picked[q] = spread[slot_ref[q]]
    pick_copies = []
    for r in (YBIT | XBIT, XBIT, YBIT, 0):
        for k in range(4):
            to, lane = place.dp(r), place.up(k)
            src = picked.at[4 * lax.div(to, 2) + lane]
            dst = context.at[blocks * z + lax.div(d, 2), core]
            if r or k:
                copy = push(src, dst, pick_send.at[2 * r + k - 1], recv.at[5], to, lane)
                pick_copies.append(copy)
            else:
                copy = pltpu.make_async_copy(src, dst, recv.at[5])
            copy.start()

    mat_copy(2).wait_recv()
    mat_copy(3).wait_recv()
    for m in range(5):
        slab[m] = jnp.concatenate([unpack(shards[k, m]) for k in range(4)], axis=1)
    rows = slab.shape[1]
    own_rows = pl.ds(pl.multiple_of(d * rows, 16), rows)
    gather = Gather(place, whole, slab.at[0:4], gather_send, gather_recv)
    gather.start(0, 1, 2, 3, 6, 7)
    pltpu.make_async_copy(slab.at[0:4], whole.at[:, own_rows, :], recv.at[6]).start()
    pltpu.make_async_copy(slab.at[4:5], wo.at[:, own_rows, :], recv.at[7]).start()

    width = upw.shape[1]

    def columns(at, start=0, size=rows):
        mine = pl.ds(pl.multiple_of(d * rows + start, 16), size)
        return ud.at[:, mine, pl.ds(pl.multiple_of(at * width, 128), width)]

    def ud_copy(i):
        if i < 4:
            src, dst = (upw, dnw)[i % 2], columns(z).at[i % 2]
            return push(src, dst, ud_send.at[i], ud_recv.at[i // 2], d, (up, down)[i // 2])
        half = rows // 2
        src = columns(down, 0, half) if i == 4 else columns(up, half, half)
        return push(src, src, ud_send.at[i], ud_recv.at[i - 2], d, (up, down)[i - 4])

    for i in range(4):
        ud_copy(i).start()
    for m, mat in enumerate((upw, dnw)):
        pltpu.make_async_copy(mat, columns(z).at[m], recv.at[8]).start()

    pick_pair = push(
        context.at[0:first, core], context.at[0:first, core], pair_send.at[0], recv.at[1], place.dp(CORE), z
    )
    settle(context.at[0:first, core], recv.at[5])
    pick_pair.start()
    gather.middle()
    settle(columns(down), ud_recv.at[0])
    ud_copy(4).start()
    settle(columns(up), ud_recv.at[1])
    ud_copy(5).start()

    lead_copy = push(
        context.at[first:], context.at[first:], pair_send.at[1], recv.at[3], place.dp(CORE), z
    )

    @pl.when(core == 0)
    def _():
        settle(context.at[first:], recv.at[3])
        lead_copy.start()

    gather.last()
    wo_gather = Gather(place, wo, slab.at[4:5], wo_send, wo_recv)
    ud_gather = Gather(place, ud, None, far_send, far_recv)
    wo_gather.start(0, 1, 2, 3, 6, 7)
    gather.wait(range(6, 14), ())
    settle(whole.at[:, own_rows, :], recv.at[6])
    keep_whole = pltpu.make_async_copy(whole, whole_out, local.at[1])
    keep_whole.start()
    settle(columns(z), recv.at[8])
    ud_copy(4).wait_recv()
    ud_copy(5).wait_recv()
    ud_gather.start(0, 1, 2, 3, 6, 7)
    gathers = (ud_gather, wo_gather)

    keep_context = pltpu.make_async_copy(context, context_out, local.at[2])

    def before_stream():
        pick_pair.wait()

        @pl.when(core == 0)
        def _():
            lead_copy.wait_send()

        @pl.when(core == 1)
        def _():
            settle(context.at[first:], recv.at[3])
            settle(stream, recv.at[4])

        keep_context.start()

    def before_context():
        for one in gathers:
            one.after((0, 1), ((8,), (9,)))

    pltpu.make_async_copy(table_hbm, table, local.at[0]).wait()
    project_step(
        whole, context, stream, table, wb_ref, pb_ref, *outs, hooks=(before_stream, before_context)
    )
    for one in gathers:
        one.after((2, 3), ((10,), (11,)))
    settle(wo.at[:, own_rows, :], recv.at[7])
    settle(all_ints, recv.at[2])
    gather.wait((), range(14))
    for one in gathers:
        one.wait(range(6, 12), (0, 1, 2, 3) + tuple(range(6, 12)))
    keep_whole.wait()
    keep_context.wait()
    for i in range(4):
        stream_copy(i, "wait")
        mat_copy(i).wait_send()
    for i in range(6):
        ud_copy(i).wait_send()
    for copy in spread_copies + int_copies + pick_copies:
        copy.wait_send()


def enter(slot_of, content, query, memory, table, ints, mats, upw, dnw, wb, pb):
    micro, part, width = content.shape
    rows = mats[0].shape[0]
    inner = upw.shape[1] * 4
    piece = part // 8
    klen, span, seq = 8 * part, table.shape[0], 4 * part
    vmem = pl.BlockSpec(memory_space=pltpu.VMEM)
    dma = lambda n: pltpu.SemaphoreType.DMA((n,))
    bf = lambda *shape: jax.ShapeDtypeStruct(shape, BF)
    return pl.pallas_call(
        enter_kernel,
        in_specs=[SMEM_SPEC] + [ANY_SPEC] * 4 + [vmem] * 10,
        out_specs=[vmem] * 6 + [ANY_SPEC] * 5,
        out_shape=[
            bf(klen, width),
            bf(klen, width),
            bf(span, width),
            bf(seq, width),
            bf(seq, width),
            bf(seq, width),
            jax.ShapeDtypeStruct((8,) + ints.shape, jnp.int32),
            bf(4, 8 * rows, width),
            bf(32, 2, piece, width),
            bf(1, 8 * rows, width),
            bf(2, 8 * rows, inner),
        ],
        scratch_shapes=[
            pltpu.VMEM((4, 8 * rows, width), BF),
            pltpu.VMEM((32, 2, piece, width), BF),
            pltpu.VMEM((seq, width), BF),
            pltpu.VMEM((span, width), BF),
            pltpu.VMEM((16, piece, width), BF),
            pltpu.VMEM((16, piece, width), BF),
            pltpu.VMEM((4, 5, rows * 3 // 2, 128), BF),
            pltpu.VMEM((5, rows, width), BF),
            dma(4),
            dma(4),
            dma(6),
            dma(4),
            dma(7),
            dma(7),
            dma(15),
            dma(4),
            dma(2),
            dma(14),
            dma(14),
            dma(14),
            dma(14),
            dma(14),
            dma(14),
            dma(9),
            dma(3),
        ],
        compiler_params=pltpu.CompilerParams(
            collective_id=1, has_side_effects=True, vmem_limit_bytes=LIMIT
        ),
        cost_estimate=pl.CostEstimate(flops=0, bytes_accessed=64 << 20, transcendentals=0),
        name="enter",
    )(
        slot_of,
        content.reshape(micro, 4, 2, piece, width),
        query,
        memory,
        table,
        ints,
        *mats,
        upw,
        dnw,
        wb,
        pb,
    )


def head_lanes(array, head):
    lane = lax.broadcasted_iota(jnp.int32, array.shape, 1)
    return jnp.where((lane >= DH) == (head == 1), array, jnp.zeros_like(array))


def attend_forward_step(
    block, qw_ref, qp_ref, k_ref, v_ref, rel_ref, thr_ref, kr_ref, vec_ref, prob_ref
):
    rows, klen = qw_ref.shape[0], k_ref.shape[0]
    width = klen + block
    keys, values = k_ref[...], v_ref[...]
    for part in range(rows // block):
        at = slice(part * block, (part + 1) * block)
        first = rows - (part + 1) * block
        qw, qp = qw_ref[at, :], qp_ref[at, :]
        rel = rel_ref[first : first + width, :]
        seen = kr_ref[...] < thr_ref[at, :]
        vecs = []
        for head in range(2):
            raw = nt(head_lanes(qp, head), rel)
            moved = pltpu.roll(raw, 0, 1, stride=1, stride_axis=0)[:, block:]
            score = nt(head_lanes(qw, head), keys) + moved
            score = jnp.where(seen, score, -1e30)
            expo = jnp.exp(score - jnp.max(score, axis=1, keepdims=True))
            prob = (expo * (1.0 / jnp.sum(expo, axis=1, keepdims=True))).astype(BF)
            prob_ref[head, at, :] = prob
            vecs.append(nn(prob, values))
        lane = lax.broadcasted_iota(jnp.int32, vecs[0].shape, 1)
        vec_ref[at, :] = jnp.where(lane < DH, vecs[0], vecs[1]).astype(BF)


def attend_forward_kernel(block, wired, *refs):
    if not wired:
        attend_forward_step(block, *refs)
        return
    ins, (ctan, qtan) = refs[:7], refs[9:11]
    outs, (wo, ud, tangent) = refs[11:13], refs[13:16]
    out_send, out_recv, ud_send, ud_recv, tan_send, recv = refs[16:]
    step, steps = pl.program_id(0), pl.num_programs(0)
    place = Place()
    d, z, core = place.d, place.z, place.core
    gathers = (
        Gather(place, ud, None, ud_send, ud_recv),
        Gather(place, wo, None, out_send, out_recv),
    )
    part = ctan.shape[1]

    def tan_copy(i, act):
        j, kind = i // 2, i % 2
        to, dp = 2 * core + j, d - core + kind
        src = (ctan, qtan)[kind].at[j]
        dst = tangent.at[pl.ds(pl.multiple_of(z * part, 16), part), :]
        here = jnp.logical_and(dp == d, to == z)
        local = pltpu.make_async_copy(src, dst, recv.at[0])
        remote = push(src, dst, tan_send.at[i], recv.at[0], dp, to)
        if act == "start":
            pl.when(here)(local.start)
            pl.when(jnp.logical_not(here))(remote.start)
        else:
            pl.when(jnp.logical_not(here))(remote.wait_send)

    @pl.when(step == 0)
    def _():
        greet(near_partners(place))
        for gather in gathers:
            gather.start(4, 5)
        for i in range(4):
            tan_copy(i, "start")

    @pl.when(step == steps - 1)
    def _():
        for gather in gathers:
            gather.after((4, 5), ((12,), (13,)))

    attend_forward_step(block, *ins, *outs)

    @pl.when(step == steps - 1)
    def _():
        for gather in gathers:
            gather.wait((12, 13), (4, 5, 12, 13))
        settle(tangent, recv.at[0])
        for i in range(4):
            tan_copy(i, "wait")


def attend_forward(qw, qp, keys, values, rel, thr, key_rank, block, wires=()):
    rows, width = qw.shape
    klen, span = keys.shape[0], rel.shape[0]
    col = lambda count: pl.BlockSpec((count, PAIR), lambda p: (0, p))
    in_specs = [
        col(rows),
        col(rows),
        col(klen),
        col(klen),
        col(span),
        pl.BlockSpec((rows, 1), lambda p: (0, 0)),
        pl.BlockSpec((1, klen), lambda p: (0, 0)),
    ]
    out_specs = [col(rows), pl.BlockSpec((2, rows, klen), lambda p: (p, 0, 0))]
    out_shape = [
        jax.ShapeDtypeStruct((rows, width), BF),
        jax.ShapeDtypeStruct((width // DH, rows, klen), BF),
    ]
    params = dict(vmem_limit_bytes=LIMIT)
    scratch = []
    if wires:
        in_specs += [ANY_SPEC] * 4
        out_specs += [ANY_SPEC] * 3
        out_shape += [
            jax.ShapeDtypeStruct(wires[0].shape, BF),
            jax.ShapeDtypeStruct(wires[1].shape, BF),
            jax.ShapeDtypeStruct((rows, width), BF),
        ]
        scratch = [pltpu.SemaphoreType.DMA((n,)) for n in (14, 14, 14, 14, 4, 1)]
        params.update(collective_id=2, has_side_effects=True)
    return pl.pallas_call(
        functools.partial(attend_forward_kernel, block, bool(wires)),
        grid=(width // PAIR,),
        in_specs=in_specs,
        out_specs=out_specs,
        out_shape=out_shape,
        scratch_shapes=scratch,
        input_output_aliases={7: 2, 8: 3} if wires else {},
        compiler_params=pltpu.CompilerParams(**params),
        cost_estimate=pl.CostEstimate(
            flops=8 * rows * klen * width, bytes_accessed=16 << 20, transcendentals=12 * rows * klen
        ),
        name="attend_forward",
    )(qw, qp, keys, values, rel, thr, key_rank, *wires)


def attend_backward_kernel(block, wired, *refs):
    if not wired:
        attend_backward_step(block, *refs)
        return
    ins, (g_ud, src) = refs[:7], refs[7:9]
    outs, grad_refs, home_refs = refs[9:14], refs[14:16], refs[16:18]
    rel_acc, home_send, home_recv = refs[18:21]
    step, steps = pl.program_id(0), pl.num_programs(0)
    place = Place()
    count = len(refs[21:]) // 2
    reduces = [
        Reduce(place, (g_ud.at[m : m + 1],), refs[21 + m * count : 21 + (m + 1) * count], grad_refs[m])
        for m in range(2)
    ]
    home = Homeward(place, src, home_refs, home_send, home_recv)

    @pl.when(step == 0)
    def _():
        greet(near_partners(place))
        for reduce in reduces:
            reduce.begin()
        home.start()

    @pl.when(step == 2)
    def _():
        reduces[0].pairs()

    @pl.when(step == 3)
    def _():
        reduces[1].pairs()

    @pl.when(step == 5)
    def _():
        reduces[0].middle()

    attend_backward_step(block, *ins, *outs, rel_acc)

    @pl.when(step == steps - 1)
    def _():
        reduces[0].late()
        reduces[1].middle()
        reduces[1].late()
        reduces[0].end()
        reduces[1].end()
        home.end()


def attend_backward_step(
    block,
    prob_ref,
    gvec_ref,
    qw_ref,
    qp_ref,
    k_ref,
    v_ref,
    rel_ref,
    dproj_ref,
    dk_ref,
    dv_ref,
    drel_ref,
    bias_ref,
    rel_acc,
):
    rows, klen = qw_ref.shape[0], k_ref.shape[0]
    width = klen + block
    keys, values = k_ref[...], v_ref[...]
    row = lax.broadcasted_iota(jnp.int32, (block, block), 0)
    col = lax.broadcasted_iota(jnp.int32, (block, block), 1)
    mirror = (row + col == block - 1).astype(BF)
    rel_acc[...] = jnp.zeros_like(rel_acc)
    d_keys, d_values = [None, None], [None, None]
    word_sum = jnp.zeros((1, PAIR), F32)
    pos_sum = jnp.zeros((1, PAIR), F32)
    for part in range(rows // block):
        at = slice(part * block, (part + 1) * block)
        first = rows - (part + 1) * block
        gvec, qw = gvec_ref[at, :], qw_ref[at, :]
        gvec_t = jnp.transpose(gvec.astype(F32)).astype(BF)
        qw_t = jnp.transpose(qw.astype(F32)).astype(BF)
        qp_t = jnp.transpose(nn(mirror, qp_ref[at, :])).astype(BF)
        rel = rel_ref[first : first + width, :]
        word_parts, pos_parts = [], []
        for head in range(2):
            own = slice(head * DH, (head + 1) * DH)
            prob = prob_ref[head, at, :]
            d_prob = nt(head_lanes(gvec, head), values)
            weight = prob.astype(F32)
            inner = jnp.sum(weight * d_prob, axis=1, keepdims=True)
            g_sum = (weight * (d_prob - inner) * 0.125).astype(BF)
            dv = nn(gvec_t[own, :], prob)
            dk = nn(qw_t[own, :], g_sum)
            d_values[head] = dv if part == 0 else d_values[head] + dv
            d_keys[head] = dk if part == 0 else d_keys[head] + dk
            turned = nn(mirror, g_sum)
            padded = jnp.concatenate([jnp.zeros((block, block), F32), turned], axis=1)
            moved = pltpu.roll(padded, width - block + 1, 1, stride=1, stride_axis=0).astype(BF)
            word_parts.append(nn(turned.astype(BF), keys))
            pos_parts.append(nn(moved, rel))
            rel_acc[own, first : first + width] += nn(qp_t[own, :], moved)
        lane = lax.broadcasted_iota(jnp.int32, word_parts[0].shape, 1)
        word = jnp.where(lane < DH, word_parts[0], word_parts[1])
        pos = jnp.where(lane < DH, pos_parts[0], pos_parts[1])
        word_sum = word_sum + jnp.sum(word, axis=0, keepdims=True)
        pos_sum = pos_sum + jnp.sum(pos, axis=0, keepdims=True)
        dproj_ref[at, :] = nn(mirror, (word + pos).astype(BF)).astype(BF)
    for head in range(2):
        own = slice(head * DH, (head + 1) * DH)
        dv_ref[own, :] = d_values[head].astype(BF)
        dk_ref[own, :] = (8.0 * d_keys[head]).astype(BF)
    drel_ref[...] = (8.0 * rel_acc[...]).astype(BF)
    bias_ref[0:1, :] = word_sum
    bias_ref[1:2, :] = pos_sum


def attend_backward(prob, gvec, qw, qp, keys, values, rel, block, wires=()):
    rows, width = qw.shape
    klen, span = keys.shape[0], rel.shape[0]
    col = lambda count: pl.BlockSpec((count, PAIR), lambda p: (0, p))
    rowb = lambda count: pl.BlockSpec((PAIR, count), lambda p: (p, 0))
    in_specs = [
        pl.BlockSpec((2, rows, klen), lambda p: (p, 0, 0)),
        col(rows),
        col(rows),
        col(rows),
        col(klen),
        col(klen),
        col(span),
    ]
    out_specs = [col(rows), rowb(klen), rowb(klen), rowb(span), col(2)]
    out_shape = [
        jax.ShapeDtypeStruct((rows, width), BF),
        jax.ShapeDtypeStruct((width, klen), BF),
        jax.ShapeDtypeStruct((width, klen), BF),
        jax.ShapeDtypeStruct((width, span), BF),
        jax.ShapeDtypeStruct((2, width), F32),
    ]
    scratch = [pltpu.VMEM((PAIR, span), F32)]
    params = dict(vmem_limit_bytes=LIMIT)
    if wires:
        inner, mine = wires[0].shape[2], width // 8
        in_specs += [ANY_SPEC, ANY_SPEC]
        out_specs += [pl.BlockSpec(memory_space=pltpu.VMEM)] * 2 + [ANY_SPEC] * 2
        out_shape += [jax.ShapeDtypeStruct((mine, inner // 4), F32)] * 2
        out_shape += [jax.ShapeDtypeStruct((2, rows // 4, width), BF)] * 2
        scratch += [pltpu.SemaphoreType.DMA((4,)), pltpu.SemaphoreType.DMA((2,))]
        scratch += 2 * Reduce.scratch(1, 1, mine, inner)
        params.update(collective_id=3, has_side_effects=True)
    return pl.pallas_call(
        functools.partial(attend_backward_kernel, block, bool(wires)),
        grid=(width // PAIR,),
        in_specs=in_specs,
        out_specs=out_specs,
        out_shape=out_shape,
        scratch_shapes=scratch,
        compiler_params=pltpu.CompilerParams(**params),
        cost_estimate=pl.CostEstimate(
            flops=16 * rows * klen * width, bytes_accessed=20 << 20, transcendentals=0
        ),
        name="attend_backward",
    )(prob, gvec, qw, qp, keys, values, rel, *wires)


def norm_parts(value):
    center = value - jnp.mean(value, axis=1, keepdims=True)
    scale = lax.rsqrt(jnp.mean(center * center, axis=1, keepdims=True) + EPS)
    return center * scale, scale


def norm_pull(normed, scale, err):
    inner = jnp.mean(err * normed, axis=1, keepdims=True)
    return (err - jnp.mean(err, axis=1, keepdims=True) - normed * inner) * scale


def sum_rows(value):
    return jnp.sum(value, axis=0, keepdims=True)


def feed_kernel(steps, *refs):
    (
        ud_hbm,
        wo_hbm,
        vec_ref,
        x_ref,
        tan_ref,
        upb_ref,
        rows_ref,
        out_ref,
        dmix_ref,
        gvec_ref,
        go_ref,
        gud_ref,
        gupb_ref,
        small_ref,
        ud_ref,
        wo_ref,
        n1_ref,
        r1_ref,
        fb_ref,
        fbt_ref,
        acc_ref,
        act_ref,
        slope_ref,
        gd_ref,
        gdt_ref,
        sems,
    ) = refs
    step = pl.program_id(0)
    chunk = act_ref.shape[2]
    dnb_ref, g1_ref, s1_ref, g2_ref, s2_ref = (rows_ref.at[i : i + 1] for i in range(5))
    cols = pl.ds(pl.multiple_of(lax.rem(step, steps) * chunk, chunk), chunk)

    @pl.when(step == 0)
    def _():
        wo_copy = pltpu.make_async_copy(wo_hbm, wo_ref, sems.at[0])
        ud_copy = pltpu.make_async_copy(ud_hbm, ud_ref, sems.at[1])
        wo_copy.start()
        ud_copy.start()
        wo_copy.wait()
        normed, scale = norm_parts(nt(vec_ref[...], wo_ref[0]) + x_ref[...].astype(F32))
        n1_ref[...] = normed
        r1_ref[...] = scale
        first = normed * g1_ref[...] + s1_ref[...]
        fb_ref[...] = first.astype(BF)
        fbt_ref[...] = jnp.transpose(first).astype(BF)
        acc_ref[...] = first + dnb_ref[...]
        ud_copy.wait()

    @pl.when(step < steps)
    def _():
        upper = nn(fb_ref[...], ud_ref[0, :, cols]) + upb_ref[...]
        square = upper * upper
        root = 0.7978845608028654
        bend = jnp.tanh(root * (upper + 0.044715 * (square * upper)))
        half = 0.5 * (1.0 + bend)
        act = (upper * half).astype(BF)
        act_ref[step] = act
        slope_ref[step] = half + 0.5 * upper * (1.0 - bend * bend) * (
            root + (3 * 0.044715 * root) * square
        )
        acc_ref[...] += nt(act, ud_ref[1, :, cols])

    @pl.when(step == steps - 1)
    def _():
        normed, scale = norm_parts(acc_ref[...])
        out_ref[...] = (normed * g2_ref[...] + s2_ref[...]).astype(BF)
        tan = tan_ref[...].astype(F32)
        d_down = norm_pull(normed, scale, tan * g2_ref[...])
        small_ref[0:1, :] = sum_rows(d_down)
        small_ref[3:4, :] = sum_rows(tan * normed)
        small_ref[4:5, :] = sum_rows(tan)
        gd_ref[...] = d_down.astype(BF)
        gdt_ref[...] = jnp.transpose(d_down).astype(BF)
        acc_ref[...] = d_down

    @pl.when(step >= steps)
    def _():
        at = step - steps
        d_up = nn(gd_ref[...], ud_ref[1, :, cols]) * slope_ref[at]
        gupb_ref[...] = sum_rows(d_up)
        g_up = d_up.astype(BF)
        acc_ref[...] += nt(g_up, ud_ref[0, :, cols])
        gud_ref[0] = nn(fbt_ref[...], g_up).astype(BF)
        gud_ref[1] = nn(gdt_ref[...], act_ref[at]).astype(BF)

    @pl.when(step == 2 * steps - 1)
    def _():
        d_first, normed = acc_ref[...], n1_ref[...]
        small_ref[1:2, :] = sum_rows(d_first * normed)
        small_ref[2:3, :] = sum_rows(d_first)
        d_mixed = norm_pull(normed, r1_ref[...], d_first * g1_ref[...])
        dmix_ref[...] = d_mixed
        gvec_ref[...] = nn(d_mixed.astype(BF), wo_ref[0]).astype(BF)
        gdt_ref[...] = jnp.transpose(d_mixed).astype(BF)
        go_ref[...] = nn(gdt_ref[...], vec_ref[...]).astype(BF)


def feed(ud, wo, vec, x, tan, upb, vecs):
    rows, width = vec.shape
    inner = upb.shape[1]
    chunk = 512
    steps = inner // chunk
    whole = lambda a, b: pl.BlockSpec((a, b), lambda i: (0, 0))
    late = lambda i: jnp.maximum(i - steps, 0)
    grads = pl.BlockSpec((2, width, chunk), lambda i: (0, 0, late(i)))
    return pl.pallas_call(
        functools.partial(feed_kernel, steps),
        grid=(2 * steps,),
        in_specs=[ANY_SPEC] * 2
        + [whole(rows, width)] * 3
        + [pl.BlockSpec((1, chunk), lambda i: (0, lax.rem(i, steps)))]
        + [whole(5, width)],
        out_specs=[
            whole(rows, width),
            whole(rows, width),
            whole(rows, width),
            whole(width, width),
            grads,
            pl.BlockSpec((1, chunk), lambda i: (0, late(i))),
            whole(8, width),
        ],
        out_shape=[
            jax.ShapeDtypeStruct((rows, width), BF),
            jax.ShapeDtypeStruct((rows, width), F32),
            jax.ShapeDtypeStruct((rows, width), BF),
            jax.ShapeDtypeStruct((width, width), BF),
            jax.ShapeDtypeStruct((2, width, inner), BF),
            jax.ShapeDtypeStruct((1, inner), F32),
            jax.ShapeDtypeStruct((8, width), F32),
        ],
        scratch_shapes=[
            pltpu.VMEM((2, width, inner), BF),
            pltpu.VMEM((1, width, width), BF),
            pltpu.VMEM((rows, width), F32),
            pltpu.VMEM((rows, 1), F32),
            pltpu.VMEM((rows, width), BF),
            pltpu.VMEM((width, rows), BF),
            pltpu.VMEM((rows, width), F32),
            pltpu.VMEM((steps, rows, chunk), BF),
            pltpu.VMEM((steps, rows, chunk), F32),
            pltpu.VMEM((rows, width), BF),
            pltpu.VMEM((width, rows), BF),
            pltpu.SemaphoreType.DMA((2,)),
        ],
        compiler_params=pltpu.CompilerParams(vmem_limit_bytes=LIMIT),
        cost_estimate=pl.CostEstimate(
            flops=12 * rows * width * inner, bytes_accessed=36 << 20, transcendentals=rows * inner
        ),
        name="feed",
    )(ud, wo, vec, x, tan, upb, vecs)


def project_step(
    w_ref,
    ctx_ref,
    q_ref,
    table_ref,
    wb_ref,
    pb_ref,
    k_ref,
    v_ref,
    rel_ref,
    qw_ref,
    qp_ref,
    x_ref,
    hooks=(),
):
    lead = lax.rem(lax.axis_index("dp"), 2) == 0
    klen, width = k_ref.shape
    back = klen - q_ref.shape[0]

    def context_rows(start):
        at = pl.ds(lax.div(start, 32), block // 32)
        return ctx_ref[at].reshape(block, width)

    block = 256

    def loop(count, step):
        def run(i, carry):
            step(pl.ds(pl.multiple_of(i * block, block), block))
            return carry

        lax.fori_loop(0, count // block, run, 0)

    def context_step(at):
        rows = context_rows(at.start)
        k_ref[at, :] = nn(rows, w_ref[0]).astype(BF)
        v_ref[at, :] = nn(rows, w_ref[1]).astype(BF)

    def stream_step(at):
        x_ref[at, :] = jnp.where(lead, context_rows(at.start + back), q_ref[at, :])
        proj = nn(x_ref[at, :], w_ref[2])
        qw_ref[at, :] = (0.125 * (proj + wb_ref[...]).astype(BF).astype(F32)).astype(BF)
        qp_ref[at, :] = (0.125 * (proj + pb_ref[...]).astype(BF).astype(F32)).astype(BF)

    def table_step(at):
        rel_ref[at, :] = nn(table_ref[at, :], w_ref[3]).astype(BF)

    loop(table_ref.shape[0], table_step)
    if hooks:
        hooks[0]()
    loop(q_ref.shape[0], stream_step)
    if hooks:
        hooks[1]()
    loop(klen, context_step)


def project(mats, context, query, table, wb, pb):
    rows, width = query.shape
    klen, span = context.shape[0], table.shape[0]
    vmem = pl.BlockSpec(memory_space=pltpu.VMEM)
    return pl.pallas_call(
        project_step,
        in_specs=[vmem] * 6,
        out_specs=[vmem] * 6,
        out_shape=[
            jax.ShapeDtypeStruct((klen, width), BF),
            jax.ShapeDtypeStruct((klen, width), BF),
            jax.ShapeDtypeStruct((span, width), BF),
            jax.ShapeDtypeStruct((rows, width), BF),
            jax.ShapeDtypeStruct((rows, width), BF),
            jax.ShapeDtypeStruct((rows, width), BF),
        ],
        compiler_params=pltpu.CompilerParams(vmem_limit_bytes=LIMIT),
        cost_estimate=pl.CostEstimate(
            flops=2 * (2 * klen + rows + span) * width * width,
            bytes_accessed=20 << 20,
            transcendentals=0,
        ),
        name="project",
    )(mats, context.reshape(klen // 32, 2, 16, width), query, table, wb, pb)


def weight_grads_kernel(xt_ref, ct_ref, tt_ref, dp_ref, dk_ref, dv_ref, dr_ref, g_ref):
    g_ref[0] = nt(ct_ref[...], dk_ref[...]).astype(BF)
    g_ref[1] = nt(ct_ref[...], dv_ref[...]).astype(BF)
    g_ref[2] = nn(xt_ref[...], dp_ref[...]).astype(BF)
    g_ref[3] = nt(tt_ref[...], dr_ref[...]).astype(BF)


def weight_grads(x_t, ctx_t, table_t, d_proj, dk_t, dv_t, drel_t):
    width, rows = x_t.shape
    klen, span = ctx_t.shape[1], table_t.shape[1]
    chunk = 256
    whole = lambda a, b: pl.BlockSpec((a, b), lambda i: (0, 0))
    rowb = lambda b: pl.BlockSpec((chunk, b), lambda i: (i, 0))
    return pl.pallas_call(
        weight_grads_kernel,
        grid=(width // chunk,),
        in_specs=[
            whole(width, rows),
            whole(width, klen),
            whole(width, span),
            pl.BlockSpec((rows, chunk), lambda i: (0, i)),
            rowb(klen),
            rowb(klen),
            rowb(span),
        ],
        out_specs=pl.BlockSpec((4, width, chunk), lambda i: (0, 0, i)),
        out_shape=jax.ShapeDtypeStruct((4, width, width), BF),
        compiler_params=pltpu.CompilerParams(vmem_limit_bytes=LIMIT),
        cost_estimate=pl.CostEstimate(
            flops=2 * (rows + 2 * klen + span) * width * width,
            bytes_accessed=20 << 20,
            transcendentals=0,
        ),
        name="weight_grads",
    )(x_t, ctx_t, table_t, d_proj, dk_t, dv_t, drel_t)


def flip(arr, bit):
    return lax.ppermute(arr, "dp", [(i, i ^ bit) for i in range(lax.axis_size("dp"))])


def scatter_sum(grads):
    mine = lax.psum_scatter(grads, "dp", scatter_dimension=1, tiled=True)
    return lax.psum_scatter(mine, "tensor", scatter_dimension=2, tiled=True).astype(F32)


def body(
    content_stream,
    query_stream,
    memory,
    content_tangent,
    query_tangent,
    seq_lengths,
    factor_order,
    memory_lengths,
    slot_sequence,
    query_weight,
    key_weight,
    value_weight,
    pos_weight,
    out_weight,
    up_weight,
    up_bias,
    down_weight,
    down_bias,
    word_bias,
    pos_bias,
    first_gain,
    first_shift,
    second_gain,
    second_shift,
):
    groups, tensors = lax.axis_size("dp"), lax.axis_size("tensor")
    micro, part_len, width = content_stream.shape
    mem_part = memory.shape[1]
    seq_len, mem_total = part_len * tensors, mem_part * tensors
    klen, span = mem_total + seq_len, mem_total + 2 * seq_len
    count = micro * groups
    here, lane = lax.axis_index("dp"), lax.axis_index("tensor")
    core = here % 2
    lead = core == 0
    block = 256
    assert 2 * micro == tensors

    def swap(arr):
        return flip(arr, CORE)

    def to_unit(first, second):
        got = swap(jnp.where(lead, second, first))
        low = jnp.where(lead, first, got)
        high = jnp.where(lead, got, second)
        both = jnp.concatenate([low, high], 0)
        both = lax.all_to_all(both, "tensor", split_axis=0, concat_axis=0, tiled=True)
        return both.reshape(seq_len, width)

    def from_unit(arr):
        both = arr.reshape(tensors, part_len, width)
        both = lax.all_to_all(both, "tensor", split_axis=0, concat_axis=0, tiled=True)
        low, high = both[:micro], both[micro:]
        got = swap(jnp.where(lead, high, low))
        return jnp.where(lead, low, got), jnp.where(lead, got, high)

    seq_id = (here // 2) * tensors + lane
    ids = jnp.arange(count, dtype=jnp.int32)
    slot_of = jnp.sum(jnp.where(slot_sequence[None, :] == ids[:, None], ids[None, :], 0), axis=1)
    counts = jnp.concatenate([seq_lengths, memory_lengths])
    slot = slot_of[seq_id]
    mats = [key_weight, value_weight, query_weight, pos_weight, out_weight]
    table = jnp.asarray(reversed_table(span, klen, width))
    row = lambda v: v.reshape(1, -1)
    wires = ()
    if groups == 8:
        ints = jnp.pad(factor_order, ((0, 6), (0, 0)))
        ints = lax.dynamic_update_slice(ints, counts[None, :], (micro, 0))
        keys, values, rel, q_word, q_pos, stream, all_ints, weights, context, *wires = enter(
            slot_of,
            content_stream,
            query_stream,
            memory,
            table,
            ints,
            mats,
            up_weight,
            down_weight,
            row(word_bias),
            row(pos_bias),
        )
        wires += [content_tangent, query_tangent]
        context = context.reshape(klen, width)
        lengths = all_ints[:, micro, : 2 * micro]
        orders = all_ints[seq_id // micro, :micro]
    else:
        lengths = lax.all_gather(counts, "dp", axis=0, tiled=False)
        orders = lax.all_gather(factor_order, "dp", axis=0, tiled=False)[seq_id // micro]
        stream = to_unit(content_stream, query_stream)
        content, query = jnp.where(lead, stream, swap(stream)), stream
        tangent = to_unit(content_tangent, query_tangent)
        piece = mem_part // groups
        spread = lax.all_to_all(
            memory.reshape(micro, groups, piece, width), "dp", split_axis=1, concat_axis=1, tiled=True
        )
        spread = spread.transpose(1, 0, 2, 3).reshape(count, piece, width)
        spread = jnp.take(spread, slot_of, axis=0)
        spread = spread.reshape(groups // 2, tensors, 2, piece // 2, width).transpose(0, 2, 1, 3, 4)
        spread = lax.all_to_all(
            spread.reshape(groups, tensors, piece // 2, width),
            "dp",
            split_axis=0,
            concat_axis=0,
            tiled=True,
        )
        spread = lax.all_to_all(spread, "tensor", split_axis=1, concat_axis=1, tiled=True)
        got = swap(spread)
        mem_rows = jnp.stack([jnp.where(lead, spread, got), jnp.where(lead, got, spread)])
        mem_rows = mem_rows.transpose(2, 1, 0, 3, 4).reshape(mem_total, width)
        context = jnp.concatenate([mem_rows, content], 0)

        def whole(mat):
            mat = lax.all_gather(mat, "tensor", axis=1, tiled=True)
            return lax.all_gather(mat, "dp", axis=0, tiled=True)

        weights = jnp.stack([whole(mat) for mat in mats[:4]])
        wo = whole(out_weight)[None]
        ud = jnp.stack([whole(up_weight), whole(down_weight)])
        keys, values, rel, q_word, q_pos, stream = project(
            weights, context, query, table, row(word_bias), row(pos_bias)
        )

    length = lengths[seq_id // micro, seq_id % micro]
    mem_valid = lengths[slot // micro, micro + slot % micro]
    rank = orders[seq_id % micro]
    key_pos = jnp.arange(klen, dtype=jnp.int32)
    hidden = jnp.int32(1 << 20)
    mem_rank = jnp.where(key_pos[:mem_total] >= mem_total - mem_valid, -1, hidden)
    own_rank = jnp.where(key_pos[:seq_len] < length, rank, hidden)
    key_rank = jnp.concatenate([mem_rank, own_rank])[None, :]
    thr = (rank + jnp.where(lead, 1, 0))[:, None]

    vec, prob, *arrived = attend_forward(
        q_word, q_pos, keys, values, rel, thr, key_rank, block, wires
    )
    if wires:
        wo, ud, tangent = arrived
    out, d_mixed, g_vec, g_out, g_ud, g_upb, small = feed(
        ud,
        wo,
        vec,
        stream,
        tangent,
        row(up_bias),
        jnp.stack([down_bias, first_gain, first_shift, second_gain, second_shift]),
    )
    backward = (prob, g_vec, q_word, q_pos, keys, values, rel, block)
    if groups == 8:
        d_proj, dk_t, dv_t, drel_t, biases, grad_up, grad_down, content_out, query_out = (
            attend_backward(*backward, (g_ud, out))
        )
    else:
        d_proj, dk_t, dv_t, drel_t, biases = attend_backward(*backward)
        content_out, query_out = from_unit(out)
        grad_up, grad_down = scatter_sum(g_ud)
    small = jnp.concatenate([g_upb.reshape(-1), small[:5].reshape(-1), biases.reshape(-1)])
    inner = up_bias.shape[0]
    table_t = jnp.asarray(np.ascontiguousarray(reversed_table(span, klen, width).T))
    if groups == 8:
        size = small.shape[0]
        small = jnp.pad(small, (0, -size % 1024)).reshape(-1, 128)
        arrays = [stream, d_proj, context, dk_t, dv_t, weights, table_t, drel_t]
        (
            grad_key,
            grad_value,
            grad_query,
            grad_pos,
            grad_out,
            content_grad,
            query_grad,
            small,
        ) = finish(arrays, g_out[None], d_mixed, small)
        small = small.reshape(-1)[:size]
    else:
        d_context = tt(dk_t[:, mem_total:], weights[0]) + tt(dv_t[:, mem_total:], weights[1])
        partner = swap(d_context.astype(BF)).astype(F32)
        d_stream = d_mixed + nt(d_proj, weights[2]) + jnp.where(lead, d_context + partner, 0.0)
        content_grad, query_grad = from_unit(d_stream.astype(BF))
        grad_key, grad_value, grad_query, grad_pos = scatter_sum(
            weight_grads(jnp.transpose(stream), jnp.transpose(context), table_t, d_proj, dk_t, dv_t, drel_t)
        )
        (grad_out,) = scatter_sum(g_out[None])
        small = lax.psum(small, ("dp", "tensor"))
    rest = small[inner:].reshape(7, width)
    return (
        content_out,
        query_out,
        content_grad,
        query_grad,
        grad_query,
        grad_key,
        grad_value,
        grad_pos,
        grad_out,
        grad_up,
        small[:inner],
        grad_down,
        rest[0],
        rest[5].reshape(HEADS, DH),
        rest[6].reshape(HEADS, DH),
        rest[1],
        rest[2],
        rest[3],
        rest[4],
    )


def solution(mesh):
    rows = P("dp", "tensor", None)
    mat = P("dp", "tensor")
    return jax.shard_map(
        body,
        mesh=mesh,
        in_specs=(rows,) * 5
        + (P("dp"), P("dp", None), P("dp"), P())
        + (mat,) * 6
        + (P(), mat)
        + (P(),) * 7,
        out_specs=(rows,) * 4 + (mat,) * 6 + (P(), mat) + (P(),) * 7,
        check_vma=False,
    )
```

```python
import functools

import jax
import jax.numpy as jnp
import numpy as np
from jax import lax
from jax.experimental import pallas as pl
from jax.experimental.pallas import tpu as pltpu
from jax.sharding import PartitionSpec as P

HEADS = 12
DH = 64
PAIR = 2 * DH
EPS = 1e-06
BF = jnp.bfloat16
F32 = jnp.float32
LIMIT = 60 * 1024 * 1024
SMEM_SPEC = pl.BlockSpec(memory_space=pltpu.SMEM)
ANY_SPEC = pl.BlockSpec(memory_space=pl.ANY)


def nn(left, right):
    return jnp.dot(left, right, preferred_element_type=F32)


def nt(left, right):
    return lax.dot_general(left, right, (((1,), (1,)), ((), ())), preferred_element_type=F32)


def tn(left, right):
    return lax.dot_general(left, right, (((0,), (0,)), ((), ())), preferred_element_type=F32)


def tt(left, right):
    return lax.dot_general(left, right, (((0,), (1,)), ((), ())), preferred_element_type=F32)


def reversed_table(count, first, width):
    dist = (first - np.arange(count)).astype(np.float32)
    half = width // 2
    power = np.arange(half).astype(np.float32) * np.float32(2.0 / width)
    freq = np.float32(1.0) / np.float32(10000.0) ** power
    angle = (dist[:, None] * freq[None, :]).astype(np.float64)
    return np.concatenate([np.sin(angle), np.cos(angle)], axis=1).astype(np.float32).astype(BF)


MESH = pl.DeviceIdType.MESH
CORE, XBIT, YBIT = 1, 2, 4


class Place:
    def __init__(self):
        self.d, self.z = lax.axis_index("dp"), lax.axis_index("tensor")
        self.core = lax.rem(self.d, 2)
        self.x = lax.rem(lax.div(self.d, 2), 2)
        self.y = lax.div(self.d, 4)

    def dp(self, bits):
        at = self.d
        if bits & CORE:
            at = at + (1 - 2 * self.core)
        if bits & XBIT:
            at = at + (2 - 4 * self.x)
        if bits & YBIT:
            at = at + (4 - 8 * self.y)
        return jnp.minimum(at, 15)

    def up(self, step):
        return lax.rem(self.z + step, 4) if step else self.z


def push(src, dst, send, recv, dp, z):
    return pltpu.make_async_remote_copy(
        src_ref=src,
        dst_ref=dst,
        send_sem=send,
        recv_sem=recv,
        device_id=(dp, z),
        device_id_type=MESH,
    )


def settle(ref, sem):
    pltpu.make_async_copy(ref, ref, sem).wait()


def greet(partners):
    barrier = pltpu.get_barrier_semaphore()
    for partner in partners:
        pl.semaphore_signal(barrier, inc=1, device_id=partner, device_id_type=MESH)
    pl.semaphore_wait(barrier, len(partners))


GATHER = (
    (0, 0, XBIT),
    (0, 1, YBIT),
    (0, 0, YBIT),
    (0, 1, XBIT),
    (XBIT, 0, YBIT),
    (YBIT, 1, XBIT),
    (0, 0, CORE),
    (0, 1, CORE),
    (XBIT, 0, CORE),
    (YBIT, 1, CORE),
    (YBIT, 0, CORE),
    (XBIT, 1, CORE),
    (XBIT | YBIT, 0, CORE),
    (XBIT | YBIT, 1, CORE),
)


class Gather:
    def __init__(self, place, dst, own, send, recv):
        self.place, self.dst, self.own = place, dst, own
        self.send, self.recv = send, recv
        self.half = dst.shape[1] // 16

    def region(self, owner, half):
        at = self.place.dp(owner) * (2 * self.half) + half * self.half
        return self.dst.at[:, pl.ds(pl.multiple_of(at, 16), self.half), :]

    def copy(self, i):
        owner, half, to = GATHER[i]
        src = self.region(owner, half)
        if owner == 0 and self.own is not None:
            src = self.own.at[:, half * self.half : (half + 1) * self.half, :]
        place = self.place
        return push(
            src, self.region(owner, half), self.send.at[i], self.recv.at[i], place.dp(to), place.z
        )

    def start(self, *which):
        for i in which:
            self.copy(i).start()

    def wait(self, received, sent):
        for i in received:
            self.copy(i).wait_recv()
        for i in sent:
            self.copy(i).wait_send()

    def after(self, arrived, started):
        for i, more in zip(arrived, started):
            self.copy(i).wait_recv()
            for j in more:
                self.copy(j).start()

    def middle(self):
        self.after((0, 1), ((4, 8), (5, 9)))

    def last(self):
        self.after((2, 3, 4, 5), ((10,), (11,), (12,), (13,)))


def chip_bits(j):
    return (XBIT if j & 1 else 0) | (YBIT if j & 2 else 0)


def add_into(dst, src):
    def run(i, carry):
        at = pl.ds(pl.multiple_of(i * 16, 16), 16)
        dst[:, at, :] = (dst[:, at, :].astype(F32) + src[:, at, :].astype(F32)).astype(BF)
        return carry

    lax.fori_loop(0, dst.shape[1] // 16, run, 0)


class Reduce:
    def __init__(self, place, sources, scratch, out):
        self.place, self.sources, self.out = place, sources, out
        self.total, self.pair, self.near, self.far, self.quarter, self.stage = scratch[:6]
        self.pair_send, self.pair_recv, self.load, self.send, self.recv, self.z_send, self.z_recv = scratch[6:]
        self.rows = self.total.shape[2]

    @staticmethod
    def scratch(count, n, rows, cols):
        part = cols // 4
        dma = lambda k: pltpu.SemaphoreType.DMA((k,))
        return [
            pltpu.VMEM((n, 4, rows, cols), BF),
            pltpu.VMEM((n, 4, rows, cols), BF),
            pltpu.VMEM((n, 2, 2, rows // 2, cols), BF),
            pltpu.VMEM((n, 2, rows // 2, cols), BF),
            pltpu.VMEM((4, n, rows, part), BF),
            pltpu.VMEM((4, n, rows, part) if part % 128 else (8, 128), BF),
            dma(4 * count),
            dma(4 * count),
            dma(4 * count),
            dma(6),
            dma(6),
            dma(3),
            dma(1),
        ]

    def pair_copies(self, j):
        place, rows = self.place, self.rows
        copies, at = [], 0
        for i, src in enumerate(self.sources):
            slot, n = len(self.sources) * j + i, src.shape[0]
            block = lambda bits: src.at[:, pl.ds(pl.multiple_of(place.dp(bits) * rows, 16), rows), :]
            remote = push(
                block(chip_bits(j) | CORE),
                self.pair.at[at : at + n, j],
                self.pair_send.at[slot],
                self.pair_recv.at[slot],
                place.dp(CORE),
                place.z,
            )
            local = pltpu.make_async_copy(
                block(chip_bits(j)), self.total.at[at : at + n, j], self.load.at[slot]
            )
            copies.append((remote, local))
            at += n
        return copies

    def half(self, j, h):
        size = self.rows // 2
        return self.total.at[:, j, h * size : (h + 1) * size, :]

    MOVES = ((3, 0, XBIT, 1), (3, 1, YBIT, 1), (1, 0, XBIT, 0), (2, 1, YBIT, 0), (2, 0, YBIT, 0), (1, 1, XBIT, 1))

    def move(self, i):
        j, h, to, where = self.MOVES[i]
        dst = self.near.at[:, h, where] if i < 4 else self.far.at[:, where]
        place = self.place
        return push(self.half(j, h), dst, self.send.at[i], self.recv.at[i], place.dp(to), place.z)

    def z_copy(self, k):
        place, part = self.place, self.quarter.shape[3]
        to = place.up(k)
        if part % 128:
            src = self.stage.at[to]
        else:
            src = self.total.at[:, 0, :, pl.ds(pl.multiple_of(to * part, 128), part)]
        dst = self.quarter.at[place.z]
        if k == 0:
            return pltpu.make_async_copy(src, dst, self.z_recv.at[0])
        return push(src, dst, self.z_send.at[k - 1], self.z_recv.at[0], place.d, to)

    def begin(self):
        for j in (3, 1, 2, 0):
            for remote, local in self.pair_copies(j):
                remote.start()
                local.start()

    def pairs(self):
        for j, moves in ((3, (0, 1)), (1, (2,)), (2, (3,)), (0, ())):
            for remote, local in self.pair_copies(j):
                local.wait()
                remote.wait_recv()
            add_into(self.total.at[:, j], self.pair.at[:, j])
            for i in moves:
                self.move(i).start()

    def middle(self):
        for i, j, h, where, more in ((0, 2, 0, 1, 4), (1, 1, 1, 1, 5), (2, 0, 0, 0, None), (3, 0, 1, 0, None)):
            self.move(i).wait_recv()
            add_into(self.half(j, h), self.near.at[:, h, where])
            if more is not None:
                self.move(more).start()

    def late(self):
        for i, h in ((4, 0), (5, 1)):
            self.move(i).wait_recv()
            add_into(self.half(0, h), self.far.at[:, h])
        part = self.quarter.shape[3]
        if part % 128:
            for k in range(4):
                for m in range(self.total.shape[0]):
                    self.stage[k, m] = self.total[m, 0, :, k * part : (k + 1) * part]
        for k in (2, 1, 3, 0):
            self.z_copy(k).start()

    def end(self):
        settle(self.quarter, self.z_recv.at[0])
        parts = [self.quarter[k].astype(F32) for k in range(4)]
        total = (parts[0] + parts[1]) + (parts[2] + parts[3])
        self.out[...] = total.reshape(self.out.shape)
        for j in range(4):
            for remote, _ in self.pair_copies(j):
                remote.wait_send()
        for i in range(6):
            self.move(i).wait_send()
        for k in range(1, 4):
            self.z_copy(k).wait_send()


class Homeward:
    def __init__(self, place, src, homes, send, recv):
        self.place, self.src, self.homes, self.send, self.recv = place, src, homes, send, recv
        self.part = homes[0].shape[1]

    def act(self, what):
        place, part = self.place, self.part
        for u in range(2):

            @pl.when(place.core == u)
            def _():
                for k in (2, 1, 3, 0):
                    to, dp = place.up(k), place.d - place.core + lax.div(place.z, 2)
                    src = self.src.at[pl.ds(pl.multiple_of(to * part, 16), part), :]
                    dst = self.homes[u].at[lax.rem(place.z, 2)]
                    recv = self.recv.at[u]
                    here = jnp.logical_and(dp == place.d, to == place.z)
                    remote = push(src, dst, self.send.at[k], recv, dp, to)
                    if what == "start":
                        pl.when(here)(pltpu.make_async_copy(src, dst, recv).start)
                        pl.when(jnp.logical_not(here))(remote.start)
                    else:
                        pl.when(jnp.logical_not(here))(remote.wait_send)

    def start(self):
        self.act("start")

    def end(self):
        for u in range(2):
            settle(self.homes[u], self.recv.at[u])
        self.act("wait")


def pair_and_z(place):
    return [(place.dp(r), place.up(k)) for k in range(4) for r in (0, CORE) if r or k]


def near_partners(place):
    return pair_and_z(place) + [(place.dp(r), place.z) for r in (XBIT, YBIT)]


INPUTS = 8


def finish_kernel(*refs):
    hbm, (go_ref, mixed_ref, small_ref) = refs[:INPUTS], refs[INPUTS : INPUTS + 3]
    grad_refs, home_refs, sums_ref = refs[INPUTS + 3 : INPUTS + 8], refs[INPUTS + 8 : INPUTS + 10], refs[INPUTS + 10]
    refs = refs[INPUTS + 11 :]
    held, refs = refs[:INPUTS], refs[INPUTS:]
    loads, x_t, ctx_t, g_ref, base, ctx, partner, stream, slots, part_sum, chips = refs[:11]
    home_send, slot_send, chip_send, one_send, recv = refs[11:16]
    refs = refs[16:]
    count = len(refs) // 5
    place = Place()
    d, z, core = place.d, place.z, place.core
    copies = [
        pltpu.make_async_copy(a.at[0:3] if i == 5 else a, b, loads.at[i])
        for i, (a, b) in enumerate(zip(hbm, held))
    ]
    for copy in copies:
        copy.start()

    def need(*which):
        for i in which:
            copies[i].wait()
        return [held[i] for i in which]

    greet(near_partners(place) + [(place.dp(XBIT | YBIT), z)])
    sources = [g_ref.at[m : m + 1] for m in range(4)] + [go_ref]
    key, value, query, pos, out = [
        Reduce(place, (src,), refs[m * count : (m + 1) * count], grad_refs[m])
        for m, src in enumerate(sources)
    ]
    out.begin()
    slot_copies = []
    others = [(r, k) for k in range(4) for r in (0, CORE) if r or k]
    for i, (r, k) in enumerate(others):
        copy = push(small_ref, slots.at[4 * core + z], slot_send.at[i], recv.at[1], place.dp(r), place.up(k))
        copy.start()
        slot_copies.append(copy)
    pltpu.make_async_copy(small_ref, slots.at[4 * core + z], recv.at[1]).start()

    width, block = g_ref.shape[1], 256

    def product(m, left, right, dot):
        def run(i, carry):
            at = pl.ds(pl.multiple_of(i * block, block), block)
            g_ref[m, at, :] = dot(left[at, :], right[...]).astype(BF)
            return carry

        lax.fori_loop(0, width // block, run, 0)

    def turn(src, dst):
        def run(i, carry):
            at = pl.ds(pl.multiple_of(i * block, block), block)
            dst[:, at] = jnp.transpose(src[at, :].astype(F32)).astype(BF)
            return carry

        lax.fori_loop(0, src.shape[0] // block, run, 0)

    x_ref, d_proj = need(0, 1)
    turn(x_ref, x_t)
    product(2, x_t, d_proj, nn)
    query.begin()
    ctx_ref, dk_t = need(2, 3)
    turn(ctx_ref, ctx_t)
    product(0, ctx_t, dk_t, nt)
    key.begin()
    out.pairs()

    dv_t, mats = need(4, 5)
    back = dk_t.shape[1] - base.shape[0]

    def from_context(i, carry):
        at = pl.ds(pl.multiple_of(i * block, block), block)
        cols = pl.ds(pl.multiple_of(i * block + back, block), block)
        turned = nn(mats[0], dk_t[:, cols]) + nn(mats[1], dv_t[:, cols])
        turned = jnp.transpose(turned)
        base[at, :] = turned
        ctx[at, :] = turned.astype(BF)
        return carry

    lax.fori_loop(0, base.shape[0] // block, from_context, 0)
    swap = push(ctx, partner, one_send.at[0], recv.at[0], place.dp(CORE), z)
    swap.start()

    def from_proj(i, carry):
        at = pl.ds(pl.multiple_of(i * block, block), block)
        own = mixed_ref[at, :] + nt(d_proj[at, :], mats[2])
        base[at, :] = own + jnp.where(core == 0, base[at, :], 0.0)
        return carry

    lax.fori_loop(0, base.shape[0] // block, from_proj, 0)
    query.pairs()
    product(1, ctx_t, dv_t, nt)
    value.begin()
    key.pairs()

    swap.wait()
    small_block = 64

    def add_partner(i, carry):
        at = pl.ds(pl.multiple_of(i * small_block, small_block), small_block)
        more = jnp.where(core == 0, partner[at, :].astype(F32), 0.0)
        stream[at, :] = (base[at, :] + more).astype(BF)
        return carry

    lax.fori_loop(0, stream.shape[0] // small_block, add_partner, 0)
    home = Homeward(place, stream, home_refs, home_send, recv.at[2:4])
    home.start()
    out.middle()

    table_t, dr_t = need(6, 7)
    product(3, table_t, dr_t, nt)
    pos.begin()
    value.pairs()
    query.middle()
    out.late()

    settle(slots, recv.at[1])
    total = slots[0]
    for i in range(1, 8):
        total = total + slots[i]
    part_sum[...] = total
    chip = lax.div(d, 2)
    chip_copies = []
    for i, r in enumerate((XBIT, YBIT, XBIT | YBIT)):
        copy = push(part_sum, chips.at[chip], chip_send.at[i], recv.at[4], place.dp(r), z)
        copy.start()
        chip_copies.append(copy)
    pltpu.make_async_copy(part_sum, chips.at[chip], recv.at[4]).start()

    pos.pairs()
    key.middle()
    query.late()
    value.middle()
    key.late()
    pos.middle()
    value.late()
    settle(chips, recv.at[4])
    sums_ref[...] = (chips[0] + chips[1]) + (chips[2] + chips[3])
    pos.late()
    for reduce in (out, query, key, value, pos):
        reduce.end()
    home.end()
    for copy in slot_copies + chip_copies:
        copy.wait_send()


def finish(arrays, g_out, mixed, small):
    total, width = arrays[0].shape
    klen = arrays[2].shape[0]
    rows = width // 8
    vmem = pl.BlockSpec(memory_space=pltpu.VMEM)
    dma = lambda k: pltpu.SemaphoreType.DMA((k,))
    scratch = [pltpu.VMEM((3,) + a.shape[1:] if a.ndim == 3 else a.shape, BF) for a in arrays]
    scratch += [
        dma(INPUTS),
        pltpu.VMEM((width, total), BF),
        pltpu.VMEM((width, klen), BF),
        pltpu.VMEM((4, width, width), BF),
        pltpu.VMEM((total, width), F32),
        pltpu.VMEM((total, width), BF),
        pltpu.VMEM((total, width), BF),
        pltpu.VMEM((total, width), BF),
        pltpu.VMEM((8,) + small.shape, F32),
        pltpu.VMEM(small.shape, F32),
        pltpu.VMEM((4,) + small.shape, F32),
        dma(4),
        dma(7),
        dma(3),
        dma(1),
        dma(5),
    ]
    for _ in range(5):
        scratch += Reduce.scratch(1, 1, rows, width)
    return pl.pallas_call(
        finish_kernel,
        in_specs=[ANY_SPEC] * (INPUTS + 1) + [vmem] * 2,
        out_specs=[vmem] * 5 + [ANY_SPEC] * 2 + [vmem],
        out_shape=[jax.ShapeDtypeStruct((rows, width // 4), F32)] * 5
        + [jax.ShapeDtypeStruct((2, total // 4, width), BF)] * 2
        + [
            jax.ShapeDtypeStruct(small.shape, F32),
        ],
        scratch_shapes=scratch,
        compiler_params=pltpu.CompilerParams(
            collective_id=4, has_side_effects=True, vmem_limit_bytes=LIMIT
        ),
        cost_estimate=pl.CostEstimate(flops=20 << 30, bytes_accessed=64 << 20, transcendentals=0),
        name="finish",
    )(*arrays, g_out, mixed, small)


def emit_kernel(small_ref, *refs):
    count = 11
    for src, dst in zip(refs[:count], refs[count : 2 * count]):
        dst[...] = src[...]
    wide, *rows, word_ref, pos_ref = refs[2 * count :]
    lanes = small_ref.shape[1]
    size = wide.shape[0] // lanes
    wide[...] = small_ref[0:size, :].reshape(wide.shape)
    for ref in rows:
        step = ref.shape[0] // lanes
        ref[...] = small_ref[size : size + step, :].reshape(ref.shape)
        size += step
    for ref in (word_ref, pos_ref):
        for h in range(HEADS):
            at = size + h * DH // lanes
            ref[h : h + 1, :] = small_ref[at : at + 1, h * DH % lanes : h * DH % lanes + DH]
        size += HEADS * DH // lanes


def emit(small, arrays, inner, width):
    vmem = pl.BlockSpec(memory_space=pltpu.VMEM)
    out_shape = [jax.ShapeDtypeStruct(a.shape, a.dtype) for a in arrays]
    out_shape += [jax.ShapeDtypeStruct((inner,), F32)]
    out_shape += [jax.ShapeDtypeStruct((width,), F32)] * 5
    out_shape += [jax.ShapeDtypeStruct((HEADS, DH), F32)] * 2
    return pl.pallas_call(
        emit_kernel,
        in_specs=[vmem] * (1 + len(arrays)),
        out_specs=[vmem] * len(out_shape),
        out_shape=out_shape,
        compiler_params=pltpu.CompilerParams(vmem_limit_bytes=LIMIT),
        name="emit",
    )(small, *arrays)


def pack(mat):
    half = mat.shape[0] // 2
    return jnp.concatenate([mat[:, :128], jnp.concatenate([mat[:half, 128:], mat[half:, 128:]], axis=1)], axis=0)


def unpack(packed):
    rows = packed.shape[0] * 2 // 3
    rest = packed[rows:, :]
    return jnp.concatenate([packed[:rows, :], jnp.concatenate([rest[:, :64], rest[:, 64:]], axis=0)], axis=1)


def enter_kernel(slot_ref, seq_ref, mem_ref, content, query, memory, table_hbm, orders, *refs):
    mats, (upw, dnw), (wb_ref, pb_ref) = refs[:5], refs[5:7], refs[7:9]
    outs, (thr_ref, key_ref, whole_out, context_out, wo, ud) = refs[9:15], refs[15:21]
    (
        ints,
        all_ints,
        whole,
        context,
        stream,
        table,
        spread,
        picked,
        shards,
        slab,
        mat_send,
        mat_recv,
        ud_send,
        ud_recv,
        int_send,
        spread_send,
        pick_send,
        stream_send,
        pair_send,
        gather_send,
        gather_recv,
        wo_send,
        wo_recv,
        far_send,
        far_recv,
        recv,
        local,
    ) = refs[21:]
    place = Place()
    d, z, core = place.d, place.z, place.core
    up, down, far = place.up(1), place.up(3), place.up(2)
    part = query.shape[1]
    micro = orders.shape[0]
    spot = lax.broadcasted_iota(jnp.int32, (1, ints.shape[1]), 1)
    lengths = jnp.where(spot == 0, seq_ref[0], seq_ref[1])
    lengths = jnp.where(spot < 2, lengths, jnp.where(spot == 2, mem_ref[0], mem_ref[1]))
    ints[...] = jnp.concatenate([orders[...], jnp.broadcast_to(lengths, (6, ints.shape[1]))], axis=0)

    def slot_of(seq):
        at = jnp.int32(0)
        for k in range(16):
            at = at + jnp.where(slot_ref[k] == seq, k, 0)
        return jnp.minimum(at, 15)

    pltpu.make_async_copy(table_hbm, table, local.at[0]).start()
    piece = spread.shape[1]
    blocks = part // piece // 2
    first = 4 * blocks
    greet([(place.dp(r), place.up(k)) for r in range(8) for k in range(4) if r or k])

    spread_copies = []
    for r in range(8):
        to = place.dp(r)
        src = memory.at[:, pl.ds(pl.multiple_of(to * piece, 16), piece), :]
        dst = spread.at[pl.ds(2 * d, 2)]
        if r == 0:
            pltpu.make_async_copy(src, dst, recv.at[0]).start()
        else:
            spread_copies.append(push(src, dst, spread_send.at[r - 1], recv.at[0], to, z))
            spread_copies[-1].start()

    for m, mat in enumerate(mats):
        shards[z, m] = pack(mat[...])
    cutoff = shards.shape[2] * 5 // 9

    def mat_copy(i):
        own = shards.at[z]
        low, high = shards.at[down, :, :cutoff], shards.at[up, :, cutoff:]
        src = (own, own, low, high)[i]
        return push(src, src, mat_send.at[i], mat_recv.at[i], d, (up, down, up, down)[i])

    mat_copy(0).start()
    mat_copy(1).start()
    rows = slab.shape[1]
    width = upw.shape[1]

    def columns(at, start=0, size=rows):
        mine = pl.ds(pl.multiple_of(d * rows + start, 16), size)
        return ud.at[:, mine, pl.ds(pl.multiple_of(at * width, 128), width)]

    def ud_copy(i):
        if i < 4:
            src, dst = (upw, dnw)[i % 2], columns(z).at[i % 2]
            return push(src, dst, ud_send.at[i], ud_recv.at[i // 2], d, (up, down)[i // 2])
        half = rows // 2
        src = columns(down, 0, half) if i == 4 else columns(up, half, half)
        return push(src, src, ud_send.at[i], ud_recv.at[i - 2], d, (up, down)[i - 4])

    for i in range(4):
        ud_copy(i).start()
    for m, mat in enumerate((upw, dnw)):
        pltpu.make_async_copy(mat, columns(z).at[m], recv.at[8]).start()

    int_copies = []
    for r in range(8):
        if r == 0:
            pltpu.make_async_copy(ints, all_ints.at[d], recv.at[2]).start()
        else:
            copy = push(ints, all_ints.at[d], int_send.at[r - 1], recv.at[2], place.dp(r), z)
            int_copies.append(copy)
            copy.start()

    def stream_copy(i, act):
        j, kind = i // 2, i % 2
        to, dp = 2 * core + j, d - core + kind
        if kind == 0:
            src, sem = content.at[j], recv.at[3]
            dst = context.at[pl.ds(first + blocks * z, blocks)]
        else:
            src, sem = query.at[j], recv.at[4]
            dst = stream.at[pl.ds(pl.multiple_of(z * part, 16), part), :]
        here = jnp.logical_and(dp == d, to == z)
        remote = push(src, dst, stream_send.at[i], sem, dp, to)
        if act == "start":
            pl.when(here)(pltpu.make_async_copy(src, dst, sem).start)
            pl.when(jnp.logical_not(here))(remote.start)
        else:
            pl.when(jnp.logical_not(here))(remote.wait_send)

    mat_copy(0).wait_recv()
    mat_copy(2).start()
    mat_copy(1).wait_recv()
    mat_copy(3).start()
    mat_copy(2).wait_recv()
    mat_copy(3).wait_recv()
    for m in range(5):
        slab[m] = jnp.concatenate([unpack(shards[k, m]) for k in range(4)], axis=1)
    own_rows = pl.ds(pl.multiple_of(d * rows, 16), rows)
    gather = Gather(place, whole, slab.at[0:4], gather_send, gather_recv)
    gather.start(0, 1, 2, 3, 6, 7)
    pltpu.make_async_copy(slab.at[0:4], whole.at[:, own_rows, :], recv.at[6]).start()
    pltpu.make_async_copy(slab.at[4:5], wo.at[:, own_rows, :], recv.at[7]).start()

    settle(columns(down), ud_recv.at[0])
    ud_copy(4).start()
    settle(columns(up), ud_recv.at[1])
    ud_copy(5).start()
    for i in range(4):
        stream_copy(i, "start")

    settle(spread, recv.at[0])
    for q in range(16):
        picked[q] = spread[slot_of(q)]
    pick_copies = []
    for r in (YBIT | XBIT, XBIT, YBIT, 0):
        for k in range(4):
            to, lane = place.dp(r), place.up(k)
            src = picked.at[4 * lax.div(to, 2) + lane]
            dst = context.at[blocks * z + lax.div(d, 2), core]
            if r or k:
                copy = push(src, dst, pick_send.at[2 * r + k - 1], recv.at[5], to, lane)
                pick_copies.append(copy)
            else:
                copy = pltpu.make_async_copy(src, dst, recv.at[5])
            copy.start()

    gather.middle()
    wo_gather = Gather(place, wo, slab.at[4:5], wo_send, wo_recv)
    ud_gather = Gather(place, ud, None, far_send, far_recv)
    gathers = (ud_gather, wo_gather)
    settle(columns(z), recv.at[8])
    ud_copy(4).wait_recv()
    ud_copy(5).wait_recv()
    for i in (0, 1, 2, 3, 6, 7):
        for one in gathers:
            one.start(i)
    gather.last()

    pick_pair = push(
        context.at[0:first, core], context.at[0:first, core], pair_send.at[0], recv.at[1], place.dp(CORE), z
    )
    settle(context.at[0:first, core], recv.at[5])
    pick_pair.start()
    lead_copy = push(
        context.at[first:], context.at[first:], pair_send.at[1], recv.at[3], place.dp(CORE), z
    )

    @pl.when(core == 0)
    def _():
        settle(context.at[first:], recv.at[3])
        lead_copy.start()

    settle(all_ints, recv.at[2])
    seq = 4 * lax.div(d, 2) + z
    slot = slot_of(seq)
    odd = lax.rem(seq, micro)
    own, other = all_ints[lax.div(seq, micro)], all_ints[lax.div(slot, micro)]

    def pick(row, at):
        return jnp.sum(jnp.where(spot == at, row.astype(F32), 0.0), axis=1, keepdims=True)

    length = pick(own[2:3], odd)
    mem_valid = pick(other[2:3], micro + lax.rem(slot, micro))
    rank = jnp.where(odd == 0, own[0:1], own[1:2])
    seq_len = rank.shape[1]
    mem_total = key_ref.shape[1] - seq_len
    where = spot.astype(F32)
    hidden = jnp.int32(1 << 20)
    key_ref[:, :mem_total] = jnp.where(where >= mem_total - mem_valid, -1, hidden)
    key_ref[:, mem_total:] = jnp.where(where < length, rank, hidden)
    ranks = jnp.transpose(jnp.broadcast_to(rank.astype(F32), (8, seq_len)))
    thr_ref[...] = ranks[:, 0:1].astype(jnp.int32) + jnp.where(core == 0, 1, 0)

    gather.wait(range(6, 14), ())
    settle(whole.at[:, own_rows, :], recv.at[6])
    keep_whole = pltpu.make_async_copy(whole, whole_out, local.at[1])
    keep_whole.start()

    keep_context = pltpu.make_async_copy(context, context_out, local.at[2])

    def before_stream():
        pick_pair.wait()

        @pl.when(core == 0)
        def _():
            lead_copy.wait_send()

        @pl.when(core == 1)
        def _():
            settle(context.at[first:], recv.at[3])
            settle(stream, recv.at[4])

        keep_context.start()

    def before_context():
        for one in gathers:
            one.after((0, 1), ((8,), (9,)))

    pltpu.make_async_copy(table_hbm, table, local.at[0]).wait()
    project_step(
        whole, context, stream, table, wb_ref, pb_ref, *outs, hooks=(before_stream, before_context)
    )
    for one in gathers:
        one.after((2, 3), ((10,), (11,)))
    settle(wo.at[:, own_rows, :], recv.at[7])
    gather.wait((), range(14))
    for one in gathers:
        one.wait(range(6, 12), (0, 1, 2, 3) + tuple(range(6, 12)))
    keep_whole.wait()
    keep_context.wait()
    for i in range(4):
        stream_copy(i, "wait")
        mat_copy(i).wait_send()
    for i in range(6):
        ud_copy(i).wait_send()
    for copy in spread_copies + int_copies + pick_copies:
        copy.wait_send()


def enter(slots, seqs, mems, content, query, memory, table, orders, mats, upw, dnw, wb, pb):
    micro, part, width = content.shape
    rows = mats[0].shape[0]
    inner = upw.shape[1] * 4
    piece = part // 8
    klen, span, seq = 8 * part, table.shape[0], 4 * part
    vmem = pl.BlockSpec(memory_space=pltpu.VMEM)
    dma = lambda n: pltpu.SemaphoreType.DMA((n,))
    bf = lambda *shape: jax.ShapeDtypeStruct(shape, BF)
    return pl.pallas_call(
        enter_kernel,
        in_specs=[SMEM_SPEC] * 3 + [ANY_SPEC] * 4 + [vmem] * 10,
        out_specs=[vmem] * 8 + [ANY_SPEC] * 4,
        out_shape=[
            bf(klen, width),
            bf(klen, width),
            bf(span, width),
            bf(seq, width),
            bf(seq, width),
            bf(seq, width),
            jax.ShapeDtypeStruct((seq, 1), jnp.int32),
            jax.ShapeDtypeStruct((1, klen), jnp.int32),
            bf(4, 8 * rows, width),
            bf(32, 2, piece, width),
            bf(1, 8 * rows, width),
            bf(2, 8 * rows, inner),
        ],
        scratch_shapes=[
            pltpu.VMEM((8, seq), jnp.int32),
            pltpu.VMEM((8, 8, seq), jnp.int32),
            pltpu.VMEM((4, 8 * rows, width), BF),
            pltpu.VMEM((32, 2, piece, width), BF),
            pltpu.VMEM((seq, width), BF),
            pltpu.VMEM((span, width), BF),
            pltpu.VMEM((16, piece, width), BF),
            pltpu.VMEM((16, piece, width), BF),
            pltpu.VMEM((4, 5, rows * 3 // 2, 128), BF),
            pltpu.VMEM((5, rows, width), BF),
            dma(4),
            dma(4),
            dma(6),
            dma(4),
            dma(7),
            dma(7),
            dma(15),
            dma(4),
            dma(2),
            dma(14),
            dma(14),
            dma(14),
            dma(14),
            dma(14),
            dma(14),
            dma(9),
            dma(3),
        ],
        compiler_params=pltpu.CompilerParams(
            collective_id=1, has_side_effects=True, vmem_limit_bytes=LIMIT
        ),
        cost_estimate=pl.CostEstimate(flops=0, bytes_accessed=64 << 20, transcendentals=0),
        name="enter",
    )(
        slots,
        seqs,
        mems,
        content.reshape(micro, 4, 2, piece, width),
        query,
        memory,
        table,
        orders,
        *mats,
        upw,
        dnw,
        wb,
        pb,
    )


def head_lanes(array, head):
    lane = lax.broadcasted_iota(jnp.int32, array.shape, 1)
    return jnp.where((lane >= DH) == (head == 1), array, jnp.zeros_like(array))


def attend_forward_step(
    block, qw_ref, qp_ref, k_ref, v_ref, rel_ref, thr_ref, kr_ref, vec_ref, prob_ref
):
    rows, klen = qw_ref.shape[0], k_ref.shape[0]
    width = klen + block
    keys, values = k_ref[...], v_ref[...]
    for part in range(rows // block):
        at = slice(part * block, (part + 1) * block)
        first = rows - (part + 1) * block
        qw, qp = qw_ref[at, :], qp_ref[at, :]
        rel = rel_ref[first : first + width, :]
        seen = kr_ref[...] < thr_ref[at, :]
        vecs = []
        for head in range(2):
            raw = nt(head_lanes(qp, head), rel)
            moved = pltpu.roll(raw, 0, 1, stride=1, stride_axis=0)[:, block:]
            score = nt(head_lanes(qw, head), keys) + moved
            score = jnp.where(seen, score, -1e30)
            expo = jnp.exp(score - jnp.max(score, axis=1, keepdims=True))
            prob = (expo * (1.0 / jnp.sum(expo, axis=1, keepdims=True))).astype(BF)
            prob_ref[head, at, :] = prob
            vecs.append(nn(prob, values))
        lane = lax.broadcasted_iota(jnp.int32, vecs[0].shape, 1)
        vec_ref[at, :] = jnp.where(lane < DH, vecs[0], vecs[1]).astype(BF)


def attend_forward_kernel(block, wired, *refs):
    if not wired:
        attend_forward_step(block, *refs)
        return
    ins, (ctan, qtan) = refs[:7], refs[9:11]
    outs, (wo, ud, tangent) = refs[11:13], refs[13:16]
    out_send, out_recv, ud_send, ud_recv, tan_send, recv = refs[16:]
    step, steps = pl.program_id(0), pl.num_programs(0)
    place = Place()
    d, z, core = place.d, place.z, place.core
    gathers = (
        Gather(place, ud, None, ud_send, ud_recv),
        Gather(place, wo, None, out_send, out_recv),
    )
    part = ctan.shape[1]

    def tan_copy(i, act):
        j, kind = i // 2, i % 2
        to, dp = 2 * core + j, d - core + kind
        src = (ctan, qtan)[kind].at[j]
        dst = tangent.at[pl.ds(pl.multiple_of(z * part, 16), part), :]
        here = jnp.logical_and(dp == d, to == z)
        local = pltpu.make_async_copy(src, dst, recv.at[0])
        remote = push(src, dst, tan_send.at[i], recv.at[0], dp, to)
        if act == "start":
            pl.when(here)(local.start)
            pl.when(jnp.logical_not(here))(remote.start)
        else:
            pl.when(jnp.logical_not(here))(remote.wait_send)

    @pl.when(step == 0)
    def _():
        greet(near_partners(place))
        for gather in gathers:
            gather.start(4, 5)
        for i in range(4):
            tan_copy(i, "start")

    @pl.when(step == steps - 1)
    def _():
        for gather in gathers:
            gather.after((4, 5), ((12,), (13,)))

    attend_forward_step(block, *ins, *outs)

    @pl.when(step == steps - 1)
    def _():
        for gather in gathers:
            gather.wait((12, 13), (4, 5, 12, 13))
        settle(tangent, recv.at[0])
        for i in range(4):
            tan_copy(i, "wait")


def attend_forward(qw, qp, keys, values, rel, thr, key_rank, block, wires=()):
    rows, width = qw.shape
    klen, span = keys.shape[0], rel.shape[0]
    col = lambda count: pl.BlockSpec((count, PAIR), lambda p: (0, p))
    in_specs = [
        col(rows),
        col(rows),
        col(klen),
        col(klen),
        col(span),
        pl.BlockSpec((rows, 1), lambda p: (0, 0)),
        pl.BlockSpec((1, klen), lambda p: (0, 0)),
    ]
    out_specs = [col(rows), pl.BlockSpec((2, rows, klen), lambda p: (p, 0, 0))]
    out_shape = [
        jax.ShapeDtypeStruct((rows, width), BF),
        jax.ShapeDtypeStruct((width // DH, rows, klen), BF),
    ]
    params = dict(vmem_limit_bytes=LIMIT)
    scratch = []
    if wires:
        in_specs += [ANY_SPEC] * 4
        out_specs += [ANY_SPEC] * 3
        out_shape += [
            jax.ShapeDtypeStruct(wires[0].shape, BF),
            jax.ShapeDtypeStruct(wires[1].shape, BF),
            jax.ShapeDtypeStruct((rows, width), BF),
        ]
        scratch = [pltpu.SemaphoreType.DMA((n,)) for n in (14, 14, 14, 14, 4, 1)]
        params.update(collective_id=2, has_side_effects=True)
    return pl.pallas_call(
        functools.partial(attend_forward_kernel, block, bool(wires)),
        grid=(width // PAIR,),
        in_specs=in_specs,
        out_specs=out_specs,
        out_shape=out_shape,
        scratch_shapes=scratch,
        input_output_aliases={7: 2, 8: 3} if wires else {},
        compiler_params=pltpu.CompilerParams(**params),
        cost_estimate=pl.CostEstimate(
            flops=8 * rows * klen * width, bytes_accessed=16 << 20, transcendentals=12 * rows * klen
        ),
        name="attend_forward",
    )(qw, qp, keys, values, rel, thr, key_rank, *wires)


def attend_backward_kernel(block, wired, *refs):
    if not wired:
        attend_backward_step(block, *refs)
        return
    ins, (g_ud, src) = refs[:7], refs[7:9]
    outs, grad_refs, home_refs = refs[9:14], refs[14:16], refs[16:18]
    rel_acc, home_send, home_recv = refs[18:21]
    step, steps = pl.program_id(0), pl.num_programs(0)
    place = Place()
    count = len(refs[21:]) // 2
    reduces = [
        Reduce(place, (g_ud.at[m : m + 1],), refs[21 + m * count : 21 + (m + 1) * count], grad_refs[m])
        for m in range(2)
    ]
    home = Homeward(place, src, home_refs, home_send, home_recv)

    @pl.when(step == 0)
    def _():
        greet(near_partners(place))
        for reduce in reduces:
            reduce.begin()
        home.start()

    @pl.when(step == 2)
    def _():
        reduces[0].pairs()

    @pl.when(step == 3)
    def _():
        reduces[1].pairs()

    @pl.when(step == 5)
    def _():
        reduces[0].middle()

    attend_backward_step(block, *ins, *outs, rel_acc)

    @pl.when(step == steps - 1)
    def _():
        reduces[0].late()
        reduces[1].middle()
        reduces[1].late()
        reduces[0].end()
        reduces[1].end()
        home.end()


def attend_backward_step(
    block,
    prob_ref,
    gvec_ref,
    qw_ref,
    qp_ref,
    k_ref,
    v_ref,
    rel_ref,
    dproj_ref,
    dk_ref,
    dv_ref,
    drel_ref,
    bias_ref,
    rel_acc,
):
    rows, klen = qw_ref.shape[0], k_ref.shape[0]
    width = klen + block
    keys, values = k_ref[...], v_ref[...]
    row = lax.broadcasted_iota(jnp.int32, (block, block), 0)
    col = lax.broadcasted_iota(jnp.int32, (block, block), 1)
    mirror = (row + col == block - 1).astype(BF)
    rel_acc[...] = jnp.zeros_like(rel_acc)
    d_keys, d_values = [None, None], [None, None]
    word_sum = jnp.zeros((1, PAIR), F32)
    pos_sum = jnp.zeros((1, PAIR), F32)
    for part in range(rows // block):
        at = slice(part * block, (part + 1) * block)
        first = rows - (part + 1) * block
        gvec, qw = gvec_ref[at, :], qw_ref[at, :]
        gvec_t = jnp.transpose(gvec.astype(F32)).astype(BF)
        qw_t = jnp.transpose(qw.astype(F32)).astype(BF)
        qp_t = jnp.transpose(nn(mirror, qp_ref[at, :])).astype(BF)
        rel = rel_ref[first : first + width, :]
        word_parts, pos_parts = [], []
        for head in range(2):
            own = slice(head * DH, (head + 1) * DH)
            prob = prob_ref[head, at, :]
            d_prob = nt(head_lanes(gvec, head), values)
            weight = prob.astype(F32)
            inner = jnp.sum(weight * d_prob, axis=1, keepdims=True)
            g_sum = (weight * (d_prob - inner) * 0.125).astype(BF)
            dv = nn(gvec_t[own, :], prob)
            dk = nn(qw_t[own, :], g_sum)
            d_values[head] = dv if part == 0 else d_values[head] + dv
            d_keys[head] = dk if part == 0 else d_keys[head] + dk
            turned = nn(mirror, g_sum)
            padded = jnp.concatenate([jnp.zeros((block, block), F32), turned], axis=1)
            moved = pltpu.roll(padded, width - block + 1, 1, stride=1, stride_axis=0).astype(BF)
            word_parts.append(nn(turned.astype(BF), keys))
            pos_parts.append(nn(moved, rel))
            rel_acc[own, first : first + width] += nn(qp_t[own, :], moved)
        lane = lax.broadcasted_iota(jnp.int32, word_parts[0].shape, 1)
        word = jnp.where(lane < DH, word_parts[0], word_parts[1])
        pos = jnp.where(lane < DH, pos_parts[0], pos_parts[1])
        word_sum = word_sum + jnp.sum(word, axis=0, keepdims=True)
        pos_sum = pos_sum + jnp.sum(pos, axis=0, keepdims=True)
        dproj_ref[at, :] = nn(mirror, (word + pos).astype(BF)).astype(BF)
    for head in range(2):
        own = slice(head * DH, (head + 1) * DH)
        dv_ref[own, :] = d_values[head].astype(BF)
        dk_ref[own, :] = (8.0 * d_keys[head]).astype(BF)
    drel_ref[...] = (8.0 * rel_acc[...]).astype(BF)
    bias_ref[0:1, :] = word_sum
    bias_ref[1:2, :] = pos_sum


def attend_backward(prob, gvec, qw, qp, keys, values, rel, block, wires=()):
    rows, width = qw.shape
    klen, span = keys.shape[0], rel.shape[0]
    col = lambda count: pl.BlockSpec((count, PAIR), lambda p: (0, p))
    rowb = lambda count: pl.BlockSpec((PAIR, count), lambda p: (p, 0))
    in_specs = [
        pl.BlockSpec((2, rows, klen), lambda p: (p, 0, 0)),
        col(rows),
        col(rows),
        col(rows),
        col(klen),
        col(klen),
        col(span),
    ]
    out_specs = [col(rows), rowb(klen), rowb(klen), rowb(span), col(2)]
    out_shape = [
        jax.ShapeDtypeStruct((rows, width), BF),
        jax.ShapeDtypeStruct((width, klen), BF),
        jax.ShapeDtypeStruct((width, klen), BF),
        jax.ShapeDtypeStruct((width, span), BF),
        jax.ShapeDtypeStruct((2, width), F32),
    ]
    scratch = [pltpu.VMEM((PAIR, span), F32)]
    params = dict(vmem_limit_bytes=LIMIT)
    if wires:
        inner, mine = wires[0].shape[2], width // 8
        in_specs += [ANY_SPEC, ANY_SPEC]
        out_specs += [pl.BlockSpec(memory_space=pltpu.VMEM)] * 2 + [ANY_SPEC] * 2
        out_shape += [jax.ShapeDtypeStruct((mine, inner // 4), F32)] * 2
        out_shape += [jax.ShapeDtypeStruct((2, rows // 4, width), BF)] * 2
        scratch += [pltpu.SemaphoreType.DMA((4,)), pltpu.SemaphoreType.DMA((2,))]
        scratch += 2 * Reduce.scratch(1, 1, mine, inner)
        params.update(collective_id=3, has_side_effects=True)
    return pl.pallas_call(
        functools.partial(attend_backward_kernel, block, bool(wires)),
        grid=(width // PAIR,),
        in_specs=in_specs,
        out_specs=out_specs,
        out_shape=out_shape,
        scratch_shapes=scratch,
        compiler_params=pltpu.CompilerParams(**params),
        cost_estimate=pl.CostEstimate(
            flops=16 * rows * klen * width, bytes_accessed=20 << 20, transcendentals=0
        ),
        name="attend_backward",
    )(prob, gvec, qw, qp, keys, values, rel, *wires)


def norm_parts(value):
    center = value - jnp.mean(value, axis=1, keepdims=True)
    scale = lax.rsqrt(jnp.mean(center * center, axis=1, keepdims=True) + EPS)
    return center * scale, scale


def norm_pull(normed, scale, err):
    inner = jnp.mean(err * normed, axis=1, keepdims=True)
    return (err - jnp.mean(err, axis=1, keepdims=True) - normed * inner) * scale


def sum_rows(value):
    return jnp.sum(value, axis=0, keepdims=True)


def feed_kernel(steps, *refs):
    (
        ud_hbm,
        wo_hbm,
        vec_ref,
        x_ref,
        tan_ref,
        upb_ref,
        dnb_ref,
        g1_ref,
        s1_ref,
        g2_ref,
        s2_ref,
        out_ref,
        dmix_ref,
        gvec_ref,
        go_ref,
        gud_ref,
        gupb_ref,
        small_ref,
        ud_ref,
        wo_ref,
        n1_ref,
        r1_ref,
        fb_ref,
        fbt_ref,
        acc_ref,
        act_ref,
        slope_ref,
        gd_ref,
        gdt_ref,
        sems,
    ) = refs
    step = pl.program_id(0)
    chunk = act_ref.shape[2]
    row = lambda ref: ref[...].reshape(1, -1)
    cols = pl.ds(pl.multiple_of(lax.rem(step, steps) * chunk, chunk), chunk)

    @pl.when(step == 0)
    def _():
        wo_copy = pltpu.make_async_copy(wo_hbm, wo_ref, sems.at[0])
        ud_copy = pltpu.make_async_copy(ud_hbm, ud_ref, sems.at[1])
        wo_copy.start()
        ud_copy.start()
        wo_copy.wait()
        normed, scale = norm_parts(nt(vec_ref[...], wo_ref[0]) + x_ref[...].astype(F32))
        n1_ref[...] = normed
        r1_ref[...] = scale
        first = normed * row(g1_ref) + row(s1_ref)
        fb_ref[...] = first.astype(BF)
        fbt_ref[...] = jnp.transpose(first).astype(BF)
        acc_ref[...] = first + row(dnb_ref)
        ud_copy.wait()

    @pl.when(step < steps)
    def _():
        upper = nn(fb_ref[...], ud_ref[0, :, cols]) + row(upb_ref)
        square = upper * upper
        root = 0.7978845608028654
        bend = jnp.tanh(root * (upper + 0.044715 * (square * upper)))
        half = 0.5 * (1.0 + bend)
        act = (upper * half).astype(BF)
        act_ref[step] = act
        slope_ref[step] = half + 0.5 * upper * (1.0 - bend * bend) * (
            root + (3 * 0.044715 * root) * square
        )
        acc_ref[...] += nt(act, ud_ref[1, :, cols])

    @pl.when(step == steps - 1)
    def _():
        normed, scale = norm_parts(acc_ref[...])
        out_ref[...] = (normed * row(g2_ref) + row(s2_ref)).astype(BF)
        tan = tan_ref[...].astype(F32)
        d_down = norm_pull(normed, scale, tan * row(g2_ref))
        small_ref[0:1, :] = sum_rows(d_down)
        small_ref[3:4, :] = sum_rows(tan * normed)
        small_ref[4:5, :] = sum_rows(tan)
        gd_ref[...] = d_down.astype(BF)
        gdt_ref[...] = jnp.transpose(d_down).astype(BF)
        acc_ref[...] = d_down

    @pl.when(step >= steps)
    def _():
        at = step - steps
        d_up = nn(gd_ref[...], ud_ref[1, :, cols]) * slope_ref[at]
        gupb_ref[...] = sum_rows(d_up)
        g_up = d_up.astype(BF)
        acc_ref[...] += nt(g_up, ud_ref[0, :, cols])
        gud_ref[0] = nn(fbt_ref[...], g_up).astype(BF)
        gud_ref[1] = nn(gdt_ref[...], act_ref[at]).astype(BF)

    @pl.when(step == 2 * steps - 1)
    def _():
        d_first, normed = acc_ref[...], n1_ref[...]
        small_ref[1:2, :] = sum_rows(d_first * normed)
        small_ref[2:3, :] = sum_rows(d_first)
        d_mixed = norm_pull(normed, r1_ref[...], d_first * row(g1_ref))
        dmix_ref[...] = d_mixed
        gvec_ref[...] = nn(d_mixed.astype(BF), wo_ref[0]).astype(BF)
        gdt_ref[...] = jnp.transpose(d_mixed).astype(BF)
        go_ref[...] = nn(gdt_ref[...], vec_ref[...]).astype(BF)


def feed(ud, wo, vec, x, tan, upb, vecs):
    rows, width = vec.shape
    inner = upb.shape[0]
    chunk = 512
    steps = inner // chunk
    whole = lambda a, b: pl.BlockSpec((a, b), lambda i: (0, 0))
    late = lambda i: jnp.maximum(i - steps, 0)
    grads = pl.BlockSpec((2, width, chunk), lambda i: (0, 0, late(i)))
    return pl.pallas_call(
        functools.partial(feed_kernel, steps),
        grid=(2 * steps,),
        in_specs=[ANY_SPEC] * 2
        + [whole(rows, width)] * 3
        + [pl.BlockSpec((chunk,), lambda i: (lax.rem(i, steps),))]
        + [pl.BlockSpec((width,), lambda i: (0,))] * 5,
        out_specs=[
            whole(rows, width),
            whole(rows, width),
            whole(rows, width),
            whole(width, width),
            grads,
            pl.BlockSpec((1, chunk), lambda i: (0, late(i))),
            whole(8, width),
        ],
        out_shape=[
            jax.ShapeDtypeStruct((rows, width), BF),
            jax.ShapeDtypeStruct((rows, width), F32),
            jax.ShapeDtypeStruct((rows, width), BF),
            jax.ShapeDtypeStruct((width, width), BF),
            jax.ShapeDtypeStruct((2, width, inner), BF),
            jax.ShapeDtypeStruct((1, inner), F32),
            jax.ShapeDtypeStruct((8, width), F32),
        ],
        scratch_shapes=[
            pltpu.VMEM((2, width, inner), BF),
            pltpu.VMEM((1, width, width), BF),
            pltpu.VMEM((rows, width), F32),
            pltpu.VMEM((rows, 1), F32),
            pltpu.VMEM((rows, width), BF),
            pltpu.VMEM((width, rows), BF),
            pltpu.VMEM((rows, width), F32),
            pltpu.VMEM((steps, rows, chunk), BF),
            pltpu.VMEM((steps, rows, chunk), F32),
            pltpu.VMEM((rows, width), BF),
            pltpu.VMEM((width, rows), BF),
            pltpu.SemaphoreType.DMA((2,)),
        ],
        compiler_params=pltpu.CompilerParams(vmem_limit_bytes=LIMIT),
        cost_estimate=pl.CostEstimate(
            flops=12 * rows * width * inner, bytes_accessed=36 << 20, transcendentals=rows * inner
        ),
        name="feed",
    )(ud, wo, vec, x, tan, upb, *vecs)


def project_step(
    w_ref,
    ctx_ref,
    q_ref,
    table_ref,
    wb_ref,
    pb_ref,
    k_ref,
    v_ref,
    rel_ref,
    qw_ref,
    qp_ref,
    x_ref,
    hooks=(),
):
    lead = lax.rem(lax.axis_index("dp"), 2) == 0
    flat = lambda ref: jnp.concatenate([ref[h : h + 1, :] for h in range(ref.shape[0])], axis=1)
    word_bias, pos_bias = flat(wb_ref), flat(pb_ref)
    klen, width = k_ref.shape
    back = klen - q_ref.shape[0]

    def context_rows(start):
        at = pl.ds(lax.div(start, 32), block // 32)
        return ctx_ref[at].reshape(block, width)

    block = 256

    def loop(count, step):
        def run(i, carry):
            step(pl.ds(pl.multiple_of(i * block, block), block))
            return carry

        lax.fori_loop(0, count // block, run, 0)

    def context_step(at):
        rows = context_rows(at.start)
        k_ref[at, :] = nn(rows, w_ref[0]).astype(BF)
        v_ref[at, :] = nn(rows, w_ref[1]).astype(BF)

    def stream_step(at):
        x_ref[at, :] = jnp.where(lead, context_rows(at.start + back), q_ref[at, :])
        proj = nn(x_ref[at, :], w_ref[2])
        qw_ref[at, :] = (0.125 * (proj + word_bias).astype(BF).astype(F32)).astype(BF)
        qp_ref[at, :] = (0.125 * (proj + pos_bias).astype(BF).astype(F32)).astype(BF)

    def table_step(at):
        rel_ref[at, :] = nn(table_ref[at, :], w_ref[3]).astype(BF)

    loop(table_ref.shape[0], table_step)
    if hooks:
        hooks[0]()
    loop(q_ref.shape[0], stream_step)
    if hooks:
        hooks[1]()
    loop(klen, context_step)


def project(mats, context, query, table, wb, pb):
    rows, width = query.shape
    klen, span = context.shape[0], table.shape[0]
    vmem = pl.BlockSpec(memory_space=pltpu.VMEM)
    return pl.pallas_call(
        project_step,
        in_specs=[vmem] * 6,
        out_specs=[vmem] * 6,
        out_shape=[
            jax.ShapeDtypeStruct((klen, width), BF),
            jax.ShapeDtypeStruct((klen, width), BF),
            jax.ShapeDtypeStruct((span, width), BF),
            jax.ShapeDtypeStruct((rows, width), BF),
            jax.ShapeDtypeStruct((rows, width), BF),
            jax.ShapeDtypeStruct((rows, width), BF),
        ],
        compiler_params=pltpu.CompilerParams(vmem_limit_bytes=LIMIT),
        cost_estimate=pl.CostEstimate(
            flops=2 * (2 * klen + rows + span) * width * width,
            bytes_accessed=20 << 20,
            transcendentals=0,
        ),
        name="project",
    )(mats, context.reshape(klen // 32, 2, 16, width), query, table, wb, pb)


def weight_grads_kernel(xt_ref, ct_ref, tt_ref, dp_ref, dk_ref, dv_ref, dr_ref, g_ref):
    g_ref[0] = nt(ct_ref[...], dk_ref[...]).astype(BF)
    g_ref[1] = nt(ct_ref[...], dv_ref[...]).astype(BF)
    g_ref[2] = nn(xt_ref[...], dp_ref[...]).astype(BF)
    g_ref[3] = nt(tt_ref[...], dr_ref[...]).astype(BF)


def weight_grads(x_t, ctx_t, table_t, d_proj, dk_t, dv_t, drel_t):
    width, rows = x_t.shape
    klen, span = ctx_t.shape[1], table_t.shape[1]
    chunk = 256
    whole = lambda a, b: pl.BlockSpec((a, b), lambda i: (0, 0))
    rowb = lambda b: pl.BlockSpec((chunk, b), lambda i: (i, 0))
    return pl.pallas_call(
        weight_grads_kernel,
        grid=(width // chunk,),
        in_specs=[
            whole(width, rows),
            whole(width, klen),
            whole(width, span),
            pl.BlockSpec((rows, chunk), lambda i: (0, i)),
            rowb(klen),
            rowb(klen),
            rowb(span),
        ],
        out_specs=pl.BlockSpec((4, width, chunk), lambda i: (0, 0, i)),
        out_shape=jax.ShapeDtypeStruct((4, width, width), BF),
        compiler_params=pltpu.CompilerParams(vmem_limit_bytes=LIMIT),
        cost_estimate=pl.CostEstimate(
            flops=2 * (rows + 2 * klen + span) * width * width,
            bytes_accessed=20 << 20,
            transcendentals=0,
        ),
        name="weight_grads",
    )(x_t, ctx_t, table_t, d_proj, dk_t, dv_t, drel_t)


def flip(arr, bit):
    return lax.ppermute(arr, "dp", [(i, i ^ bit) for i in range(lax.axis_size("dp"))])


def scatter_sum(grads):
    mine = lax.psum_scatter(grads, "dp", scatter_dimension=1, tiled=True)
    return lax.psum_scatter(mine, "tensor", scatter_dimension=2, tiled=True).astype(F32)


def body(
    content_stream,
    query_stream,
    memory,
    content_tangent,
    query_tangent,
    seq_lengths,
    factor_order,
    memory_lengths,
    slot_sequence,
    query_weight,
    key_weight,
    value_weight,
    pos_weight,
    out_weight,
    up_weight,
    up_bias,
    down_weight,
    down_bias,
    word_bias,
    pos_bias,
    first_gain,
    first_shift,
    second_gain,
    second_shift,
):
    groups, tensors = lax.axis_size("dp"), lax.axis_size("tensor")
    micro, part_len, width = content_stream.shape
    mem_part = memory.shape[1]
    seq_len, mem_total = part_len * tensors, mem_part * tensors
    klen, span = mem_total + seq_len, mem_total + 2 * seq_len
    count = micro * groups
    here, lane = lax.axis_index("dp"), lax.axis_index("tensor")
    core = here % 2
    lead = core == 0
    block = 256
    assert 2 * micro == tensors

    def swap(arr):
        return flip(arr, CORE)

    def to_unit(first, second):
        got = swap(jnp.where(lead, second, first))
        low = jnp.where(lead, first, got)
        high = jnp.where(lead, got, second)
        both = jnp.concatenate([low, high], 0)
        both = lax.all_to_all(both, "tensor", split_axis=0, concat_axis=0, tiled=True)
        return both.reshape(seq_len, width)

    def from_unit(arr):
        both = arr.reshape(tensors, part_len, width)
        both = lax.all_to_all(both, "tensor", split_axis=0, concat_axis=0, tiled=True)
        low, high = both[:micro], both[micro:]
        got = swap(jnp.where(lead, high, low))
        return jnp.where(lead, low, got), jnp.where(lead, got, high)

    seq_id = (here // 2) * tensors + lane
    mats = [key_weight, value_weight, query_weight, pos_weight, out_weight]
    table = jnp.asarray(reversed_table(span, klen, width))
    wires = ()
    if groups == 8:
        keys, values, rel, q_word, q_pos, stream, thr, key_rank, weights, context, *wires = enter(
            slot_sequence,
            seq_lengths,
            memory_lengths,
            content_stream,
            query_stream,
            memory,
            table,
            factor_order,
            mats,
            up_weight,
            down_weight,
            word_bias,
            pos_bias,
        )
        wires += [content_tangent, query_tangent]
        context = context.reshape(klen, width)
    else:
        ids = jnp.arange(count, dtype=jnp.int32)
        slot_of = jnp.sum(jnp.where(slot_sequence[None, :] == ids[:, None], ids[None, :], 0), axis=1)
        counts = jnp.concatenate([seq_lengths, memory_lengths])
        slot = slot_of[seq_id]
        lengths = lax.all_gather(counts, "dp", axis=0, tiled=False)
        orders = lax.all_gather(factor_order, "dp", axis=0, tiled=False)[seq_id // micro]
        stream = to_unit(content_stream, query_stream)
        content, query = jnp.where(lead, stream, swap(stream)), stream
        tangent = to_unit(content_tangent, query_tangent)
        piece = mem_part // groups
        spread = lax.all_to_all(
            memory.reshape(micro, groups, piece, width), "dp", split_axis=1, concat_axis=1, tiled=True
        )
        spread = spread.transpose(1, 0, 2, 3).reshape(count, piece, width)
        spread = jnp.take(spread, slot_of, axis=0)
        spread = spread.reshape(groups // 2, tensors, 2, piece // 2, width).transpose(0, 2, 1, 3, 4)
        spread = lax.all_to_all(
            spread.reshape(groups, tensors, piece // 2, width),
            "dp",
            split_axis=0,
            concat_axis=0,
            tiled=True,
        )
        spread = lax.all_to_all(spread, "tensor", split_axis=1, concat_axis=1, tiled=True)
        got = swap(spread)
        mem_rows = jnp.stack([jnp.where(lead, spread, got), jnp.where(lead, got, spread)])
        mem_rows = mem_rows.transpose(2, 1, 0, 3, 4).reshape(mem_total, width)
        context = jnp.concatenate([mem_rows, content], 0)

        def whole(mat):
            mat = lax.all_gather(mat, "tensor", axis=1, tiled=True)
            return lax.all_gather(mat, "dp", axis=0, tiled=True)

        weights = jnp.stack([whole(mat) for mat in mats[:4]])
        wo = whole(out_weight)[None]
        ud = jnp.stack([whole(up_weight), whole(down_weight)])
        keys, values, rel, q_word, q_pos, stream = project(
            weights, context, query, table, word_bias, pos_bias
        )
        length = lengths[seq_id // micro, seq_id % micro]
        mem_valid = lengths[slot // micro, micro + slot % micro]
        rank = orders[seq_id % micro]
        key_pos = jnp.arange(klen, dtype=jnp.int32)
        hidden = jnp.int32(1 << 20)
        mem_rank = jnp.where(key_pos[:mem_total] >= mem_total - mem_valid, -1, hidden)
        own_rank = jnp.where(key_pos[:seq_len] < length, rank, hidden)
        key_rank = jnp.concatenate([mem_rank, own_rank])[None, :]
        thr = (rank + jnp.where(lead, 1, 0))[:, None]

    vec, prob, *arrived = attend_forward(
        q_word, q_pos, keys, values, rel, thr, key_rank, block, wires
    )
    if wires:
        wo, ud, tangent = arrived
    out, d_mixed, g_vec, g_out, g_ud, g_upb, small = feed(
        ud,
        wo,
        vec,
        stream,
        tangent,
        up_bias,
        (down_bias, first_gain, first_shift, second_gain, second_shift),
    )
    backward = (prob, g_vec, q_word, q_pos, keys, values, rel, block)
    if groups == 8:
        d_proj, dk_t, dv_t, drel_t, biases, grad_up, grad_down, content_out, query_out = (
            attend_backward(*backward, (g_ud, out))
        )
    else:
        d_proj, dk_t, dv_t, drel_t, biases = attend_backward(*backward)
        content_out, query_out = from_unit(out)
        grad_up, grad_down = scatter_sum(g_ud)
    small = jnp.concatenate([g_upb.reshape(-1), small[:5].reshape(-1), biases.reshape(-1)])
    inner = up_bias.shape[0]
    table_t = jnp.asarray(np.ascontiguousarray(reversed_table(span, klen, width).T))
    if groups == 8:
        small = jnp.pad(small, (0, -small.shape[0] % 1024)).reshape(-1, 128)
        arrays = [stream, d_proj, context, dk_t, dv_t, weights, table_t, drel_t]
        (
            grad_key,
            grad_value,
            grad_query,
            grad_pos,
            grad_out,
            content_grad,
            query_grad,
            small,
        ) = finish(arrays, g_out[None], d_mixed, small)
        arrays = [content_out, query_out, content_grad, query_grad, grad_query, grad_key]
        arrays += [grad_value, grad_pos, grad_out, grad_up, grad_down]
        *arrays, up_sum, down_sum, a1, b1, a2, b2, word_sum, pos_sum = emit(
            small, arrays, inner, width
        )
        return *arrays[:10], up_sum, arrays[10], down_sum, word_sum, pos_sum, a1, b1, a2, b2
    else:
        d_context = tt(dk_t[:, mem_total:], weights[0]) + tt(dv_t[:, mem_total:], weights[1])
        partner = swap(d_context.astype(BF)).astype(F32)
        d_stream = d_mixed + nt(d_proj, weights[2]) + jnp.where(lead, d_context + partner, 0.0)
        content_grad, query_grad = from_unit(d_stream.astype(BF))
        grad_key, grad_value, grad_query, grad_pos = scatter_sum(
            weight_grads(jnp.transpose(stream), jnp.transpose(context), table_t, d_proj, dk_t, dv_t, drel_t)
        )
        (grad_out,) = scatter_sum(g_out[None])
        small = lax.psum(small, ("dp", "tensor"))
    rest = small[inner:].reshape(7, width)
    return (
        content_out,
        query_out,
        content_grad,
        query_grad,
        grad_query,
        grad_key,
        grad_value,
        grad_pos,
        grad_out,
        grad_up,
        small[:inner],
        grad_down,
        rest[0],
        rest[5].reshape(HEADS, DH),
        rest[6].reshape(HEADS, DH),
        rest[1],
        rest[2],
        rest[3],
        rest[4],
    )


def solution(mesh):
    rows = P("dp", "tensor", None)
    mat = P("dp", "tensor")
    return jax.shard_map(
        body,
        mesh=mesh,
        in_specs=(rows,) * 5
        + (P("dp"), P("dp", None), P("dp"), P())
        + (mat,) * 6
        + (P(), mat)
        + (P(),) * 7,
        out_specs=(rows,) * 4 + (mat,) * 6 + (P(), mat) + (P(),) * 7,
        check_vma=False,
    )
```

```python
import functools

import jax
import jax.numpy as jnp
import numpy as np
from jax import lax
from jax.experimental import pallas as pl
from jax.experimental.pallas import tpu as pltpu
from jax.sharding import PartitionSpec as P

HEADS = 12
DH = 64
PAIR = 2 * DH
EPS = 1e-06
BF = jnp.bfloat16
F32 = jnp.float32
LIMIT = 60 * 1024 * 1024
SMEM_SPEC = pl.BlockSpec(memory_space=pltpu.SMEM)
ANY_SPEC = pl.BlockSpec(memory_space=pl.ANY)


def nn(left, right):
    return jnp.dot(left, right, preferred_element_type=F32)


def nt(left, right):
    return lax.dot_general(left, right, (((1,), (1,)), ((), ())), preferred_element_type=F32)


def tn(left, right):
    return lax.dot_general(left, right, (((0,), (0,)), ((), ())), preferred_element_type=F32)


def tt(left, right):
    return lax.dot_general(left, right, (((0,), (1,)), ((), ())), preferred_element_type=F32)


def reversed_table(count, first, width):
    dist = (first - np.arange(count)).astype(np.float32)
    half = width // 2
    power = np.arange(half).astype(np.float32) * np.float32(2.0 / width)
    freq = np.float32(1.0) / np.float32(10000.0) ** power
    angle = (dist[:, None] * freq[None, :]).astype(np.float64)
    return np.concatenate([np.sin(angle), np.cos(angle)], axis=1).astype(np.float32).astype(BF)


MESH = pl.DeviceIdType.MESH
CORE, XBIT, YBIT = 1, 2, 4


class Place:
    def __init__(self):
        self.d, self.z = lax.axis_index("dp"), lax.axis_index("tensor")
        self.core = lax.rem(self.d, 2)
        self.x = lax.rem(lax.div(self.d, 2), 2)
        self.y = lax.div(self.d, 4)

    def dp(self, bits):
        at = self.d
        if bits & CORE:
            at = at + (1 - 2 * self.core)
        if bits & XBIT:
            at = at + (2 - 4 * self.x)
        if bits & YBIT:
            at = at + (4 - 8 * self.y)
        return at

    def up(self, step):
        return lax.rem(self.z + step, 4) if step else self.z


def push(src, dst, send, recv, dp, z):
    return pltpu.make_async_remote_copy(
        src_ref=src,
        dst_ref=dst,
        send_sem=send,
        recv_sem=recv,
        device_id=(dp, z),
        device_id_type=MESH,
    )


def settle(ref, sem):
    pltpu.make_async_copy(ref, ref, sem).wait()


def greet(partners):
    barrier = pltpu.get_barrier_semaphore()
    for partner in partners:
        pl.semaphore_signal(barrier, inc=1, device_id=partner, device_id_type=MESH)
    pl.semaphore_wait(barrier, len(partners))


GATHER = (
    (0, 0, XBIT),
    (0, 1, YBIT),
    (0, 0, YBIT),
    (0, 1, XBIT),
    (XBIT, 0, YBIT),
    (YBIT, 1, XBIT),
    (0, 0, CORE),
    (0, 1, CORE),
    (XBIT, 0, CORE),
    (YBIT, 1, CORE),
    (YBIT, 0, CORE),
    (XBIT, 1, CORE),
    (XBIT | YBIT, 0, CORE),
    (XBIT | YBIT, 1, CORE),
)


class Gather:
    def __init__(self, place, dst, own, send, recv):
        self.place, self.dst, self.own = place, dst, own
        self.send, self.recv = send, recv
        self.half = dst.shape[1] // 16

    def region(self, owner, half):
        at = self.place.dp(owner) * (2 * self.half) + half * self.half
        return self.dst.at[:, pl.ds(pl.multiple_of(at, 16), self.half), :]

    def copy(self, i):
        owner, half, to = GATHER[i]
        src = self.region(owner, half)
        if owner == 0 and self.own is not None:
            src = self.own.at[:, half * self.half : (half + 1) * self.half, :]
        place = self.place
        return push(
            src, self.region(owner, half), self.send.at[i], self.recv.at[i], place.dp(to), place.z
        )

    def start(self, *which):
        for i in which:
            self.copy(i).start()

    def wait(self, received, sent):
        for i in received:
            self.copy(i).wait_recv()
        for i in sent:
            self.copy(i).wait_send()

    def after(self, arrived, started):
        for i, more in zip(arrived, started):
            self.copy(i).wait_recv()
            for j in more:
                self.copy(j).start()

    def middle(self):
        self.after((0, 1), ((4, 8), (5, 9)))

    def last(self):
        self.after((2, 3, 4, 5), ((10,), (11,), (12,), (13,)))


def chip_bits(j):
    return (XBIT if j & 1 else 0) | (YBIT if j & 2 else 0)


def add_into(dst, src):
    def run(i, carry):
        at = pl.ds(pl.multiple_of(i * 16, 16), 16)
        dst[:, at, :] = (dst[:, at, :].astype(F32) + src[:, at, :].astype(F32)).astype(BF)
        return carry

    lax.fori_loop(0, dst.shape[1] // 16, run, 0)


class Reduce:
    def __init__(self, place, sources, scratch, out, paired=False):
        self.place, self.sources, self.out, self.paired = place, sources, out, paired
        self.total, self.pair, self.near, self.far, self.quarter, self.stage = scratch[:6]
        self.pair_send, self.pair_recv, self.load, self.send, self.recv, self.z_send, self.z_recv = scratch[6:]
        self.rows = self.total.shape[2]

    @staticmethod
    def scratch(count, n, rows, cols, paired=False):
        part = cols // 4
        dma = lambda k: pltpu.SemaphoreType.DMA((k,))
        return [
            pltpu.VMEM((n, 4, rows, cols), BF),
            pltpu.VMEM((8, 128) if paired else (n, 4, rows, cols), BF),
            pltpu.VMEM((n, 2, 2, rows // 2, cols), BF),
            pltpu.VMEM((n, 2, rows // 2, cols), BF),
            pltpu.VMEM((4, n, rows, part), BF),
            pltpu.VMEM((4, n, rows, part) if part % 128 else (8, 128), BF),
            dma(4 * count),
            dma(4 * count),
            dma(4 * count),
            dma(6),
            dma(6),
            dma(3),
            dma(1),
        ]

    def pair_copies(self, j):
        place, rows = self.place, self.rows
        copies, at = [], 0
        for i, src in enumerate(self.sources):
            slot, n = len(self.sources) * j + i, src.shape[0]
            block = lambda bits: src.at[:, pl.ds(pl.multiple_of(place.dp(bits) * rows, 16), rows), :]
            remote = push(
                block(chip_bits(j) | CORE),
                self.pair.at[at : at + n, j],
                self.pair_send.at[slot],
                self.pair_recv.at[slot],
                place.dp(CORE),
                place.z,
            )
            local = pltpu.make_async_copy(
                block(chip_bits(j)), self.total.at[at : at + n, j], self.load.at[slot]
            )
            copies.append((remote, local))
            at += n
        return copies

    def half(self, j, h):
        size = self.rows // 2
        return self.total.at[:, j, h * size : (h + 1) * size, :]

    MOVES = ((3, 0, XBIT, 1), (3, 1, YBIT, 1), (1, 0, XBIT, 0), (2, 1, YBIT, 0), (2, 0, YBIT, 0), (1, 1, XBIT, 1))

    def move(self, i):
        j, h, to, where = self.MOVES[i]
        dst = self.near.at[:, h, where] if i < 4 else self.far.at[:, where]
        place = self.place
        return push(self.half(j, h), dst, self.send.at[i], self.recv.at[i], place.dp(to), place.z)

    def z_copy(self, k):
        place, part = self.place, self.quarter.shape[3]
        to = place.up(k)
        if part % 128:
            src = self.stage.at[to]
        else:
            src = self.total.at[:, 0, :, pl.ds(pl.multiple_of(to * part, 128), part)]
        dst = self.quarter.at[place.z]
        if k == 0:
            return pltpu.make_async_copy(src, dst, self.z_recv.at[0])
        return push(src, dst, self.z_send.at[k - 1], self.z_recv.at[0], place.d, to)

    def loaded(self, j):
        return pltpu.make_async_copy(self.sources[0].at[:, j], self.total.at[:, j], self.load.at[j])

    def begin(self):
        for j in (3, 1, 2, 0):
            if self.paired:
                self.loaded(j).start()
                continue
            for remote, local in self.pair_copies(j):
                remote.start()
                local.start()

    def pairs(self):
        for j, moves in ((3, (0, 1)), (1, (2,)), (2, (3,)), (0, ())):
            if self.paired:
                self.loaded(j).wait()
            else:
                for remote, local in self.pair_copies(j):
                    local.wait()
                    remote.wait_recv()
                add_into(self.total.at[:, j], self.pair.at[:, j])
            for i in moves:
                self.move(i).start()

    def middle(self):
        for i, j, h, where, more in ((0, 2, 0, 1, 4), (1, 1, 1, 1, 5), (2, 0, 0, 0, None), (3, 0, 1, 0, None)):
            self.move(i).wait_recv()
            add_into(self.half(j, h), self.near.at[:, h, where])
            if more is not None:
                self.move(more).start()

    def late(self):
        for i, h in ((4, 0), (5, 1)):
            self.move(i).wait_recv()
            add_into(self.half(0, h), self.far.at[:, h])
        part = self.quarter.shape[3]
        if part % 128:
            for k in range(4):
                for m in range(self.total.shape[0]):
                    self.stage[k, m] = self.total[m, 0, :, k * part : (k + 1) * part]
        for k in (2, 1, 3, 0):
            self.z_copy(k).start()

    def end(self):
        settle(self.quarter, self.z_recv.at[0])
        parts = [self.quarter[k].astype(F32) for k in range(4)]
        total = (parts[0] + parts[1]) + (parts[2] + parts[3])
        self.out[...] = total.reshape(self.out.shape)
        if not self.paired:
            for j in range(4):
                for remote, _ in self.pair_copies(j):
                    remote.wait_send()
        for i in range(6):
            self.move(i).wait_send()
        for k in range(1, 4):
            self.z_copy(k).wait_send()


class Homeward:
    def __init__(self, place, src, homes, send, recv):
        self.place, self.src, self.homes, self.send, self.recv = place, src, homes, send, recv
        self.part = homes[0].shape[1]

    def act(self, what):
        place, part = self.place, self.part
        for u in range(2):

            @pl.when(place.core == u)
            def _():
                for k in (2, 1, 3, 0):
                    to, dp = place.up(k), place.d - place.core + lax.div(place.z, 2)
                    src = self.src.at[pl.ds(pl.multiple_of(to * part, 16), part), :]
                    dst = self.homes[u].at[lax.rem(place.z, 2)]
                    recv = self.recv.at[u]
                    here = jnp.logical_and(dp == place.d, to == place.z)
                    remote = push(src, dst, self.send.at[k], recv, dp, to)
                    if what == "start":
                        pl.when(here)(pltpu.make_async_copy(src, dst, recv).start)
                        pl.when(jnp.logical_not(here))(remote.start)
                    else:
                        pl.when(jnp.logical_not(here))(remote.wait_send)

    def start(self):
        self.act("start")

    def end(self):
        for u in range(2):
            settle(self.homes[u], self.recv.at[u])
        self.act("wait")


def pair_and_z(place):
    return [(place.dp(r), place.up(k)) for k in range(4) for r in (0, CORE) if r or k]


def near_partners(place):
    return pair_and_z(place) + [(place.dp(r), place.z) for r in (XBIT, YBIT)]


INPUTS = 8


def finish_kernel(*refs):
    hbm, (go_ref, mixed_ref, small_ref) = refs[:INPUTS], refs[INPUTS : INPUTS + 3]
    grad_refs, home_refs, sums_ref = refs[INPUTS + 3 : INPUTS + 8], refs[INPUTS + 8 : INPUTS + 10], refs[INPUTS + 10]
    refs = refs[INPUTS + 11 :]
    held, refs = refs[:INPUTS], refs[INPUTS:]
    loads, x_t, ctx_t, g_ref, base, ctx, partner, stream, slots, part_sum, chips = refs[:11]
    home_send, slot_send, chip_send, one_send, recv = refs[11:16]
    refs = refs[16:]
    count = len(refs) // 5
    place = Place()
    d, z, core = place.d, place.z, place.core
    copies = [
        pltpu.make_async_copy(a.at[0:3] if i == 5 else a, b, loads.at[i])
        for i, (a, b) in enumerate(zip(hbm, held))
    ]
    for copy in copies:
        copy.start()

    def need(*which):
        for i in which:
            copies[i].wait()
        return [held[i] for i in which]

    greet(near_partners(place) + [(place.dp(XBIT | YBIT), z)])
    sources = [g_ref.at[m : m + 1] for m in range(4)] + [go_ref]
    key, value, query, pos, out = [
        Reduce(place, (src,), refs[m * count : (m + 1) * count], grad_refs[m])
        for m, src in enumerate(sources)
    ]
    out.begin()
    slot_copies = []
    others = [(r, k) for k in range(4) for r in (0, CORE) if r or k]
    for i, (r, k) in enumerate(others):
        copy = push(small_ref, slots.at[4 * core + z], slot_send.at[i], recv.at[1], place.dp(r), place.up(k))
        copy.start()
        slot_copies.append(copy)
    pltpu.make_async_copy(small_ref, slots.at[4 * core + z], recv.at[1]).start()

    width, block = g_ref.shape[1], 256

    def product(m, left, right, dot):
        def run(i, carry):
            at = pl.ds(pl.multiple_of(i * block, block), block)
            g_ref[m, at, :] = dot(left[at, :], right[...]).astype(BF)
            return carry

        lax.fori_loop(0, width // block, run, 0)

    def turn(src, dst):
        def run(i, carry):
            at = pl.ds(pl.multiple_of(i * block, block), block)
            dst[:, at] = jnp.transpose(src[at, :].astype(F32)).astype(BF)
            return carry

        lax.fori_loop(0, src.shape[0] // block, run, 0)

    x_ref, d_proj = need(0, 1)
    turn(x_ref, x_t)
    product(2, x_t, d_proj, nn)
    query.begin()
    ctx_ref, dk_t = need(2, 3)
    turn(ctx_ref, ctx_t)
    product(0, ctx_t, dk_t, nt)
    key.begin()
    out.pairs()

    dv_t, mats = need(4, 5)
    back = dk_t.shape[1] - base.shape[0]

    def from_context(i, carry):
        at = pl.ds(pl.multiple_of(i * block, block), block)
        cols = pl.ds(pl.multiple_of(i * block + back, block), block)
        turned = nn(mats[0], dk_t[:, cols]) + nn(mats[1], dv_t[:, cols])
        turned = jnp.transpose(turned)
        base[at, :] = turned
        ctx[at, :] = turned.astype(BF)
        return carry

    lax.fori_loop(0, base.shape[0] // block, from_context, 0)
    swap = push(ctx, partner, one_send.at[0], recv.at[0], place.dp(CORE), z)
    swap.start()

    def from_proj(i, carry):
        at = pl.ds(pl.multiple_of(i * block, block), block)
        own = mixed_ref[at, :] + nt(d_proj[at, :], mats[2])
        base[at, :] = own + jnp.where(core == 0, base[at, :], 0.0)
        return carry

    lax.fori_loop(0, base.shape[0] // block, from_proj, 0)
    query.pairs()
    product(1, ctx_t, dv_t, nt)
    value.begin()
    key.pairs()

    swap.wait()
    small_block = 64

    def add_partner(i, carry):
        at = pl.ds(pl.multiple_of(i * small_block, small_block), small_block)
        more = jnp.where(core == 0, partner[at, :].astype(F32), 0.0)
        stream[at, :] = (base[at, :] + more).astype(BF)
        return carry

    lax.fori_loop(0, stream.shape[0] // small_block, add_partner, 0)
    home = Homeward(place, stream, home_refs, home_send, recv.at[2:4])
    home.start()
    out.middle()

    table_t, dr_t = need(6, 7)
    product(3, table_t, dr_t, nt)
    pos.begin()
    value.pairs()
    query.middle()
    out.late()

    settle(slots, recv.at[1])
    total = slots[0]
    for i in range(1, 8):
        total = total + slots[i]
    part_sum[...] = total
    chip = lax.div(d, 2)
    chip_copies = []
    for i, r in enumerate((XBIT, YBIT, XBIT | YBIT)):
        copy = push(part_sum, chips.at[chip], chip_send.at[i], recv.at[4], place.dp(r), z)
        copy.start()
        chip_copies.append(copy)
    pltpu.make_async_copy(part_sum, chips.at[chip], recv.at[4]).start()

    pos.pairs()
    key.middle()
    query.late()
    value.middle()
    key.late()
    pos.middle()
    value.late()
    settle(chips, recv.at[4])
    sums_ref[...] = (chips[0] + chips[1]) + (chips[2] + chips[3])
    pos.late()
    for reduce in (out, query, key, value, pos):
        reduce.end()
    home.end()
    for copy in slot_copies + chip_copies:
        copy.wait_send()


def finish(arrays, g_out, mixed, small):
    total, width = arrays[0].shape
    klen = arrays[2].shape[0]
    rows = width // 8
    vmem = pl.BlockSpec(memory_space=pltpu.VMEM)
    dma = lambda k: pltpu.SemaphoreType.DMA((k,))
    scratch = [pltpu.VMEM((3,) + a.shape[1:] if a.ndim == 3 else a.shape, BF) for a in arrays]
    scratch += [
        dma(INPUTS),
        pltpu.VMEM((width, total), BF),
        pltpu.VMEM((width, klen), BF),
        pltpu.VMEM((4, width, width), BF),
        pltpu.VMEM((total, width), F32),
        pltpu.VMEM((total, width), BF),
        pltpu.VMEM((total, width), BF),
        pltpu.VMEM((total, width), BF),
        pltpu.VMEM((8,) + small.shape, F32),
        pltpu.VMEM(small.shape, F32),
        pltpu.VMEM((4,) + small.shape, F32),
        dma(4),
        dma(7),
        dma(3),
        dma(1),
        dma(5),
    ]
    for _ in range(5):
        scratch += Reduce.scratch(1, 1, rows, width)
    return pl.pallas_call(
        finish_kernel,
        in_specs=[ANY_SPEC] * (INPUTS + 1) + [vmem] * 2,
        out_specs=[vmem] * 5 + [ANY_SPEC] * 2 + [vmem],
        out_shape=[jax.ShapeDtypeStruct((rows, width // 4), F32)] * 5
        + [jax.ShapeDtypeStruct((2, total // 4, width), BF)] * 2
        + [
            jax.ShapeDtypeStruct(small.shape, F32),
        ],
        scratch_shapes=scratch,
        compiler_params=pltpu.CompilerParams(
            collective_id=4, has_side_effects=True, vmem_limit_bytes=LIMIT
        ),
        cost_estimate=pl.CostEstimate(flops=20 << 30, bytes_accessed=64 << 20, transcendentals=0),
        name="finish",
    )(*arrays, g_out, mixed, small)


def emit_kernel(small_ref, *refs):
    count = 11
    for src, dst in zip(refs[:count], refs[count : 2 * count]):
        dst[...] = src[...]
    wide, *rows, word_ref, pos_ref = refs[2 * count :]
    lanes = small_ref.shape[1]
    size = wide.shape[0] // lanes
    wide[...] = small_ref[0:size, :].reshape(wide.shape)
    for ref in rows:
        step = ref.shape[0] // lanes
        ref[...] = small_ref[size : size + step, :].reshape(ref.shape)
        size += step
    for ref in (word_ref, pos_ref):
        for h in range(HEADS):
            at = size + h * DH // lanes
            ref[h : h + 1, :] = small_ref[at : at + 1, h * DH % lanes : h * DH % lanes + DH]
        size += HEADS * DH // lanes


def emit(small, arrays, inner, width):
    vmem = pl.BlockSpec(memory_space=pltpu.VMEM)
    out_shape = [jax.ShapeDtypeStruct(a.shape, a.dtype) for a in arrays]
    out_shape += [jax.ShapeDtypeStruct((inner,), F32)]
    out_shape += [jax.ShapeDtypeStruct((width,), F32)] * 5
    out_shape += [jax.ShapeDtypeStruct((HEADS, DH), F32)] * 2
    return pl.pallas_call(
        emit_kernel,
        in_specs=[vmem] * (1 + len(arrays)),
        out_specs=[vmem] * len(out_shape),
        out_shape=out_shape,
        compiler_params=pltpu.CompilerParams(vmem_limit_bytes=LIMIT),
        name="emit",
    )(small, *arrays)


def pack(mat):
    half = mat.shape[0] // 2
    return jnp.concatenate([mat[:, :128], jnp.concatenate([mat[:half, 128:], mat[half:, 128:]], axis=1)], axis=0)


def unpack(packed):
    rows = packed.shape[0] * 2 // 3
    rest = packed[rows:, :]
    return jnp.concatenate([packed[:rows, :], jnp.concatenate([rest[:, :64], rest[:, 64:]], axis=0)], axis=1)


def enter_kernel(slot_ref, seq_ref, mem_ref, content, query, memory, table_hbm, orders, *refs):
    mats, (upw, dnw), (wb_ref, pb_ref) = refs[:5], refs[5:7], refs[7:9]
    outs, (thr_ref, key_ref, whole_out, context_out, wo, ud) = refs[9:15], refs[15:21]
    (
        ints,
        all_ints,
        whole,
        context,
        stream,
        table,
        spread,
        picked,
        shards,
        slab,
        mat_send,
        mat_recv,
        ud_send,
        ud_recv,
        int_send,
        spread_send,
        pick_send,
        stream_send,
        pair_send,
        gather_send,
        gather_recv,
        wo_send,
        wo_recv,
        far_send,
        far_recv,
        recv,
        local,
    ) = refs[21:]
    place = Place()
    d, z, core = place.d, place.z, place.core
    up, down, far = place.up(1), place.up(3), place.up(2)
    part = query.shape[1]
    micro = orders.shape[0]
    spot = lax.broadcasted_iota(jnp.int32, (1, ints.shape[1]), 1)
    lengths = jnp.where(spot == 0, seq_ref[0], seq_ref[1])
    lengths = jnp.where(spot < 2, lengths, jnp.where(spot == 2, mem_ref[0], mem_ref[1]))
    ints[...] = jnp.concatenate([orders[...], jnp.broadcast_to(lengths, (6, ints.shape[1]))], axis=0)

    def slot_of(seq):
        at = jnp.int32(0)
        for k in range(16):
            at = at + jnp.where(slot_ref[k] == seq, k, 0)
        return jnp.minimum(at, 15)

    pltpu.make_async_copy(table_hbm, table, local.at[0]).start()
    piece = spread.shape[1]
    blocks = part // piece // 2
    first = 4 * blocks
    greet([(place.dp(r), place.up(k)) for r in range(8) for k in range(4) if r or k])

    spread_copies = []
    for r in range(8):
        to = place.dp(r)
        src = memory.at[:, pl.ds(pl.multiple_of(to * piece, 16), piece), :]
        dst = spread.at[pl.ds(2 * d, 2)]
        if r == 0:
            pltpu.make_async_copy(src, dst, recv.at[0]).start()
        else:
            spread_copies.append(push(src, dst, spread_send.at[r - 1], recv.at[0], to, z))
            spread_copies[-1].start()

    for m, mat in enumerate(mats):
        shards[z, m] = pack(mat[...])
    cutoff = shards.shape[2] * 5 // 9

    def mat_copy(i):
        own = shards.at[z]
        low, high = shards.at[down, :, :cutoff], shards.at[up, :, cutoff:]
        src = (own, own, low, high)[i]
        return push(src, src, mat_send.at[i], mat_recv.at[i], d, (up, down, up, down)[i])

    mat_copy(0).start()
    mat_copy(1).start()
    rows = slab.shape[1]
    width = upw.shape[1]

    def columns(at, start=0, size=rows):
        mine = pl.ds(pl.multiple_of(d * rows + start, 16), size)
        return ud.at[:, mine, pl.ds(pl.multiple_of(at * width, 128), width)]

    def ud_copy(i):
        if i < 4:
            src, dst = (upw, dnw)[i % 2], columns(z).at[i % 2]
            return push(src, dst, ud_send.at[i], ud_recv.at[i // 2], d, (up, down)[i // 2])
        half = rows // 2
        src = columns(down, 0, half) if i == 4 else columns(up, half, half)
        return push(src, src, ud_send.at[i], ud_recv.at[i - 2], d, (up, down)[i - 4])

    for m, mat in enumerate((upw, dnw)):
        pltpu.make_async_copy(mat, columns(z).at[m], recv.at[8]).start()

    int_copies = []
    for r in range(8):
        if r == 0:
            pltpu.make_async_copy(ints, all_ints.at[d], recv.at[2]).start()
        else:
            copy = push(ints, all_ints.at[d], int_send.at[r - 1], recv.at[2], place.dp(r), z)
            int_copies.append(copy)
            copy.start()

    def stream_copy(i, act):
        j, kind = i // 2, i % 2
        to, dp = 2 * core + j, d - core + kind
        if kind == 0:
            src, sem = content.at[j], recv.at[3]
            dst = context.at[pl.ds(first + blocks * z, blocks)]
        else:
            src, sem = query.at[j], recv.at[4]
            dst = stream.at[pl.ds(pl.multiple_of(z * part, 16), part), :]
        here = jnp.logical_and(dp == d, to == z)
        remote = push(src, dst, stream_send.at[i], sem, dp, to)
        if act == "start":
            pl.when(here)(pltpu.make_async_copy(src, dst, sem).start)
            pl.when(jnp.logical_not(here))(remote.start)
        else:
            pl.when(jnp.logical_not(here))(remote.wait_send)

    mat_copy(0).wait_recv()
    mat_copy(2).start()
    mat_copy(1).wait_recv()
    mat_copy(3).start()
    for i in range(4):
        ud_copy(i).start()
    mat_copy(2).wait_recv()
    mat_copy(3).wait_recv()
    for m in range(5):
        slab[m] = jnp.concatenate([unpack(shards[k, m]) for k in range(4)], axis=1)
    own_rows = pl.ds(pl.multiple_of(d * rows, 16), rows)
    gather = Gather(place, whole, slab.at[0:4], gather_send, gather_recv)
    gather.start(0, 1, 2, 3, 6, 7)
    pltpu.make_async_copy(slab.at[0:4], whole.at[:, own_rows, :], recv.at[6]).start()
    pltpu.make_async_copy(slab.at[4:5], wo.at[:, own_rows, :], recv.at[7]).start()

    settle(columns(down), ud_recv.at[0])
    ud_copy(4).start()
    settle(columns(up), ud_recv.at[1])
    ud_copy(5).start()
    for i in range(4):
        stream_copy(i, "start")

    settle(spread, recv.at[0])
    for q in range(16):
        picked[q] = spread[slot_of(q)]
    pick_copies = []
    for r in (YBIT | XBIT, XBIT, YBIT, 0):
        for k in range(4):
            to, lane = place.dp(r), place.up(k)
            src = picked.at[4 * lax.div(to, 2) + lane]
            dst = context.at[blocks * z + lax.div(d, 2), core]
            if r or k:
                copy = push(src, dst, pick_send.at[2 * r + k - 1], recv.at[5], to, lane)
                pick_copies.append(copy)
            else:
                copy = pltpu.make_async_copy(src, dst, recv.at[5])
            copy.start()

    gather.middle()
    wo_gather = Gather(place, wo, slab.at[4:5], wo_send, wo_recv)
    ud_gather = Gather(place, ud, None, far_send, far_recv)
    gathers = (ud_gather, wo_gather)
    settle(columns(z), recv.at[8])
    ud_copy(4).wait_recv()
    ud_copy(5).wait_recv()
    for i in (0, 1, 2, 3, 6, 7):
        for one in gathers:
            one.start(i)
    gather.last()

    pick_pair = push(
        context.at[0:first, core], context.at[0:first, core], pair_send.at[0], recv.at[1], place.dp(CORE), z
    )
    settle(context.at[0:first, core], recv.at[5])
    pick_pair.start()
    lead_copy = push(
        context.at[first:], context.at[first:], pair_send.at[1], recv.at[3], place.dp(CORE), z
    )

    @pl.when(core == 0)
    def _():
        settle(context.at[first:], recv.at[3])
        lead_copy.start()

    settle(all_ints, recv.at[2])
    seq = 4 * lax.div(d, 2) + z
    slot = slot_of(seq)
    odd = lax.rem(seq, micro)
    own, other = all_ints[lax.div(seq, micro)], all_ints[lax.div(slot, micro)]

    def pick(row, at):
        return jnp.sum(jnp.where(spot == at, row.astype(F32), 0.0), axis=1, keepdims=True)

    length = pick(own[2:3], odd)
    mem_valid = pick(other[2:3], micro + lax.rem(slot, micro))
    rank = jnp.where(odd == 0, own[0:1], own[1:2])
    seq_len = rank.shape[1]
    mem_total = key_ref.shape[1] - seq_len
    where = spot.astype(F32)
    hidden = jnp.int32(1 << 20)
    key_ref[:, :mem_total] = jnp.where(where >= mem_total - mem_valid, -1, hidden)
    key_ref[:, mem_total:] = jnp.where(where < length, rank, hidden)
    ranks = jnp.transpose(jnp.broadcast_to(rank.astype(F32), (8, seq_len)))
    thr_ref[...] = ranks[:, 0:1].astype(jnp.int32) + jnp.where(core == 0, 1, 0)

    gather.wait(range(6, 14), ())
    settle(whole.at[:, own_rows, :], recv.at[6])
    keep_whole = pltpu.make_async_copy(whole, whole_out, local.at[1])
    keep_whole.start()

    keep_context = pltpu.make_async_copy(context, context_out, local.at[2])

    def before_stream():
        pick_pair.wait()

        @pl.when(core == 0)
        def _():
            lead_copy.wait_send()

        @pl.when(core == 1)
        def _():
            settle(context.at[first:], recv.at[3])
            settle(stream, recv.at[4])

        keep_context.start()

    def before_context():
        for one in gathers:
            one.after((0, 1), ((8,), (9,)))

    pltpu.make_async_copy(table_hbm, table, local.at[0]).wait()
    project_step(
        whole, context, stream, table, wb_ref, pb_ref, *outs, hooks=(before_stream, before_context)
    )
    for one in gathers:
        one.after((2, 3), ((10,), (11,)))
    settle(wo.at[:, own_rows, :], recv.at[7])
    gather.wait((), range(14))
    for one in gathers:
        one.wait(range(6, 12), (0, 1, 2, 3) + tuple(range(6, 12)))
    keep_whole.wait()
    keep_context.wait()
    for i in range(4):
        stream_copy(i, "wait")
        mat_copy(i).wait_send()
    for i in range(6):
        ud_copy(i).wait_send()
    for copy in spread_copies + int_copies + pick_copies:
        copy.wait_send()


def enter(slots, seqs, mems, content, query, memory, table, orders, mats, upw, dnw, wb, pb):
    micro, part, width = content.shape
    rows = mats[0].shape[0]
    inner = upw.shape[1] * 4
    piece = part // 8
    klen, span, seq = 8 * part, table.shape[0], 4 * part
    vmem = pl.BlockSpec(memory_space=pltpu.VMEM)
    dma = lambda n: pltpu.SemaphoreType.DMA((n,))
    bf = lambda *shape: jax.ShapeDtypeStruct(shape, BF)
    return pl.pallas_call(
        enter_kernel,
        in_specs=[SMEM_SPEC] * 3 + [ANY_SPEC] * 4 + [vmem] * 10,
        out_specs=[vmem] * 8 + [ANY_SPEC] * 4,
        out_shape=[
            bf(klen, width),
            bf(klen, width),
            bf(span, width),
            bf(seq, width),
            bf(seq, width),
            bf(seq, width),
            jax.ShapeDtypeStruct((seq, 1), jnp.int32),
            jax.ShapeDtypeStruct((1, klen), jnp.int32),
            bf(4, 8 * rows, width),
            bf(32, 2, piece, width),
            bf(1, 8 * rows, width),
            bf(2, 8 * rows, inner),
        ],
        scratch_shapes=[
            pltpu.VMEM((8, seq), jnp.int32),
            pltpu.VMEM((8, 8, seq), jnp.int32),
            pltpu.VMEM((4, 8 * rows, width), BF),
            pltpu.VMEM((32, 2, piece, width), BF),
            pltpu.VMEM((seq, width), BF),
            pltpu.VMEM((span, width), BF),
            pltpu.VMEM((16, piece, width), BF),
            pltpu.VMEM((16, piece, width), BF),
            pltpu.VMEM((4, 5, rows * 3 // 2, 128), BF),
            pltpu.VMEM((5, rows, width), BF),
            dma(4),
            dma(4),
            dma(6),
            dma(4),
            dma(7),
            dma(7),
            dma(15),
            dma(4),
            dma(2),
            dma(14),
            dma(14),
            dma(14),
            dma(14),
            dma(14),
            dma(14),
            dma(9),
            dma(3),
        ],
        compiler_params=pltpu.CompilerParams(
            collective_id=1, has_side_effects=True, vmem_limit_bytes=LIMIT
        ),
        cost_estimate=pl.CostEstimate(flops=0, bytes_accessed=64 << 20, transcendentals=0),
        name="enter",
    )(
        slots,
        seqs,
        mems,
        content.reshape(micro, 4, 2, piece, width),
        query,
        memory,
        table,
        orders,
        *mats,
        upw,
        dnw,
        wb,
        pb,
    )


def head_lanes(array, head):
    lane = lax.broadcasted_iota(jnp.int32, array.shape, 1)
    return jnp.where((lane >= DH) == (head == 1), array, jnp.zeros_like(array))


def attend_forward_step(
    block, qw_ref, qp_ref, k_ref, v_ref, rel_ref, thr_ref, kr_ref, vec_ref, prob_ref
):
    rows, klen = qw_ref.shape[0], k_ref.shape[0]
    width = klen + block
    keys, values = k_ref[...], v_ref[...]
    for part in range(rows // block):
        at = slice(part * block, (part + 1) * block)
        first = rows - (part + 1) * block
        qw, qp = qw_ref[at, :], qp_ref[at, :]
        rel = rel_ref[first : first + width, :]
        seen = kr_ref[...] < thr_ref[at, :]
        vecs = []
        for head in range(2):
            raw = nt(head_lanes(qp, head), rel)
            moved = pltpu.roll(raw, 0, 1, stride=1, stride_axis=0)[:, block:]
            score = nt(head_lanes(qw, head), keys) + moved
            score = jnp.where(seen, score, -1e30)
            expo = jnp.exp(score - jnp.max(score, axis=1, keepdims=True))
            prob = (expo * (1.0 / jnp.sum(expo, axis=1, keepdims=True))).astype(BF)
            prob_ref[head, at, :] = prob
            vecs.append(nn(prob, values))
        lane = lax.broadcasted_iota(jnp.int32, vecs[0].shape, 1)
        vec_ref[at, :] = jnp.where(lane < DH, vecs[0], vecs[1]).astype(BF)


def attend_forward_kernel(block, wired, *refs):
    if not wired:
        attend_forward_step(block, *refs)
        return
    ins, (ctan, qtan) = refs[:7], refs[9:11]
    outs, (wo, ud, tangent) = refs[11:13], refs[13:16]
    out_send, out_recv, ud_send, ud_recv, tan_send, recv = refs[16:]
    step, steps = pl.program_id(0), pl.num_programs(0)
    place = Place()
    d, z, core = place.d, place.z, place.core
    gathers = (
        Gather(place, ud, None, ud_send, ud_recv),
        Gather(place, wo, None, out_send, out_recv),
    )
    part = ctan.shape[1]

    def tan_copy(i, act):
        j, kind = i // 2, i % 2
        to, dp = 2 * core + j, d - core + kind
        src = (ctan, qtan)[kind].at[j]
        dst = tangent.at[pl.ds(pl.multiple_of(z * part, 16), part), :]
        here = jnp.logical_and(dp == d, to == z)
        local = pltpu.make_async_copy(src, dst, recv.at[0])
        remote = push(src, dst, tan_send.at[i], recv.at[0], dp, to)
        if act == "start":
            pl.when(here)(local.start)
            pl.when(jnp.logical_not(here))(remote.start)
        else:
            pl.when(jnp.logical_not(here))(remote.wait_send)

    @pl.when(step == 0)
    def _():
        greet(near_partners(place))
        for gather in gathers:
            gather.start(4, 5)
        for i in range(4):
            tan_copy(i, "start")

    @pl.when(step == steps - 1)
    def _():
        for gather in gathers:
            gather.after((4, 5), ((12,), (13,)))

    attend_forward_step(block, *ins, *outs)

    @pl.when(step == steps - 1)
    def _():
        for gather in gathers:
            gather.wait((12, 13), (4, 5, 12, 13))
        settle(tangent, recv.at[0])
        for i in range(4):
            tan_copy(i, "wait")


def attend_forward(qw, qp, keys, values, rel, thr, key_rank, block, wires=()):
    rows, width = qw.shape
    klen, span = keys.shape[0], rel.shape[0]
    col = lambda count: pl.BlockSpec((count, PAIR), lambda p: (0, p))
    in_specs = [
        col(rows),
        col(rows),
        col(klen),
        col(klen),
        col(span),
        pl.BlockSpec((rows, 1), lambda p: (0, 0)),
        pl.BlockSpec((1, klen), lambda p: (0, 0)),
    ]
    out_specs = [col(rows), pl.BlockSpec((2, rows, klen), lambda p: (p, 0, 0))]
    out_shape = [
        jax.ShapeDtypeStruct((rows, width), BF),
        jax.ShapeDtypeStruct((width // DH, rows, klen), BF),
    ]
    params = dict(vmem_limit_bytes=LIMIT)
    scratch = []
    if wires:
        in_specs += [ANY_SPEC] * 4
        out_specs += [ANY_SPEC] * 3
        out_shape += [
            jax.ShapeDtypeStruct(wires[0].shape, BF),
            jax.ShapeDtypeStruct(wires[1].shape, BF),
            jax.ShapeDtypeStruct((rows, width), BF),
        ]
        scratch = [pltpu.SemaphoreType.DMA((n,)) for n in (14, 14, 14, 14, 4, 1)]
        params.update(collective_id=2, has_side_effects=True)
    return pl.pallas_call(
        functools.partial(attend_forward_kernel, block, bool(wires)),
        grid=(width // PAIR,),
        in_specs=in_specs,
        out_specs=out_specs,
        out_shape=out_shape,
        scratch_shapes=scratch,
        input_output_aliases={7: 2, 8: 3} if wires else {},
        compiler_params=pltpu.CompilerParams(**params),
        cost_estimate=pl.CostEstimate(
            flops=8 * rows * klen * width, bytes_accessed=16 << 20, transcendentals=12 * rows * klen
        ),
        name="attend_forward",
    )(qw, qp, keys, values, rel, thr, key_rank, *wires)


def attend_backward_kernel(block, wired, *refs):
    if not wired:
        attend_backward_step(block, *refs)
        return
    ins, (g_ud, src) = refs[:7], refs[7:9]
    outs, grad_refs, home_refs = refs[9:14], refs[14:16], refs[16:18]
    rel_acc, home_send, home_recv = refs[18:21]
    step, steps = pl.program_id(0), pl.num_programs(0)
    place = Place()
    count = len(refs[21:]) // 2
    reduces = [
        Reduce(place, (g_ud.at[m : m + 1],), refs[21 + m * count : 21 + (m + 1) * count], grad_refs[m], True)
        for m in range(2)
    ]
    home = Homeward(place, src, home_refs, home_send, home_recv)

    @pl.when(step == 0)
    def _():
        greet(near_partners(place))
        for reduce in reduces:
            reduce.begin()
        home.start()
        for reduce in reduces:
            reduce.pairs()

    @pl.when(step == 3)
    def _():
        reduces[0].middle()

    @pl.when(step == 5)
    def _():
        reduces[1].middle()

    attend_backward_step(block, *ins, *outs, rel_acc)

    @pl.when(step == steps - 1)
    def _():
        reduces[0].late()
        reduces[1].late()
        reduces[0].end()
        reduces[1].end()
        home.end()


def attend_backward_step(
    block,
    prob_ref,
    gvec_ref,
    qw_ref,
    qp_ref,
    k_ref,
    v_ref,
    rel_ref,
    dproj_ref,
    dk_ref,
    dv_ref,
    drel_ref,
    bias_ref,
    rel_acc,
):
    rows, klen = qw_ref.shape[0], k_ref.shape[0]
    width = klen + block
    keys, values = k_ref[...], v_ref[...]
    row = lax.broadcasted_iota(jnp.int32, (block, block), 0)
    col = lax.broadcasted_iota(jnp.int32, (block, block), 1)
    mirror = (row + col == block - 1).astype(BF)
    rel_acc[...] = jnp.zeros_like(rel_acc)
    d_keys, d_values = [None, None], [None, None]
    word_sum = jnp.zeros((1, PAIR), F32)
    pos_sum = jnp.zeros((1, PAIR), F32)
    for part in range(rows // block):
        at = slice(part * block, (part + 1) * block)
        first = rows - (part + 1) * block
        gvec, qw = gvec_ref[at, :], qw_ref[at, :]
        gvec_t = jnp.transpose(gvec.astype(F32)).astype(BF)
        qw_t = jnp.transpose(qw.astype(F32)).astype(BF)
        qp_t = jnp.transpose(nn(mirror, qp_ref[at, :])).astype(BF)
        rel = rel_ref[first : first + width, :]
        word_parts, pos_parts = [], []
        for head in range(2):
            own = slice(head * DH, (head + 1) * DH)
            prob = prob_ref[head, at, :]
            d_prob = nt(head_lanes(gvec, head), values)
            weight = prob.astype(F32)
            inner = jnp.sum(weight * d_prob, axis=1, keepdims=True)
            g_sum = (weight * (d_prob - inner) * 0.125).astype(BF)
            dv = nn(gvec_t[own, :], prob)
            dk = nn(qw_t[own, :], g_sum)
            d_values[head] = dv if part == 0 else d_values[head] + dv
            d_keys[head] = dk if part == 0 else d_keys[head] + dk
            turned = nn(mirror, g_sum)
            padded = jnp.concatenate([jnp.zeros((block, block), F32), turned], axis=1)
            moved = pltpu.roll(padded, width - block + 1, 1, stride=1, stride_axis=0).astype(BF)
            word_parts.append(nn(turned.astype(BF), keys))
            pos_parts.append(nn(moved, rel))
            rel_acc[own, first : first + width] += nn(qp_t[own, :], moved)
        lane = lax.broadcasted_iota(jnp.int32, word_parts[0].shape, 1)
        word = jnp.where(lane < DH, word_parts[0], word_parts[1])
        pos = jnp.where(lane < DH, pos_parts[0], pos_parts[1])
        word_sum = word_sum + jnp.sum(word, axis=0, keepdims=True)
        pos_sum = pos_sum + jnp.sum(pos, axis=0, keepdims=True)
        dproj_ref[at, :] = nn(mirror, (word + pos).astype(BF)).astype(BF)
    for head in range(2):
        own = slice(head * DH, (head + 1) * DH)
        dv_ref[own, :] = d_values[head].astype(BF)
        dk_ref[own, :] = (8.0 * d_keys[head]).astype(BF)
    drel_ref[...] = (8.0 * rel_acc[...]).astype(BF)
    bias_ref[0:1, :] = word_sum
    bias_ref[1:2, :] = pos_sum


def attend_backward(prob, gvec, qw, qp, keys, values, rel, block, wires=()):
    rows, width = qw.shape
    klen, span = keys.shape[0], rel.shape[0]
    col = lambda count: pl.BlockSpec((count, PAIR), lambda p: (0, p))
    rowb = lambda count: pl.BlockSpec((PAIR, count), lambda p: (p, 0))
    in_specs = [
        pl.BlockSpec((2, rows, klen), lambda p: (p, 0, 0)),
        col(rows),
        col(rows),
        col(rows),
        col(klen),
        col(klen),
        col(span),
    ]
    out_specs = [col(rows), rowb(klen), rowb(klen), rowb(span), col(2)]
    out_shape = [
        jax.ShapeDtypeStruct((rows, width), BF),
        jax.ShapeDtypeStruct((width, klen), BF),
        jax.ShapeDtypeStruct((width, klen), BF),
        jax.ShapeDtypeStruct((width, span), BF),
        jax.ShapeDtypeStruct((2, width), F32),
    ]
    scratch = [pltpu.VMEM((PAIR, span), F32)]
    params = dict(vmem_limit_bytes=LIMIT)
    if wires:
        inner, mine = wires[0].shape[3], width // 8
        in_specs += [ANY_SPEC, ANY_SPEC]
        out_specs += [pl.BlockSpec(memory_space=pltpu.VMEM)] * 2 + [ANY_SPEC] * 2
        out_shape += [jax.ShapeDtypeStruct((mine, inner // 4), F32)] * 2
        out_shape += [jax.ShapeDtypeStruct((2, rows // 4, width), BF)] * 2
        scratch += [pltpu.SemaphoreType.DMA((4,)), pltpu.SemaphoreType.DMA((2,))]
        scratch += 2 * Reduce.scratch(1, 1, mine, inner, True)
        params.update(collective_id=3, has_side_effects=True)
    return pl.pallas_call(
        functools.partial(attend_backward_kernel, block, bool(wires)),
        grid=(width // PAIR,),
        in_specs=in_specs,
        out_specs=out_specs,
        out_shape=out_shape,
        scratch_shapes=scratch,
        compiler_params=pltpu.CompilerParams(**params),
        cost_estimate=pl.CostEstimate(
            flops=16 * rows * klen * width, bytes_accessed=20 << 20, transcendentals=0
        ),
        name="attend_backward",
    )(prob, gvec, qw, qp, keys, values, rel, *wires)


def norm_parts(value):
    center = value - jnp.mean(value, axis=1, keepdims=True)
    scale = lax.rsqrt(jnp.mean(center * center, axis=1, keepdims=True) + EPS)
    return center * scale, scale


def norm_pull(normed, scale, err):
    inner = jnp.mean(err * normed, axis=1, keepdims=True)
    return (err - jnp.mean(err, axis=1, keepdims=True) - normed * inner) * scale


def sum_rows(value):
    return jnp.sum(value, axis=0, keepdims=True)


def feed_kernel(steps, wired, *refs):
    (
        ud_hbm,
        wo_hbm,
        vec_ref,
        x_ref,
        tan_ref,
        upb_ref,
        dnb_ref,
        g1_ref,
        s1_ref,
        g2_ref,
        s2_ref,
        out_ref,
        dmix_ref,
        gvec_ref,
        go_ref,
        gud_ref,
        gupb_ref,
        small_ref,
        ud_ref,
        wo_ref,
        n1_ref,
        r1_ref,
        fb_ref,
        fbt_ref,
        acc_ref,
        act_ref,
        slope_ref,
        gd_ref,
        gdt_ref,
        sems,
        *pair_refs,
    ) = refs
    step = pl.program_id(0)
    chunk = act_ref.shape[2]
    row = lambda ref: ref[...].reshape(1, -1)
    cols = pl.ds(pl.multiple_of(lax.rem(step, steps) * chunk, chunk), chunk)

    if wired:
        own_ref, pair_ref, sum_ref, send, recv, keep = pair_refs
        place = Place()
        rows = pair_ref.shape[2]

        def span(c):
            return pl.ds(pl.multiple_of(c * chunk, chunk), chunk)

        def block(bits):
            return pl.ds(pl.multiple_of(place.dp(bits) * rows, 16), rows)

        def pair_copy(c, j):
            slot = lax.rem(c, 2)
            return push(
                own_ref.at[slot, :, block(chip_bits(j) | CORE), :],
                pair_ref.at[:, j, :, span(c)],
                send.at[slot, j],
                recv.at[c],
                place.dp(CORE),
                place.z,
            )

        def keep_copy(c):
            slot = lax.rem(c, 2)
            return pltpu.make_async_copy(sum_ref.at[slot], gud_ref.at[:, :, :, span(c)], keep.at[slot])

        def join(c):
            slot = lax.rem(c, 2)
            settle(pair_ref.at[:, :, :, span(c)], recv.at[c])
            pl.when(c >= 2)(lambda: keep_copy(c - 2).wait())
            for j in range(4):
                mine = own_ref[slot, :, block(chip_bits(j)), :].astype(F32)
                sum_ref[slot, :, j] = (mine + pair_ref[:, j, :, span(c)].astype(F32)).astype(BF)
            keep_copy(c).start()

        def send_wait(c):
            for j in range(4):
                pair_copy(c, j).wait_send()

        @pl.when(step == 0)
        def _():
            greet([(place.dp(CORE), place.z)])

    @pl.when(step == 0)
    def _():
        wo_copy = pltpu.make_async_copy(wo_hbm, wo_ref, sems.at[0])
        ud_copy = pltpu.make_async_copy(ud_hbm, ud_ref, sems.at[1])
        wo_copy.start()
        ud_copy.start()
        wo_copy.wait()
        normed, scale = norm_parts(nt(vec_ref[...], wo_ref[0]) + x_ref[...].astype(F32))
        n1_ref[...] = normed
        r1_ref[...] = scale
        first = normed * row(g1_ref) + row(s1_ref)
        fb_ref[...] = first.astype(BF)
        fbt_ref[...] = jnp.transpose(first).astype(BF)
        acc_ref[...] = first + row(dnb_ref)
        ud_copy.wait()

    @pl.when(step < steps)
    def _():
        upper = nn(fb_ref[...], ud_ref[0, :, cols]) + row(upb_ref)
        square = upper * upper
        root = 0.7978845608028654
        bend = jnp.tanh(root * (upper + 0.044715 * (square * upper)))
        half = 0.5 * (1.0 + bend)
        act = (upper * half).astype(BF)
        act_ref[step] = act
        slope_ref[step] = half + 0.5 * upper * (1.0 - bend * bend) * (
            root + (3 * 0.044715 * root) * square
        )
        acc_ref[...] += nt(act, ud_ref[1, :, cols])

    @pl.when(step == steps - 1)
    def _():
        normed, scale = norm_parts(acc_ref[...])
        out_ref[...] = (normed * row(g2_ref) + row(s2_ref)).astype(BF)
        tan = tan_ref[...].astype(F32)
        d_down = norm_pull(normed, scale, tan * row(g2_ref))
        small_ref[0:1, :] = sum_rows(d_down)
        small_ref[3:4, :] = sum_rows(tan * normed)
        small_ref[4:5, :] = sum_rows(tan)
        gd_ref[...] = d_down.astype(BF)
        gdt_ref[...] = jnp.transpose(d_down).astype(BF)
        acc_ref[...] = d_down

    @pl.when(step >= steps)
    def _():
        at = step - steps
        d_up = nn(gd_ref[...], ud_ref[1, :, cols]) * slope_ref[at]
        gupb_ref[...] = sum_rows(d_up)
        g_up = d_up.astype(BF)
        acc_ref[...] += nt(g_up, ud_ref[0, :, cols])
        if not wired:
            gud_ref[0] = nn(fbt_ref[...], g_up).astype(BF)
            gud_ref[1] = nn(gdt_ref[...], act_ref[at]).astype(BF)
            return
        pl.when(at >= 2)(lambda: send_wait(at - 2))
        slot = lax.rem(at, 2)
        own_ref[slot, 0] = nn(fbt_ref[...], g_up).astype(BF)
        own_ref[slot, 1] = nn(gdt_ref[...], act_ref[at]).astype(BF)
        for j in range(4):
            pair_copy(at, j).start()
        pl.when(at >= 1)(lambda: join(at - 1))

    @pl.when(step == 2 * steps - 1)
    def _():
        d_first, normed = acc_ref[...], n1_ref[...]
        small_ref[1:2, :] = sum_rows(d_first * normed)
        small_ref[2:3, :] = sum_rows(d_first)
        d_mixed = norm_pull(normed, r1_ref[...], d_first * row(g1_ref))
        dmix_ref[...] = d_mixed
        gvec_ref[...] = nn(d_mixed.astype(BF), wo_ref[0]).astype(BF)
        gdt_ref[...] = jnp.transpose(d_mixed).astype(BF)
        go_ref[...] = nn(gdt_ref[...], vec_ref[...]).astype(BF)
        if wired:
            join(steps - 1)
            for c in (steps - 2, steps - 1):
                send_wait(c)
                keep_copy(c).wait()


def feed(ud, wo, vec, x, tan, upb, vecs, wired):
    rows, width = vec.shape
    inner = upb.shape[0]
    chunk = 512
    steps = inner // chunk
    whole = lambda a, b: pl.BlockSpec((a, b), lambda i: (0, 0))
    late = lambda i: jnp.maximum(i - steps, 0)
    grads = pl.BlockSpec((2, width, chunk), lambda i: (0, 0, late(i)))
    grad_shape = (2, width, inner)
    params = dict(vmem_limit_bytes=LIMIT)
    scratch = []
    if wired:
        mine = width // 8
        grads, grad_shape = ANY_SPEC, (2, 4, mine, inner)
        scratch = [
            pltpu.VMEM((2, 2, width, chunk), BF),
            pltpu.VMEM(grad_shape, BF),
            pltpu.VMEM((2, 2, 4, mine, chunk), BF),
            pltpu.SemaphoreType.DMA((2, 4)),
            pltpu.SemaphoreType.DMA((steps,)),
            pltpu.SemaphoreType.DMA((2,)),
        ]
        params.update(collective_id=6, has_side_effects=True)
    return pl.pallas_call(
        functools.partial(feed_kernel, steps, wired),
        grid=(2 * steps,),
        in_specs=[ANY_SPEC] * 2
        + [whole(rows, width)] * 3
        + [pl.BlockSpec((chunk,), lambda i: (lax.rem(i, steps),))]
        + [pl.BlockSpec((width,), lambda i: (0,))] * 5,
        out_specs=[
            whole(rows, width),
            whole(rows, width),
            whole(rows, width),
            whole(width, width),
            grads,
            pl.BlockSpec((1, chunk), lambda i: (0, late(i))),
            whole(8, width),
        ],
        out_shape=[
            jax.ShapeDtypeStruct((rows, width), BF),
            jax.ShapeDtypeStruct((rows, width), F32),
            jax.ShapeDtypeStruct((rows, width), BF),
            jax.ShapeDtypeStruct((width, width), BF),
            jax.ShapeDtypeStruct(grad_shape, BF),
            jax.ShapeDtypeStruct((1, inner), F32),
            jax.ShapeDtypeStruct((8, width), F32),
        ],
        scratch_shapes=[
            pltpu.VMEM((2, width, inner), BF),
            pltpu.VMEM((1, width, width), BF),
            pltpu.VMEM((rows, width), F32),
            pltpu.VMEM((rows, 1), F32),
            pltpu.VMEM((rows, width), BF),
            pltpu.VMEM((width, rows), BF),
            pltpu.VMEM((rows, width), F32),
            pltpu.VMEM((steps, rows, chunk), BF),
            pltpu.VMEM((steps, rows, chunk), F32),
            pltpu.VMEM((rows, width), BF),
            pltpu.VMEM((width, rows), BF),
            pltpu.SemaphoreType.DMA((2,)),
        ]
        + scratch,
        compiler_params=pltpu.CompilerParams(**params),
        cost_estimate=pl.CostEstimate(
            flops=12 * rows * width * inner, bytes_accessed=36 << 20, transcendentals=rows * inner
        ),
        name="feed",
    )(ud, wo, vec, x, tan, upb, *vecs)


def project_step(
    w_ref,
    ctx_ref,
    q_ref,
    table_ref,
    wb_ref,
    pb_ref,
    k_ref,
    v_ref,
    rel_ref,
    qw_ref,
    qp_ref,
    x_ref,
    hooks=(),
):
    lead = lax.rem(lax.axis_index("dp"), 2) == 0
    flat = lambda ref: jnp.concatenate([ref[h : h + 1, :] for h in range(ref.shape[0])], axis=1)
    word_bias, pos_bias = flat(wb_ref), flat(pb_ref)
    klen, width = k_ref.shape
    back = klen - q_ref.shape[0]

    def context_rows(start):
        at = pl.ds(lax.div(start, 32), block // 32)
        return ctx_ref[at].reshape(block, width)

    block = 256

    def loop(count, step):
        def run(i, carry):
            step(pl.ds(pl.multiple_of(i * block, block), block))
            return carry

        lax.fori_loop(0, count // block, run, 0)

    def context_step(at):
        rows = context_rows(at.start)
        k_ref[at, :] = nn(rows, w_ref[0]).astype(BF)
        v_ref[at, :] = nn(rows, w_ref[1]).astype(BF)

    def stream_step(at):
        x_ref[at, :] = jnp.where(lead, context_rows(at.start + back), q_ref[at, :])
        proj = nn(x_ref[at, :], w_ref[2])
        qw_ref[at, :] = (0.125 * (proj + word_bias).astype(BF).astype(F32)).astype(BF)
        qp_ref[at, :] = (0.125 * (proj + pos_bias).astype(BF).astype(F32)).astype(BF)

    def table_step(at):
        rel_ref[at, :] = nn(table_ref[at, :], w_ref[3]).astype(BF)

    loop(table_ref.shape[0], table_step)
    if hooks:
        hooks[0]()
    loop(q_ref.shape[0], stream_step)
    if hooks:
        hooks[1]()
    loop(klen, context_step)


def project(mats, context, query, table, wb, pb):
    rows, width = query.shape
    klen, span = context.shape[0], table.shape[0]
    vmem = pl.BlockSpec(memory_space=pltpu.VMEM)
    return pl.pallas_call(
        project_step,
        in_specs=[vmem] * 6,
        out_specs=[vmem] * 6,
        out_shape=[
            jax.ShapeDtypeStruct((klen, width), BF),
            jax.ShapeDtypeStruct((klen, width), BF),
            jax.ShapeDtypeStruct((span, width), BF),
            jax.ShapeDtypeStruct((rows, width), BF),
            jax.ShapeDtypeStruct((rows, width), BF),
            jax.ShapeDtypeStruct((rows, width), BF),
        ],
        compiler_params=pltpu.CompilerParams(vmem_limit_bytes=LIMIT),
        cost_estimate=pl.CostEstimate(
            flops=2 * (2 * klen + rows + span) * width * width,
            bytes_accessed=20 << 20,
            transcendentals=0,
        ),
        name="project",
    )(mats, context.reshape(klen // 32, 2, 16, width), query, table, wb, pb)


def weight_grads_kernel(xt_ref, ct_ref, tt_ref, dp_ref, dk_ref, dv_ref, dr_ref, g_ref):
    g_ref[0] = nt(ct_ref[...], dk_ref[...]).astype(BF)
    g_ref[1] = nt(ct_ref[...], dv_ref[...]).astype(BF)
    g_ref[2] = nn(xt_ref[...], dp_ref[...]).astype(BF)
    g_ref[3] = nt(tt_ref[...], dr_ref[...]).astype(BF)


def weight_grads(x_t, ctx_t, table_t, d_proj, dk_t, dv_t, drel_t):
    width, rows = x_t.shape
    klen, span = ctx_t.shape[1], table_t.shape[1]
    chunk = 256
    whole = lambda a, b: pl.BlockSpec((a, b), lambda i: (0, 0))
    rowb = lambda b: pl.BlockSpec((chunk, b), lambda i: (i, 0))
    return pl.pallas_call(
        weight_grads_kernel,
        grid=(width // chunk,),
        in_specs=[
            whole(width, rows),
            whole(width, klen),
            whole(width, span),
            pl.BlockSpec((rows, chunk), lambda i: (0, i)),
            rowb(klen),
            rowb(klen),
            rowb(span),
        ],
        out_specs=pl.BlockSpec((4, width, chunk), lambda i: (0, 0, i)),
        out_shape=jax.ShapeDtypeStruct((4, width, width), BF),
        compiler_params=pltpu.CompilerParams(vmem_limit_bytes=LIMIT),
        cost_estimate=pl.CostEstimate(
            flops=2 * (rows + 2 * klen + span) * width * width,
            bytes_accessed=20 << 20,
            transcendentals=0,
        ),
        name="weight_grads",
    )(x_t, ctx_t, table_t, d_proj, dk_t, dv_t, drel_t)


def flip(arr, bit):
    return lax.ppermute(arr, "dp", [(i, i ^ bit) for i in range(lax.axis_size("dp"))])


def scatter_sum(grads):
    mine = lax.psum_scatter(grads, "dp", scatter_dimension=1, tiled=True)
    return lax.psum_scatter(mine, "tensor", scatter_dimension=2, tiled=True).astype(F32)


def body(
    content_stream,
    query_stream,
    memory,
    content_tangent,
    query_tangent,
    seq_lengths,
    factor_order,
    memory_lengths,
    slot_sequence,
    query_weight,
    key_weight,
    value_weight,
    pos_weight,
    out_weight,
    up_weight,
    up_bias,
    down_weight,
    down_bias,
    word_bias,
    pos_bias,
    first_gain,
    first_shift,
    second_gain,
    second_shift,
):
    groups, tensors = lax.axis_size("dp"), lax.axis_size("tensor")
    micro, part_len, width = content_stream.shape
    mem_part = memory.shape[1]
    seq_len, mem_total = part_len * tensors, mem_part * tensors
    klen, span = mem_total + seq_len, mem_total + 2 * seq_len
    count = micro * groups
    here, lane = lax.axis_index("dp"), lax.axis_index("tensor")
    core = here % 2
    lead = core == 0
    block = 256
    assert 2 * micro == tensors

    def swap(arr):
        return flip(arr, CORE)

    def to_unit(first, second):
        got = swap(jnp.where(lead, second, first))
        low = jnp.where(lead, first, got)
        high = jnp.where(lead, got, second)
        both = jnp.concatenate([low, high], 0)
        both = lax.all_to_all(both, "tensor", split_axis=0, concat_axis=0, tiled=True)
        return both.reshape(seq_len, width)

    def from_unit(arr):
        both = arr.reshape(tensors, part_len, width)
        both = lax.all_to_all(both, "tensor", split_axis=0, concat_axis=0, tiled=True)
        low, high = both[:micro], both[micro:]
        got = swap(jnp.where(lead, high, low))
        return jnp.where(lead, low, got), jnp.where(lead, got, high)

    seq_id = (here // 2) * tensors + lane
    mats = [key_weight, value_weight, query_weight, pos_weight, out_weight]
    table = jnp.asarray(reversed_table(span, klen, width))
    wires = ()
    if groups == 8:
        keys, values, rel, q_word, q_pos, stream, thr, key_rank, weights, context, *wires = enter(
            slot_sequence,
            seq_lengths,
            memory_lengths,
            content_stream,
            query_stream,
            memory,
            table,
            factor_order,
            mats,
            up_weight,
            down_weight,
            word_bias,
            pos_bias,
        )
        wires += [content_tangent, query_tangent]
        context = context.reshape(klen, width)
    else:
        ids = jnp.arange(count, dtype=jnp.int32)
        slot_of = jnp.sum(jnp.where(slot_sequence[None, :] == ids[:, None], ids[None, :], 0), axis=1)
        counts = jnp.concatenate([seq_lengths, memory_lengths])
        slot = slot_of[seq_id]
        lengths = lax.all_gather(counts, "dp", axis=0, tiled=False)
        orders = lax.all_gather(factor_order, "dp", axis=0, tiled=False)[seq_id // micro]
        stream = to_unit(content_stream, query_stream)
        content, query = jnp.where(lead, stream, swap(stream)), stream
        tangent = to_unit(content_tangent, query_tangent)
        piece = mem_part // groups
        spread = lax.all_to_all(
            memory.reshape(micro, groups, piece, width), "dp", split_axis=1, concat_axis=1, tiled=True
        )
        spread = spread.transpose(1, 0, 2, 3).reshape(count, piece, width)
        spread = jnp.take(spread, slot_of, axis=0)
        spread = spread.reshape(groups // 2, tensors, 2, piece // 2, width).transpose(0, 2, 1, 3, 4)
        spread = lax.all_to_all(
            spread.reshape(groups, tensors, piece // 2, width),
            "dp",
            split_axis=0,
            concat_axis=0,
            tiled=True,
        )
        spread = lax.all_to_all(spread, "tensor", split_axis=1, concat_axis=1, tiled=True)
        got = swap(spread)
        mem_rows = jnp.stack([jnp.where(lead, spread, got), jnp.where(lead, got, spread)])
        mem_rows = mem_rows.transpose(2, 1, 0, 3, 4).reshape(mem_total, width)
        context = jnp.concatenate([mem_rows, content], 0)

        def whole(mat):
            mat = lax.all_gather(mat, "tensor", axis=1, tiled=True)
            return lax.all_gather(mat, "dp", axis=0, tiled=True)

        weights = jnp.stack([whole(mat) for mat in mats[:4]])
        wo = whole(out_weight)[None]
        ud = jnp.stack([whole(up_weight), whole(down_weight)])
        keys, values, rel, q_word, q_pos, stream = project(
            weights, context, query, table, word_bias, pos_bias
        )
        length = lengths[seq_id // micro, seq_id % micro]
        mem_valid = lengths[slot // micro, micro + slot % micro]
        rank = orders[seq_id % micro]
        key_pos = jnp.arange(klen, dtype=jnp.int32)
        hidden = jnp.int32(1 << 20)
        mem_rank = jnp.where(key_pos[:mem_total] >= mem_total - mem_valid, -1, hidden)
        own_rank = jnp.where(key_pos[:seq_len] < length, rank, hidden)
        key_rank = jnp.concatenate([mem_rank, own_rank])[None, :]
        thr = (rank + jnp.where(lead, 1, 0))[:, None]

    vec, prob, *arrived = attend_forward(
        q_word, q_pos, keys, values, rel, thr, key_rank, block, wires
    )
    if wires:
        wo, ud, tangent = arrived
    out, d_mixed, g_vec, g_out, g_ud, g_upb, small = feed(
        ud,
        wo,
        vec,
        stream,
        tangent,
        up_bias,
        (down_bias, first_gain, first_shift, second_gain, second_shift),
        groups == 8,
    )
    backward = (prob, g_vec, q_word, q_pos, keys, values, rel, block)
    if groups == 8:
        d_proj, dk_t, dv_t, drel_t, biases, grad_up, grad_down, content_out, query_out = (
            attend_backward(*backward, (g_ud, out))
        )
    else:
        d_proj, dk_t, dv_t, drel_t, biases = attend_backward(*backward)
        content_out, query_out = from_unit(out)
        grad_up, grad_down = scatter_sum(g_ud)
    small = jnp.concatenate([g_upb.reshape(-1), small[:5].reshape(-1), biases.reshape(-1)])
    inner = up_bias.shape[0]
    table_t = jnp.asarray(np.ascontiguousarray(reversed_table(span, klen, width).T))
    if groups == 8:
        small = jnp.pad(small, (0, -small.shape[0] % 1024)).reshape(-1, 128)
        arrays = [stream, d_proj, context, dk_t, dv_t, weights, table_t, drel_t]
        (
            grad_key,
            grad_value,
            grad_query,
            grad_pos,
            grad_out,
            content_grad,
            query_grad,
            small,
        ) = finish(arrays, g_out[None], d_mixed, small)
        arrays = [content_out, query_out, content_grad, query_grad, grad_query, grad_key]
        arrays += [grad_value, grad_pos, grad_out, grad_up, grad_down]
        *arrays, up_sum, down_sum, a1, b1, a2, b2, word_sum, pos_sum = emit(
            small, arrays, inner, width
        )
        return *arrays[:10], up_sum, arrays[10], down_sum, word_sum, pos_sum, a1, b1, a2, b2
    else:
        d_context = tt(dk_t[:, mem_total:], weights[0]) + tt(dv_t[:, mem_total:], weights[1])
        partner = swap(d_context.astype(BF)).astype(F32)
        d_stream = d_mixed + nt(d_proj, weights[2]) + jnp.where(lead, d_context + partner, 0.0)
        content_grad, query_grad = from_unit(d_stream.astype(BF))
        grad_key, grad_value, grad_query, grad_pos = scatter_sum(
            weight_grads(jnp.transpose(stream), jnp.transpose(context), table_t, d_proj, dk_t, dv_t, drel_t)
        )
        (grad_out,) = scatter_sum(g_out[None])
        small = lax.psum(small, ("dp", "tensor"))
    rest = small[inner:].reshape(7, width)
    return (
        content_out,
        query_out,
        content_grad,
        query_grad,
        grad_query,
        grad_key,
        grad_value,
        grad_pos,
        grad_out,
        grad_up,
        small[:inner],
        grad_down,
        rest[0],
        rest[5].reshape(HEADS, DH),
        rest[6].reshape(HEADS, DH),
        rest[1],
        rest[2],
        rest[3],
        rest[4],
    )


def solution(mesh):
    rows = P("dp", "tensor", None)
    mat = P("dp", "tensor")
    return jax.shard_map(
        body,
        mesh=mesh,
        in_specs=(rows,) * 5
        + (P("dp"), P("dp", None), P("dp"), P())
        + (mat,) * 6
        + (P(), mat)
        + (P(),) * 7,
        out_specs=(rows,) * 4 + (mat,) * 6 + (P(), mat) + (P(),) * 7,
        check_vma=False,
    )
```

```python
import functools

import jax
import jax.numpy as jnp
import numpy as np
from jax import lax
from jax.experimental import pallas as pl
from jax.experimental.pallas import tpu as pltpu
from jax.sharding import PartitionSpec as P

HEADS = 12
DH = 64
PAIR = 2 * DH
EPS = 1e-06
BF = jnp.bfloat16
F32 = jnp.float32
LIMIT = 60 * 1024 * 1024
SMEM_SPEC = pl.BlockSpec(memory_space=pltpu.SMEM)
ANY_SPEC = pl.BlockSpec(memory_space=pl.ANY)


def nn(left, right):
    return jnp.dot(left, right, preferred_element_type=F32)


def nt(left, right):
    return lax.dot_general(left, right, (((1,), (1,)), ((), ())), preferred_element_type=F32)


def tn(left, right):
    return lax.dot_general(left, right, (((0,), (0,)), ((), ())), preferred_element_type=F32)


def tt(left, right):
    return lax.dot_general(left, right, (((0,), (1,)), ((), ())), preferred_element_type=F32)


def reversed_table(count, first, width):
    dist = (first - np.arange(count)).astype(np.float32)
    half = width // 2
    power = np.arange(half).astype(np.float32) * np.float32(2.0 / width)
    freq = np.float32(1.0) / np.float32(10000.0) ** power
    angle = (dist[:, None] * freq[None, :]).astype(np.float64)
    return np.concatenate([np.sin(angle), np.cos(angle)], axis=1).astype(np.float32).astype(BF)


MESH = pl.DeviceIdType.MESH
CORE, XBIT, YBIT = 1, 2, 4


class Place:
    def __init__(self):
        self.d, self.z = lax.axis_index("dp"), lax.axis_index("tensor")
        self.core = lax.rem(self.d, 2)
        self.x = lax.rem(lax.div(self.d, 2), 2)
        self.y = lax.div(self.d, 4)

    def dp(self, bits):
        at = self.d
        if bits & CORE:
            at = at + (1 - 2 * self.core)
        if bits & XBIT:
            at = at + (2 - 4 * self.x)
        if bits & YBIT:
            at = at + (4 - 8 * self.y)
        return at

    def up(self, step):
        return lax.rem(self.z + step, 4) if step else self.z


def push(src, dst, send, recv, dp, z):
    return pltpu.make_async_remote_copy(
        src_ref=src,
        dst_ref=dst,
        send_sem=send,
        recv_sem=recv,
        device_id=(dp, z),
        device_id_type=MESH,
    )


def settle(ref, sem):
    pltpu.make_async_copy(ref, ref, sem).wait()


def greet(partners):
    barrier = pltpu.get_barrier_semaphore()
    for partner in partners:
        pl.semaphore_signal(barrier, inc=1, device_id=partner, device_id_type=MESH)
    pl.semaphore_wait(barrier, len(partners))


GATHER = (
    (0, 0, XBIT),
    (0, 1, YBIT),
    (0, 0, YBIT),
    (0, 1, XBIT),
    (XBIT, 0, YBIT),
    (YBIT, 1, XBIT),
    (0, 0, CORE),
    (0, 1, CORE),
    (XBIT, 0, CORE),
    (YBIT, 1, CORE),
    (YBIT, 0, CORE),
    (XBIT, 1, CORE),
    (XBIT | YBIT, 0, CORE),
    (XBIT | YBIT, 1, CORE),
)


class Gather:
    def __init__(self, place, dst, own, send, recv):
        self.place, self.dst, self.own = place, dst, own
        self.send, self.recv = send, recv
        self.half = dst.shape[1] // 16

    def region(self, owner, half):
        at = self.place.dp(owner) * (2 * self.half) + half * self.half
        return self.dst.at[:, pl.ds(pl.multiple_of(at, 16), self.half), :]

    def copy(self, i):
        owner, half, to = GATHER[i]
        src = self.region(owner, half)
        if owner == 0 and self.own is not None:
            src = self.own.at[:, half * self.half : (half + 1) * self.half, :]
        place = self.place
        return push(
            src, self.region(owner, half), self.send.at[i], self.recv.at[i], place.dp(to), place.z
        )

    def start(self, *which):
        for i in which:
            self.copy(i).start()

    def wait(self, received, sent):
        for i in received:
            self.copy(i).wait_recv()
        for i in sent:
            self.copy(i).wait_send()

    def after(self, arrived, started):
        for i, more in zip(arrived, started):
            self.copy(i).wait_recv()
            for j in more:
                self.copy(j).start()

    def middle(self):
        self.after((0, 1), ((4, 8), (5, 9)))

    def last(self):
        self.after((2, 3, 4, 5), ((10,), (11,), (12,), (13,)))


def chip_bits(j):
    return (XBIT if j & 1 else 0) | (YBIT if j & 2 else 0)


def add_into(dst, src):
    def run(i, carry):
        at = pl.ds(pl.multiple_of(i * 16, 16), 16)
        dst[:, at, :] = (dst[:, at, :].astype(F32) + src[:, at, :].astype(F32)).astype(BF)
        return carry

    lax.fori_loop(0, dst.shape[1] // 16, run, 0)


class Reduce:
    def __init__(self, place, sources, scratch, out, paired=False):
        self.place, self.sources, self.out, self.paired = place, sources, out, paired
        self.total, self.pair, self.near, self.far, self.quarter, self.stage = scratch[:6]
        self.pair_send, self.pair_recv, self.load, self.send, self.recv, self.z_send, self.z_recv = scratch[6:]
        self.rows = self.total.shape[2]

    @staticmethod
    def scratch(count, n, rows, cols, paired=False):
        part = cols // 4
        dma = lambda k: pltpu.SemaphoreType.DMA((k,))
        return [
            pltpu.VMEM((n, 4, rows, cols), BF),
            pltpu.VMEM((8, 128) if paired else (n, 4, rows, cols), BF),
            pltpu.VMEM((n, 2, 2, rows // 2, cols), BF),
            pltpu.VMEM((n, 2, rows // 2, cols), BF),
            pltpu.VMEM((4, n, rows, part), BF),
            pltpu.VMEM((4, n, rows, part) if part % 128 else (8, 128), BF),
            dma(4 * count),
            dma(4 * count),
            dma(4 * count),
            dma(6),
            dma(6),
            dma(3),
            dma(1),
        ]

    def pair_copies(self, j):
        place, rows = self.place, self.rows
        copies, at = [], 0
        for i, src in enumerate(self.sources):
            slot, n = len(self.sources) * j + i, src.shape[0]
            block = lambda bits: src.at[:, pl.ds(pl.multiple_of(place.dp(bits) * rows, 16), rows), :]
            remote = push(
                block(chip_bits(j) | CORE),
                self.pair.at[at : at + n, j],
                self.pair_send.at[slot],
                self.pair_recv.at[slot],
                place.dp(CORE),
                place.z,
            )
            local = pltpu.make_async_copy(
                block(chip_bits(j)), self.total.at[at : at + n, j], self.load.at[slot]
            )
            copies.append((remote, local))
            at += n
        return copies

    def half(self, j, h):
        size = self.rows // 2
        return self.total.at[:, j, h * size : (h + 1) * size, :]

    MOVES = ((3, 0, XBIT, 1), (3, 1, YBIT, 1), (1, 0, XBIT, 0), (2, 1, YBIT, 0), (2, 0, YBIT, 0), (1, 1, XBIT, 1))

    def move(self, i):
        j, h, to, where = self.MOVES[i]
        dst = self.near.at[:, h, where] if i < 4 else self.far.at[:, where]
        place = self.place
        return push(self.half(j, h), dst, self.send.at[i], self.recv.at[i], place.dp(to), place.z)

    def z_copy(self, k):
        place, part = self.place, self.quarter.shape[3]
        to = place.up(k)
        if part % 128:
            src = self.stage.at[to]
        else:
            src = self.total.at[:, 0, :, pl.ds(pl.multiple_of(to * part, 128), part)]
        dst = self.quarter.at[place.z]
        if k == 0:
            return pltpu.make_async_copy(src, dst, self.z_recv.at[0])
        return push(src, dst, self.z_send.at[k - 1], self.z_recv.at[0], place.d, to)

    def loaded(self, j):
        src, near = self.sources
        if j == 3:
            return pltpu.make_async_copy(near, self.near, self.load.at[3])
        return pltpu.make_async_copy(src.at[:, j], self.total.at[:, j], self.load.at[j])

    def begin(self):
        for j in (3, 1, 2, 0):
            if self.paired:
                self.loaded(j).start()
                continue
            for remote, local in self.pair_copies(j):
                remote.start()
                local.start()

    def pairs(self):
        for j, moves in ((3, (0, 1)), (1, (2,)), (2, (3,)), (0, ())):
            for remote, local in self.pair_copies(j):
                local.wait()
                remote.wait_recv()
            add_into(self.total.at[:, j], self.pair.at[:, j])
            for i in moves:
                self.move(i).start()

    def middle(self):
        for i, j, h, where, more in ((0, 2, 0, 1, 4), (1, 1, 1, 1, 5), (2, 0, 0, 0, None), (3, 0, 1, 0, None)):
            if not self.paired:
                self.move(i).wait_recv()
            elif i == 0:
                for k in range(4):
                    self.loaded(k).wait()
            add_into(self.half(j, h), self.near.at[:, h, where])
            if more is not None:
                self.move(more).start()

    def late(self):
        for i, h in ((4, 0), (5, 1)):
            self.move(i).wait_recv()
            add_into(self.half(0, h), self.far.at[:, h])
        part = self.quarter.shape[3]
        if part % 128:
            for k in range(4):
                for m in range(self.total.shape[0]):
                    self.stage[k, m] = self.total[m, 0, :, k * part : (k + 1) * part]
        for k in (2, 1, 3, 0):
            self.z_copy(k).start()

    def end(self):
        settle(self.quarter, self.z_recv.at[0])
        parts = [self.quarter[k].astype(F32) for k in range(4)]
        total = (parts[0] + parts[1]) + (parts[2] + parts[3])
        self.out[...] = total.reshape(self.out.shape)
        if not self.paired:
            for j in range(4):
                for remote, _ in self.pair_copies(j):
                    remote.wait_send()
        for i in range(4 if self.paired else 0, 6):
            self.move(i).wait_send()
        for k in range(1, 4):
            self.z_copy(k).wait_send()


class Homeward:
    def __init__(self, place, src, homes, send, recv):
        self.place, self.src, self.homes, self.send, self.recv = place, src, homes, send, recv
        self.part = homes[0].shape[1]

    def act(self, what):
        place, part = self.place, self.part
        for u in range(2):

            @pl.when(place.core == u)
            def _():
                for k in (2, 1, 3, 0):
                    to, dp = place.up(k), place.d - place.core + lax.div(place.z, 2)
                    src = self.src.at[pl.ds(pl.multiple_of(to * part, 16), part), :]
                    dst = self.homes[u].at[lax.rem(place.z, 2)]
                    recv = self.recv.at[u]
                    here = jnp.logical_and(dp == place.d, to == place.z)
                    remote = push(src, dst, self.send.at[k], recv, dp, to)
                    if what == "start":
                        pl.when(here)(pltpu.make_async_copy(src, dst, recv).start)
                        pl.when(jnp.logical_not(here))(remote.start)
                    else:
                        pl.when(jnp.logical_not(here))(remote.wait_send)

    def start(self):
        self.act("start")

    def end(self):
        for u in range(2):
            settle(self.homes[u], self.recv.at[u])
        self.act("wait")


def pair_and_z(place):
    return [(place.dp(r), place.up(k)) for k in range(4) for r in (0, CORE) if r or k]


def near_partners(place):
    return pair_and_z(place) + [(place.dp(r), place.z) for r in (XBIT, YBIT)]


INPUTS = 8


def finish_kernel(*refs):
    hbm, (mixed_ref, small_ref) = refs[:INPUTS], refs[INPUTS : INPUTS + 2]
    grad_refs, home_refs, sums_ref = refs[INPUTS + 2 : INPUTS + 6], refs[INPUTS + 6 : INPUTS + 8], refs[INPUTS + 8]
    refs = refs[INPUTS + 9 :]
    held, refs = refs[:INPUTS], refs[INPUTS:]
    loads, x_t, ctx_t, g_ref, base, ctx, partner, stream, slots, part_sum, chips = refs[:11]
    home_send, slot_send, chip_send, one_send, recv = refs[11:16]
    refs = refs[16:]
    count = len(refs) // 4
    place = Place()
    d, z, core = place.d, place.z, place.core
    copies = [
        pltpu.make_async_copy(a.at[0:3] if i == 5 else a, b, loads.at[i])
        for i, (a, b) in enumerate(zip(hbm, held))
    ]
    for copy in copies:
        copy.start()

    def need(*which):
        for i in which:
            copies[i].wait()
        return [held[i] for i in which]

    greet(near_partners(place) + [(place.dp(XBIT | YBIT), z)])
    sources = [g_ref.at[m : m + 1] for m in range(4)]
    key, value, query, pos = [
        Reduce(place, (src,), refs[m * count : (m + 1) * count], grad_refs[m])
        for m, src in enumerate(sources)
    ]
    slot_copies = []
    others = [(r, k) for k in range(4) for r in (0, CORE) if r or k]
    for i, (r, k) in enumerate(others):
        copy = push(small_ref, slots.at[4 * core + z], slot_send.at[i], recv.at[1], place.dp(r), place.up(k))
        copy.start()
        slot_copies.append(copy)
    pltpu.make_async_copy(small_ref, slots.at[4 * core + z], recv.at[1]).start()

    width, block = g_ref.shape[1], 256

    def product(m, left, right, dot):
        def run(i, carry):
            at = pl.ds(pl.multiple_of(i * block, block), block)
            g_ref[m, at, :] = dot(left[at, :], right[...]).astype(BF)
            return carry

        lax.fori_loop(0, width // block, run, 0)

    def turn(src, dst):
        def run(i, carry):
            at = pl.ds(pl.multiple_of(i * block, block), block)
            dst[:, at] = jnp.transpose(src[at, :].astype(F32)).astype(BF)
            return carry

        lax.fori_loop(0, src.shape[0] // block, run, 0)

    x_ref, d_proj = need(0, 1)
    turn(x_ref, x_t)
    product(2, x_t, d_proj, nn)
    query.begin()
    ctx_ref, dk_t = need(2, 3)
    turn(ctx_ref, ctx_t)
    product(0, ctx_t, dk_t, nt)
    key.begin()

    dv_t, mats = need(4, 5)
    back = dk_t.shape[1] - base.shape[0]

    def from_context(i, carry):
        at = pl.ds(pl.multiple_of(i * block, block), block)
        cols = pl.ds(pl.multiple_of(i * block + back, block), block)
        turned = nn(mats[0], dk_t[:, cols]) + nn(mats[1], dv_t[:, cols])
        turned = jnp.transpose(turned)
        base[at, :] = turned
        ctx[at, :] = turned.astype(BF)
        return carry

    lax.fori_loop(0, base.shape[0] // block, from_context, 0)
    swap = push(ctx, partner, one_send.at[0], recv.at[0], place.dp(CORE), z)
    swap.start()

    def from_proj(i, carry):
        at = pl.ds(pl.multiple_of(i * block, block), block)
        own = mixed_ref[at, :] + nt(d_proj[at, :], mats[2])
        base[at, :] = own + jnp.where(core == 0, base[at, :], 0.0)
        return carry

    lax.fori_loop(0, base.shape[0] // block, from_proj, 0)
    query.pairs()
    product(1, ctx_t, dv_t, nt)
    value.begin()
    key.pairs()

    swap.wait()
    small_block = 64

    def add_partner(i, carry):
        at = pl.ds(pl.multiple_of(i * small_block, small_block), small_block)
        more = jnp.where(core == 0, partner[at, :].astype(F32), 0.0)
        stream[at, :] = (base[at, :] + more).astype(BF)
        return carry

    lax.fori_loop(0, stream.shape[0] // small_block, add_partner, 0)
    home = Homeward(place, stream, home_refs, home_send, recv.at[2:4])
    home.start()

    table_t, dr_t = need(6, 7)
    product(3, table_t, dr_t, nt)
    pos.begin()
    value.pairs()
    query.middle()

    settle(slots, recv.at[1])
    total = slots[0]
    for i in range(1, 8):
        total = total + slots[i]
    part_sum[...] = total
    chip = lax.div(d, 2)
    chip_copies = []
    for i, r in enumerate((XBIT, YBIT, XBIT | YBIT)):
        copy = push(part_sum, chips.at[chip], chip_send.at[i], recv.at[4], place.dp(r), z)
        copy.start()
        chip_copies.append(copy)
    pltpu.make_async_copy(part_sum, chips.at[chip], recv.at[4]).start()

    pos.pairs()
    key.middle()
    query.late()
    value.middle()
    key.late()
    pos.middle()
    value.late()
    settle(chips, recv.at[4])
    sums_ref[...] = (chips[0] + chips[1]) + (chips[2] + chips[3])
    pos.late()
    for reduce in (query, key, value, pos):
        reduce.end()
    home.end()
    for copy in slot_copies + chip_copies:
        copy.wait_send()


def finish(arrays, mixed, small):
    total, width = arrays[0].shape
    klen = arrays[2].shape[0]
    rows = width // 8
    vmem = pl.BlockSpec(memory_space=pltpu.VMEM)
    dma = lambda k: pltpu.SemaphoreType.DMA((k,))
    scratch = [pltpu.VMEM((3,) + a.shape[1:] if a.ndim == 3 else a.shape, BF) for a in arrays]
    scratch += [
        dma(INPUTS),
        pltpu.VMEM((width, total), BF),
        pltpu.VMEM((width, klen), BF),
        pltpu.VMEM((4, width, width), BF),
        pltpu.VMEM((total, width), F32),
        pltpu.VMEM((total, width), BF),
        pltpu.VMEM((total, width), BF),
        pltpu.VMEM((total, width), BF),
        pltpu.VMEM((8,) + small.shape, F32),
        pltpu.VMEM(small.shape, F32),
        pltpu.VMEM((4,) + small.shape, F32),
        dma(4),
        dma(7),
        dma(3),
        dma(1),
        dma(5),
    ]
    for _ in range(4):
        scratch += Reduce.scratch(1, 1, rows, width)
    return pl.pallas_call(
        finish_kernel,
        in_specs=[ANY_SPEC] * INPUTS + [vmem] * 2,
        out_specs=[vmem] * 4 + [ANY_SPEC] * 2 + [vmem],
        out_shape=[jax.ShapeDtypeStruct((rows, width // 4), F32)] * 4
        + [jax.ShapeDtypeStruct((2, total // 4, width), BF)] * 2
        + [
            jax.ShapeDtypeStruct(small.shape, F32),
        ],
        scratch_shapes=scratch,
        compiler_params=pltpu.CompilerParams(
            collective_id=4, has_side_effects=True, vmem_limit_bytes=LIMIT
        ),
        cost_estimate=pl.CostEstimate(flops=20 << 30, bytes_accessed=64 << 20, transcendentals=0),
        name="finish",
    )(*arrays, mixed, small)


def emit_kernel(small_ref, *refs):
    count = 11
    for src, dst in zip(refs[:count], refs[count : 2 * count]):
        dst[...] = src[...]
    wide, *rows, word_ref, pos_ref = refs[2 * count :]
    lanes = small_ref.shape[1]
    size = wide.shape[0] // lanes
    wide[...] = small_ref[0:size, :].reshape(wide.shape)
    for ref in rows:
        step = ref.shape[0] // lanes
        ref[...] = small_ref[size : size + step, :].reshape(ref.shape)
        size += step
    for ref in (word_ref, pos_ref):
        for h in range(HEADS):
            at = size + h * DH // lanes
            ref[h : h + 1, :] = small_ref[at : at + 1, h * DH % lanes : h * DH % lanes + DH]
        size += HEADS * DH // lanes


def emit(small, arrays, inner, width):
    vmem = pl.BlockSpec(memory_space=pltpu.VMEM)
    out_shape = [jax.ShapeDtypeStruct(a.shape, a.dtype) for a in arrays]
    out_shape += [jax.ShapeDtypeStruct((inner,), F32)]
    out_shape += [jax.ShapeDtypeStruct((width,), F32)] * 5
    out_shape += [jax.ShapeDtypeStruct((HEADS, DH), F32)] * 2
    return pl.pallas_call(
        emit_kernel,
        in_specs=[vmem] * (1 + len(arrays)),
        out_specs=[vmem] * len(out_shape),
        out_shape=out_shape,
        compiler_params=pltpu.CompilerParams(vmem_limit_bytes=LIMIT),
        name="emit",
    )(small, *arrays)


def pack(mat):
    half = mat.shape[0] // 2
    return jnp.concatenate([mat[:, :128], jnp.concatenate([mat[:half, 128:], mat[half:, 128:]], axis=1)], axis=0)


def unpack(packed):
    rows = packed.shape[0] * 2 // 3
    rest = packed[rows:, :]
    return jnp.concatenate([packed[:rows, :], jnp.concatenate([rest[:, :64], rest[:, 64:]], axis=0)], axis=1)


def enter_kernel(slot_ref, seq_ref, mem_ref, content, query, memory, table_hbm, orders, *refs):
    mats, (upw, dnw), (wb_ref, pb_ref) = refs[:5], refs[5:7], refs[7:9]
    outs, (thr_ref, key_ref, whole_out, context_out, wo, ud) = refs[9:15], refs[15:21]
    (
        ints,
        all_ints,
        whole,
        context,
        stream,
        table,
        spread,
        picked,
        shards,
        slab,
        mat_send,
        mat_recv,
        ud_send,
        ud_recv,
        int_send,
        spread_send,
        pick_send,
        stream_send,
        pair_send,
        gather_send,
        gather_recv,
        wo_send,
        wo_recv,
        far_send,
        far_recv,
        recv,
        local,
    ) = refs[21:]
    place = Place()
    d, z, core = place.d, place.z, place.core
    up, down, far = place.up(1), place.up(3), place.up(2)
    part = query.shape[1]
    micro = orders.shape[0]
    spot = lax.broadcasted_iota(jnp.int32, (1, ints.shape[1]), 1)
    lengths = jnp.where(spot == 0, seq_ref[0], seq_ref[1])
    lengths = jnp.where(spot < 2, lengths, jnp.where(spot == 2, mem_ref[0], mem_ref[1]))
    ints[...] = jnp.concatenate([orders[...], jnp.broadcast_to(lengths, (6, ints.shape[1]))], axis=0)

    def slot_of(seq):
        at = jnp.int32(0)
        for k in range(16):
            at = at + jnp.where(slot_ref[k] == seq, k, 0)
        return jnp.minimum(at, 15)

    pltpu.make_async_copy(table_hbm, table, local.at[0]).start()
    piece = spread.shape[1]
    blocks = part // piece // 2
    first = 4 * blocks
    greet([(place.dp(r), place.up(k)) for r in range(8) for k in range(4) if r or k])

    spread_copies = []
    for r in range(8):
        to = place.dp(r)
        src = memory.at[:, pl.ds(pl.multiple_of(to * piece, 16), piece), :]
        dst = spread.at[pl.ds(2 * d, 2)]
        if r == 0:
            pltpu.make_async_copy(src, dst, recv.at[0]).start()
        else:
            spread_copies.append(push(src, dst, spread_send.at[r - 1], recv.at[0], to, z))
            spread_copies[-1].start()

    for m, mat in enumerate(mats):
        shards[z, m] = pack(mat[...])
    cutoff = shards.shape[2] * 5 // 9

    def mat_copy(i):
        own = shards.at[z]
        low, high = shards.at[down, :, :cutoff], shards.at[up, :, cutoff:]
        src = (own, own, low, high)[i]
        return push(src, src, mat_send.at[i], mat_recv.at[i], d, (up, down, up, down)[i])

    mat_copy(0).start()
    mat_copy(1).start()
    rows = slab.shape[1]
    width = upw.shape[1]

    def columns(at, start=0, size=rows):
        mine = pl.ds(pl.multiple_of(d * rows + start, 16), size)
        return ud.at[:, mine, pl.ds(pl.multiple_of(at * width, 128), width)]

    def ud_copy(i):
        if i < 4:
            src, dst = (upw, dnw)[i % 2], columns(z).at[i % 2]
            return push(src, dst, ud_send.at[i], ud_recv.at[i // 2], d, (up, down)[i // 2])
        half = rows // 2
        src = columns(down, 0, half) if i == 4 else columns(up, half, half)
        return push(src, src, ud_send.at[i], ud_recv.at[i - 2], d, (up, down)[i - 4])

    for m, mat in enumerate((upw, dnw)):
        pltpu.make_async_copy(mat, columns(z).at[m], recv.at[8]).start()

    int_copies = []
    for r in range(8):
        if r == 0:
            pltpu.make_async_copy(ints, all_ints.at[d], recv.at[2]).start()
        else:
            copy = push(ints, all_ints.at[d], int_send.at[r - 1], recv.at[2], place.dp(r), z)
            int_copies.append(copy)
            copy.start()

    def stream_copy(i, act):
        j, kind = i // 2, i % 2
        to, dp = 2 * core + j, d - core + kind
        if kind == 0:
            src, sem = content.at[j], recv.at[3]
            dst = context.at[pl.ds(first + blocks * z, blocks)]
        else:
            src, sem = query.at[j], recv.at[4]
            dst = stream.at[pl.ds(pl.multiple_of(z * part, 16), part), :]
        here = jnp.logical_and(dp == d, to == z)
        remote = push(src, dst, stream_send.at[i], sem, dp, to)
        if act == "start":
            pl.when(here)(pltpu.make_async_copy(src, dst, sem).start)
            pl.when(jnp.logical_not(here))(remote.start)
        else:
            pl.when(jnp.logical_not(here))(remote.wait_send)

    mat_copy(0).wait_recv()
    mat_copy(2).start()
    mat_copy(1).wait_recv()
    mat_copy(3).start()
    for i in range(4):
        ud_copy(i).start()
    mat_copy(2).wait_recv()
    mat_copy(3).wait_recv()
    for m in range(5):
        slab[m] = jnp.concatenate([unpack(shards[k, m]) for k in range(4)], axis=1)
    own_rows = pl.ds(pl.multiple_of(d * rows, 16), rows)
    gather = Gather(place, whole, slab.at[0:4], gather_send, gather_recv)
    gather.start(0, 1, 2, 3, 6, 7)
    pltpu.make_async_copy(slab.at[0:4], whole.at[:, own_rows, :], recv.at[6]).start()
    pltpu.make_async_copy(slab.at[4:5], wo.at[:, own_rows, :], recv.at[7]).start()

    settle(columns(down), ud_recv.at[0])
    ud_copy(4).start()
    settle(columns(up), ud_recv.at[1])
    ud_copy(5).start()
    for i in range(4):
        stream_copy(i, "start")

    settle(spread, recv.at[0])
    for q in range(16):
        picked[q] = spread[slot_of(q)]
    pick_copies = []
    for r in (YBIT | XBIT, XBIT, YBIT, 0):
        for k in range(4):
            to, lane = place.dp(r), place.up(k)
            src = picked.at[4 * lax.div(to, 2) + lane]
            dst = context.at[blocks * z + lax.div(d, 2), core]
            if r or k:
                copy = push(src, dst, pick_send.at[2 * r + k - 1], recv.at[5], to, lane)
                pick_copies.append(copy)
            else:
                copy = pltpu.make_async_copy(src, dst, recv.at[5])
            copy.start()

    gather.middle()
    wo_gather = Gather(place, wo, slab.at[4:5], wo_send, wo_recv)
    ud_gather = Gather(place, ud, None, far_send, far_recv)
    gathers = (ud_gather, wo_gather)
    settle(columns(z), recv.at[8])
    ud_copy(4).wait_recv()
    ud_copy(5).wait_recv()
    for i in (0, 1, 2, 3, 6, 7):
        for one in gathers:
            one.start(i)
    gather.last()

    pick_pair = push(
        context.at[0:first, core], context.at[0:first, core], pair_send.at[0], recv.at[1], place.dp(CORE), z
    )
    settle(context.at[0:first, core], recv.at[5])
    pick_pair.start()
    lead_copy = push(
        context.at[first:], context.at[first:], pair_send.at[1], recv.at[3], place.dp(CORE), z
    )

    @pl.when(core == 0)
    def _():
        settle(context.at[first:], recv.at[3])
        lead_copy.start()

    settle(all_ints, recv.at[2])
    seq = 4 * lax.div(d, 2) + z
    slot = slot_of(seq)
    odd = lax.rem(seq, micro)
    own, other = all_ints[lax.div(seq, micro)], all_ints[lax.div(slot, micro)]

    def pick(row, at):
        return jnp.sum(jnp.where(spot == at, row.astype(F32), 0.0), axis=1, keepdims=True)

    length = pick(own[2:3], odd)
    mem_valid = pick(other[2:3], micro + lax.rem(slot, micro))
    rank = jnp.where(odd == 0, own[0:1], own[1:2])
    seq_len = rank.shape[1]
    mem_total = key_ref.shape[1] - seq_len
    where = spot.astype(F32)
    hidden = jnp.int32(1 << 20)
    key_ref[:, :mem_total] = jnp.where(where >= mem_total - mem_valid, -1, hidden)
    key_ref[:, mem_total:] = jnp.where(where < length, rank, hidden)
    ranks = jnp.transpose(jnp.broadcast_to(rank.astype(F32), (8, seq_len)))
    thr_ref[...] = ranks[:, 0:1].astype(jnp.int32) + jnp.where(core == 0, 1, 0)

    gather.wait(range(6, 14), ())
    settle(whole.at[:, own_rows, :], recv.at[6])
    keep_whole = pltpu.make_async_copy(whole, whole_out, local.at[1])
    keep_whole.start()

    keep_context = pltpu.make_async_copy(context, context_out, local.at[2])

    def before_stream():
        pick_pair.wait()

        @pl.when(core == 0)
        def _():
            lead_copy.wait_send()

        @pl.when(core == 1)
        def _():
            settle(context.at[first:], recv.at[3])
            settle(stream, recv.at[4])

        keep_context.start()

    def before_context():
        for one in gathers:
            one.after((0, 1), ((8,), (9,)))

    pltpu.make_async_copy(table_hbm, table, local.at[0]).wait()
    project_step(
        whole, context, stream, table, wb_ref, pb_ref, *outs, hooks=(before_stream, before_context)
    )
    for one in gathers:
        one.after((2, 3), ((10,), (11,)))
    settle(wo.at[:, own_rows, :], recv.at[7])
    gather.wait((), range(14))
    for one in gathers:
        one.wait(range(6, 12), (0, 1, 2, 3) + tuple(range(6, 12)))
    keep_whole.wait()
    keep_context.wait()
    for i in range(4):
        stream_copy(i, "wait")
        mat_copy(i).wait_send()
    for i in range(6):
        ud_copy(i).wait_send()
    for copy in spread_copies + int_copies + pick_copies:
        copy.wait_send()


def enter(slots, seqs, mems, content, query, memory, table, orders, mats, upw, dnw, wb, pb):
    micro, part, width = content.shape
    rows = mats[0].shape[0]
    inner = upw.shape[1] * 4
    piece = part // 8
    klen, span, seq = 8 * part, table.shape[0], 4 * part
    vmem = pl.BlockSpec(memory_space=pltpu.VMEM)
    dma = lambda n: pltpu.SemaphoreType.DMA((n,))
    bf = lambda *shape: jax.ShapeDtypeStruct(shape, BF)
    return pl.pallas_call(
        enter_kernel,
        in_specs=[SMEM_SPEC] * 3 + [ANY_SPEC] * 4 + [vmem] * 10,
        out_specs=[vmem] * 8 + [ANY_SPEC] * 4,
        out_shape=[
            bf(klen, width),
            bf(klen, width),
            bf(span, width),
            bf(seq, width),
            bf(seq, width),
            bf(seq, width),
            jax.ShapeDtypeStruct((seq, 1), jnp.int32),
            jax.ShapeDtypeStruct((1, klen), jnp.int32),
            bf(4, 8 * rows, width),
            bf(32, 2, piece, width),
            bf(1, 8 * rows, width),
            bf(2, 8 * rows, inner),
        ],
        scratch_shapes=[
            pltpu.VMEM((8, seq), jnp.int32),
            pltpu.VMEM((8, 8, seq), jnp.int32),
            pltpu.VMEM((4, 8 * rows, width), BF),
            pltpu.VMEM((32, 2, piece, width), BF),
            pltpu.VMEM((seq, width), BF),
            pltpu.VMEM((span, width), BF),
            pltpu.VMEM((16, piece, width), BF),
            pltpu.VMEM((16, piece, width), BF),
            pltpu.VMEM((4, 5, rows * 3 // 2, 128), BF),
            pltpu.VMEM((5, rows, width), BF),
            dma(4),
            dma(4),
            dma(6),
            dma(4),
            dma(7),
            dma(7),
            dma(15),
            dma(4),
            dma(2),
            dma(14),
            dma(14),
            dma(14),
            dma(14),
            dma(14),
            dma(14),
            dma(9),
            dma(3),
        ],
        compiler_params=pltpu.CompilerParams(
            collective_id=1, has_side_effects=True, vmem_limit_bytes=LIMIT
        ),
        cost_estimate=pl.CostEstimate(flops=0, bytes_accessed=64 << 20, transcendentals=0),
        name="enter",
    )(
        slots,
        seqs,
        mems,
        content.reshape(micro, 4, 2, piece, width),
        query,
        memory,
        table,
        orders,
        *mats,
        upw,
        dnw,
        wb,
        pb,
    )


def head_lanes(array, head):
    lane = lax.broadcasted_iota(jnp.int32, array.shape, 1)
    return jnp.where((lane >= DH) == (head == 1), array, jnp.zeros_like(array))


def attend_forward_step(
    block, qw_ref, qp_ref, k_ref, v_ref, rel_ref, thr_ref, kr_ref, vec_ref, prob_ref
):
    rows, klen = qw_ref.shape[0], k_ref.shape[0]
    width = klen + block
    keys, values = k_ref[...], v_ref[...]
    for part in range(rows // block):
        at = slice(part * block, (part + 1) * block)
        first = rows - (part + 1) * block
        qw, qp = qw_ref[at, :], qp_ref[at, :]
        rel = rel_ref[first : first + width, :]
        seen = kr_ref[...] < thr_ref[at, :]
        vecs = []
        for head in range(2):
            raw = nt(head_lanes(qp, head), rel)
            moved = pltpu.roll(raw, 0, 1, stride=1, stride_axis=0)[:, block:]
            score = nt(head_lanes(qw, head), keys) + moved
            score = jnp.where(seen, score, -1e30)
            expo = jnp.exp(score - jnp.max(score, axis=1, keepdims=True))
            prob = (expo * (1.0 / jnp.sum(expo, axis=1, keepdims=True))).astype(BF)
            prob_ref[head, at, :] = prob
            vecs.append(nn(prob, values))
        lane = lax.broadcasted_iota(jnp.int32, vecs[0].shape, 1)
        vec_ref[at, :] = jnp.where(lane < DH, vecs[0], vecs[1]).astype(BF)


def attend_forward_kernel(block, wired, *refs):
    if not wired:
        attend_forward_step(block, *refs)
        return
    ins, (ctan, qtan) = refs[:7], refs[9:11]
    outs, (wo, ud, tangent) = refs[11:13], refs[13:16]
    out_send, out_recv, ud_send, ud_recv, tan_send, recv = refs[16:]
    step, steps = pl.program_id(0), pl.num_programs(0)
    place = Place()
    d, z, core = place.d, place.z, place.core
    gathers = (
        Gather(place, ud, None, ud_send, ud_recv),
        Gather(place, wo, None, out_send, out_recv),
    )
    part = ctan.shape[1]

    def tan_copy(i, act):
        j, kind = i // 2, i % 2
        to, dp = 2 * core + j, d - core + kind
        src = (ctan, qtan)[kind].at[j]
        dst = tangent.at[pl.ds(pl.multiple_of(z * part, 16), part), :]
        here = jnp.logical_and(dp == d, to == z)
        local = pltpu.make_async_copy(src, dst, recv.at[0])
        remote = push(src, dst, tan_send.at[i], recv.at[0], dp, to)
        if act == "start":
            pl.when(here)(local.start)
            pl.when(jnp.logical_not(here))(remote.start)
        else:
            pl.when(jnp.logical_not(here))(remote.wait_send)

    @pl.when(step == 0)
    def _():
        greet(near_partners(place))
        for gather in gathers:
            gather.start(4, 5)
        for i in range(4):
            tan_copy(i, "start")

    @pl.when(step == steps - 1)
    def _():
        for gather in gathers:
            gather.after((4, 5), ((12,), (13,)))

    attend_forward_step(block, *ins, *outs)

    @pl.when(step == steps - 1)
    def _():
        for gather in gathers:
            gather.wait((12, 13), (4, 5, 12, 13))
        settle(tangent, recv.at[0])
        for i in range(4):
            tan_copy(i, "wait")


def attend_forward(qw, qp, keys, values, rel, thr, key_rank, block, wires=()):
    rows, width = qw.shape
    klen, span = keys.shape[0], rel.shape[0]
    col = lambda count: pl.BlockSpec((count, PAIR), lambda p: (0, p))
    in_specs = [
        col(rows),
        col(rows),
        col(klen),
        col(klen),
        col(span),
        pl.BlockSpec((rows, 1), lambda p: (0, 0)),
        pl.BlockSpec((1, klen), lambda p: (0, 0)),
    ]
    out_specs = [col(rows), pl.BlockSpec((2, rows, klen), lambda p: (p, 0, 0))]
    out_shape = [
        jax.ShapeDtypeStruct((rows, width), BF),
        jax.ShapeDtypeStruct((width // DH, rows, klen), BF),
    ]
    params = dict(vmem_limit_bytes=LIMIT)
    scratch = []
    if wires:
        in_specs += [ANY_SPEC] * 4
        out_specs += [ANY_SPEC] * 3
        out_shape += [
            jax.ShapeDtypeStruct(wires[0].shape, BF),
            jax.ShapeDtypeStruct(wires[1].shape, BF),
            jax.ShapeDtypeStruct((rows, width), BF),
        ]
        scratch = [pltpu.SemaphoreType.DMA((n,)) for n in (14, 14, 14, 14, 4, 1)]
        params.update(collective_id=2, has_side_effects=True)
    return pl.pallas_call(
        functools.partial(attend_forward_kernel, block, bool(wires)),
        grid=(width // PAIR,),
        in_specs=in_specs,
        out_specs=out_specs,
        out_shape=out_shape,
        scratch_shapes=scratch,
        input_output_aliases={7: 2, 8: 3} if wires else {},
        compiler_params=pltpu.CompilerParams(**params),
        cost_estimate=pl.CostEstimate(
            flops=8 * rows * klen * width, bytes_accessed=16 << 20, transcendentals=12 * rows * klen
        ),
        name="attend_forward",
    )(qw, qp, keys, values, rel, thr, key_rank, *wires)


def attend_backward_kernel(block, wired, *refs):
    if not wired:
        attend_backward_step(block, *refs)
        return
    ins, (g_ud, near_ud, g_out, src) = refs[:7], refs[7:11]
    outs, grad_refs, home_refs = refs[11:16], refs[16:19], refs[19:21]
    rel_acc, home_send, home_recv = refs[21:24]
    refs = refs[24:]
    step, steps = pl.program_id(0), pl.num_programs(0)
    place = Place()
    count = len(refs) // 3
    held = [refs[m * count : (m + 1) * count] for m in range(3)]
    reduces = [
        Reduce(place, (g_ud.at[m : m + 1], near_ud.at[m : m + 1]), held[m], grad_refs[m], True)
        for m in range(2)
    ]
    out = Reduce(place, (g_out,), held[2], grad_refs[2])
    home = Homeward(place, src, home_refs, home_send, home_recv)

    @pl.when(step == 0)
    def _():
        greet(near_partners(place))
        for reduce in reduces:
            reduce.begin()
        out.begin()
        home.start()

    @pl.when(step == 1)
    def _():
        for reduce in reduces:
            reduce.middle()
        out.pairs()

    @pl.when(step == 3)
    def _():
        reduces[0].late()

    @pl.when(step == 4)
    def _():
        reduces[1].late()
        out.middle()

    @pl.when(step == 5)
    def _():
        out.late()

    attend_backward_step(block, *ins, *outs, rel_acc)

    @pl.when(step == steps - 1)
    def _():
        for reduce in reduces:
            reduce.end()
        out.end()
        home.end()


def attend_backward_step(
    block,
    prob_ref,
    gvec_ref,
    qw_ref,
    qp_ref,
    k_ref,
    v_ref,
    rel_ref,
    dproj_ref,
    dk_ref,
    dv_ref,
    drel_ref,
    bias_ref,
    rel_acc,
):
    rows, klen = qw_ref.shape[0], k_ref.shape[0]
    width = klen + block
    keys, values = k_ref[...], v_ref[...]
    row = lax.broadcasted_iota(jnp.int32, (block, block), 0)
    col = lax.broadcasted_iota(jnp.int32, (block, block), 1)
    mirror = (row + col == block - 1).astype(BF)
    rel_acc[...] = jnp.zeros_like(rel_acc)
    d_keys, d_values = [None, None], [None, None]
    word_sum = jnp.zeros((1, PAIR), F32)
    pos_sum = jnp.zeros((1, PAIR), F32)
    for part in range(rows // block):
        at = slice(part * block, (part + 1) * block)
        first = rows - (part + 1) * block
        gvec, qw = gvec_ref[at, :], qw_ref[at, :]
        gvec_t = jnp.transpose(gvec.astype(F32)).astype(BF)
        qw_t = jnp.transpose(qw.astype(F32)).astype(BF)
        qp_t = jnp.transpose(nn(mirror, qp_ref[at, :])).astype(BF)
        rel = rel_ref[first : first + width, :]
        word_parts, pos_parts = [], []
        for head in range(2):
            own = slice(head * DH, (head + 1) * DH)
            prob = prob_ref[head, at, :]
            d_prob = nt(head_lanes(gvec, head), values)
            weight = prob.astype(F32)
            inner = jnp.sum(weight * d_prob, axis=1, keepdims=True)
            g_sum = (weight * (d_prob - inner) * 0.125).astype(BF)
            dv = nn(gvec_t[own, :], prob)
            dk = nn(qw_t[own, :], g_sum)
            d_values[head] = dv if part == 0 else d_values[head] + dv
            d_keys[head] = dk if part == 0 else d_keys[head] + dk
            turned = nn(mirror, g_sum)
            padded = jnp.concatenate([jnp.zeros((block, block), F32), turned], axis=1)
            moved = pltpu.roll(padded, width - block + 1, 1, stride=1, stride_axis=0).astype(BF)
            word_parts.append(nn(turned.astype(BF), keys))
            pos_parts.append(nn(moved, rel))
            rel_acc[own, first : first + width] += nn(qp_t[own, :], moved)
        lane = lax.broadcasted_iota(jnp.int32, word_parts[0].shape, 1)
        word = jnp.where(lane < DH, word_parts[0], word_parts[1])
        pos = jnp.where(lane < DH, pos_parts[0], pos_parts[1])
        word_sum = word_sum + jnp.sum(word, axis=0, keepdims=True)
        pos_sum = pos_sum + jnp.sum(pos, axis=0, keepdims=True)
        dproj_ref[at, :] = nn(mirror, (word + pos).astype(BF)).astype(BF)
    for head in range(2):
        own = slice(head * DH, (head + 1) * DH)
        dv_ref[own, :] = d_values[head].astype(BF)
        dk_ref[own, :] = (8.0 * d_keys[head]).astype(BF)
    drel_ref[...] = (8.0 * rel_acc[...]).astype(BF)
    bias_ref[0:1, :] = word_sum
    bias_ref[1:2, :] = pos_sum


def attend_backward(prob, gvec, qw, qp, keys, values, rel, block, wires=()):
    rows, width = qw.shape
    klen, span = keys.shape[0], rel.shape[0]
    col = lambda count: pl.BlockSpec((count, PAIR), lambda p: (0, p))
    rowb = lambda count: pl.BlockSpec((PAIR, count), lambda p: (p, 0))
    in_specs = [
        pl.BlockSpec((2, rows, klen), lambda p: (p, 0, 0)),
        col(rows),
        col(rows),
        col(rows),
        col(klen),
        col(klen),
        col(span),
    ]
    out_specs = [col(rows), rowb(klen), rowb(klen), rowb(span), col(2)]
    out_shape = [
        jax.ShapeDtypeStruct((rows, width), BF),
        jax.ShapeDtypeStruct((width, klen), BF),
        jax.ShapeDtypeStruct((width, klen), BF),
        jax.ShapeDtypeStruct((width, span), BF),
        jax.ShapeDtypeStruct((2, width), F32),
    ]
    scratch = [pltpu.VMEM((PAIR, span), F32)]
    params = dict(vmem_limit_bytes=LIMIT)
    if wires:
        inner, mine = wires[0].shape[3], width // 8
        in_specs += [ANY_SPEC] * 4
        out_specs += [pl.BlockSpec(memory_space=pltpu.VMEM)] * 3 + [ANY_SPEC] * 2
        out_shape += [jax.ShapeDtypeStruct((mine, inner // 4), F32)] * 2
        out_shape += [jax.ShapeDtypeStruct((mine, width // 4), F32)]
        out_shape += [jax.ShapeDtypeStruct((2, rows // 4, width), BF)] * 2
        scratch += [pltpu.SemaphoreType.DMA((4,)), pltpu.SemaphoreType.DMA((2,))]
        scratch += 2 * Reduce.scratch(1, 1, mine, inner, True) + Reduce.scratch(1, 1, mine, width)
        params.update(collective_id=3, has_side_effects=True)
    return pl.pallas_call(
        functools.partial(attend_backward_kernel, block, bool(wires)),
        grid=(width // PAIR,),
        in_specs=in_specs,
        out_specs=out_specs,
        out_shape=out_shape,
        scratch_shapes=scratch,
        compiler_params=pltpu.CompilerParams(**params),
        cost_estimate=pl.CostEstimate(
            flops=16 * rows * klen * width, bytes_accessed=20 << 20, transcendentals=0
        ),
        name="attend_backward",
    )(prob, gvec, qw, qp, keys, values, rel, *wires)


def norm_parts(value):
    center = value - jnp.mean(value, axis=1, keepdims=True)
    scale = lax.rsqrt(jnp.mean(center * center, axis=1, keepdims=True) + EPS)
    return center * scale, scale


def norm_pull(normed, scale, err):
    inner = jnp.mean(err * normed, axis=1, keepdims=True)
    return (err - jnp.mean(err, axis=1, keepdims=True) - normed * inner) * scale


def sum_rows(value):
    return jnp.sum(value, axis=0, keepdims=True)


def feed_kernel(steps, wired, *refs):
    (
        ud_hbm,
        wo_hbm,
        vec_ref,
        x_ref,
        tan_ref,
        upb_ref,
        dnb_ref,
        g1_ref,
        s1_ref,
        g2_ref,
        s2_ref,
        out_ref,
        dmix_ref,
        gvec_ref,
        go_ref,
        gud_ref,
        gupb_ref,
        small_ref,
        *refs,
    ) = refs
    near_ref, *refs = refs if wired else (None, *refs)
    (
        ud_ref,
        wo_ref,
        n1_ref,
        r1_ref,
        fb_ref,
        fbt_ref,
        acc_ref,
        act_ref,
        slope_ref,
        gd_ref,
        gdt_ref,
        sems,
        *pair_refs,
    ) = refs
    step = pl.program_id(0)
    chunk = act_ref.shape[2]
    row = lambda ref: ref[...].reshape(1, -1)
    cols = pl.ds(pl.multiple_of(lax.rem(step, steps) * chunk, chunk), chunk)

    if wired:
        own_ref, pair_ref, sum_ref, send, recv, keep, move_send, move_recv = pair_refs
        place = Place()
        rows = pair_ref.shape[2]

        def span(c):
            return pl.ds(pl.multiple_of(c * chunk, chunk), chunk)

        def block(bits):
            return pl.ds(pl.multiple_of(place.dp(bits) * rows, 16), rows)

        def pair_copy(c, j):
            slot = lax.rem(c, 2)
            return push(
                own_ref.at[slot, :, block(chip_bits(j) | CORE), :],
                pair_ref.at[:, j, :, span(c)],
                send.at[slot, j],
                recv.at[c],
                place.dp(CORE),
                place.z,
            )

        def keep_copy(c):
            return pltpu.make_async_copy(sum_ref.at[c], gud_ref.at[:, :, :, span(c)], keep.at[c])

        def move(c, i):
            j, h, to, where = Reduce.MOVES[i]
            return push(
                sum_ref.at[c, :, j, h * (rows // 2) : (h + 1) * (rows // 2), :],
                near_ref.at[:, h, where, :, span(c)],
                move_send.at[c, i],
                move_recv.at[c],
                place.dp(to),
                place.z,
            )

        def join(c):
            slot = lax.rem(c, 2)
            settle(pair_ref.at[:, :, :, span(c)], recv.at[c])
            for j in (3, 1, 2, 0):
                mine = own_ref[slot, :, block(chip_bits(j)), :].astype(F32)
                sum_ref[c, :, j] = (mine + pair_ref[:, j, :, span(c)].astype(F32)).astype(BF)
            for i in range(4):
                move(c, i).start()
            keep_copy(c).start()

        def send_wait(c):
            for j in range(4):
                pair_copy(c, j).wait_send()

        @pl.when(step == 0)
        def _():
            greet([(place.dp(r), place.z) for r in (CORE, XBIT, YBIT)])

    @pl.when(step == 0)
    def _():
        wo_copy = pltpu.make_async_copy(wo_hbm, wo_ref, sems.at[0])
        ud_copy = pltpu.make_async_copy(ud_hbm, ud_ref, sems.at[1])
        wo_copy.start()
        ud_copy.start()
        wo_copy.wait()
        normed, scale = norm_parts(nt(vec_ref[...], wo_ref[0]) + x_ref[...].astype(F32))
        n1_ref[...] = normed
        r1_ref[...] = scale
        first = normed * row(g1_ref) + row(s1_ref)
        fb_ref[...] = first.astype(BF)
        fbt_ref[...] = jnp.transpose(first).astype(BF)
        acc_ref[...] = first + row(dnb_ref)
        ud_copy.wait()

    @pl.when(step < steps)
    def _():
        upper = nn(fb_ref[...], ud_ref[0, :, cols]) + row(upb_ref)
        square = upper * upper
        root = 0.7978845608028654
        bend = jnp.tanh(root * (upper + 0.044715 * (square * upper)))
        half = 0.5 * (1.0 + bend)
        act = (upper * half).astype(BF)
        act_ref[step] = act
        slope_ref[step] = half + 0.5 * upper * (1.0 - bend * bend) * (
            root + (3 * 0.044715 * root) * square
        )
        acc_ref[...] += nt(act, ud_ref[1, :, cols])

    @pl.when(step == steps - 1)
    def _():
        normed, scale = norm_parts(acc_ref[...])
        out_ref[...] = (normed * row(g2_ref) + row(s2_ref)).astype(BF)
        tan = tan_ref[...].astype(F32)
        d_down = norm_pull(normed, scale, tan * row(g2_ref))
        small_ref[0:1, :] = sum_rows(d_down)
        small_ref[3:4, :] = sum_rows(tan * normed)
        small_ref[4:5, :] = sum_rows(tan)
        gd_ref[...] = d_down.astype(BF)
        gdt_ref[...] = jnp.transpose(d_down).astype(BF)
        acc_ref[...] = d_down

    @pl.when(step >= steps)
    def _():
        at = step - steps
        d_up = nn(gd_ref[...], ud_ref[1, :, cols]) * slope_ref[at]
        gupb_ref[...] = sum_rows(d_up)
        g_up = d_up.astype(BF)
        acc_ref[...] += nt(g_up, ud_ref[0, :, cols])
        if not wired:
            gud_ref[0] = nn(fbt_ref[...], g_up).astype(BF)
            gud_ref[1] = nn(gdt_ref[...], act_ref[at]).astype(BF)
            return
        pl.when(at >= 2)(lambda: send_wait(at - 2))
        slot = lax.rem(at, 2)
        own_ref[slot, 0] = nn(fbt_ref[...], g_up).astype(BF)
        own_ref[slot, 1] = nn(gdt_ref[...], act_ref[at]).astype(BF)
        for j in range(4):
            pair_copy(at, j).start()
        pl.when(at >= 1)(lambda: join(at - 1))

    @pl.when(step == 2 * steps - 1)
    def _():
        d_first, normed = acc_ref[...], n1_ref[...]
        small_ref[1:2, :] = sum_rows(d_first * normed)
        small_ref[2:3, :] = sum_rows(d_first)
        d_mixed = norm_pull(normed, r1_ref[...], d_first * row(g1_ref))
        dmix_ref[...] = d_mixed
        gvec_ref[...] = nn(d_mixed.astype(BF), wo_ref[0]).astype(BF)
        gdt_ref[...] = jnp.transpose(d_mixed).astype(BF)
        go_ref[...] = nn(gdt_ref[...], vec_ref[...]).astype(BF)
        if wired:
            join(steps - 1)
            for c in (steps - 2, steps - 1):
                send_wait(c)
            for c in range(steps):
                keep_copy(c).wait()
                settle(near_ref.at[:, :, :, :, span(c)], move_recv.at[c])
                for i in range(4):
                    move(c, i).wait_send()


def feed(ud, wo, vec, x, tan, upb, vecs, wired):
    rows, width = vec.shape
    inner = upb.shape[0]
    chunk = 512
    steps = inner // chunk
    whole = lambda a, b: pl.BlockSpec((a, b), lambda i: (0, 0))
    late = lambda i: jnp.maximum(i - steps, 0)
    grads = pl.BlockSpec((2, width, chunk), lambda i: (0, 0, late(i)))
    grad_shape = (2, width, inner)
    params = dict(vmem_limit_bytes=LIMIT)
    scratch, near_shape = [], []
    if wired:
        mine = width // 8
        grads, grad_shape = ANY_SPEC, (2, 4, mine, inner)
        scratch = [
            pltpu.VMEM((2, 2, width, chunk), BF),
            pltpu.VMEM(grad_shape, BF),
            pltpu.VMEM((steps, 2, 4, mine, chunk), BF),
            pltpu.SemaphoreType.DMA((2, 4)),
            pltpu.SemaphoreType.DMA((steps,)),
            pltpu.SemaphoreType.DMA((steps,)),
            pltpu.SemaphoreType.DMA((steps, 4)),
            pltpu.SemaphoreType.DMA((steps,)),
        ]
        near_shape = [jax.ShapeDtypeStruct((2, 2, 2, mine // 2, inner), BF)]
        params.update(collective_id=6, has_side_effects=True)
    return pl.pallas_call(
        functools.partial(feed_kernel, steps, wired),
        grid=(2 * steps,),
        in_specs=[ANY_SPEC] * 2
        + [whole(rows, width)] * 3
        + [pl.BlockSpec((chunk,), lambda i: (lax.rem(i, steps),))]
        + [pl.BlockSpec((width,), lambda i: (0,))] * 5,
        out_specs=[
            whole(rows, width),
            whole(rows, width),
            whole(rows, width),
            whole(width, width),
            grads,
            pl.BlockSpec((1, chunk), lambda i: (0, late(i))),
            whole(8, width),
        ]
        + [ANY_SPEC] * len(near_shape),
        out_shape=[
            jax.ShapeDtypeStruct((rows, width), BF),
            jax.ShapeDtypeStruct((rows, width), F32),
            jax.ShapeDtypeStruct((rows, width), BF),
            jax.ShapeDtypeStruct((width, width), BF),
            jax.ShapeDtypeStruct(grad_shape, BF),
            jax.ShapeDtypeStruct((1, inner), F32),
            jax.ShapeDtypeStruct((8, width), F32),
        ]
        + near_shape,
        scratch_shapes=[
            pltpu.VMEM((2, width, inner), BF),
            pltpu.VMEM((1, width, width), BF),
            pltpu.VMEM((rows, width), F32),
            pltpu.VMEM((rows, 1), F32),
            pltpu.VMEM((rows, width), BF),
            pltpu.VMEM((width, rows), BF),
            pltpu.VMEM((rows, width), F32),
            pltpu.VMEM((steps, rows, chunk), BF),
            pltpu.VMEM((steps, rows, chunk), F32),
            pltpu.VMEM((rows, width), BF),
            pltpu.VMEM((width, rows), BF),
            pltpu.SemaphoreType.DMA((2,)),
        ]
        + scratch,
        compiler_params=pltpu.CompilerParams(**params),
        cost_estimate=pl.CostEstimate(
            flops=12 * rows * width * inner, bytes_accessed=36 << 20, transcendentals=rows * inner
        ),
        name="feed",
    )(ud, wo, vec, x, tan, upb, *vecs)


def project_step(
    w_ref,
    ctx_ref,
    q_ref,
    table_ref,
    wb_ref,
    pb_ref,
    k_ref,
    v_ref,
    rel_ref,
    qw_ref,
    qp_ref,
    x_ref,
    hooks=(),
):
    lead = lax.rem(lax.axis_index("dp"), 2) == 0
    flat = lambda ref: jnp.concatenate([ref[h : h + 1, :] for h in range(ref.shape[0])], axis=1)
    word_bias, pos_bias = flat(wb_ref), flat(pb_ref)
    klen, width = k_ref.shape
    back = klen - q_ref.shape[0]

    def context_rows(start):
        at = pl.ds(lax.div(start, 32), block // 32)
        return ctx_ref[at].reshape(block, width)

    block = 256

    def loop(count, step):
        def run(i, carry):
            step(pl.ds(pl.multiple_of(i * block, block), block))
            return carry

        lax.fori_loop(0, count // block, run, 0)

    def context_step(at):
        rows = context_rows(at.start)
        k_ref[at, :] = nn(rows, w_ref[0]).astype(BF)
        v_ref[at, :] = nn(rows, w_ref[1]).astype(BF)

    def stream_step(at):
        x_ref[at, :] = jnp.where(lead, context_rows(at.start + back), q_ref[at, :])
        proj = nn(x_ref[at, :], w_ref[2])
        qw_ref[at, :] = (0.125 * (proj + word_bias).astype(BF).astype(F32)).astype(BF)
        qp_ref[at, :] = (0.125 * (proj + pos_bias).astype(BF).astype(F32)).astype(BF)

    def table_step(at):
        rel_ref[at, :] = nn(table_ref[at, :], w_ref[3]).astype(BF)

    loop(table_ref.shape[0], table_step)
    if hooks:
        hooks[0]()
    loop(q_ref.shape[0], stream_step)
    if hooks:
        hooks[1]()
    loop(klen, context_step)


def project(mats, context, query, table, wb, pb):
    rows, width = query.shape
    klen, span = context.shape[0], table.shape[0]
    vmem = pl.BlockSpec(memory_space=pltpu.VMEM)
    return pl.pallas_call(
        project_step,
        in_specs=[vmem] * 6,
        out_specs=[vmem] * 6,
        out_shape=[
            jax.ShapeDtypeStruct((klen, width), BF),
            jax.ShapeDtypeStruct((klen, width), BF),
            jax.ShapeDtypeStruct((span, width), BF),
            jax.ShapeDtypeStruct((rows, width), BF),
            jax.ShapeDtypeStruct((rows, width), BF),
            jax.ShapeDtypeStruct((rows, width), BF),
        ],
        compiler_params=pltpu.CompilerParams(vmem_limit_bytes=LIMIT),
        cost_estimate=pl.CostEstimate(
            flops=2 * (2 * klen + rows + span) * width * width,
            bytes_accessed=20 << 20,
            transcendentals=0,
        ),
        name="project",
    )(mats, context.reshape(klen // 32, 2, 16, width), query, table, wb, pb)


def weight_grads_kernel(xt_ref, ct_ref, tt_ref, dp_ref, dk_ref, dv_ref, dr_ref, g_ref):
    g_ref[0] = nt(ct_ref[...], dk_ref[...]).astype(BF)
    g_ref[1] = nt(ct_ref[...], dv_ref[...]).astype(BF)
    g_ref[2] = nn(xt_ref[...], dp_ref[...]).astype(BF)
    g_ref[3] = nt(tt_ref[...], dr_ref[...]).astype(BF)


def weight_grads(x_t, ctx_t, table_t, d_proj, dk_t, dv_t, drel_t):
    width, rows = x_t.shape
    klen, span = ctx_t.shape[1], table_t.shape[1]
    chunk = 256
    whole = lambda a, b: pl.BlockSpec((a, b), lambda i: (0, 0))
    rowb = lambda b: pl.BlockSpec((chunk, b), lambda i: (i, 0))
    return pl.pallas_call(
        weight_grads_kernel,
        grid=(width // chunk,),
        in_specs=[
            whole(width, rows),
            whole(width, klen),
            whole(width, span),
            pl.BlockSpec((rows, chunk), lambda i: (0, i)),
            rowb(klen),
            rowb(klen),
            rowb(span),
        ],
        out_specs=pl.BlockSpec((4, width, chunk), lambda i: (0, 0, i)),
        out_shape=jax.ShapeDtypeStruct((4, width, width), BF),
        compiler_params=pltpu.CompilerParams(vmem_limit_bytes=LIMIT),
        cost_estimate=pl.CostEstimate(
            flops=2 * (rows + 2 * klen + span) * width * width,
            bytes_accessed=20 << 20,
            transcendentals=0,
        ),
        name="weight_grads",
    )(x_t, ctx_t, table_t, d_proj, dk_t, dv_t, drel_t)


def flip(arr, bit):
    return lax.ppermute(arr, "dp", [(i, i ^ bit) for i in range(lax.axis_size("dp"))])


def scatter_sum(grads):
    mine = lax.psum_scatter(grads, "dp", scatter_dimension=1, tiled=True)
    return lax.psum_scatter(mine, "tensor", scatter_dimension=2, tiled=True).astype(F32)


def body(
    content_stream,
    query_stream,
    memory,
    content_tangent,
    query_tangent,
    seq_lengths,
    factor_order,
    memory_lengths,
    slot_sequence,
    query_weight,
    key_weight,
    value_weight,
    pos_weight,
    out_weight,
    up_weight,
    up_bias,
    down_weight,
    down_bias,
    word_bias,
    pos_bias,
    first_gain,
    first_shift,
    second_gain,
    second_shift,
):
    groups, tensors = lax.axis_size("dp"), lax.axis_size("tensor")
    micro, part_len, width = content_stream.shape
    mem_part = memory.shape[1]
    seq_len, mem_total = part_len * tensors, mem_part * tensors
    klen, span = mem_total + seq_len, mem_total + 2 * seq_len
    count = micro * groups
    here, lane = lax.axis_index("dp"), lax.axis_index("tensor")
    core = here % 2
    lead = core == 0
    block = 256
    assert 2 * micro == tensors

    def swap(arr):
        return flip(arr, CORE)

    def to_unit(first, second):
        got = swap(jnp.where(lead, second, first))
        low = jnp.where(lead, first, got)
        high = jnp.where(lead, got, second)
        both = jnp.concatenate([low, high], 0)
        both = lax.all_to_all(both, "tensor", split_axis=0, concat_axis=0, tiled=True)
        return both.reshape(seq_len, width)

    def from_unit(arr):
        both = arr.reshape(tensors, part_len, width)
        both = lax.all_to_all(both, "tensor", split_axis=0, concat_axis=0, tiled=True)
        low, high = both[:micro], both[micro:]
        got = swap(jnp.where(lead, high, low))
        return jnp.where(lead, low, got), jnp.where(lead, got, high)

    seq_id = (here // 2) * tensors + lane
    mats = [key_weight, value_weight, query_weight, pos_weight, out_weight]
    table = jnp.asarray(reversed_table(span, klen, width))
    wires = ()
    if groups == 8:
        keys, values, rel, q_word, q_pos, stream, thr, key_rank, weights, context, *wires = enter(
            slot_sequence,
            seq_lengths,
            memory_lengths,
            content_stream,
            query_stream,
            memory,
            table,
            factor_order,
            mats,
            up_weight,
            down_weight,
            word_bias,
            pos_bias,
        )
        wires += [content_tangent, query_tangent]
        context = context.reshape(klen, width)
    else:
        ids = jnp.arange(count, dtype=jnp.int32)
        slot_of = jnp.sum(jnp.where(slot_sequence[None, :] == ids[:, None], ids[None, :], 0), axis=1)
        counts = jnp.concatenate([seq_lengths, memory_lengths])
        slot = slot_of[seq_id]
        lengths = lax.all_gather(counts, "dp", axis=0, tiled=False)
        orders = lax.all_gather(factor_order, "dp", axis=0, tiled=False)[seq_id // micro]
        stream = to_unit(content_stream, query_stream)
        content, query = jnp.where(lead, stream, swap(stream)), stream
        tangent = to_unit(content_tangent, query_tangent)
        piece = mem_part // groups
        spread = lax.all_to_all(
            memory.reshape(micro, groups, piece, width), "dp", split_axis=1, concat_axis=1, tiled=True
        )
        spread = spread.transpose(1, 0, 2, 3).reshape(count, piece, width)
        spread = jnp.take(spread, slot_of, axis=0)
        spread = spread.reshape(groups // 2, tensors, 2, piece // 2, width).transpose(0, 2, 1, 3, 4)
        spread = lax.all_to_all(
            spread.reshape(groups, tensors, piece // 2, width),
            "dp",
            split_axis=0,
            concat_axis=0,
            tiled=True,
        )
        spread = lax.all_to_all(spread, "tensor", split_axis=1, concat_axis=1, tiled=True)
        got = swap(spread)
        mem_rows = jnp.stack([jnp.where(lead, spread, got), jnp.where(lead, got, spread)])
        mem_rows = mem_rows.transpose(2, 1, 0, 3, 4).reshape(mem_total, width)
        context = jnp.concatenate([mem_rows, content], 0)

        def whole(mat):
            mat = lax.all_gather(mat, "tensor", axis=1, tiled=True)
            return lax.all_gather(mat, "dp", axis=0, tiled=True)

        weights = jnp.stack([whole(mat) for mat in mats[:4]])
        wo = whole(out_weight)[None]
        ud = jnp.stack([whole(up_weight), whole(down_weight)])
        keys, values, rel, q_word, q_pos, stream = project(
            weights, context, query, table, word_bias, pos_bias
        )
        length = lengths[seq_id // micro, seq_id % micro]
        mem_valid = lengths[slot // micro, micro + slot % micro]
        rank = orders[seq_id % micro]
        key_pos = jnp.arange(klen, dtype=jnp.int32)
        hidden = jnp.int32(1 << 20)
        mem_rank = jnp.where(key_pos[:mem_total] >= mem_total - mem_valid, -1, hidden)
        own_rank = jnp.where(key_pos[:seq_len] < length, rank, hidden)
        key_rank = jnp.concatenate([mem_rank, own_rank])[None, :]
        thr = (rank + jnp.where(lead, 1, 0))[:, None]

    vec, prob, *arrived = attend_forward(
        q_word, q_pos, keys, values, rel, thr, key_rank, block, wires
    )
    if wires:
        wo, ud, tangent = arrived
    out, d_mixed, g_vec, g_out, g_ud, g_upb, small, *near = feed(
        ud,
        wo,
        vec,
        stream,
        tangent,
        up_bias,
        (down_bias, first_gain, first_shift, second_gain, second_shift),
        groups == 8,
    )
    backward = (prob, g_vec, q_word, q_pos, keys, values, rel, block)
    if groups == 8:
        d_proj, dk_t, dv_t, drel_t, biases, grad_up, grad_down, grad_out, content_out, query_out = (
            attend_backward(*backward, (g_ud, *near, g_out[None], out))
        )
    else:
        d_proj, dk_t, dv_t, drel_t, biases = attend_backward(*backward)
        content_out, query_out = from_unit(out)
        grad_up, grad_down = scatter_sum(g_ud)
    small = jnp.concatenate([g_upb.reshape(-1), small[:5].reshape(-1), biases.reshape(-1)])
    inner = up_bias.shape[0]
    table_t = jnp.asarray(np.ascontiguousarray(reversed_table(span, klen, width).T))
    if groups == 8:
        small = jnp.pad(small, (0, -small.shape[0] % 1024)).reshape(-1, 128)
        arrays = [stream, d_proj, context, dk_t, dv_t, weights, table_t, drel_t]
        (
            grad_key,
            grad_value,
            grad_query,
            grad_pos,
            content_grad,
            query_grad,
            small,
        ) = finish(arrays, d_mixed, small)
        arrays = [content_out, query_out, content_grad, query_grad, grad_query, grad_key]
        arrays += [grad_value, grad_pos, grad_out, grad_up, grad_down]
        *arrays, up_sum, down_sum, a1, b1, a2, b2, word_sum, pos_sum = emit(
            small, arrays, inner, width
        )
        return *arrays[:10], up_sum, arrays[10], down_sum, word_sum, pos_sum, a1, b1, a2, b2
    else:
        d_context = tt(dk_t[:, mem_total:], weights[0]) + tt(dv_t[:, mem_total:], weights[1])
        partner = swap(d_context.astype(BF)).astype(F32)
        d_stream = d_mixed + nt(d_proj, weights[2]) + jnp.where(lead, d_context + partner, 0.0)
        content_grad, query_grad = from_unit(d_stream.astype(BF))
        grad_key, grad_value, grad_query, grad_pos = scatter_sum(
            weight_grads(jnp.transpose(stream), jnp.transpose(context), table_t, d_proj, dk_t, dv_t, drel_t)
        )
        (grad_out,) = scatter_sum(g_out[None])
        small = lax.psum(small, ("dp", "tensor"))
    rest = small[inner:].reshape(7, width)
    return (
        content_out,
        query_out,
        content_grad,
        query_grad,
        grad_query,
        grad_key,
        grad_value,
        grad_pos,
        grad_out,
        grad_up,
        small[:inner],
        grad_down,
        rest[0],
        rest[5].reshape(HEADS, DH),
        rest[6].reshape(HEADS, DH),
        rest[1],
        rest[2],
        rest[3],
        rest[4],
    )


def solution(mesh):
    rows = P("dp", "tensor", None)
    mat = P("dp", "tensor")
    return jax.shard_map(
        body,
        mesh=mesh,
        in_specs=(rows,) * 5
        + (P("dp"), P("dp", None), P("dp"), P())
        + (mat,) * 6
        + (P(), mat)
        + (P(),) * 7,
        out_specs=(rows,) * 4 + (mat,) * 6 + (P(), mat) + (P(),) * 7,
        check_vma=False,
    )
```

```python
import functools

import jax
import jax.numpy as jnp
import numpy as np
from jax import lax
from jax.experimental import pallas as pl
from jax.experimental.pallas import tpu as pltpu
from jax.sharding import PartitionSpec as P

HEADS = 12
DH = 64
PAIR = 2 * DH
EPS = 1e-06
BF = jnp.bfloat16
F32 = jnp.float32
LIMIT = 60 * 1024 * 1024
SMEM_SPEC = pl.BlockSpec(memory_space=pltpu.SMEM)
ANY_SPEC = pl.BlockSpec(memory_space=pl.ANY)


def nn(left, right):
    return jnp.dot(left, right, preferred_element_type=F32)


def nt(left, right):
    return lax.dot_general(left, right, (((1,), (1,)), ((), ())), preferred_element_type=F32)


def tn(left, right):
    return lax.dot_general(left, right, (((0,), (0,)), ((), ())), preferred_element_type=F32)


def tt(left, right):
    return lax.dot_general(left, right, (((0,), (1,)), ((), ())), preferred_element_type=F32)


def reversed_table(count, first, width):
    dist = (first - np.arange(count)).astype(np.float32)
    half = width // 2
    power = np.arange(half).astype(np.float32) * np.float32(2.0 / width)
    freq = np.float32(1.0) / np.float32(10000.0) ** power
    angle = (dist[:, None] * freq[None, :]).astype(np.float64)
    return np.concatenate([np.sin(angle), np.cos(angle)], axis=1).astype(np.float32).astype(BF)


MESH = pl.DeviceIdType.MESH
CORE, XBIT, YBIT = 1, 2, 4


class Place:
    def __init__(self):
        self.d, self.z = lax.axis_index("dp"), lax.axis_index("tensor")
        self.core = lax.rem(self.d, 2)
        self.x = lax.rem(lax.div(self.d, 2), 2)
        self.y = lax.div(self.d, 4)

    def dp(self, bits):
        at = self.d
        if bits & CORE:
            at = at + (1 - 2 * self.core)
        if bits & XBIT:
            at = at + (2 - 4 * self.x)
        if bits & YBIT:
            at = at + (4 - 8 * self.y)
        return at

    def up(self, step):
        return lax.rem(self.z + step, 4) if step else self.z


def push(src, dst, send, recv, dp, z):
    return pltpu.make_async_remote_copy(
        src_ref=src,
        dst_ref=dst,
        send_sem=send,
        recv_sem=recv,
        device_id=(dp, z),
        device_id_type=MESH,
    )


def settle(ref, sem):
    pltpu.make_async_copy(ref, ref, sem).wait()


def greet(partners):
    barrier = pltpu.get_barrier_semaphore()
    for partner in partners:
        pl.semaphore_signal(barrier, inc=1, device_id=partner, device_id_type=MESH)
    pl.semaphore_wait(barrier, len(partners))


GATHER = (
    (0, 0, XBIT),
    (0, 1, YBIT),
    (0, 0, YBIT),
    (0, 1, XBIT),
    (XBIT, 0, YBIT),
    (YBIT, 1, XBIT),
    (0, 0, CORE),
    (0, 1, CORE),
    (XBIT, 0, CORE),
    (YBIT, 1, CORE),
    (YBIT, 0, CORE),
    (XBIT, 1, CORE),
    (XBIT | YBIT, 0, CORE),
    (XBIT | YBIT, 1, CORE),
)


class Gather:
    def __init__(self, place, dst, own, send, recv):
        self.place, self.dst, self.own = place, dst, own
        self.send, self.recv = send, recv
        self.half = dst.shape[1] // 16

    def region(self, owner, half):
        at = self.place.dp(owner) * (2 * self.half) + half * self.half
        return self.dst.at[:, pl.ds(pl.multiple_of(at, 16), self.half), :]

    def copy(self, i):
        owner, half, to = GATHER[i]
        src = self.region(owner, half)
        if owner == 0 and self.own is not None:
            src = self.own.at[:, half * self.half : (half + 1) * self.half, :]
        place = self.place
        return push(
            src, self.region(owner, half), self.send.at[i], self.recv.at[i], place.dp(to), place.z
        )

    def start(self, *which):
        for i in which:
            self.copy(i).start()

    def wait(self, received, sent):
        for i in received:
            self.copy(i).wait_recv()
        for i in sent:
            self.copy(i).wait_send()

    def after(self, arrived, started):
        for i, more in zip(arrived, started):
            self.copy(i).wait_recv()
            for j in more:
                self.copy(j).start()

    def middle(self):
        self.after((0, 1), ((4, 8), (5, 9)))

    def last(self):
        self.after((2, 3, 4, 5), ((10,), (11,), (12,), (13,)))


def chip_bits(j):
    return (XBIT if j & 1 else 0) | (YBIT if j & 2 else 0)


def add_into(dst, src):
    def run(i, carry):
        at = pl.ds(pl.multiple_of(i * 16, 16), 16)
        dst[:, at, :] = (dst[:, at, :].astype(F32) + src[:, at, :].astype(F32)).astype(BF)
        return carry

    lax.fori_loop(0, dst.shape[1] // 16, run, 0)


class Reduce:
    def __init__(self, place, sources, scratch, out, paired=False):
        self.place, self.sources, self.out, self.paired = place, sources, out, paired
        self.total, self.pair, self.near, self.far, self.quarter, self.stage = scratch[:6]
        self.pair_send, self.pair_recv, self.load, self.send, self.recv, self.z_send, self.z_recv = scratch[6:]
        self.rows = self.total.shape[2]

    @staticmethod
    def scratch(count, n, rows, cols, paired=False):
        part = cols // 4
        dma = lambda k: pltpu.SemaphoreType.DMA((k,))
        return [
            pltpu.VMEM((n, 4, rows, cols), BF),
            pltpu.VMEM((8, 128) if paired else (n, 4, rows, cols), BF),
            pltpu.VMEM((n, 2, 2, rows // 2, cols), BF),
            pltpu.VMEM((n, 2, rows // 2, cols), BF),
            pltpu.VMEM((4, n, rows, part), BF),
            pltpu.VMEM((4, n, rows, part) if part % 128 else (8, 128), BF),
            dma(4 * count),
            dma(4 * count),
            dma(4 * count),
            dma(6),
            dma(6),
            dma(3),
            dma(1),
        ]

    def pair_copies(self, j):
        place, rows = self.place, self.rows
        copies, at = [], 0
        for i, src in enumerate(self.sources):
            slot, n = len(self.sources) * j + i, src.shape[0]
            block = lambda bits: src.at[:, pl.ds(pl.multiple_of(place.dp(bits) * rows, 16), rows), :]
            remote = push(
                block(chip_bits(j) | CORE),
                self.pair.at[at : at + n, j],
                self.pair_send.at[slot],
                self.pair_recv.at[slot],
                place.dp(CORE),
                place.z,
            )
            local = pltpu.make_async_copy(
                block(chip_bits(j)), self.total.at[at : at + n, j], self.load.at[slot]
            )
            copies.append((remote, local))
            at += n
        return copies

    def half(self, j, h):
        size = self.rows // 2
        return self.total.at[:, j, h * size : (h + 1) * size, :]

    MOVES = ((3, 0, XBIT, 1), (3, 1, YBIT, 1), (1, 0, XBIT, 0), (2, 1, YBIT, 0), (2, 0, YBIT, 0), (1, 1, XBIT, 1))

    def move(self, i):
        j, h, to, where = self.MOVES[i]
        dst = self.near.at[:, h, where] if i < 4 else self.far.at[:, where]
        place = self.place
        return push(self.half(j, h), dst, self.send.at[i], self.recv.at[i], place.dp(to), place.z)

    def z_copy(self, k):
        place, part = self.place, self.quarter.shape[3]
        to = place.up(k)
        if part % 128:
            src = self.stage.at[to]
        else:
            src = self.total.at[:, 0, :, pl.ds(pl.multiple_of(to * part, 128), part)]
        dst = self.quarter.at[place.z]
        if k == 0:
            return pltpu.make_async_copy(src, dst, self.z_recv.at[0])
        return push(src, dst, self.z_send.at[k - 1], self.z_recv.at[0], place.d, to)

    def loaded(self, j):
        src, near = self.sources
        if j == 3:
            return pltpu.make_async_copy(near, self.near, self.load.at[3])
        return pltpu.make_async_copy(src.at[:, j], self.total.at[:, j], self.load.at[j])

    def begin(self):
        for j in (3, 1, 2, 0):
            if self.paired:
                self.loaded(j).start()
                continue
            for remote, local in self.pair_copies(j):
                remote.start()
                local.start()

    def pairs(self):
        for j, moves in ((3, (0, 1)), (1, (2,)), (2, (3,)), (0, ())):
            for remote, local in self.pair_copies(j):
                local.wait()
                remote.wait_recv()
            add_into(self.total.at[:, j], self.pair.at[:, j])
            for i in moves:
                self.move(i).start()

    def middle(self):
        for i, j, h, where, more in ((0, 2, 0, 1, 4), (1, 1, 1, 1, 5), (2, 0, 0, 0, None), (3, 0, 1, 0, None)):
            if not self.paired:
                self.move(i).wait_recv()
            elif i == 0:
                for k in range(4):
                    self.loaded(k).wait()
            add_into(self.half(j, h), self.near.at[:, h, where])
            if more is not None:
                self.move(more).start()

    def late(self):
        for i, h in ((4, 0), (5, 1)):
            self.move(i).wait_recv()
            add_into(self.half(0, h), self.far.at[:, h])
        part = self.quarter.shape[3]
        if part % 128:
            for k in range(4):
                for m in range(self.total.shape[0]):
                    self.stage[k, m] = self.total[m, 0, :, k * part : (k + 1) * part]
        for k in (2, 1, 3, 0):
            self.z_copy(k).start()

    def end(self):
        settle(self.quarter, self.z_recv.at[0])
        parts = [self.quarter[k].astype(F32) for k in range(4)]
        total = (parts[0] + parts[1]) + (parts[2] + parts[3])
        self.out[...] = total.reshape(self.out.shape)
        if not self.paired:
            for j in range(4):
                for remote, _ in self.pair_copies(j):
                    remote.wait_send()
        for i in range(4 if self.paired else 0, 6):
            self.move(i).wait_send()
        for k in range(1, 4):
            self.z_copy(k).wait_send()


class Homeward:
    def __init__(self, place, src, homes, send, recv):
        self.place, self.src, self.homes, self.send, self.recv = place, src, homes, send, recv
        self.part = homes[0].shape[1]

    def act(self, what):
        place, part = self.place, self.part
        for u in range(2):

            @pl.when(place.core == u)
            def _():
                for k in (2, 1, 3, 0):
                    to, dp = place.up(k), place.d - place.core + lax.div(place.z, 2)
                    src = self.src.at[pl.ds(pl.multiple_of(to * part, 16), part), :]
                    dst = self.homes[u].at[lax.rem(place.z, 2)]
                    recv = self.recv.at[u]
                    here = jnp.logical_and(dp == place.d, to == place.z)
                    remote = push(src, dst, self.send.at[k], recv, dp, to)
                    if what == "start":
                        pl.when(here)(pltpu.make_async_copy(src, dst, recv).start)
                        pl.when(jnp.logical_not(here))(remote.start)
                    else:
                        pl.when(jnp.logical_not(here))(remote.wait_send)

    def start(self):
        self.act("start")

    def end(self):
        for u in range(2):
            settle(self.homes[u], self.recv.at[u])
        self.act("wait")


def pair_and_z(place):
    return [(place.dp(r), place.up(k)) for k in range(4) for r in (0, CORE) if r or k]


def near_partners(place):
    return pair_and_z(place) + [(place.dp(r), place.z) for r in (XBIT, YBIT)]


INPUTS = 8


def finish_kernel(*refs):
    hbm, (mixed_ref, small_ref) = refs[:INPUTS], refs[INPUTS : INPUTS + 2]
    grad_refs, home_refs, sums_ref = refs[INPUTS + 2 : INPUTS + 6], refs[INPUTS + 6 : INPUTS + 8], refs[INPUTS + 8]
    refs = refs[INPUTS + 9 :]
    held, refs = refs[:INPUTS], refs[INPUTS:]
    loads, x_t, ctx_t, g_ref, base, ctx, partner, stream, slots, part_sum, chips = refs[:11]
    home_send, slot_send, chip_send, one_send, recv = refs[11:16]
    refs = refs[16:]
    count = len(refs) // 4
    place = Place()
    d, z, core = place.d, place.z, place.core
    copies = [
        pltpu.make_async_copy(a.at[0:3] if i == 5 else a, b, loads.at[i])
        for i, (a, b) in enumerate(zip(hbm, held))
    ]
    for copy in copies:
        copy.start()

    def need(*which):
        for i in which:
            copies[i].wait()
        return [held[i] for i in which]

    greet(near_partners(place) + [(place.dp(XBIT | YBIT), z)])
    sources = [g_ref.at[m : m + 1] for m in range(4)]
    key, value, query, pos = [
        Reduce(place, (src,), refs[m * count : (m + 1) * count], grad_refs[m])
        for m, src in enumerate(sources)
    ]
    slot_copies = []
    others = [(r, k) for k in range(4) for r in (0, CORE) if r or k]
    for i, (r, k) in enumerate(others):
        copy = push(small_ref, slots.at[4 * core + z], slot_send.at[i], recv.at[1], place.dp(r), place.up(k))
        copy.start()
        slot_copies.append(copy)
    pltpu.make_async_copy(small_ref, slots.at[4 * core + z], recv.at[1]).start()

    width, block = g_ref.shape[1], 256

    def product(m, left, right, dot):
        def run(i, carry):
            at = pl.ds(pl.multiple_of(i * block, block), block)
            g_ref[m, at, :] = dot(left[at, :], right[...]).astype(BF)
            return carry

        lax.fori_loop(0, width // block, run, 0)

    def turn(src, dst):
        def run(i, carry):
            at = pl.ds(pl.multiple_of(i * block, block), block)
            dst[:, at] = jnp.transpose(src[at, :].astype(F32)).astype(BF)
            return carry

        lax.fori_loop(0, src.shape[0] // block, run, 0)

    x_ref, d_proj = need(0, 1)
    turn(x_ref, x_t)
    product(2, x_t, d_proj, nn)
    query.begin()
    ctx_ref, dk_t = need(2, 3)
    turn(ctx_ref, ctx_t)
    product(0, ctx_t, dk_t, nt)
    key.begin()

    dv_t, mats = need(4, 5)
    back = dk_t.shape[1] - base.shape[0]

    def from_context(i, carry):
        at = pl.ds(pl.multiple_of(i * block, block), block)
        cols = pl.ds(pl.multiple_of(i * block + back, block), block)
        turned = nn(mats[0], dk_t[:, cols]) + nn(mats[1], dv_t[:, cols])
        turned = jnp.transpose(turned)
        base[at, :] = turned
        ctx[at, :] = turned.astype(BF)
        return carry

    lax.fori_loop(0, base.shape[0] // block, from_context, 0)
    swap = push(ctx, partner, one_send.at[0], recv.at[0], place.dp(CORE), z)
    swap.start()

    def from_proj(i, carry):
        at = pl.ds(pl.multiple_of(i * block, block), block)
        own = mixed_ref[at, :] + nt(d_proj[at, :], mats[2])
        base[at, :] = own + jnp.where(core == 0, base[at, :], 0.0)
        return carry

    lax.fori_loop(0, base.shape[0] // block, from_proj, 0)
    query.pairs()
    product(1, ctx_t, dv_t, nt)
    value.begin()
    key.pairs()

    swap.wait()
    small_block = 64

    def add_partner(i, carry):
        at = pl.ds(pl.multiple_of(i * small_block, small_block), small_block)
        more = jnp.where(core == 0, partner[at, :].astype(F32), 0.0)
        stream[at, :] = (base[at, :] + more).astype(BF)
        return carry

    lax.fori_loop(0, stream.shape[0] // small_block, add_partner, 0)
    home = Homeward(place, stream, home_refs, home_send, recv.at[2:4])
    home.start()

    table_t, dr_t = need(6, 7)
    product(3, table_t, dr_t, nt)
    pos.begin()
    value.pairs()
    query.middle()

    settle(slots, recv.at[1])
    total = slots[0]
    for i in range(1, 8):
        total = total + slots[i]
    part_sum[...] = total
    chip = lax.div(d, 2)
    chip_copies = []
    for i, r in enumerate((XBIT, YBIT, XBIT | YBIT)):
        copy = push(part_sum, chips.at[chip], chip_send.at[i], recv.at[4], place.dp(r), z)
        copy.start()
        chip_copies.append(copy)
    pltpu.make_async_copy(part_sum, chips.at[chip], recv.at[4]).start()

    pos.pairs()
    key.middle()
    query.late()
    value.middle()
    key.late()
    pos.middle()
    value.late()
    settle(chips, recv.at[4])
    sums_ref[...] = (chips[0] + chips[1]) + (chips[2] + chips[3])
    pos.late()
    for reduce in (query, key, value, pos):
        reduce.end()
    home.end()
    for copy in slot_copies + chip_copies:
        copy.wait_send()


def finish(arrays, mixed, small):
    total, width = arrays[0].shape
    klen = arrays[2].shape[0]
    rows = width // 8
    vmem = pl.BlockSpec(memory_space=pltpu.VMEM)
    dma = lambda k: pltpu.SemaphoreType.DMA((k,))
    scratch = [pltpu.VMEM((3,) + a.shape[1:] if a.ndim == 3 else a.shape, BF) for a in arrays]
    scratch += [
        dma(INPUTS),
        pltpu.VMEM((width, total), BF),
        pltpu.VMEM((width, klen), BF),
        pltpu.VMEM((4, width, width), BF),
        pltpu.VMEM((total, width), F32),
        pltpu.VMEM((total, width), BF),
        pltpu.VMEM((total, width), BF),
        pltpu.VMEM((total, width), BF),
        pltpu.VMEM((8,) + small.shape, F32),
        pltpu.VMEM(small.shape, F32),
        pltpu.VMEM((4,) + small.shape, F32),
        dma(4),
        dma(7),
        dma(3),
        dma(1),
        dma(5),
    ]
    for _ in range(4):
        scratch += Reduce.scratch(1, 1, rows, width)
    return pl.pallas_call(
        finish_kernel,
        in_specs=[ANY_SPEC] * INPUTS + [vmem] * 2,
        out_specs=[vmem] * 4 + [ANY_SPEC] * 2 + [vmem],
        out_shape=[jax.ShapeDtypeStruct((rows, width // 4), F32)] * 4
        + [jax.ShapeDtypeStruct((2, total // 4, width), BF)] * 2
        + [
            jax.ShapeDtypeStruct(small.shape, F32),
        ],
        scratch_shapes=scratch,
        compiler_params=pltpu.CompilerParams(
            collective_id=4, has_side_effects=True, vmem_limit_bytes=LIMIT
        ),
        cost_estimate=pl.CostEstimate(flops=20 << 30, bytes_accessed=64 << 20, transcendentals=0),
        name="finish",
    )(*arrays, mixed, small)


def emit_kernel(small_ref, *refs):
    count = 11
    for src, dst in zip(refs[:count], refs[count : 2 * count]):
        dst[...] = src[...]
    wide, *rows, word_ref, pos_ref = refs[2 * count :]
    lanes = small_ref.shape[1]
    size = wide.shape[0] // lanes
    wide[...] = small_ref[0:size, :].reshape(wide.shape)
    for ref in rows:
        step = ref.shape[0] // lanes
        ref[...] = small_ref[size : size + step, :].reshape(ref.shape)
        size += step
    for ref in (word_ref, pos_ref):
        for h in range(HEADS):
            at = size + h * DH // lanes
            ref[h : h + 1, :] = small_ref[at : at + 1, h * DH % lanes : h * DH % lanes + DH]
        size += HEADS * DH // lanes


def emit(small, arrays, inner, width):
    vmem = pl.BlockSpec(memory_space=pltpu.VMEM)
    out_shape = [jax.ShapeDtypeStruct(a.shape, a.dtype) for a in arrays]
    out_shape += [jax.ShapeDtypeStruct((inner,), F32)]
    out_shape += [jax.ShapeDtypeStruct((width,), F32)] * 5
    out_shape += [jax.ShapeDtypeStruct((HEADS, DH), F32)] * 2
    return pl.pallas_call(
        emit_kernel,
        in_specs=[vmem] * (1 + len(arrays)),
        out_specs=[vmem] * len(out_shape),
        out_shape=out_shape,
        compiler_params=pltpu.CompilerParams(vmem_limit_bytes=LIMIT),
        name="emit",
    )(small, *arrays)


def pack(mat):
    half = mat.shape[0] // 2
    return jnp.concatenate([mat[:, :128], jnp.concatenate([mat[:half, 128:], mat[half:, 128:]], axis=1)], axis=0)


def unpack(packed):
    rows = packed.shape[0] * 2 // 3
    rest = packed[rows:, :]
    return jnp.concatenate([packed[:rows, :], jnp.concatenate([rest[:, :64], rest[:, 64:]], axis=0)], axis=1)


def enter_kernel(slot_ref, seq_ref, mem_ref, content, query, memory, table_hbm, orders, *refs):
    mats, (upw, dnw), (wb_ref, pb_ref) = refs[:5], refs[5:7], refs[7:9]
    outs, (thr_ref, key_ref, whole_out, context_out, wo, ud) = refs[9:15], refs[15:21]
    (
        ints,
        all_ints,
        whole,
        context,
        stream,
        table,
        spread,
        picked,
        shards,
        slab,
        mat_send,
        mat_recv,
        ud_send,
        ud_recv,
        int_send,
        spread_send,
        pick_send,
        stream_send,
        pair_send,
        gather_send,
        gather_recv,
        wo_send,
        wo_recv,
        far_send,
        far_recv,
        recv,
        local,
    ) = refs[21:]
    place = Place()
    d, z, core = place.d, place.z, place.core
    up, down, far = place.up(1), place.up(3), place.up(2)
    part = query.shape[1]
    micro = orders.shape[0]
    spot = lax.broadcasted_iota(jnp.int32, (1, ints.shape[1]), 1)
    lengths = jnp.where(spot == 0, seq_ref[0], seq_ref[1])
    lengths = jnp.where(spot < 2, lengths, jnp.where(spot == 2, mem_ref[0], mem_ref[1]))
    ints[...] = jnp.concatenate([orders[...], jnp.broadcast_to(lengths, (6, ints.shape[1]))], axis=0)

    def slot_of(seq):
        at = jnp.int32(0)
        for k in range(16):
            at = at + jnp.where(slot_ref[k] == seq, k, 0)
        return jnp.minimum(at, 15)

    pltpu.make_async_copy(table_hbm, table, local.at[0]).start()
    piece = spread.shape[1]
    blocks = part // piece // 2
    first = 4 * blocks
    greet([(place.dp(r), place.up(k)) for r in range(8) for k in range(4) if r or k])

    spread_copies = []
    for r in range(8):
        to = place.dp(r)
        src = memory.at[:, pl.ds(pl.multiple_of(to * piece, 16), piece), :]
        dst = spread.at[pl.ds(2 * d, 2)]
        if r == 0:
            pltpu.make_async_copy(src, dst, recv.at[0]).start()
        else:
            spread_copies.append(push(src, dst, spread_send.at[r - 1], recv.at[0], to, z))
            spread_copies[-1].start()

    for m, mat in enumerate(mats):
        shards[z, m] = pack(mat[...])
    cutoff = shards.shape[2] * 5 // 9

    def mat_copy(i):
        own = shards.at[z]
        low, high = shards.at[down, :, :cutoff], shards.at[up, :, cutoff:]
        src = (own, own, low, high)[i]
        return push(src, src, mat_send.at[i], mat_recv.at[i], d, (up, down, up, down)[i])

    mat_copy(0).start()
    mat_copy(1).start()
    rows = slab.shape[1]
    width = upw.shape[1]

    def columns(at, start=0, size=rows):
        mine = pl.ds(pl.multiple_of(d * rows + start, 16), size)
        return ud.at[:, mine, pl.ds(pl.multiple_of(at * width, 128), width)]

    def ud_copy(i):
        if i < 4:
            src, dst = (upw, dnw)[i % 2], columns(z).at[i % 2]
            return push(src, dst, ud_send.at[i], ud_recv.at[i // 2], d, (up, down)[i // 2])
        half = rows // 2
        src = columns(down, 0, half) if i == 4 else columns(up, half, half)
        return push(src, src, ud_send.at[i], ud_recv.at[i - 2], d, (up, down)[i - 4])

    for m, mat in enumerate((upw, dnw)):
        pltpu.make_async_copy(mat, columns(z).at[m], recv.at[8]).start()

    int_copies = []
    for r in range(8):
        if r == 0:
            pltpu.make_async_copy(ints, all_ints.at[d], recv.at[2]).start()
        else:
            copy = push(ints, all_ints.at[d], int_send.at[r - 1], recv.at[2], place.dp(r), z)
            int_copies.append(copy)
            copy.start()

    def stream_copy(i, act):
        j, kind = i // 2, i % 2
        to, dp = 2 * core + j, d - core + kind
        if kind == 0:
            src, sem = content.at[j], recv.at[3]
            dst = context.at[pl.ds(first + blocks * z, blocks)]
        else:
            src, sem = query.at[j], recv.at[4]
            dst = stream.at[pl.ds(pl.multiple_of(z * part, 16), part), :]
        here = jnp.logical_and(dp == d, to == z)
        remote = push(src, dst, stream_send.at[i], sem, dp, to)
        if act == "start":
            pl.when(here)(pltpu.make_async_copy(src, dst, sem).start)
            pl.when(jnp.logical_not(here))(remote.start)
        else:
            pl.when(jnp.logical_not(here))(remote.wait_send)

    mat_copy(0).wait_recv()
    mat_copy(2).start()
    mat_copy(1).wait_recv()
    mat_copy(3).start()
    for i in range(4):
        ud_copy(i).start()
    mat_copy(2).wait_recv()
    mat_copy(3).wait_recv()
    for m in range(5):
        slab[m] = jnp.concatenate([unpack(shards[k, m]) for k in range(4)], axis=1)
    own_rows = pl.ds(pl.multiple_of(d * rows, 16), rows)
    gather = Gather(place, whole, slab.at[0:4], gather_send, gather_recv)
    gather.start(0, 1, 2, 3, 6, 7)
    pltpu.make_async_copy(slab.at[0:4], whole.at[:, own_rows, :], recv.at[6]).start()
    pltpu.make_async_copy(slab.at[4:5], wo.at[:, own_rows, :], recv.at[7]).start()

    settle(columns(down), ud_recv.at[0])
    ud_copy(4).start()
    settle(columns(up), ud_recv.at[1])
    ud_copy(5).start()
    for i in range(4):
        stream_copy(i, "start")

    settle(spread, recv.at[0])
    for q in range(16):
        picked[q] = spread[slot_of(q)]
    pick_copies = []
    for r in (YBIT | XBIT, XBIT, YBIT, 0):
        for k in range(4):
            to, lane = place.dp(r), place.up(k)
            src = picked.at[4 * lax.div(to, 2) + lane]
            dst = context.at[blocks * z + lax.div(d, 2), core]
            if r or k:
                copy = push(src, dst, pick_send.at[2 * r + k - 1], recv.at[5], to, lane)
                pick_copies.append(copy)
            else:
                copy = pltpu.make_async_copy(src, dst, recv.at[5])
            copy.start()

    gather.middle()
    wo_gather = Gather(place, wo, slab.at[4:5], wo_send, wo_recv)
    ud_gather = Gather(place, ud, None, far_send, far_recv)
    gathers = (ud_gather, wo_gather)
    settle(columns(z), recv.at[8])
    ud_copy(4).wait_recv()
    ud_copy(5).wait_recv()
    for i in (0, 1, 6, 7):
        for one in gathers:
            one.start(i)
    gather.last()

    pick_pair = push(
        context.at[0:first, core], context.at[0:first, core], pair_send.at[0], recv.at[1], place.dp(CORE), z
    )
    settle(context.at[0:first, core], recv.at[5])
    pick_pair.start()
    lead_copy = push(
        context.at[first:], context.at[first:], pair_send.at[1], recv.at[3], place.dp(CORE), z
    )

    @pl.when(core == 0)
    def _():
        settle(context.at[first:], recv.at[3])
        lead_copy.start()

    settle(all_ints, recv.at[2])
    seq = 4 * lax.div(d, 2) + z
    slot = slot_of(seq)
    odd = lax.rem(seq, micro)
    own, other = all_ints[lax.div(seq, micro)], all_ints[lax.div(slot, micro)]

    def pick(row, at):
        return jnp.sum(jnp.where(spot == at, row.astype(F32), 0.0), axis=1, keepdims=True)

    length = pick(own[2:3], odd)
    mem_valid = pick(other[2:3], micro + lax.rem(slot, micro))
    rank = jnp.where(odd == 0, own[0:1], own[1:2])
    seq_len = rank.shape[1]
    mem_total = key_ref.shape[1] - seq_len
    where = spot.astype(F32)
    hidden = jnp.int32(1 << 20)
    key_ref[:, :mem_total] = jnp.where(where >= mem_total - mem_valid, -1, hidden)
    key_ref[:, mem_total:] = jnp.where(where < length, rank, hidden)
    ranks = jnp.transpose(jnp.broadcast_to(rank.astype(F32), (8, seq_len)))
    thr_ref[...] = ranks[:, 0:1].astype(jnp.int32) + jnp.where(core == 0, 1, 0)

    gather.wait(range(6, 14), ())
    settle(whole.at[:, own_rows, :], recv.at[6])
    keep_whole = pltpu.make_async_copy(whole, whole_out, local.at[1])
    keep_whole.start()

    keep_context = pltpu.make_async_copy(context, context_out, local.at[2])

    def before_stream():
        pick_pair.wait()

        @pl.when(core == 0)
        def _():
            lead_copy.wait_send()

        @pl.when(core == 1)
        def _():
            settle(context.at[first:], recv.at[3])
            settle(stream, recv.at[4])

        keep_context.start()

    def before_context():
        for one in gathers:
            one.after((0, 1), ((8,), (9,)))

    pltpu.make_async_copy(table_hbm, table, local.at[0]).wait()
    project_step(
        whole, context, stream, table, wb_ref, pb_ref, *outs, hooks=(before_stream, before_context)
    )
    settle(wo.at[:, own_rows, :], recv.at[7])
    gather.wait((), range(14))
    for one in gathers:
        one.wait(range(6, 10), (0, 1, 6, 7, 8, 9))
    keep_whole.wait()
    keep_context.wait()
    for i in range(4):
        stream_copy(i, "wait")
        mat_copy(i).wait_send()
    for i in range(6):
        ud_copy(i).wait_send()
    for copy in spread_copies + int_copies + pick_copies:
        copy.wait_send()


def enter(slots, seqs, mems, content, query, memory, table, orders, mats, upw, dnw, wb, pb):
    micro, part, width = content.shape
    rows = mats[0].shape[0]
    inner = upw.shape[1] * 4
    piece = part // 8
    klen, span, seq = 8 * part, table.shape[0], 4 * part
    vmem = pl.BlockSpec(memory_space=pltpu.VMEM)
    dma = lambda n: pltpu.SemaphoreType.DMA((n,))
    bf = lambda *shape: jax.ShapeDtypeStruct(shape, BF)
    return pl.pallas_call(
        enter_kernel,
        in_specs=[SMEM_SPEC] * 3 + [ANY_SPEC] * 4 + [vmem] * 10,
        out_specs=[vmem] * 8 + [ANY_SPEC] * 4,
        out_shape=[
            bf(klen, width),
            bf(klen, width),
            bf(span, width),
            bf(seq, width),
            bf(seq, width),
            bf(seq, width),
            jax.ShapeDtypeStruct((seq, 1), jnp.int32),
            jax.ShapeDtypeStruct((1, klen), jnp.int32),
            bf(4, 8 * rows, width),
            bf(32, 2, piece, width),
            bf(1, 8 * rows, width),
            bf(2, 8 * rows, inner),
        ],
        scratch_shapes=[
            pltpu.VMEM((8, seq), jnp.int32),
            pltpu.VMEM((8, 8, seq), jnp.int32),
            pltpu.VMEM((4, 8 * rows, width), BF),
            pltpu.VMEM((32, 2, piece, width), BF),
            pltpu.VMEM((seq, width), BF),
            pltpu.VMEM((span, width), BF),
            pltpu.VMEM((16, piece, width), BF),
            pltpu.VMEM((16, piece, width), BF),
            pltpu.VMEM((4, 5, rows * 3 // 2, 128), BF),
            pltpu.VMEM((5, rows, width), BF),
            dma(4),
            dma(4),
            dma(6),
            dma(4),
            dma(7),
            dma(7),
            dma(15),
            dma(4),
            dma(2),
            dma(14),
            dma(14),
            dma(14),
            dma(14),
            dma(14),
            dma(14),
            dma(9),
            dma(3),
        ],
        compiler_params=pltpu.CompilerParams(
            collective_id=1, has_side_effects=True, vmem_limit_bytes=LIMIT
        ),
        cost_estimate=pl.CostEstimate(flops=0, bytes_accessed=64 << 20, transcendentals=0),
        name="enter",
    )(
        slots,
        seqs,
        mems,
        content.reshape(micro, 4, 2, piece, width),
        query,
        memory,
        table,
        orders,
        *mats,
        upw,
        dnw,
        wb,
        pb,
    )


def head_lanes(array, head):
    lane = lax.broadcasted_iota(jnp.int32, array.shape, 1)
    return jnp.where((lane >= DH) == (head == 1), array, jnp.zeros_like(array))


def attend_forward_step(
    block, qw_ref, qp_ref, k_ref, v_ref, rel_ref, thr_ref, kr_ref, vec_ref, prob_ref
):
    rows, klen = qw_ref.shape[0], k_ref.shape[0]
    width = klen + block
    keys, values = k_ref[...], v_ref[...]
    for part in range(rows // block):
        at = slice(part * block, (part + 1) * block)
        first = rows - (part + 1) * block
        qw, qp = qw_ref[at, :], qp_ref[at, :]
        rel = rel_ref[first : first + width, :]
        seen = kr_ref[...] < thr_ref[at, :]
        vecs = []
        for head in range(2):
            raw = nt(head_lanes(qp, head), rel)
            moved = pltpu.roll(raw, 0, 1, stride=1, stride_axis=0)[:, block:]
            score = nt(head_lanes(qw, head), keys) + moved
            score = jnp.where(seen, score, -1e30)
            expo = jnp.exp(score - jnp.max(score, axis=1, keepdims=True))
            prob = (expo * (1.0 / jnp.sum(expo, axis=1, keepdims=True))).astype(BF)
            prob_ref[head, at, :] = prob
            vecs.append(nn(prob, values))
        lane = lax.broadcasted_iota(jnp.int32, vecs[0].shape, 1)
        vec_ref[at, :] = jnp.where(lane < DH, vecs[0], vecs[1]).astype(BF)


def attend_forward_kernel(block, wired, *refs):
    if not wired:
        attend_forward_step(block, *refs)
        return
    ins, (ctan, qtan) = refs[:7], refs[9:11]
    outs, (wo, ud, tangent) = refs[11:13], refs[13:16]
    out_send, out_recv, ud_send, ud_recv, tan_send, recv = refs[16:]
    step, steps = pl.program_id(0), pl.num_programs(0)
    place = Place()
    d, z, core = place.d, place.z, place.core
    gathers = (
        Gather(place, ud, None, ud_send, ud_recv),
        Gather(place, wo, None, out_send, out_recv),
    )
    part = ctan.shape[1]

    def tan_copy(i, act):
        j, kind = i // 2, i % 2
        to, dp = 2 * core + j, d - core + kind
        src = (ctan, qtan)[kind].at[j]
        dst = tangent.at[pl.ds(pl.multiple_of(z * part, 16), part), :]
        here = jnp.logical_and(dp == d, to == z)
        local = pltpu.make_async_copy(src, dst, recv.at[0])
        remote = push(src, dst, tan_send.at[i], recv.at[0], dp, to)
        if act == "start":
            pl.when(here)(local.start)
            pl.when(jnp.logical_not(here))(remote.start)
        else:
            pl.when(jnp.logical_not(here))(remote.wait_send)

    @pl.when(step == 0)
    def _():
        greet(near_partners(place))
        for gather in gathers:
            gather.start(2, 3)
        for gather in gathers:
            gather.start(4, 5)
        for i in range(4):
            tan_copy(i, "start")

    @pl.when(step == 4)
    def _():
        for gather in gathers:
            gather.after((2, 3), ((10,), (11,)))

    attend_forward_step(block, *ins, *outs)

    @pl.when(step == steps - 1)
    def _():
        for gather in gathers:
            gather.after((4, 5), ((12,), (13,)))
        for gather in gathers:
            gather.wait(range(10, 14), (2, 3, 4, 5) + tuple(range(10, 14)))
        settle(tangent, recv.at[0])
        for i in range(4):
            tan_copy(i, "wait")


def attend_forward(qw, qp, keys, values, rel, thr, key_rank, block, wires=()):
    rows, width = qw.shape
    klen, span = keys.shape[0], rel.shape[0]
    col = lambda count: pl.BlockSpec((count, PAIR), lambda p: (0, p))
    in_specs = [
        col(rows),
        col(rows),
        col(klen),
        col(klen),
        col(span),
        pl.BlockSpec((rows, 1), lambda p: (0, 0)),
        pl.BlockSpec((1, klen), lambda p: (0, 0)),
    ]
    out_specs = [col(rows), pl.BlockSpec((2, rows, klen), lambda p: (p, 0, 0))]
    out_shape = [
        jax.ShapeDtypeStruct((rows, width), BF),
        jax.ShapeDtypeStruct((width // DH, rows, klen), BF),
    ]
    params = dict(vmem_limit_bytes=LIMIT)
    scratch = []
    if wires:
        in_specs += [ANY_SPEC] * 4
        out_specs += [ANY_SPEC] * 3
        out_shape += [
            jax.ShapeDtypeStruct(wires[0].shape, BF),
            jax.ShapeDtypeStruct(wires[1].shape, BF),
            jax.ShapeDtypeStruct((rows, width), BF),
        ]
        scratch = [pltpu.SemaphoreType.DMA((n,)) for n in (14, 14, 14, 14, 4, 1)]
        params.update(collective_id=2, has_side_effects=True)
    return pl.pallas_call(
        functools.partial(attend_forward_kernel, block, bool(wires)),
        grid=(width // PAIR,),
        in_specs=in_specs,
        out_specs=out_specs,
        out_shape=out_shape,
        scratch_shapes=scratch,
        input_output_aliases={7: 2, 8: 3} if wires else {},
        compiler_params=pltpu.CompilerParams(**params),
        cost_estimate=pl.CostEstimate(
            flops=8 * rows * klen * width, bytes_accessed=16 << 20, transcendentals=12 * rows * klen
        ),
        name="attend_forward",
    )(qw, qp, keys, values, rel, thr, key_rank, *wires)


def attend_backward_kernel(block, wired, *refs):
    if not wired:
        attend_backward_step(block, *refs)
        return
    ins, (g_ud, near_ud, g_out, src) = refs[:7], refs[7:11]
    outs, grad_refs, home_refs = refs[11:16], refs[16:19], refs[19:21]
    rel_acc, home_send, home_recv = refs[21:24]
    refs = refs[24:]
    step, steps = pl.program_id(0), pl.num_programs(0)
    place = Place()
    count = len(refs) // 3
    held = [refs[m * count : (m + 1) * count] for m in range(3)]
    reduces = [
        Reduce(place, (g_ud.at[m : m + 1], near_ud.at[m : m + 1]), held[m], grad_refs[m], True)
        for m in range(2)
    ]
    out = Reduce(place, (g_out,), held[2], grad_refs[2])
    home = Homeward(place, src, home_refs, home_send, home_recv)

    @pl.when(step == 0)
    def _():
        greet(near_partners(place))
        for reduce in reduces:
            reduce.begin()
        out.begin()
        home.start()

    @pl.when(step == 1)
    def _():
        for reduce in reduces:
            reduce.middle()
        out.pairs()

    @pl.when(step == 3)
    def _():
        reduces[0].late()

    @pl.when(step == 4)
    def _():
        reduces[1].late()
        out.middle()

    @pl.when(step == 5)
    def _():
        out.late()

    attend_backward_step(block, *ins, *outs, rel_acc)

    @pl.when(step == steps - 1)
    def _():
        for reduce in reduces:
            reduce.end()
        out.end()
        home.end()


def attend_backward_step(
    block,
    prob_ref,
    gvec_ref,
    qw_ref,
    qp_ref,
    k_ref,
    v_ref,
    rel_ref,
    dproj_ref,
    dk_ref,
    dv_ref,
    drel_ref,
    bias_ref,
    rel_acc,
):
    rows, klen = qw_ref.shape[0], k_ref.shape[0]
    width = klen + block
    keys, values = k_ref[...], v_ref[...]
    row = lax.broadcasted_iota(jnp.int32, (block, block), 0)
    col = lax.broadcasted_iota(jnp.int32, (block, block), 1)
    mirror = (row + col == block - 1).astype(BF)
    rel_acc[...] = jnp.zeros_like(rel_acc)
    d_keys, d_values = [None, None], [None, None]
    word_sum = jnp.zeros((1, PAIR), F32)
    pos_sum = jnp.zeros((1, PAIR), F32)
    for part in range(rows // block):
        at = slice(part * block, (part + 1) * block)
        first = rows - (part + 1) * block
        gvec, qw = gvec_ref[at, :], qw_ref[at, :]
        gvec_t = jnp.transpose(gvec.astype(F32)).astype(BF)
        qw_t = jnp.transpose(qw.astype(F32)).astype(BF)
        qp_t = jnp.transpose(nn(mirror, qp_ref[at, :])).astype(BF)
        rel = rel_ref[first : first + width, :]
        word_parts, pos_parts = [], []
        for head in range(2):
            own = slice(head * DH, (head + 1) * DH)
            prob = prob_ref[head, at, :]
            d_prob = nt(head_lanes(gvec, head), values)
            weight = prob.astype(F32)
            inner = jnp.sum(weight * d_prob, axis=1, keepdims=True)
            g_sum = (weight * (d_prob - inner) * 0.125).astype(BF)
            dv = nn(gvec_t[own, :], prob)
            dk = nn(qw_t[own, :], g_sum)
            d_values[head] = dv if part == 0 else d_values[head] + dv
            d_keys[head] = dk if part == 0 else d_keys[head] + dk
            turned = nn(mirror, g_sum)
            padded = jnp.concatenate([jnp.zeros((block, block), F32), turned], axis=1)
            moved = pltpu.roll(padded, width - block + 1, 1, stride=1, stride_axis=0).astype(BF)
            word_parts.append(nn(turned.astype(BF), keys))
            pos_parts.append(nn(moved, rel))
            rel_acc[own, first : first + width] += nn(qp_t[own, :], moved)
        lane = lax.broadcasted_iota(jnp.int32, word_parts[0].shape, 1)
        word = jnp.where(lane < DH, word_parts[0], word_parts[1])
        pos = jnp.where(lane < DH, pos_parts[0], pos_parts[1])
        word_sum = word_sum + jnp.sum(word, axis=0, keepdims=True)
        pos_sum = pos_sum + jnp.sum(pos, axis=0, keepdims=True)
        dproj_ref[at, :] = nn(mirror, (word + pos).astype(BF)).astype(BF)
    for head in range(2):
        own = slice(head * DH, (head + 1) * DH)
        dv_ref[own, :] = d_values[head].astype(BF)
        dk_ref[own, :] = (8.0 * d_keys[head]).astype(BF)
    drel_ref[...] = (8.0 * rel_acc[...]).astype(BF)
    bias_ref[0:1, :] = word_sum
    bias_ref[1:2, :] = pos_sum


def attend_backward(prob, gvec, qw, qp, keys, values, rel, block, wires=()):
    rows, width = qw.shape
    klen, span = keys.shape[0], rel.shape[0]
    col = lambda count: pl.BlockSpec((count, PAIR), lambda p: (0, p))
    rowb = lambda count: pl.BlockSpec((PAIR, count), lambda p: (p, 0))
    in_specs = [
        pl.BlockSpec((2, rows, klen), lambda p: (p, 0, 0)),
        col(rows),
        col(rows),
        col(rows),
        col(klen),
        col(klen),
        col(span),
    ]
    out_specs = [col(rows), rowb(klen), rowb(klen), rowb(span), col(2)]
    out_shape = [
        jax.ShapeDtypeStruct((rows, width), BF),
        jax.ShapeDtypeStruct((width, klen), BF),
        jax.ShapeDtypeStruct((width, klen), BF),
        jax.ShapeDtypeStruct((width, span), BF),
        jax.ShapeDtypeStruct((2, width), F32),
    ]
    scratch = [pltpu.VMEM((PAIR, span), F32)]
    params = dict(vmem_limit_bytes=LIMIT)
    if wires:
        inner, mine = wires[0].shape[3], width // 8
        in_specs += [ANY_SPEC] * 4
        out_specs += [pl.BlockSpec(memory_space=pltpu.VMEM)] * 3 + [ANY_SPEC] * 2
        out_shape += [jax.ShapeDtypeStruct((mine, inner // 4), F32)] * 2
        out_shape += [jax.ShapeDtypeStruct((mine, width // 4), F32)]
        out_shape += [jax.ShapeDtypeStruct((2, rows // 4, width), BF)] * 2
        scratch += [pltpu.SemaphoreType.DMA((4,)), pltpu.SemaphoreType.DMA((2,))]
        scratch += 2 * Reduce.scratch(1, 1, mine, inner, True) + Reduce.scratch(1, 1, mine, width)
        params.update(collective_id=3, has_side_effects=True)
    return pl.pallas_call(
        functools.partial(attend_backward_kernel, block, bool(wires)),
        grid=(width // PAIR,),
        in_specs=in_specs,
        out_specs=out_specs,
        out_shape=out_shape,
        scratch_shapes=scratch,
        compiler_params=pltpu.CompilerParams(**params),
        cost_estimate=pl.CostEstimate(
            flops=16 * rows * klen * width, bytes_accessed=20 << 20, transcendentals=0
        ),
        name="attend_backward",
    )(prob, gvec, qw, qp, keys, values, rel, *wires)


def norm_parts(value):
    center = value - jnp.mean(value, axis=1, keepdims=True)
    scale = lax.rsqrt(jnp.mean(center * center, axis=1, keepdims=True) + EPS)
    return center * scale, scale


def norm_pull(normed, scale, err):
    inner = jnp.mean(err * normed, axis=1, keepdims=True)
    return (err - jnp.mean(err, axis=1, keepdims=True) - normed * inner) * scale


def sum_rows(value):
    return jnp.sum(value, axis=0, keepdims=True)


def feed_kernel(steps, wired, *refs):
    (
        ud_hbm,
        wo_hbm,
        vec_ref,
        x_ref,
        tan_ref,
        upb_ref,
        dnb_ref,
        g1_ref,
        s1_ref,
        g2_ref,
        s2_ref,
        out_ref,
        dmix_ref,
        gvec_ref,
        go_ref,
        gud_ref,
        gupb_ref,
        small_ref,
        *refs,
    ) = refs
    near_ref, *refs = refs if wired else (None, *refs)
    (
        ud_ref,
        wo_ref,
        n1_ref,
        r1_ref,
        fb_ref,
        fbt_ref,
        acc_ref,
        act_ref,
        slope_ref,
        gd_ref,
        gdt_ref,
        sems,
        *pair_refs,
    ) = refs
    step = pl.program_id(0)
    chunk = act_ref.shape[2]
    row = lambda ref: ref[...].reshape(1, -1)
    cols = pl.ds(pl.multiple_of(lax.rem(step, steps) * chunk, chunk), chunk)

    if wired:
        own_ref, pair_ref, sum_ref, send, recv, keep, move_send, move_recv = pair_refs
        place = Place()
        rows = pair_ref.shape[2]

        def span(c):
            return pl.ds(pl.multiple_of(c * chunk, chunk), chunk)

        def block(bits):
            return pl.ds(pl.multiple_of(place.dp(bits) * rows, 16), rows)

        def pair_copy(c, j):
            slot = lax.rem(c, 2)
            return push(
                own_ref.at[slot, :, block(chip_bits(j) | CORE), :],
                pair_ref.at[:, j, :, span(c)],
                send.at[slot, j],
                recv.at[c],
                place.dp(CORE),
                place.z,
            )

        def keep_copy(c):
            return pltpu.make_async_copy(sum_ref.at[c], gud_ref.at[:, :, :, span(c)], keep.at[c])

        def move(c, i):
            j, h, to, where = Reduce.MOVES[i]
            return push(
                sum_ref.at[c, :, j, h * (rows // 2) : (h + 1) * (rows // 2), :],
                near_ref.at[:, h, where, :, span(c)],
                move_send.at[c, i],
                move_recv.at[c],
                place.dp(to),
                place.z,
            )

        def join(c):
            slot = lax.rem(c, 2)
            settle(pair_ref.at[:, :, :, span(c)], recv.at[c])
            for j in (3, 1, 2, 0):
                mine = own_ref[slot, :, block(chip_bits(j)), :].astype(F32)
                sum_ref[c, :, j] = (mine + pair_ref[:, j, :, span(c)].astype(F32)).astype(BF)
            for i in range(4):
                move(c, i).start()
            keep_copy(c).start()

        def send_wait(c):
            for j in range(4):
                pair_copy(c, j).wait_send()

        @pl.when(step == 0)
        def _():
            greet([(place.dp(r), place.z) for r in (CORE, XBIT, YBIT)])

    @pl.when(step == 0)
    def _():
        wo_copy = pltpu.make_async_copy(wo_hbm, wo_ref, sems.at[0])
        ud_copy = pltpu.make_async_copy(ud_hbm, ud_ref, sems.at[1])
        wo_copy.start()
        ud_copy.start()
        wo_copy.wait()
        normed, scale = norm_parts(nt(vec_ref[...], wo_ref[0]) + x_ref[...].astype(F32))
        n1_ref[...] = normed
        r1_ref[...] = scale
        first = normed * row(g1_ref) + row(s1_ref)
        fb_ref[...] = first.astype(BF)
        fbt_ref[...] = jnp.transpose(first).astype(BF)
        acc_ref[...] = first + row(dnb_ref)
        ud_copy.wait()

    @pl.when(step < steps)
    def _():
        upper = nn(fb_ref[...], ud_ref[0, :, cols]) + row(upb_ref)
        square = upper * upper
        root = 0.7978845608028654
        bend = jnp.tanh(root * (upper + 0.044715 * (square * upper)))
        half = 0.5 * (1.0 + bend)
        act = (upper * half).astype(BF)
        act_ref[step] = act
        slope_ref[step] = half + 0.5 * upper * (1.0 - bend * bend) * (
            root + (3 * 0.044715 * root) * square
        )
        acc_ref[...] += nt(act, ud_ref[1, :, cols])

    @pl.when(step == steps - 1)
    def _():
        normed, scale = norm_parts(acc_ref[...])
        out_ref[...] = (normed * row(g2_ref) + row(s2_ref)).astype(BF)
        tan = tan_ref[...].astype(F32)
        d_down = norm_pull(normed, scale, tan * row(g2_ref))
        small_ref[0:1, :] = sum_rows(d_down)
        small_ref[3:4, :] = sum_rows(tan * normed)
        small_ref[4:5, :] = sum_rows(tan)
        gd_ref[...] = d_down.astype(BF)
        gdt_ref[...] = jnp.transpose(d_down).astype(BF)
        acc_ref[...] = d_down

    @pl.when(step >= steps)
    def _():
        at = step - steps
        d_up = nn(gd_ref[...], ud_ref[1, :, cols]) * slope_ref[at]
        gupb_ref[...] = sum_rows(d_up)
        g_up = d_up.astype(BF)
        acc_ref[...] += nt(g_up, ud_ref[0, :, cols])
        if not wired:
            gud_ref[0] = nn(fbt_ref[...], g_up).astype(BF)
            gud_ref[1] = nn(gdt_ref[...], act_ref[at]).astype(BF)
            return
        pl.when(at >= 2)(lambda: send_wait(at - 2))
        slot = lax.rem(at, 2)
        own_ref[slot, 0] = nn(fbt_ref[...], g_up).astype(BF)
        own_ref[slot, 1] = nn(gdt_ref[...], act_ref[at]).astype(BF)
        for j in range(4):
            pair_copy(at, j).start()
        pl.when(at >= 1)(lambda: join(at - 1))

    @pl.when(step == 2 * steps - 1)
    def _():
        d_first, normed = acc_ref[...], n1_ref[...]
        small_ref[1:2, :] = sum_rows(d_first * normed)
        small_ref[2:3, :] = sum_rows(d_first)
        d_mixed = norm_pull(normed, r1_ref[...], d_first * row(g1_ref))
        dmix_ref[...] = d_mixed
        gvec_ref[...] = nn(d_mixed.astype(BF), wo_ref[0]).astype(BF)
        gdt_ref[...] = jnp.transpose(d_mixed).astype(BF)
        go_ref[...] = nn(gdt_ref[...], vec_ref[...]).astype(BF)
        if wired:
            join(steps - 1)
            for c in (steps - 2, steps - 1):
                send_wait(c)
            for c in range(steps):
                keep_copy(c).wait()
                settle(near_ref.at[:, :, :, :, span(c)], move_recv.at[c])
                for i in range(4):
                    move(c, i).wait_send()


def feed(ud, wo, vec, x, tan, upb, vecs, wired):
    rows, width = vec.shape
    inner = upb.shape[0]
    chunk = 512
    steps = inner // chunk
    whole = lambda a, b: pl.BlockSpec((a, b), lambda i: (0, 0))
    late = lambda i: jnp.maximum(i - steps, 0)
    grads = pl.BlockSpec((2, width, chunk), lambda i: (0, 0, late(i)))
    grad_shape = (2, width, inner)
    params = dict(vmem_limit_bytes=LIMIT)
    scratch, near_shape = [], []
    if wired:
        mine = width // 8
        grads, grad_shape = ANY_SPEC, (2, 4, mine, inner)
        scratch = [
            pltpu.VMEM((2, 2, width, chunk), BF),
            pltpu.VMEM(grad_shape, BF),
            pltpu.VMEM((steps, 2, 4, mine, chunk), BF),
            pltpu.SemaphoreType.DMA((2, 4)),
            pltpu.SemaphoreType.DMA((steps,)),
            pltpu.SemaphoreType.DMA((steps,)),
            pltpu.SemaphoreType.DMA((steps, 4)),
            pltpu.SemaphoreType.DMA((steps,)),
        ]
        near_shape = [jax.ShapeDtypeStruct((2, 2, 2, mine // 2, inner), BF)]
        params.update(collective_id=6, has_side_effects=True)
    return pl.pallas_call(
        functools.partial(feed_kernel, steps, wired),
        grid=(2 * steps,),
        in_specs=[ANY_SPEC] * 2
        + [whole(rows, width)] * 3
        + [pl.BlockSpec((chunk,), lambda i: (lax.rem(i, steps),))]
        + [pl.BlockSpec((width,), lambda i: (0,))] * 5,
        out_specs=[
            whole(rows, width),
            whole(rows, width),
            whole(rows, width),
            whole(width, width),
            grads,
            pl.BlockSpec((1, chunk), lambda i: (0, late(i))),
            whole(8, width),
        ]
        + [ANY_SPEC] * len(near_shape),
        out_shape=[
            jax.ShapeDtypeStruct((rows, width), BF),
            jax.ShapeDtypeStruct((rows, width), F32),
            jax.ShapeDtypeStruct((rows, width), BF),
            jax.ShapeDtypeStruct((width, width), BF),
            jax.ShapeDtypeStruct(grad_shape, BF),
            jax.ShapeDtypeStruct((1, inner), F32),
            jax.ShapeDtypeStruct((8, width), F32),
        ]
        + near_shape,
        scratch_shapes=[
            pltpu.VMEM((2, width, inner), BF),
            pltpu.VMEM((1, width, width), BF),
            pltpu.VMEM((rows, width), F32),
            pltpu.VMEM((rows, 1), F32),
            pltpu.VMEM((rows, width), BF),
            pltpu.VMEM((width, rows), BF),
            pltpu.VMEM((rows, width), F32),
            pltpu.VMEM((steps, rows, chunk), BF),
            pltpu.VMEM((steps, rows, chunk), F32),
            pltpu.VMEM((rows, width), BF),
            pltpu.VMEM((width, rows), BF),
            pltpu.SemaphoreType.DMA((2,)),
        ]
        + scratch,
        compiler_params=pltpu.CompilerParams(**params),
        cost_estimate=pl.CostEstimate(
            flops=12 * rows * width * inner, bytes_accessed=36 << 20, transcendentals=rows * inner
        ),
        name="feed",
    )(ud, wo, vec, x, tan, upb, *vecs)


def project_step(
    w_ref,
    ctx_ref,
    q_ref,
    table_ref,
    wb_ref,
    pb_ref,
    k_ref,
    v_ref,
    rel_ref,
    qw_ref,
    qp_ref,
    x_ref,
    hooks=(),
):
    lead = lax.rem(lax.axis_index("dp"), 2) == 0
    flat = lambda ref: jnp.concatenate([ref[h : h + 1, :] for h in range(ref.shape[0])], axis=1)
    word_bias, pos_bias = flat(wb_ref), flat(pb_ref)
    klen, width = k_ref.shape
    back = klen - q_ref.shape[0]

    def context_rows(start):
        at = pl.ds(lax.div(start, 32), block // 32)
        return ctx_ref[at].reshape(block, width)

    block = 256

    def loop(count, step):
        def run(i, carry):
            step(pl.ds(pl.multiple_of(i * block, block), block))
            return carry

        lax.fori_loop(0, count // block, run, 0)

    def context_step(at):
        rows = context_rows(at.start)
        k_ref[at, :] = nn(rows, w_ref[0]).astype(BF)
        v_ref[at, :] = nn(rows, w_ref[1]).astype(BF)

    def stream_step(at):
        x_ref[at, :] = jnp.where(lead, context_rows(at.start + back), q_ref[at, :])
        proj = nn(x_ref[at, :], w_ref[2])
        qw_ref[at, :] = (0.125 * (proj + word_bias).astype(BF).astype(F32)).astype(BF)
        qp_ref[at, :] = (0.125 * (proj + pos_bias).astype(BF).astype(F32)).astype(BF)

    def table_step(at):
        rel_ref[at, :] = nn(table_ref[at, :], w_ref[3]).astype(BF)

    loop(table_ref.shape[0], table_step)
    if hooks:
        hooks[0]()
    loop(q_ref.shape[0], stream_step)
    if hooks:
        hooks[1]()
    loop(klen, context_step)


def project(mats, context, query, table, wb, pb):
    rows, width = query.shape
    klen, span = context.shape[0], table.shape[0]
    vmem = pl.BlockSpec(memory_space=pltpu.VMEM)
    return pl.pallas_call(
        project_step,
        in_specs=[vmem] * 6,
        out_specs=[vmem] * 6,
        out_shape=[
            jax.ShapeDtypeStruct((klen, width), BF),
            jax.ShapeDtypeStruct((klen, width), BF),
            jax.ShapeDtypeStruct((span, width), BF),
            jax.ShapeDtypeStruct((rows, width), BF),
            jax.ShapeDtypeStruct((rows, width), BF),
            jax.ShapeDtypeStruct((rows, width), BF),
        ],
        compiler_params=pltpu.CompilerParams(vmem_limit_bytes=LIMIT),
        cost_estimate=pl.CostEstimate(
            flops=2 * (2 * klen + rows + span) * width * width,
            bytes_accessed=20 << 20,
            transcendentals=0,
        ),
        name="project",
    )(mats, context.reshape(klen // 32, 2, 16, width), query, table, wb, pb)


def weight_grads_kernel(xt_ref, ct_ref, tt_ref, dp_ref, dk_ref, dv_ref, dr_ref, g_ref):
    g_ref[0] = nt(ct_ref[...], dk_ref[...]).astype(BF)
    g_ref[1] = nt(ct_ref[...], dv_ref[...]).astype(BF)
    g_ref[2] = nn(xt_ref[...], dp_ref[...]).astype(BF)
    g_ref[3] = nt(tt_ref[...], dr_ref[...]).astype(BF)


def weight_grads(x_t, ctx_t, table_t, d_proj, dk_t, dv_t, drel_t):
    width, rows = x_t.shape
    klen, span = ctx_t.shape[1], table_t.shape[1]
    chunk = 256
    whole = lambda a, b: pl.BlockSpec((a, b), lambda i: (0, 0))
    rowb = lambda b: pl.BlockSpec((chunk, b), lambda i: (i, 0))
    return pl.pallas_call(
        weight_grads_kernel,
        grid=(width // chunk,),
        in_specs=[
            whole(width, rows),
            whole(width, klen),
            whole(width, span),
            pl.BlockSpec((rows, chunk), lambda i: (0, i)),
            rowb(klen),
            rowb(klen),
            rowb(span),
        ],
        out_specs=pl.BlockSpec((4, width, chunk), lambda i: (0, 0, i)),
        out_shape=jax.ShapeDtypeStruct((4, width, width), BF),
        compiler_params=pltpu.CompilerParams(vmem_limit_bytes=LIMIT),
        cost_estimate=pl.CostEstimate(
            flops=2 * (rows + 2 * klen + span) * width * width,
            bytes_accessed=20 << 20,
            transcendentals=0,
        ),
        name="weight_grads",
    )(x_t, ctx_t, table_t, d_proj, dk_t, dv_t, drel_t)


def flip(arr, bit):
    return lax.ppermute(arr, "dp", [(i, i ^ bit) for i in range(lax.axis_size("dp"))])


def scatter_sum(grads):
    mine = lax.psum_scatter(grads, "dp", scatter_dimension=1, tiled=True)
    return lax.psum_scatter(mine, "tensor", scatter_dimension=2, tiled=True).astype(F32)


def body(
    content_stream,
    query_stream,
    memory,
    content_tangent,
    query_tangent,
    seq_lengths,
    factor_order,
    memory_lengths,
    slot_sequence,
    query_weight,
    key_weight,
    value_weight,
    pos_weight,
    out_weight,
    up_weight,
    up_bias,
    down_weight,
    down_bias,
    word_bias,
    pos_bias,
    first_gain,
    first_shift,
    second_gain,
    second_shift,
):
    groups, tensors = lax.axis_size("dp"), lax.axis_size("tensor")
    micro, part_len, width = content_stream.shape
    mem_part = memory.shape[1]
    seq_len, mem_total = part_len * tensors, mem_part * tensors
    klen, span = mem_total + seq_len, mem_total + 2 * seq_len
    count = micro * groups
    here, lane = lax.axis_index("dp"), lax.axis_index("tensor")
    core = here % 2
    lead = core == 0
    block = 256
    assert 2 * micro == tensors

    def swap(arr):
        return flip(arr, CORE)

    def to_unit(first, second):
        got = swap(jnp.where(lead, second, first))
        low = jnp.where(lead, first, got)
        high = jnp.where(lead, got, second)
        both = jnp.concatenate([low, high], 0)
        both = lax.all_to_all(both, "tensor", split_axis=0, concat_axis=0, tiled=True)
        return both.reshape(seq_len, width)

    def from_unit(arr):
        both = arr.reshape(tensors, part_len, width)
        both = lax.all_to_all(both, "tensor", split_axis=0, concat_axis=0, tiled=True)
        low, high = both[:micro], both[micro:]
        got = swap(jnp.where(lead, high, low))
        return jnp.where(lead, low, got), jnp.where(lead, got, high)

    seq_id = (here // 2) * tensors + lane
    mats = [key_weight, value_weight, query_weight, pos_weight, out_weight]
    table = jnp.asarray(reversed_table(span, klen, width))
    wires = ()
    if groups == 8:
        keys, values, rel, q_word, q_pos, stream, thr, key_rank, weights, context, *wires = enter(
            slot_sequence,
            seq_lengths,
            memory_lengths,
            content_stream,
            query_stream,
            memory,
            table,
            factor_order,
            mats,
            up_weight,
            down_weight,
            word_bias,
            pos_bias,
        )
        wires += [content_tangent, query_tangent]
        context = context.reshape(klen, width)
    else:
        ids = jnp.arange(count, dtype=jnp.int32)
        slot_of = jnp.sum(jnp.where(slot_sequence[None, :] == ids[:, None], ids[None, :], 0), axis=1)
        counts = jnp.concatenate([seq_lengths, memory_lengths])
        slot = slot_of[seq_id]
        lengths = lax.all_gather(counts, "dp", axis=0, tiled=False)
        orders = lax.all_gather(factor_order, "dp", axis=0, tiled=False)[seq_id // micro]
        stream = to_unit(content_stream, query_stream)
        content, query = jnp.where(lead, stream, swap(stream)), stream
        tangent = to_unit(content_tangent, query_tangent)
        piece = mem_part // groups
        spread = lax.all_to_all(
            memory.reshape(micro, groups, piece, width), "dp", split_axis=1, concat_axis=1, tiled=True
        )
        spread = spread.transpose(1, 0, 2, 3).reshape(count, piece, width)
        spread = jnp.take(spread, slot_of, axis=0)
        spread = spread.reshape(groups // 2, tensors, 2, piece // 2, width).transpose(0, 2, 1, 3, 4)
        spread = lax.all_to_all(
            spread.reshape(groups, tensors, piece // 2, width),
            "dp",
            split_axis=0,
            concat_axis=0,
            tiled=True,
        )
        spread = lax.all_to_all(spread, "tensor", split_axis=1, concat_axis=1, tiled=True)
        got = swap(spread)
        mem_rows = jnp.stack([jnp.where(lead, spread, got), jnp.where(lead, got, spread)])
        mem_rows = mem_rows.transpose(2, 1, 0, 3, 4).reshape(mem_total, width)
        context = jnp.concatenate([mem_rows, content], 0)

        def whole(mat):
            mat = lax.all_gather(mat, "tensor", axis=1, tiled=True)
            return lax.all_gather(mat, "dp", axis=0, tiled=True)

        weights = jnp.stack([whole(mat) for mat in mats[:4]])
        wo = whole(out_weight)[None]
        ud = jnp.stack([whole(up_weight), whole(down_weight)])
        keys, values, rel, q_word, q_pos, stream = project(
            weights, context, query, table, word_bias, pos_bias
        )
        length = lengths[seq_id // micro, seq_id % micro]
        mem_valid = lengths[slot // micro, micro + slot % micro]
        rank = orders[seq_id % micro]
        key_pos = jnp.arange(klen, dtype=jnp.int32)
        hidden = jnp.int32(1 << 20)
        mem_rank = jnp.where(key_pos[:mem_total] >= mem_total - mem_valid, -1, hidden)
        own_rank = jnp.where(key_pos[:seq_len] < length, rank, hidden)
        key_rank = jnp.concatenate([mem_rank, own_rank])[None, :]
        thr = (rank + jnp.where(lead, 1, 0))[:, None]

    vec, prob, *arrived = attend_forward(
        q_word, q_pos, keys, values, rel, thr, key_rank, block, wires
    )
    if wires:
        wo, ud, tangent = arrived
    out, d_mixed, g_vec, g_out, g_ud, g_upb, small, *near = feed(
        ud,
        wo,
        vec,
        stream,
        tangent,
        up_bias,
        (down_bias, first_gain, first_shift, second_gain, second_shift),
        groups == 8,
    )
    backward = (prob, g_vec, q_word, q_pos, keys, values, rel, block)
    if groups == 8:
        d_proj, dk_t, dv_t, drel_t, biases, grad_up, grad_down, grad_out, content_out, query_out = (
            attend_backward(*backward, (g_ud, *near, g_out[None], out))
        )
    else:
        d_proj, dk_t, dv_t, drel_t, biases = attend_backward(*backward)
        content_out, query_out = from_unit(out)
        grad_up, grad_down = scatter_sum(g_ud)
    small = jnp.concatenate([g_upb.reshape(-1), small[:5].reshape(-1), biases.reshape(-1)])
    inner = up_bias.shape[0]
    table_t = jnp.asarray(np.ascontiguousarray(reversed_table(span, klen, width).T))
    if groups == 8:
        small = jnp.pad(small, (0, -small.shape[0] % 1024)).reshape(-1, 128)
        arrays = [stream, d_proj, context, dk_t, dv_t, weights, table_t, drel_t]
        (
            grad_key,
            grad_value,
            grad_query,
            grad_pos,
            content_grad,
            query_grad,
            small,
        ) = finish(arrays, d_mixed, small)
        arrays = [content_out, query_out, content_grad, query_grad, grad_query, grad_key]
        arrays += [grad_value, grad_pos, grad_out, grad_up, grad_down]
        *arrays, up_sum, down_sum, a1, b1, a2, b2, word_sum, pos_sum = emit(
            small, arrays, inner, width
        )
        return *arrays[:10], up_sum, arrays[10], down_sum, word_sum, pos_sum, a1, b1, a2, b2
    else:
        d_context = tt(dk_t[:, mem_total:], weights[0]) + tt(dv_t[:, mem_total:], weights[1])
        partner = swap(d_context.astype(BF)).astype(F32)
        d_stream = d_mixed + nt(d_proj, weights[2]) + jnp.where(lead, d_context + partner, 0.0)
        content_grad, query_grad = from_unit(d_stream.astype(BF))
        grad_key, grad_value, grad_query, grad_pos = scatter_sum(
            weight_grads(jnp.transpose(stream), jnp.transpose(context), table_t, d_proj, dk_t, dv_t, drel_t)
        )
        (grad_out,) = scatter_sum(g_out[None])
        small = lax.psum(small, ("dp", "tensor"))
    rest = small[inner:].reshape(7, width)
    return (
        content_out,
        query_out,
        content_grad,
        query_grad,
        grad_query,
        grad_key,
        grad_value,
        grad_pos,
        grad_out,
        grad_up,
        small[:inner],
        grad_down,
        rest[0],
        rest[5].reshape(HEADS, DH),
        rest[6].reshape(HEADS, DH),
        rest[1],
        rest[2],
        rest[3],
        rest[4],
    )


def solution(mesh):
    rows = P("dp", "tensor", None)
    mat = P("dp", "tensor")
    return jax.shard_map(
        body,
        mesh=mesh,
        in_specs=(rows,) * 5
        + (P("dp"), P("dp", None), P("dp"), P())
        + (mat,) * 6
        + (P(), mat)
        + (P(),) * 7,
        out_specs=(rows,) * 4 + (mat,) * 6 + (P(), mat) + (P(),) * 7,
        check_vma=False,
    )
```

```python
import functools

import jax
import jax.numpy as jnp
import numpy as np
from jax import lax
from jax.experimental import pallas as pl
from jax.experimental.pallas import tpu as pltpu
from jax.sharding import PartitionSpec as P

HEADS = 12
DH = 64
PAIR = 2 * DH
EPS = 1e-06
BF = jnp.bfloat16
F32 = jnp.float32
LIMIT = 60 * 1024 * 1024
SMEM_SPEC = pl.BlockSpec(memory_space=pltpu.SMEM)
ANY_SPEC = pl.BlockSpec(memory_space=pl.ANY)


def nn(left, right):
    return jnp.dot(left, right, preferred_element_type=F32)


def nt(left, right):
    return lax.dot_general(left, right, (((1,), (1,)), ((), ())), preferred_element_type=F32)


def tn(left, right):
    return lax.dot_general(left, right, (((0,), (0,)), ((), ())), preferred_element_type=F32)


def tt(left, right):
    return lax.dot_general(left, right, (((0,), (1,)), ((), ())), preferred_element_type=F32)


def reversed_table(count, first, width):
    dist = (first - np.arange(count)).astype(np.float32)
    half = width // 2
    power = np.arange(half).astype(np.float32) * np.float32(2.0 / width)
    freq = np.float32(1.0) / np.float32(10000.0) ** power
    angle = (dist[:, None] * freq[None, :]).astype(np.float64)
    return np.concatenate([np.sin(angle), np.cos(angle)], axis=1).astype(np.float32).astype(BF)


MESH = pl.DeviceIdType.MESH
CORE, XBIT, YBIT = 1, 2, 4


class Place:
    def __init__(self):
        self.d, self.z = lax.axis_index("dp"), lax.axis_index("tensor")
        self.core = lax.rem(self.d, 2)
        self.x = lax.rem(lax.div(self.d, 2), 2)
        self.y = lax.div(self.d, 4)

    def dp(self, bits):
        at = self.d
        if bits & CORE:
            at = at + (1 - 2 * self.core)
        if bits & XBIT:
            at = at + (2 - 4 * self.x)
        if bits & YBIT:
            at = at + (4 - 8 * self.y)
        return at

    def up(self, step):
        return lax.rem(self.z + step, 4) if step else self.z


def push(src, dst, send, recv, dp, z):
    return pltpu.make_async_remote_copy(
        src_ref=src,
        dst_ref=dst,
        send_sem=send,
        recv_sem=recv,
        device_id=(dp, z),
        device_id_type=MESH,
    )


def settle(ref, sem):
    pltpu.make_async_copy(ref, ref, sem).wait()


def greet(partners):
    barrier = pltpu.get_barrier_semaphore()
    for partner in partners:
        pl.semaphore_signal(barrier, inc=1, device_id=partner, device_id_type=MESH)
    pl.semaphore_wait(barrier, len(partners))


GATHER = (
    (0, 0, XBIT),
    (0, 1, YBIT),
    (0, 0, YBIT),
    (0, 1, XBIT),
    (XBIT, 0, YBIT),
    (YBIT, 1, XBIT),
    (0, 0, CORE),
    (0, 1, CORE),
    (XBIT, 0, CORE),
    (YBIT, 1, CORE),
    (YBIT, 0, CORE),
    (XBIT, 1, CORE),
    (XBIT | YBIT, 0, CORE),
    (XBIT | YBIT, 1, CORE),
)


class Gather:
    def __init__(self, place, dst, own, send, recv):
        self.place, self.dst, self.own = place, dst, own
        self.send, self.recv = send, recv
        self.half = dst.shape[1] // 16

    def region(self, owner, half):
        at = self.place.dp(owner) * (2 * self.half) + half * self.half
        return self.dst.at[:, pl.ds(pl.multiple_of(at, 16), self.half), :]

    def copy(self, i):
        owner, half, to = GATHER[i]
        src = self.region(owner, half)
        if owner == 0 and self.own is not None:
            src = self.own.at[:, half * self.half : (half + 1) * self.half, :]
        place = self.place
        return push(
            src, self.region(owner, half), self.send.at[i], self.recv.at[i], place.dp(to), place.z
        )

    def start(self, *which):
        for i in which:
            self.copy(i).start()

    def wait(self, received, sent):
        for i in received:
            self.copy(i).wait_recv()
        for i in sent:
            self.copy(i).wait_send()

    def after(self, arrived, started):
        for i, more in zip(arrived, started):
            self.copy(i).wait_recv()
            for j in more:
                self.copy(j).start()

    def middle(self):
        self.after((0, 1), ((4, 8), (5, 9)))

    def last(self):
        self.after((2, 3, 4, 5), ((10,), (11,), (12,), (13,)))


def chip_bits(j):
    return (XBIT if j & 1 else 0) | (YBIT if j & 2 else 0)


def add_into(dst, src):
    def run(i, carry):
        at = pl.ds(pl.multiple_of(i * 16, 16), 16)
        dst[:, at, :] = (dst[:, at, :].astype(F32) + src[:, at, :].astype(F32)).astype(BF)
        return carry

    lax.fori_loop(0, dst.shape[1] // 16, run, 0)


class Reduce:
    def __init__(self, place, sources, scratch, out, paired=False):
        self.place, self.sources, self.out, self.paired = place, sources, out, paired
        self.total, self.pair, self.near, self.far, self.quarter, self.stage = scratch[:6]
        self.pair_send, self.pair_recv, self.load, self.send, self.recv, self.z_send, self.z_recv = scratch[6:]
        self.rows = self.total.shape[2]

    @staticmethod
    def scratch(count, n, rows, cols, paired=False):
        part = cols // 4
        dma = lambda k: pltpu.SemaphoreType.DMA((k,))
        return [
            pltpu.VMEM((n, 4, rows, cols), BF),
            pltpu.VMEM((8, 128) if paired else (n, 4, rows, cols), BF),
            pltpu.VMEM((n, 2, 2, rows // 2, cols), BF),
            pltpu.VMEM((n, 2, rows // 2, cols), BF),
            pltpu.VMEM((4, n, rows, part), BF),
            pltpu.VMEM((4, n, rows, part) if part % 128 else (8, 128), BF),
            dma(4 * count),
            dma(4 * count),
            dma(4 * count),
            dma(6),
            dma(6),
            dma(3),
            dma(1),
        ]

    def pair_copies(self, j):
        place, rows = self.place, self.rows
        copies, at = [], 0
        for i, src in enumerate(self.sources):
            slot, n = len(self.sources) * j + i, src.shape[0]
            block = lambda bits: src.at[:, pl.ds(pl.multiple_of(place.dp(bits) * rows, 16), rows), :]
            remote = push(
                block(chip_bits(j) | CORE),
                self.pair.at[at : at + n, j],
                self.pair_send.at[slot],
                self.pair_recv.at[slot],
                place.dp(CORE),
                place.z,
            )
            local = pltpu.make_async_copy(
                block(chip_bits(j)), self.total.at[at : at + n, j], self.load.at[slot]
            )
            copies.append((remote, local))
            at += n
        return copies

    def half(self, j, h):
        size = self.rows // 2
        return self.total.at[:, j, h * size : (h + 1) * size, :]

    MOVES = ((3, 0, XBIT, 1), (3, 1, YBIT, 1), (1, 0, XBIT, 0), (2, 1, YBIT, 0), (2, 0, YBIT, 0), (1, 1, XBIT, 1))

    def move(self, i):
        j, h, to, where = self.MOVES[i]
        dst = self.near.at[:, h, where] if i < 4 else self.far.at[:, where]
        place = self.place
        return push(self.half(j, h), dst, self.send.at[i], self.recv.at[i], place.dp(to), place.z)

    def z_copy(self, k):
        place, part = self.place, self.quarter.shape[3]
        to = place.up(k)
        if part % 128:
            src = self.stage.at[to]
        else:
            src = self.total.at[:, 0, :, pl.ds(pl.multiple_of(to * part, 128), part)]
        dst = self.quarter.at[place.z]
        if k == 0:
            return pltpu.make_async_copy(src, dst, self.z_recv.at[0])
        return push(src, dst, self.z_send.at[k - 1], self.z_recv.at[0], place.d, to)

    def loaded(self, j):
        src, near = self.sources
        if j == 3:
            return pltpu.make_async_copy(near, self.near, self.load.at[3])
        return pltpu.make_async_copy(src.at[:, j], self.total.at[:, j], self.load.at[j])

    def begin(self):
        for j in (3, 1, 2, 0):
            if self.paired:
                self.loaded(j).start()
                continue
            for remote, local in self.pair_copies(j):
                remote.start()
                local.start()

    def pairs(self):
        for j, moves in ((3, (0, 1)), (1, (2,)), (2, (3,)), (0, ())):
            for remote, local in self.pair_copies(j):
                local.wait()
                remote.wait_recv()
            add_into(self.total.at[:, j], self.pair.at[:, j])
            for i in moves:
                self.move(i).start()

    def middle(self):
        for i, j, h, where, more in ((0, 2, 0, 1, 4), (1, 1, 1, 1, 5), (2, 0, 0, 0, None), (3, 0, 1, 0, None)):
            if not self.paired:
                self.move(i).wait_recv()
            elif i == 0:
                for k in range(4):
                    self.loaded(k).wait()
            add_into(self.half(j, h), self.near.at[:, h, where])
            if more is not None:
                self.move(more).start()

    def late(self):
        for i, h in ((4, 0), (5, 1)):
            self.move(i).wait_recv()
            add_into(self.half(0, h), self.far.at[:, h])
        part = self.quarter.shape[3]
        if part % 128:
            for k in range(4):
                for m in range(self.total.shape[0]):
                    self.stage[k, m] = self.total[m, 0, :, k * part : (k + 1) * part]
        for k in (2, 1, 3, 0):
            self.z_copy(k).start()

    def end(self):
        settle(self.quarter, self.z_recv.at[0])
        parts = [self.quarter[k].astype(F32) for k in range(4)]
        total = (parts[0] + parts[1]) + (parts[2] + parts[3])
        self.out[...] = total.reshape(self.out.shape)
        if not self.paired:
            for j in range(4):
                for remote, _ in self.pair_copies(j):
                    remote.wait_send()
        for i in range(4 if self.paired else 0, 6):
            self.move(i).wait_send()
        for k in range(1, 4):
            self.z_copy(k).wait_send()


class Homeward:
    def __init__(self, place, src, homes, send, recv):
        self.place, self.src, self.homes, self.send, self.recv = place, src, homes, send, recv
        self.part = homes[0].shape[1]

    def act(self, what):
        place, part = self.place, self.part
        for u in range(2):

            @pl.when(place.core == u)
            def _():
                for k in (2, 1, 3, 0):
                    to, dp = place.up(k), place.d - place.core + lax.div(place.z, 2)
                    src = self.src.at[pl.ds(pl.multiple_of(to * part, 16), part), :]
                    dst = self.homes[u].at[lax.rem(place.z, 2)]
                    recv = self.recv.at[u]
                    here = jnp.logical_and(dp == place.d, to == place.z)
                    remote = push(src, dst, self.send.at[k], recv, dp, to)
                    if what == "start":
                        pl.when(here)(pltpu.make_async_copy(src, dst, recv).start)
                        pl.when(jnp.logical_not(here))(remote.start)
                    else:
                        pl.when(jnp.logical_not(here))(remote.wait_send)

    def start(self):
        self.act("start")

    def end(self):
        for u in range(2):
            settle(self.homes[u], self.recv.at[u])
        self.act("wait")


def pair_and_z(place):
    return [(place.dp(r), place.up(k)) for k in range(4) for r in (0, CORE) if r or k]


def near_partners(place):
    return pair_and_z(place) + [(place.dp(r), place.z) for r in (XBIT, YBIT)]


INPUTS = 8


def finish_kernel(*refs):
    hbm, (mixed_ref, small_ref) = refs[:INPUTS], refs[INPUTS : INPUTS + 2]
    grad_refs, home_refs, sums_ref = refs[INPUTS + 2 : INPUTS + 6], refs[INPUTS + 6 : INPUTS + 8], refs[INPUTS + 8]
    refs = refs[INPUTS + 9 :]
    held, refs = refs[:INPUTS], refs[INPUTS:]
    loads, x_t, ctx_t, g_ref, base, ctx, partner, stream, slots, part_sum, chips = refs[:11]
    home_send, slot_send, chip_send, one_send, recv = refs[11:16]
    refs = refs[16:]
    count = len(refs) // 4
    place = Place()
    d, z, core = place.d, place.z, place.core
    copies = [
        pltpu.make_async_copy(a.at[0:3] if i == 5 else a, b, loads.at[i])
        for i, (a, b) in enumerate(zip(hbm, held))
    ]
    for copy in copies:
        copy.start()

    def need(*which):
        for i in which:
            copies[i].wait()
        return [held[i] for i in which]

    greet(near_partners(place) + [(place.dp(XBIT | YBIT), z)])
    sources = [g_ref.at[m : m + 1] for m in range(4)]
    key, value, query, pos = [
        Reduce(place, (src,), refs[m * count : (m + 1) * count], grad_refs[m])
        for m, src in enumerate(sources)
    ]
    slot_copies = []
    others = [(r, k) for k in range(4) for r in (0, CORE) if r or k]
    for i, (r, k) in enumerate(others):
        copy = push(small_ref, slots.at[4 * core + z], slot_send.at[i], recv.at[1], place.dp(r), place.up(k))
        copy.start()
        slot_copies.append(copy)
    pltpu.make_async_copy(small_ref, slots.at[4 * core + z], recv.at[1]).start()

    width, block = g_ref.shape[1], 256

    def product(m, left, right, dot):
        def run(i, carry):
            at = pl.ds(pl.multiple_of(i * block, block), block)
            g_ref[m, at, :] = dot(left[at, :], right[...]).astype(BF)
            return carry

        lax.fori_loop(0, width // block, run, 0)

    def turn(src, dst):
        def run(i, carry):
            at = pl.ds(pl.multiple_of(i * block, block), block)
            dst[:, at] = jnp.transpose(src[at, :].astype(F32)).astype(BF)
            return carry

        lax.fori_loop(0, src.shape[0] // block, run, 0)

    x_ref, d_proj = need(0, 1)
    turn(x_ref, x_t)
    product(2, x_t, d_proj, nn)
    query.begin()
    ctx_ref, dk_t = need(2, 3)
    turn(ctx_ref, ctx_t)
    product(0, ctx_t, dk_t, nt)
    key.begin()

    dv_t, mats = need(4, 5)
    back = dk_t.shape[1] - base.shape[0]

    def from_context(i, carry):
        at = pl.ds(pl.multiple_of(i * block, block), block)
        cols = pl.ds(pl.multiple_of(i * block + back, block), block)
        turned = nn(mats[0], dk_t[:, cols]) + nn(mats[1], dv_t[:, cols])
        turned = jnp.transpose(turned)
        base[at, :] = turned
        ctx[at, :] = turned.astype(BF)
        return carry

    lax.fori_loop(0, base.shape[0] // block, from_context, 0)
    swap = push(ctx, partner, one_send.at[0], recv.at[0], place.dp(CORE), z)
    swap.start()

    def from_proj(i, carry):
        at = pl.ds(pl.multiple_of(i * block, block), block)
        own = mixed_ref[at, :] + nt(d_proj[at, :], mats[2])
        base[at, :] = own + jnp.where(core == 0, base[at, :], 0.0)
        return carry

    lax.fori_loop(0, base.shape[0] // block, from_proj, 0)
    query.pairs()
    product(1, ctx_t, dv_t, nt)
    value.begin()
    key.pairs()

    swap.wait()
    small_block = 64

    def add_partner(i, carry):
        at = pl.ds(pl.multiple_of(i * small_block, small_block), small_block)
        more = jnp.where(core == 0, partner[at, :].astype(F32), 0.0)
        stream[at, :] = (base[at, :] + more).astype(BF)
        return carry

    lax.fori_loop(0, stream.shape[0] // small_block, add_partner, 0)
    home = Homeward(place, stream, home_refs, home_send, recv.at[2:4])
    home.start()

    table_t, dr_t = need(6, 7)
    product(3, table_t, dr_t, nt)
    pos.begin()
    value.pairs()
    query.middle()

    settle(slots, recv.at[1])
    total = slots[0]
    for i in range(1, 8):
        total = total + slots[i]
    part_sum[...] = total
    chip = lax.div(d, 2)
    chip_copies = []
    for i, r in enumerate((XBIT, YBIT, XBIT | YBIT)):
        copy = push(part_sum, chips.at[chip], chip_send.at[i], recv.at[4], place.dp(r), z)
        copy.start()
        chip_copies.append(copy)
    pltpu.make_async_copy(part_sum, chips.at[chip], recv.at[4]).start()

    pos.pairs()
    key.middle()
    query.late()
    value.middle()
    key.late()
    pos.middle()
    value.late()
    settle(chips, recv.at[4])
    sums_ref[...] = (chips[0] + chips[1]) + (chips[2] + chips[3])
    pos.late()
    for reduce in (query, key, value, pos):
        reduce.end()
    home.end()
    for copy in slot_copies + chip_copies:
        copy.wait_send()


def finish(arrays, mixed, small):
    total, width = arrays[0].shape
    klen = arrays[2].shape[0]
    rows = width // 8
    vmem = pl.BlockSpec(memory_space=pltpu.VMEM)
    dma = lambda k: pltpu.SemaphoreType.DMA((k,))
    scratch = [pltpu.VMEM((3,) + a.shape[1:] if a.ndim == 3 else a.shape, BF) for a in arrays]
    scratch += [
        dma(INPUTS),
        pltpu.VMEM((width, total), BF),
        pltpu.VMEM((width, klen), BF),
        pltpu.VMEM((4, width, width), BF),
        pltpu.VMEM((total, width), F32),
        pltpu.VMEM((total, width), BF),
        pltpu.VMEM((total, width), BF),
        pltpu.VMEM((total, width), BF),
        pltpu.VMEM((8,) + small.shape, F32),
        pltpu.VMEM(small.shape, F32),
        pltpu.VMEM((4,) + small.shape, F32),
        dma(4),
        dma(7),
        dma(3),
        dma(1),
        dma(5),
    ]
    for _ in range(4):
        scratch += Reduce.scratch(1, 1, rows, width)
    return pl.pallas_call(
        finish_kernel,
        in_specs=[ANY_SPEC] * INPUTS + [vmem] * 2,
        out_specs=[vmem] * 4 + [ANY_SPEC] * 2 + [vmem],
        out_shape=[jax.ShapeDtypeStruct((rows, width // 4), F32)] * 4
        + [jax.ShapeDtypeStruct((2, total // 4, width), BF)] * 2
        + [
            jax.ShapeDtypeStruct(small.shape, F32),
        ],
        scratch_shapes=scratch,
        compiler_params=pltpu.CompilerParams(
            collective_id=4, has_side_effects=True, vmem_limit_bytes=LIMIT
        ),
        cost_estimate=pl.CostEstimate(flops=20 << 30, bytes_accessed=64 << 20, transcendentals=0),
        name="finish",
    )(*arrays, mixed, small)


def emit_kernel(small_ref, *refs):
    count = 11
    for src, dst in zip(refs[:count], refs[count : 2 * count]):
        dst[...] = src[...]
    wide, *rows, word_ref, pos_ref = refs[2 * count :]
    lanes = small_ref.shape[1]
    size = wide.shape[0] // lanes
    wide[...] = small_ref[0:size, :].reshape(wide.shape)
    for ref in rows:
        step = ref.shape[0] // lanes
        ref[...] = small_ref[size : size + step, :].reshape(ref.shape)
        size += step
    for ref in (word_ref, pos_ref):
        for h in range(HEADS):
            at = size + h * DH // lanes
            ref[h : h + 1, :] = small_ref[at : at + 1, h * DH % lanes : h * DH % lanes + DH]
        size += HEADS * DH // lanes


def emit(small, arrays, inner, width):
    vmem = pl.BlockSpec(memory_space=pltpu.VMEM)
    out_shape = [jax.ShapeDtypeStruct(a.shape, a.dtype) for a in arrays]
    out_shape += [jax.ShapeDtypeStruct((inner,), F32)]
    out_shape += [jax.ShapeDtypeStruct((width,), F32)] * 5
    out_shape += [jax.ShapeDtypeStruct((HEADS, DH), F32)] * 2
    return pl.pallas_call(
        emit_kernel,
        in_specs=[vmem] * (1 + len(arrays)),
        out_specs=[vmem] * len(out_shape),
        out_shape=out_shape,
        compiler_params=pltpu.CompilerParams(vmem_limit_bytes=LIMIT),
        name="emit",
    )(small, *arrays)


def pack(mat):
    half = mat.shape[0] // 2
    return jnp.concatenate([mat[:, :128], jnp.concatenate([mat[:half, 128:], mat[half:, 128:]], axis=1)], axis=0)


def unpack(packed):
    rows = packed.shape[0] * 2 // 3
    rest = packed[rows:, :]
    return jnp.concatenate([packed[:rows, :], jnp.concatenate([rest[:, :64], rest[:, 64:]], axis=0)], axis=1)


def enter_kernel(slot_ref, seq_ref, mem_ref, content, query, memory, table_hbm, orders, *refs):
    mats, (upw, dnw), (wb_ref, pb_ref) = refs[:5], refs[5:7], refs[7:9]
    outs, (thr_ref, key_ref, whole_out, context_out, wo, ud) = refs[9:15], refs[15:21]
    (
        ints,
        all_ints,
        whole,
        context,
        stream,
        table,
        spread,
        picked,
        shards,
        slab,
        mat_send,
        mat_recv,
        ud_send,
        ud_recv,
        int_send,
        spread_send,
        pick_send,
        stream_send,
        pair_send,
        gather_send,
        gather_recv,
        wo_send,
        wo_recv,
        far_send,
        far_recv,
        recv,
        local,
    ) = refs[21:]
    place = Place()
    d, z, core = place.d, place.z, place.core
    up, down, far = place.up(1), place.up(3), place.up(2)
    part = query.shape[1]
    micro = orders.shape[0]
    spot = lax.broadcasted_iota(jnp.int32, (1, ints.shape[1]), 1)
    lengths = jnp.where(spot == 0, seq_ref[0], seq_ref[1])
    lengths = jnp.where(spot < 2, lengths, jnp.where(spot == 2, mem_ref[0], mem_ref[1]))
    ints[...] = jnp.concatenate([orders[...], jnp.broadcast_to(lengths, (6, ints.shape[1]))], axis=0)

    def slot_of(seq):
        at = jnp.int32(0)
        for k in range(16):
            at = at + jnp.where(slot_ref[k] == seq, k, 0)
        return jnp.minimum(at, 15)

    pltpu.make_async_copy(table_hbm, table, local.at[0]).start()
    piece = spread.shape[1]
    blocks = part // piece // 2
    first = 4 * blocks
    greet([(place.dp(r), place.up(k)) for r in range(8) for k in range(4) if r or k])

    spread_copies = []
    for r in range(8):
        to = place.dp(r)
        src = memory.at[:, pl.ds(pl.multiple_of(to * piece, 16), piece), :]
        dst = spread.at[pl.ds(2 * d, 2)]
        if r == 0:
            pltpu.make_async_copy(src, dst, recv.at[0]).start()
        else:
            spread_copies.append(push(src, dst, spread_send.at[r - 1], recv.at[0], to, z))
            spread_copies[-1].start()

    for m, mat in enumerate(mats):
        shards[z, m] = pack(mat[...])
    cutoff = shards.shape[2] * 5 // 9

    def mat_copy(i):
        own = shards.at[z]
        low, high = shards.at[down, :, :cutoff], shards.at[up, :, cutoff:]
        src = (own, own, low, high)[i]
        return push(src, src, mat_send.at[i], mat_recv.at[i], d, (up, down, up, down)[i])

    mat_copy(0).start()
    mat_copy(1).start()
    rows = slab.shape[1]
    width = upw.shape[1]

    def columns(at, start=0, size=rows):
        mine = pl.ds(pl.multiple_of(d * rows + start, 16), size)
        return ud.at[:, mine, pl.ds(pl.multiple_of(at * width, 128), width)]

    def ud_copy(i):
        if i < 4:
            src, dst = (upw, dnw)[i % 2], columns(z).at[i % 2]
            return push(src, dst, ud_send.at[i], ud_recv.at[i // 2], d, (up, down)[i // 2])
        half = rows // 2
        src = columns(down, 0, half) if i == 4 else columns(up, half, half)
        return push(src, src, ud_send.at[i], ud_recv.at[i - 2], d, (up, down)[i - 4])

    for m, mat in enumerate((upw, dnw)):
        pltpu.make_async_copy(mat, columns(z).at[m], recv.at[8]).start()

    int_copies = []
    for r in range(8):
        if r == 0:
            pltpu.make_async_copy(ints, all_ints.at[d], recv.at[2]).start()
        else:
            copy = push(ints, all_ints.at[d], int_send.at[r - 1], recv.at[2], place.dp(r), z)
            int_copies.append(copy)
            copy.start()

    def stream_copy(i, act):
        j, kind = i // 2, i % 2
        to, dp = 2 * core + j, d - core + kind
        if kind == 0:
            src, sem = content.at[j], recv.at[3]
            dst = context.at[pl.ds(first + blocks * z, blocks)]
        else:
            src, sem = query.at[j], recv.at[4]
            dst = stream.at[pl.ds(pl.multiple_of(z * part, 16), part), :]
        here = jnp.logical_and(dp == d, to == z)
        remote = push(src, dst, stream_send.at[i], sem, dp, to)
        if act == "start":
            pl.when(here)(pltpu.make_async_copy(src, dst, sem).start)
            pl.when(jnp.logical_not(here))(remote.start)
        else:
            pl.when(jnp.logical_not(here))(remote.wait_send)

    mat_copy(0).wait_recv()
    mat_copy(2).start()
    mat_copy(1).wait_recv()
    mat_copy(3).start()
    for i in range(4):
        stream_copy(i, "start")

    mat_copy(2).wait_recv()
    mat_copy(3).wait_recv()
    for m in range(5):
        slab[m] = jnp.concatenate([unpack(shards[k, m]) for k in range(4)], axis=1)
    own_rows = pl.ds(pl.multiple_of(d * rows, 16), rows)
    gather = Gather(place, whole, slab.at[0:4], gather_send, gather_recv)
    gather.start(0, 1, 2, 3, 6, 7)
    pltpu.make_async_copy(slab.at[0:4], whole.at[:, own_rows, :], recv.at[6]).start()
    pltpu.make_async_copy(slab.at[4:5], wo.at[:, own_rows, :], recv.at[7]).start()

    settle(spread, recv.at[0])
    for q in range(16):
        picked[q] = spread[slot_of(q)]
    pick_copies = []
    for r in (YBIT | XBIT, XBIT, YBIT, 0):
        for k in range(4):
            to, lane = place.dp(r), place.up(k)
            src = picked.at[4 * lax.div(to, 2) + lane]
            dst = context.at[blocks * z + lax.div(d, 2), core]
            if r or k:
                copy = push(src, dst, pick_send.at[2 * r + k - 1], recv.at[5], to, lane)
                pick_copies.append(copy)
            else:
                copy = pltpu.make_async_copy(src, dst, recv.at[5])
            copy.start()

    for i in range(4):
        ud_copy(i).start()
    gather.middle()
    wo_gather = Gather(place, wo, slab.at[4:5], wo_send, wo_recv)
    ud_gather = Gather(place, ud, None, far_send, far_recv)
    gathers = (ud_gather, wo_gather)
    gather.last()

    pick_pair = push(
        context.at[0:first, core], context.at[0:first, core], pair_send.at[0], recv.at[1], place.dp(CORE), z
    )
    settle(context.at[0:first, core], recv.at[5])
    pick_pair.start()
    lead_copy = push(
        context.at[first:], context.at[first:], pair_send.at[1], recv.at[3], place.dp(CORE), z
    )

    @pl.when(core == 0)
    def _():
        settle(context.at[first:], recv.at[3])
        lead_copy.start()

    settle(columns(down), ud_recv.at[0])
    ud_copy(4).start()
    settle(columns(up), ud_recv.at[1])
    ud_copy(5).start()

    settle(all_ints, recv.at[2])
    seq = 4 * lax.div(d, 2) + z
    slot = slot_of(seq)
    odd = lax.rem(seq, micro)
    own, other = all_ints[lax.div(seq, micro)], all_ints[lax.div(slot, micro)]

    def pick(row, at):
        return jnp.sum(jnp.where(spot == at, row.astype(F32), 0.0), axis=1, keepdims=True)

    length = pick(own[2:3], odd)
    mem_valid = pick(other[2:3], micro + lax.rem(slot, micro))
    rank = jnp.where(odd == 0, own[0:1], own[1:2])
    seq_len = rank.shape[1]
    mem_total = key_ref.shape[1] - seq_len
    where = spot.astype(F32)
    hidden = jnp.int32(1 << 20)
    key_ref[:, :mem_total] = jnp.where(where >= mem_total - mem_valid, -1, hidden)
    key_ref[:, mem_total:] = jnp.where(where < length, rank, hidden)
    ranks = jnp.transpose(jnp.broadcast_to(rank.astype(F32), (8, seq_len)))
    thr_ref[...] = ranks[:, 0:1].astype(jnp.int32) + jnp.where(core == 0, 1, 0)

    settle(columns(z), recv.at[8])
    ud_copy(4).wait_recv()
    ud_copy(5).wait_recv()
    for i in (0, 1, 6, 7):
        for one in gathers:
            one.start(i)
    gather.wait(range(6, 14), ())
    settle(whole.at[:, own_rows, :], recv.at[6])
    keep_whole = pltpu.make_async_copy(whole, whole_out, local.at[1])
    keep_whole.start()

    keep_context = pltpu.make_async_copy(context, context_out, local.at[2])

    def before_stream():
        pick_pair.wait()

        @pl.when(core == 0)
        def _():
            lead_copy.wait_send()

        @pl.when(core == 1)
        def _():
            settle(context.at[first:], recv.at[3])
            settle(stream, recv.at[4])

        keep_context.start()

    def before_context():
        for one in gathers:
            one.after((0, 1), ((8,), (9,)))

    pltpu.make_async_copy(table_hbm, table, local.at[0]).wait()
    project_step(
        whole, context, stream, table, wb_ref, pb_ref, *outs, hooks=(before_stream, before_context)
    )
    settle(wo.at[:, own_rows, :], recv.at[7])
    gather.wait((), range(14))
    for one in gathers:
        one.wait(range(6, 10), (0, 1, 6, 7, 8, 9))
    keep_whole.wait()
    keep_context.wait()
    for i in range(4):
        stream_copy(i, "wait")
        mat_copy(i).wait_send()
    for i in range(6):
        ud_copy(i).wait_send()
    for copy in spread_copies + int_copies + pick_copies:
        copy.wait_send()


def enter(slots, seqs, mems, content, query, memory, table, orders, mats, upw, dnw, wb, pb):
    micro, part, width = content.shape
    rows = mats[0].shape[0]
    inner = upw.shape[1] * 4
    piece = part // 8
    klen, span, seq = 8 * part, table.shape[0], 4 * part
    vmem = pl.BlockSpec(memory_space=pltpu.VMEM)
    dma = lambda n: pltpu.SemaphoreType.DMA((n,))
    bf = lambda *shape: jax.ShapeDtypeStruct(shape, BF)
    return pl.pallas_call(
        enter_kernel,
        in_specs=[SMEM_SPEC] * 3 + [ANY_SPEC] * 4 + [vmem] * 10,
        out_specs=[vmem] * 8 + [ANY_SPEC] * 4,
        out_shape=[
            bf(klen, width),
            bf(klen, width),
            bf(span, width),
            bf(seq, width),
            bf(seq, width),
            bf(seq, width),
            jax.ShapeDtypeStruct((seq, 1), jnp.int32),
            jax.ShapeDtypeStruct((1, klen), jnp.int32),
            bf(4, 8 * rows, width),
            bf(32, 2, piece, width),
            bf(1, 8 * rows, width),
            bf(2, 8 * rows, inner),
        ],
        scratch_shapes=[
            pltpu.VMEM((8, seq), jnp.int32),
            pltpu.VMEM((8, 8, seq), jnp.int32),
            pltpu.VMEM((4, 8 * rows, width), BF),
            pltpu.VMEM((32, 2, piece, width), BF),
            pltpu.VMEM((seq, width), BF),
            pltpu.VMEM((span, width), BF),
            pltpu.VMEM((16, piece, width), BF),
            pltpu.VMEM((16, piece, width), BF),
            pltpu.VMEM((4, 5, rows * 3 // 2, 128), BF),
            pltpu.VMEM((5, rows, width), BF),
            dma(4),
            dma(4),
            dma(6),
            dma(4),
            dma(7),
            dma(7),
            dma(15),
            dma(4),
            dma(2),
            dma(14),
            dma(14),
            dma(14),
            dma(14),
            dma(14),
            dma(14),
            dma(9),
            dma(3),
        ],
        compiler_params=pltpu.CompilerParams(
            collective_id=1, has_side_effects=True, vmem_limit_bytes=LIMIT
        ),
        cost_estimate=pl.CostEstimate(flops=0, bytes_accessed=64 << 20, transcendentals=0),
        name="enter",
    )(
        slots,
        seqs,
        mems,
        content.reshape(micro, 4, 2, piece, width),
        query,
        memory,
        table,
        orders,
        *mats,
        upw,
        dnw,
        wb,
        pb,
    )


def head_lanes(array, head):
    lane = lax.broadcasted_iota(jnp.int32, array.shape, 1)
    return jnp.where((lane >= DH) == (head == 1), array, jnp.zeros_like(array))


def attend_forward_step(
    block, qw_ref, qp_ref, k_ref, v_ref, rel_ref, thr_ref, kr_ref, vec_ref, prob_ref
):
    rows, klen = qw_ref.shape[0], k_ref.shape[0]
    width = klen + block
    keys, values = k_ref[...], v_ref[...]
    for part in range(rows // block):
        at = slice(part * block, (part + 1) * block)
        first = rows - (part + 1) * block
        qw, qp = qw_ref[at, :], qp_ref[at, :]
        rel = rel_ref[first : first + width, :]
        seen = kr_ref[...] < thr_ref[at, :]
        vecs = []
        for head in range(2):
            raw = nt(head_lanes(qp, head), rel)
            moved = pltpu.roll(raw, 0, 1, stride=1, stride_axis=0)[:, block:]
            score = nt(head_lanes(qw, head), keys) + moved
            score = jnp.where(seen, score, -1e30)
            expo = jnp.exp(score - jnp.max(score, axis=1, keepdims=True))
            prob = (expo * (1.0 / jnp.sum(expo, axis=1, keepdims=True))).astype(BF)
            prob_ref[head, at, :] = prob
            vecs.append(nn(prob, values))
        lane = lax.broadcasted_iota(jnp.int32, vecs[0].shape, 1)
        vec_ref[at, :] = jnp.where(lane < DH, vecs[0], vecs[1]).astype(BF)


def attend_forward_kernel(block, wired, *refs):
    if not wired:
        attend_forward_step(block, *refs)
        return
    ins, (ctan, qtan) = refs[:7], refs[9:11]
    outs, (wo, ud, tangent) = refs[11:13], refs[13:16]
    out_send, out_recv, ud_send, ud_recv, tan_send, recv = refs[16:]
    step, steps = pl.program_id(0), pl.num_programs(0)
    place = Place()
    d, z, core = place.d, place.z, place.core
    gathers = (
        Gather(place, ud, None, ud_send, ud_recv),
        Gather(place, wo, None, out_send, out_recv),
    )
    part = ctan.shape[1]

    def tan_copy(i, act):
        j, kind = i // 2, i % 2
        to, dp = 2 * core + j, d - core + kind
        src = (ctan, qtan)[kind].at[j]
        dst = tangent.at[pl.ds(pl.multiple_of(z * part, 16), part), :]
        here = jnp.logical_and(dp == d, to == z)
        local = pltpu.make_async_copy(src, dst, recv.at[0])
        remote = push(src, dst, tan_send.at[i], recv.at[0], dp, to)
        if act == "start":
            pl.when(here)(local.start)
            pl.when(jnp.logical_not(here))(remote.start)
        else:
            pl.when(jnp.logical_not(here))(remote.wait_send)

    @pl.when(step == 0)
    def _():
        greet(near_partners(place))
        for gather in gathers:
            gather.start(2, 3)
        for gather in gathers:
            gather.start(4, 5)
        for i in range(4):
            tan_copy(i, "start")

    @pl.when(step == 4)
    def _():
        for gather in gathers:
            gather.after((2, 3), ((10,), (11,)))

    attend_forward_step(block, *ins, *outs)

    @pl.when(step == steps - 1)
    def _():
        for gather in gathers:
            gather.after((4, 5), ((12,), (13,)))
        for gather in gathers:
            gather.wait(range(10, 14), (2, 3, 4, 5) + tuple(range(10, 14)))
        settle(tangent, recv.at[0])
        for i in range(4):
            tan_copy(i, "wait")


def attend_forward(qw, qp, keys, values, rel, thr, key_rank, block, wires=()):
    rows, width = qw.shape
    klen, span = keys.shape[0], rel.shape[0]
    col = lambda count: pl.BlockSpec((count, PAIR), lambda p: (0, p))
    in_specs = [
        col(rows),
        col(rows),
        col(klen),
        col(klen),
        col(span),
        pl.BlockSpec((rows, 1), lambda p: (0, 0)),
        pl.BlockSpec((1, klen), lambda p: (0, 0)),
    ]
    out_specs = [col(rows), pl.BlockSpec((2, rows, klen), lambda p: (p, 0, 0))]
    out_shape = [
        jax.ShapeDtypeStruct((rows, width), BF),
        jax.ShapeDtypeStruct((width // DH, rows, klen), BF),
    ]
    params = dict(vmem_limit_bytes=LIMIT)
    scratch = []
    if wires:
        in_specs += [ANY_SPEC] * 4
        out_specs += [ANY_SPEC] * 3
        out_shape += [
            jax.ShapeDtypeStruct(wires[0].shape, BF),
            jax.ShapeDtypeStruct(wires[1].shape, BF),
            jax.ShapeDtypeStruct((rows, width), BF),
        ]
        scratch = [pltpu.SemaphoreType.DMA((n,)) for n in (14, 14, 14, 14, 4, 1)]
        params.update(collective_id=2, has_side_effects=True)
    return pl.pallas_call(
        functools.partial(attend_forward_kernel, block, bool(wires)),
        grid=(width // PAIR,),
        in_specs=in_specs,
        out_specs=out_specs,
        out_shape=out_shape,
        scratch_shapes=scratch,
        input_output_aliases={7: 2, 8: 3} if wires else {},
        compiler_params=pltpu.CompilerParams(**params),
        cost_estimate=pl.CostEstimate(
            flops=8 * rows * klen * width, bytes_accessed=16 << 20, transcendentals=12 * rows * klen
        ),
        name="attend_forward",
    )(qw, qp, keys, values, rel, thr, key_rank, *wires)


def attend_backward_kernel(block, wired, *refs):
    if not wired:
        attend_backward_step(block, *refs)
        return
    ins, (g_ud, near_ud, g_out, src) = refs[:7], refs[7:11]
    outs, grad_refs, home_refs = refs[11:16], refs[16:19], refs[19:21]
    rel_acc, home_send, home_recv = refs[21:24]
    refs = refs[24:]
    step, steps = pl.program_id(0), pl.num_programs(0)
    place = Place()
    count = len(refs) // 3
    held = [refs[m * count : (m + 1) * count] for m in range(3)]
    reduces = [
        Reduce(place, (g_ud.at[m : m + 1], near_ud.at[m : m + 1]), held[m], grad_refs[m], True)
        for m in range(2)
    ]
    out = Reduce(place, (g_out,), held[2], grad_refs[2])
    home = Homeward(place, src, home_refs, home_send, home_recv)

    @pl.when(step == 0)
    def _():
        greet(near_partners(place))
        for reduce in reduces:
            reduce.begin()
        out.begin()
        home.start()

    @pl.when(step == 1)
    def _():
        for reduce in reduces:
            reduce.middle()
        out.pairs()

    @pl.when(step == 3)
    def _():
        reduces[0].late()

    @pl.when(step == 4)
    def _():
        reduces[1].late()
        out.middle()

    @pl.when(step == 5)
    def _():
        out.late()

    attend_backward_step(block, *ins, *outs, rel_acc)

    @pl.when(step == steps - 1)
    def _():
        for reduce in reduces:
            reduce.end()
        out.end()
        home.end()


def attend_backward_step(
    block,
    prob_ref,
    gvec_ref,
    qw_ref,
    qp_ref,
    k_ref,
    v_ref,
    rel_ref,
    dproj_ref,
    dk_ref,
    dv_ref,
    drel_ref,
    bias_ref,
    rel_acc,
):
    rows, klen = qw_ref.shape[0], k_ref.shape[0]
    width = klen + block
    keys, values = k_ref[...], v_ref[...]
    row = lax.broadcasted_iota(jnp.int32, (block, block), 0)
    col = lax.broadcasted_iota(jnp.int32, (block, block), 1)
    mirror = (row + col == block - 1).astype(BF)
    rel_acc[...] = jnp.zeros_like(rel_acc)
    d_keys, d_values = [None, None], [None, None]
    word_sum = jnp.zeros((1, PAIR), F32)
    pos_sum = jnp.zeros((1, PAIR), F32)
    for part in range(rows // block):
        at = slice(part * block, (part + 1) * block)
        first = rows - (part + 1) * block
        gvec, qw = gvec_ref[at, :], qw_ref[at, :]
        gvec_t = jnp.transpose(gvec.astype(F32)).astype(BF)
        qw_t = jnp.transpose(qw.astype(F32)).astype(BF)
        qp_t = jnp.transpose(nn(mirror, qp_ref[at, :])).astype(BF)
        rel = rel_ref[first : first + width, :]
        word_parts, pos_parts = [], []
        for head in range(2):
            own = slice(head * DH, (head + 1) * DH)
            prob = prob_ref[head, at, :]
            d_prob = nt(head_lanes(gvec, head), values)
            weight = prob.astype(F32)
            inner = jnp.sum(weight * d_prob, axis=1, keepdims=True)
            g_sum = (weight * (d_prob - inner) * 0.125).astype(BF)
            dv = nn(gvec_t[own, :], prob)
            dk = nn(qw_t[own, :], g_sum)
            d_values[head] = dv if part == 0 else d_values[head] + dv
            d_keys[head] = dk if part == 0 else d_keys[head] + dk
            turned = nn(mirror, g_sum)
            padded = jnp.concatenate([jnp.zeros((block, block), F32), turned], axis=1)
            moved = pltpu.roll(padded, width - block + 1, 1, stride=1, stride_axis=0).astype(BF)
            word_parts.append(nn(turned.astype(BF), keys))
            pos_parts.append(nn(moved, rel))
            rel_acc[own, first : first + width] += nn(qp_t[own, :], moved)
        lane = lax.broadcasted_iota(jnp.int32, word_parts[0].shape, 1)
        word = jnp.where(lane < DH, word_parts[0], word_parts[1])
        pos = jnp.where(lane < DH, pos_parts[0], pos_parts[1])
        word_sum = word_sum + jnp.sum(word, axis=0, keepdims=True)
        pos_sum = pos_sum + jnp.sum(pos, axis=0, keepdims=True)
        dproj_ref[at, :] = nn(mirror, (word + pos).astype(BF)).astype(BF)
    for head in range(2):
        own = slice(head * DH, (head + 1) * DH)
        dv_ref[own, :] = d_values[head].astype(BF)
        dk_ref[own, :] = (8.0 * d_keys[head]).astype(BF)
    drel_ref[...] = (8.0 * rel_acc[...]).astype(BF)
    bias_ref[0:1, :] = word_sum
    bias_ref[1:2, :] = pos_sum


def attend_backward(prob, gvec, qw, qp, keys, values, rel, block, wires=()):
    rows, width = qw.shape
    klen, span = keys.shape[0], rel.shape[0]
    col = lambda count: pl.BlockSpec((count, PAIR), lambda p: (0, p))
    rowb = lambda count: pl.BlockSpec((PAIR, count), lambda p: (p, 0))
    in_specs = [
        pl.BlockSpec((2, rows, klen), lambda p: (p, 0, 0)),
        col(rows),
        col(rows),
        col(rows),
        col(klen),
        col(klen),
        col(span),
    ]
    out_specs = [col(rows), rowb(klen), rowb(klen), rowb(span), col(2)]
    out_shape = [
        jax.ShapeDtypeStruct((rows, width), BF),
        jax.ShapeDtypeStruct((width, klen), BF),
        jax.ShapeDtypeStruct((width, klen), BF),
        jax.ShapeDtypeStruct((width, span), BF),
        jax.ShapeDtypeStruct((2, width), F32),
    ]
    scratch = [pltpu.VMEM((PAIR, span), F32)]
    params = dict(vmem_limit_bytes=LIMIT)
    if wires:
        inner, mine = wires[0].shape[3], width // 8
        in_specs += [ANY_SPEC] * 4
        out_specs += [pl.BlockSpec(memory_space=pltpu.VMEM)] * 3 + [ANY_SPEC] * 2
        out_shape += [jax.ShapeDtypeStruct((mine, inner // 4), F32)] * 2
        out_shape += [jax.ShapeDtypeStruct((mine, width // 4), F32)]
        out_shape += [jax.ShapeDtypeStruct((2, rows // 4, width), BF)] * 2
        scratch += [pltpu.SemaphoreType.DMA((4,)), pltpu.SemaphoreType.DMA((2,))]
        scratch += 2 * Reduce.scratch(1, 1, mine, inner, True) + Reduce.scratch(1, 1, mine, width)
        params.update(collective_id=3, has_side_effects=True)
    return pl.pallas_call(
        functools.partial(attend_backward_kernel, block, bool(wires)),
        grid=(width // PAIR,),
        in_specs=in_specs,
        out_specs=out_specs,
        out_shape=out_shape,
        scratch_shapes=scratch,
        compiler_params=pltpu.CompilerParams(**params),
        cost_estimate=pl.CostEstimate(
            flops=16 * rows * klen * width, bytes_accessed=20 << 20, transcendentals=0
        ),
        name="attend_backward",
    )(prob, gvec, qw, qp, keys, values, rel, *wires)


def norm_parts(value):
    center = value - jnp.mean(value, axis=1, keepdims=True)
    scale = lax.rsqrt(jnp.mean(center * center, axis=1, keepdims=True) + EPS)
    return center * scale, scale


def norm_pull(normed, scale, err):
    inner = jnp.mean(err * normed, axis=1, keepdims=True)
    return (err - jnp.mean(err, axis=1, keepdims=True) - normed * inner) * scale


def sum_rows(value):
    return jnp.sum(value, axis=0, keepdims=True)


def feed_kernel(steps, wired, *refs):
    (
        ud_hbm,
        wo_hbm,
        vec_ref,
        x_ref,
        tan_ref,
        upb_ref,
        dnb_ref,
        g1_ref,
        s1_ref,
        g2_ref,
        s2_ref,
        out_ref,
        dmix_ref,
        gvec_ref,
        go_ref,
        gud_ref,
        gupb_ref,
        small_ref,
        *refs,
    ) = refs
    near_ref, *refs = refs if wired else (None, *refs)
    (
        ud_ref,
        wo_ref,
        n1_ref,
        r1_ref,
        fb_ref,
        fbt_ref,
        acc_ref,
        act_ref,
        slope_ref,
        gd_ref,
        gdt_ref,
        sems,
        *pair_refs,
    ) = refs
    step = pl.program_id(0)
    chunk = act_ref.shape[2]
    row = lambda ref: ref[...].reshape(1, -1)
    cols = pl.ds(pl.multiple_of(lax.rem(step, steps) * chunk, chunk), chunk)

    if wired:
        own_ref, pair_ref, sum_ref, send, recv, keep, move_send, move_recv = pair_refs
        place = Place()
        rows = pair_ref.shape[2]

        def span(c):
            return pl.ds(pl.multiple_of(c * chunk, chunk), chunk)

        def block(bits):
            return pl.ds(pl.multiple_of(place.dp(bits) * rows, 16), rows)

        def pair_copy(c, j):
            slot = lax.rem(c, 2)
            return push(
                own_ref.at[slot, :, block(chip_bits(j) | CORE), :],
                pair_ref.at[:, j, :, span(c)],
                send.at[slot, j],
                recv.at[c],
                place.dp(CORE),
                place.z,
            )

        def keep_copy(c):
            return pltpu.make_async_copy(sum_ref.at[c], gud_ref.at[:, :, :, span(c)], keep.at[c])

        def move(c, i):
            j, h, to, where = Reduce.MOVES[i]
            return push(
                sum_ref.at[c, :, j, h * (rows // 2) : (h + 1) * (rows // 2), :],
                near_ref.at[:, h, where, :, span(c)],
                move_send.at[c, i],
                move_recv.at[c],
                place.dp(to),
                place.z,
            )

        def join(c):
            slot = lax.rem(c, 2)
            settle(pair_ref.at[:, :, :, span(c)], recv.at[c])
            for j in (3, 1, 2, 0):
                mine = own_ref[slot, :, block(chip_bits(j)), :].astype(F32)
                sum_ref[c, :, j] = (mine + pair_ref[:, j, :, span(c)].astype(F32)).astype(BF)
            for i in range(4):
                move(c, i).start()
            keep_copy(c).start()

        def send_wait(c):
            for j in range(4):
                pair_copy(c, j).wait_send()

        @pl.when(step == 0)
        def _():
            greet([(place.dp(r), place.z) for r in (CORE, XBIT, YBIT)])

    @pl.when(step == 0)
    def _():
        wo_copy = pltpu.make_async_copy(wo_hbm, wo_ref, sems.at[0])
        ud_copy = pltpu.make_async_copy(ud_hbm, ud_ref, sems.at[1])
        wo_copy.start()
        ud_copy.start()
        wo_copy.wait()
        normed, scale = norm_parts(nt(vec_ref[...], wo_ref[0]) + x_ref[...].astype(F32))
        n1_ref[...] = normed
        r1_ref[...] = scale
        first = normed * row(g1_ref) + row(s1_ref)
        fb_ref[...] = first.astype(BF)
        fbt_ref[...] = jnp.transpose(first).astype(BF)
        acc_ref[...] = first + row(dnb_ref)
        ud_copy.wait()

    @pl.when(step < steps)
    def _():
        upper = nn(fb_ref[...], ud_ref[0, :, cols]) + row(upb_ref)
        square = upper * upper
        root = 0.7978845608028654
        bend = jnp.tanh(root * (upper + 0.044715 * (square * upper)))
        half = 0.5 * (1.0 + bend)
        act = (upper * half).astype(BF)
        act_ref[step] = act
        slope_ref[step] = half + 0.5 * upper * (1.0 - bend * bend) * (
            root + (3 * 0.044715 * root) * square
        )
        acc_ref[...] += nt(act, ud_ref[1, :, cols])

    @pl.when(step == steps - 1)
    def _():
        normed, scale = norm_parts(acc_ref[...])
        out_ref[...] = (normed * row(g2_ref) + row(s2_ref)).astype(BF)
        tan = tan_ref[...].astype(F32)
        d_down = norm_pull(normed, scale, tan * row(g2_ref))
        small_ref[0:1, :] = sum_rows(d_down)
        small_ref[3:4, :] = sum_rows(tan * normed)
        small_ref[4:5, :] = sum_rows(tan)
        gd_ref[...] = d_down.astype(BF)
        gdt_ref[...] = jnp.transpose(d_down).astype(BF)
        acc_ref[...] = d_down

    @pl.when(step >= steps)
    def _():
        at = step - steps
        d_up = nn(gd_ref[...], ud_ref[1, :, cols]) * slope_ref[at]
        gupb_ref[...] = sum_rows(d_up)
        g_up = d_up.astype(BF)
        acc_ref[...] += nt(g_up, ud_ref[0, :, cols])
        if not wired:
            gud_ref[0] = nn(fbt_ref[...], g_up).astype(BF)
            gud_ref[1] = nn(gdt_ref[...], act_ref[at]).astype(BF)
            return
        pl.when(at >= 2)(lambda: send_wait(at - 2))
        slot = lax.rem(at, 2)
        own_ref[slot, 0] = nn(fbt_ref[...], g_up).astype(BF)
        own_ref[slot, 1] = nn(gdt_ref[...], act_ref[at]).astype(BF)
        for j in range(4):
            pair_copy(at, j).start()
        pl.when(at >= 1)(lambda: join(at - 1))

    @pl.when(step == 2 * steps - 1)
    def _():
        d_first, normed = acc_ref[...], n1_ref[...]
        small_ref[1:2, :] = sum_rows(d_first * normed)
        small_ref[2:3, :] = sum_rows(d_first)
        d_mixed = norm_pull(normed, r1_ref[...], d_first * row(g1_ref))
        dmix_ref[...] = d_mixed
        gvec_ref[...] = nn(d_mixed.astype(BF), wo_ref[0]).astype(BF)
        gdt_ref[...] = jnp.transpose(d_mixed).astype(BF)
        go_ref[...] = nn(gdt_ref[...], vec_ref[...]).astype(BF)
        if wired:
            join(steps - 1)
            for c in (steps - 2, steps - 1):
                send_wait(c)
            for c in range(steps):
                keep_copy(c).wait()
                settle(near_ref.at[:, :, :, :, span(c)], move_recv.at[c])
                for i in range(4):
                    move(c, i).wait_send()


def feed(ud, wo, vec, x, tan, upb, vecs, wired):
    rows, width = vec.shape
    inner = upb.shape[0]
    chunk = 512
    steps = inner // chunk
    whole = lambda a, b: pl.BlockSpec((a, b), lambda i: (0, 0))
    late = lambda i: jnp.maximum(i - steps, 0)
    grads = pl.BlockSpec((2, width, chunk), lambda i: (0, 0, late(i)))
    grad_shape = (2, width, inner)
    params = dict(vmem_limit_bytes=LIMIT)
    scratch, near_shape = [], []
    if wired:
        mine = width // 8
        grads, grad_shape = ANY_SPEC, (2, 4, mine, inner)
        scratch = [
            pltpu.VMEM((2, 2, width, chunk), BF),
            pltpu.VMEM(grad_shape, BF),
            pltpu.VMEM((steps, 2, 4, mine, chunk), BF),
            pltpu.SemaphoreType.DMA((2, 4)),
            pltpu.SemaphoreType.DMA((steps,)),
            pltpu.SemaphoreType.DMA((steps,)),
            pltpu.SemaphoreType.DMA((steps, 4)),
            pltpu.SemaphoreType.DMA((steps,)),
        ]
        near_shape = [jax.ShapeDtypeStruct((2, 2, 2, mine // 2, inner), BF)]
        params.update(collective_id=6, has_side_effects=True)
    return pl.pallas_call(
        functools.partial(feed_kernel, steps, wired),
        grid=(2 * steps,),
        in_specs=[ANY_SPEC] * 2
        + [whole(rows, width)] * 3
        + [pl.BlockSpec((chunk,), lambda i: (lax.rem(i, steps),))]
        + [pl.BlockSpec((width,), lambda i: (0,))] * 5,
        out_specs=[
            whole(rows, width),
            whole(rows, width),
            whole(rows, width),
            whole(width, width),
            grads,
            pl.BlockSpec((1, chunk), lambda i: (0, late(i))),
            whole(8, width),
        ]
        + [ANY_SPEC] * len(near_shape),
        out_shape=[
            jax.ShapeDtypeStruct((rows, width), BF),
            jax.ShapeDtypeStruct((rows, width), F32),
            jax.ShapeDtypeStruct((rows, width), BF),
            jax.ShapeDtypeStruct((width, width), BF),
            jax.ShapeDtypeStruct(grad_shape, BF),
            jax.ShapeDtypeStruct((1, inner), F32),
            jax.ShapeDtypeStruct((8, width), F32),
        ]
        + near_shape,
        scratch_shapes=[
            pltpu.VMEM((2, width, inner), BF),
            pltpu.VMEM((1, width, width), BF),
            pltpu.VMEM((rows, width), F32),
            pltpu.VMEM((rows, 1), F32),
            pltpu.VMEM((rows, width), BF),
            pltpu.VMEM((width, rows), BF),
            pltpu.VMEM((rows, width), F32),
            pltpu.VMEM((steps, rows, chunk), BF),
            pltpu.VMEM((steps, rows, chunk), F32),
            pltpu.VMEM((rows, width), BF),
            pltpu.VMEM((width, rows), BF),
            pltpu.SemaphoreType.DMA((2,)),
        ]
        + scratch,
        compiler_params=pltpu.CompilerParams(**params),
        cost_estimate=pl.CostEstimate(
            flops=12 * rows * width * inner, bytes_accessed=36 << 20, transcendentals=rows * inner
        ),
        name="feed",
    )(ud, wo, vec, x, tan, upb, *vecs)


def project_step(
    w_ref,
    ctx_ref,
    q_ref,
    table_ref,
    wb_ref,
    pb_ref,
    k_ref,
    v_ref,
    rel_ref,
    qw_ref,
    qp_ref,
    x_ref,
    hooks=(),
):
    lead = lax.rem(lax.axis_index("dp"), 2) == 0
    flat = lambda ref: jnp.concatenate([ref[h : h + 1, :] for h in range(ref.shape[0])], axis=1)
    word_bias, pos_bias = flat(wb_ref), flat(pb_ref)
    klen, width = k_ref.shape
    back = klen - q_ref.shape[0]

    def context_rows(start):
        at = pl.ds(lax.div(start, 32), block // 32)
        return ctx_ref[at].reshape(block, width)

    block = 256

    def loop(count, step):
        def run(i, carry):
            step(pl.ds(pl.multiple_of(i * block, block), block))
            return carry

        lax.fori_loop(0, count // block, run, 0)

    def context_step(at):
        rows = context_rows(at.start)
        k_ref[at, :] = nn(rows, w_ref[0]).astype(BF)
        v_ref[at, :] = nn(rows, w_ref[1]).astype(BF)

    def stream_step(at):
        x_ref[at, :] = jnp.where(lead, context_rows(at.start + back), q_ref[at, :])
        proj = nn(x_ref[at, :], w_ref[2])
        qw_ref[at, :] = (0.125 * (proj + word_bias).astype(BF).astype(F32)).astype(BF)
        qp_ref[at, :] = (0.125 * (proj + pos_bias).astype(BF).astype(F32)).astype(BF)

    def table_step(at):
        rel_ref[at, :] = nn(table_ref[at, :], w_ref[3]).astype(BF)

    loop(table_ref.shape[0], table_step)
    if hooks:
        hooks[0]()
    loop(q_ref.shape[0], stream_step)
    if hooks:
        hooks[1]()
    loop(klen, context_step)


def project(mats, context, query, table, wb, pb):
    rows, width = query.shape
    klen, span = context.shape[0], table.shape[0]
    vmem = pl.BlockSpec(memory_space=pltpu.VMEM)
    return pl.pallas_call(
        project_step,
        in_specs=[vmem] * 6,
        out_specs=[vmem] * 6,
        out_shape=[
            jax.ShapeDtypeStruct((klen, width), BF),
            jax.ShapeDtypeStruct((klen, width), BF),
            jax.ShapeDtypeStruct((span, width), BF),
            jax.ShapeDtypeStruct((rows, width), BF),
            jax.ShapeDtypeStruct((rows, width), BF),
            jax.ShapeDtypeStruct((rows, width), BF),
        ],
        compiler_params=pltpu.CompilerParams(vmem_limit_bytes=LIMIT),
        cost_estimate=pl.CostEstimate(
            flops=2 * (2 * klen + rows + span) * width * width,
            bytes_accessed=20 << 20,
            transcendentals=0,
        ),
        name="project",
    )(mats, context.reshape(klen // 32, 2, 16, width), query, table, wb, pb)


def weight_grads_kernel(xt_ref, ct_ref, tt_ref, dp_ref, dk_ref, dv_ref, dr_ref, g_ref):
    g_ref[0] = nt(ct_ref[...], dk_ref[...]).astype(BF)
    g_ref[1] = nt(ct_ref[...], dv_ref[...]).astype(BF)
    g_ref[2] = nn(xt_ref[...], dp_ref[...]).astype(BF)
    g_ref[3] = nt(tt_ref[...], dr_ref[...]).astype(BF)


def weight_grads(x_t, ctx_t, table_t, d_proj, dk_t, dv_t, drel_t):
    width, rows = x_t.shape
    klen, span = ctx_t.shape[1], table_t.shape[1]
    chunk = 256
    whole = lambda a, b: pl.BlockSpec((a, b), lambda i: (0, 0))
    rowb = lambda b: pl.BlockSpec((chunk, b), lambda i: (i, 0))
    return pl.pallas_call(
        weight_grads_kernel,
        grid=(width // chunk,),
        in_specs=[
            whole(width, rows),
            whole(width, klen),
            whole(width, span),
            pl.BlockSpec((rows, chunk), lambda i: (0, i)),
            rowb(klen),
            rowb(klen),
            rowb(span),
        ],
        out_specs=pl.BlockSpec((4, width, chunk), lambda i: (0, 0, i)),
        out_shape=jax.ShapeDtypeStruct((4, width, width), BF),
        compiler_params=pltpu.CompilerParams(vmem_limit_bytes=LIMIT),
        cost_estimate=pl.CostEstimate(
            flops=2 * (rows + 2 * klen + span) * width * width,
            bytes_accessed=20 << 20,
            transcendentals=0,
        ),
        name="weight_grads",
    )(x_t, ctx_t, table_t, d_proj, dk_t, dv_t, drel_t)


def flip(arr, bit):
    return lax.ppermute(arr, "dp", [(i, i ^ bit) for i in range(lax.axis_size("dp"))])


def scatter_sum(grads):
    mine = lax.psum_scatter(grads, "dp", scatter_dimension=1, tiled=True)
    return lax.psum_scatter(mine, "tensor", scatter_dimension=2, tiled=True).astype(F32)


def body(
    content_stream,
    query_stream,
    memory,
    content_tangent,
    query_tangent,
    seq_lengths,
    factor_order,
    memory_lengths,
    slot_sequence,
    query_weight,
    key_weight,
    value_weight,
    pos_weight,
    out_weight,
    up_weight,
    up_bias,
    down_weight,
    down_bias,
    word_bias,
    pos_bias,
    first_gain,
    first_shift,
    second_gain,
    second_shift,
):
    groups, tensors = lax.axis_size("dp"), lax.axis_size("tensor")
    micro, part_len, width = content_stream.shape
    mem_part = memory.shape[1]
    seq_len, mem_total = part_len * tensors, mem_part * tensors
    klen, span = mem_total + seq_len, mem_total + 2 * seq_len
    count = micro * groups
    here, lane = lax.axis_index("dp"), lax.axis_index("tensor")
    core = here % 2
    lead = core == 0
    block = 256
    assert 2 * micro == tensors

    def swap(arr):
        return flip(arr, CORE)

    def to_unit(first, second):
        got = swap(jnp.where(lead, second, first))
        low = jnp.where(lead, first, got)
        high = jnp.where(lead, got, second)
        both = jnp.concatenate([low, high], 0)
        both = lax.all_to_all(both, "tensor", split_axis=0, concat_axis=0, tiled=True)
        return both.reshape(seq_len, width)

    def from_unit(arr):
        both = arr.reshape(tensors, part_len, width)
        both = lax.all_to_all(both, "tensor", split_axis=0, concat_axis=0, tiled=True)
        low, high = both[:micro], both[micro:]
        got = swap(jnp.where(lead, high, low))
        return jnp.where(lead, low, got), jnp.where(lead, got, high)

    seq_id = (here // 2) * tensors + lane
    mats = [key_weight, value_weight, query_weight, pos_weight, out_weight]
    table = jnp.asarray(reversed_table(span, klen, width))
    wires = ()
    if groups == 8:
        keys, values, rel, q_word, q_pos, stream, thr, key_rank, weights, context, *wires = enter(
            slot_sequence,
            seq_lengths,
            memory_lengths,
            content_stream,
            query_stream,
            memory,
            table,
            factor_order,
            mats,
            up_weight,
            down_weight,
            word_bias,
            pos_bias,
        )
        wires += [content_tangent, query_tangent]
        context = context.reshape(klen, width)
    else:
        ids = jnp.arange(count, dtype=jnp.int32)
        slot_of = jnp.sum(jnp.where(slot_sequence[None, :] == ids[:, None], ids[None, :], 0), axis=1)
        counts = jnp.concatenate([seq_lengths, memory_lengths])
        slot = slot_of[seq_id]
        lengths = lax.all_gather(counts, "dp", axis=0, tiled=False)
        orders = lax.all_gather(factor_order, "dp", axis=0, tiled=False)[seq_id // micro]
        stream = to_unit(content_stream, query_stream)
        content, query = jnp.where(lead, stream, swap(stream)), stream
        tangent = to_unit(content_tangent, query_tangent)
        piece = mem_part // groups
        spread = lax.all_to_all(
            memory.reshape(micro, groups, piece, width), "dp", split_axis=1, concat_axis=1, tiled=True
        )
        spread = spread.transpose(1, 0, 2, 3).reshape(count, piece, width)
        spread = jnp.take(spread, slot_of, axis=0)
        spread = spread.reshape(groups // 2, tensors, 2, piece // 2, width).transpose(0, 2, 1, 3, 4)
        spread = lax.all_to_all(
            spread.reshape(groups, tensors, piece // 2, width),
            "dp",
            split_axis=0,
            concat_axis=0,
            tiled=True,
        )
        spread = lax.all_to_all(spread, "tensor", split_axis=1, concat_axis=1, tiled=True)
        got = swap(spread)
        mem_rows = jnp.stack([jnp.where(lead, spread, got), jnp.where(lead, got, spread)])
        mem_rows = mem_rows.transpose(2, 1, 0, 3, 4).reshape(mem_total, width)
        context = jnp.concatenate([mem_rows, content], 0)

        def whole(mat):
            mat = lax.all_gather(mat, "tensor", axis=1, tiled=True)
            return lax.all_gather(mat, "dp", axis=0, tiled=True)

        weights = jnp.stack([whole(mat) for mat in mats[:4]])
        wo = whole(out_weight)[None]
        ud = jnp.stack([whole(up_weight), whole(down_weight)])
        keys, values, rel, q_word, q_pos, stream = project(
            weights, context, query, table, word_bias, pos_bias
        )
        length = lengths[seq_id // micro, seq_id % micro]
        mem_valid = lengths[slot // micro, micro + slot % micro]
        rank = orders[seq_id % micro]
        key_pos = jnp.arange(klen, dtype=jnp.int32)
        hidden = jnp.int32(1 << 20)
        mem_rank = jnp.where(key_pos[:mem_total] >= mem_total - mem_valid, -1, hidden)
        own_rank = jnp.where(key_pos[:seq_len] < length, rank, hidden)
        key_rank = jnp.concatenate([mem_rank, own_rank])[None, :]
        thr = (rank + jnp.where(lead, 1, 0))[:, None]

    vec, prob, *arrived = attend_forward(
        q_word, q_pos, keys, values, rel, thr, key_rank, block, wires
    )
    if wires:
        wo, ud, tangent = arrived
    out, d_mixed, g_vec, g_out, g_ud, g_upb, small, *near = feed(
        ud,
        wo,
        vec,
        stream,
        tangent,
        up_bias,
        (down_bias, first_gain, first_shift, second_gain, second_shift),
        groups == 8,
    )
    backward = (prob, g_vec, q_word, q_pos, keys, values, rel, block)
    if groups == 8:
        d_proj, dk_t, dv_t, drel_t, biases, grad_up, grad_down, grad_out, content_out, query_out = (
            attend_backward(*backward, (g_ud, *near, g_out[None], out))
        )
    else:
        d_proj, dk_t, dv_t, drel_t, biases = attend_backward(*backward)
        content_out, query_out = from_unit(out)
        grad_up, grad_down = scatter_sum(g_ud)
    small = jnp.concatenate([g_upb.reshape(-1), small[:5].reshape(-1), biases.reshape(-1)])
    inner = up_bias.shape[0]
    table_t = jnp.asarray(np.ascontiguousarray(reversed_table(span, klen, width).T))
    if groups == 8:
        small = jnp.pad(small, (0, -small.shape[0] % 1024)).reshape(-1, 128)
        arrays = [stream, d_proj, context, dk_t, dv_t, weights, table_t, drel_t]
        (
            grad_key,
            grad_value,
            grad_query,
            grad_pos,
            content_grad,
            query_grad,
            small,
        ) = finish(arrays, d_mixed, small)
        arrays = [content_out, query_out, content_grad, query_grad, grad_query, grad_key]
        arrays += [grad_value, grad_pos, grad_out, grad_up, grad_down]
        *arrays, up_sum, down_sum, a1, b1, a2, b2, word_sum, pos_sum = emit(
            small, arrays, inner, width
        )
        return *arrays[:10], up_sum, arrays[10], down_sum, word_sum, pos_sum, a1, b1, a2, b2
    else:
        d_context = tt(dk_t[:, mem_total:], weights[0]) + tt(dv_t[:, mem_total:], weights[1])
        partner = swap(d_context.astype(BF)).astype(F32)
        d_stream = d_mixed + nt(d_proj, weights[2]) + jnp.where(lead, d_context + partner, 0.0)
        content_grad, query_grad = from_unit(d_stream.astype(BF))
        grad_key, grad_value, grad_query, grad_pos = scatter_sum(
            weight_grads(jnp.transpose(stream), jnp.transpose(context), table_t, d_proj, dk_t, dv_t, drel_t)
        )
        (grad_out,) = scatter_sum(g_out[None])
        small = lax.psum(small, ("dp", "tensor"))
    rest = small[inner:].reshape(7, width)
    return (
        content_out,
        query_out,
        content_grad,
        query_grad,
        grad_query,
        grad_key,
        grad_value,
        grad_pos,
        grad_out,
        grad_up,
        small[:inner],
        grad_down,
        rest[0],
        rest[5].reshape(HEADS, DH),
        rest[6].reshape(HEADS, DH),
        rest[1],
        rest[2],
        rest[3],
        rest[4],
    )


def solution(mesh):
    rows = P("dp", "tensor", None)
    mat = P("dp", "tensor")
    return jax.shard_map(
        body,
        mesh=mesh,
        in_specs=(rows,) * 5
        + (P("dp"), P("dp", None), P("dp"), P())
        + (mat,) * 6
        + (P(), mat)
        + (P(),) * 7,
        out_specs=(rows,) * 4 + (mat,) * 6 + (P(), mat) + (P(),) * 7,
        check_vma=False,
    )
```
